32 devices in a mesh: rep: 8 (over y, x, core), shard: 4 (over z).
Axes of the slice: x: 2, y: 2, z: 4, core: 2. Of those that a mesh axis runs over, the one named last changes fastest.
Arguments:
- tokens: bfloat16 [2, 8192, 2048], P(None, ('rep', 'shard')), may hold values from -6 to 6
- cotangent: bfloat16 [2, 8192, 2048], P(None, ('rep', 'shard')), may hold values from -6 to 6
- lengths: int32 [2, 8, 2], P(None, 'rep'), may hold values from 1 to 768, 1024 in all within a row
- decay_rates: float32 [16], replicated, may hold values from 0.00048828125 to 0.05
- w_query: bfloat16 [2048, 2048], P('shard'), may hold values from -0.125 to 0.125
- w_key: bfloat16 [2048, 2048], P('shard'), may hold values from -0.125 to 0.125
- w_value: bfloat16 [2048, 2048], P('shard'), may hold values from -0.125 to 0.125
- w_gate: bfloat16 [2048, 2048], P('shard'), may hold values from -0.125 to 0.125
- w_out: bfloat16 [2048, 2048], P('shard'), may hold values from -0.125 to 0.125
- w_one: bfloat16 [2048, 5632], P('shard'), may hold values from -0.125 to 0.125
- w_two: bfloat16 [2048, 5632], P('shard'), may hold values from -0.125 to 0.125
- w_down: bfloat16 [2048, 5632], P('shard'), may hold values from -0.078125 to 0.078125
Outputs:
- output: bfloat16 [2, 8192, 2048], P(None, ('rep', 'shard'))
- input_grad: bfloat16 [2, 8192, 2048], P(None, ('rep', 'shard'))
- grad_query: float32 [2048, 2048], P('shard')
- grad_key: float32 [2048, 2048], P('shard')
- grad_value: float32 [2048, 2048], P('shard')
- grad_gate: float32 [2048, 2048], P('shard')
- grad_out: float32 [2048, 2048], P('shard')
- grad_one: float32 [2048, 5632], P('shard')
- grad_two: float32 [2048, 5632], P('shard')
- grad_down: float32 [2048, 5632], P('shard')
The draws below stay inside these ranges and needn't reach their ends.
Inputs may be any that keep to these rules, and one draw needn't show every extreme that they name: Each row of lengths sums to 1024, and its largest entry is at most 768.
All inputs are finite; a program needn't handle non-finite values.
Results may differ from the reference program's by a relative error of at most 0.022.
Values may be sent and summed in bfloat16 or wider, within the bound.
No kernel may reach another device: no remote copies, remote signals or barrier semaphores. Data moves between devices by JAX's collectives and lax.ppermute only.
A program may use at most 640 MiB of HBM per device.

```python
import math
import jax
import jax.numpy as jnp
import numpy as np
from jax import lax

D = 2048
FF = 5632
HEADS = 16
HEAD_DIM = 128
STREAM = 1024
MB = 2
SEQS = 2
TOKENS = 8192
N_REP = 8


def steps_of(stream_key, shape, split, smallest, largest):
    gain, own = 1.0, jax.random.fold_in(stream_key, 6)
    for position, parts in split:
        draws = jnp.exp(jax.random.uniform(jax.random.fold_in(own, position), (parts,), jnp.float32, smallest / len(split), largest / len(split)))
        gain = gain * jnp.repeat(draws, shape[position] // parts).reshape([-1 if axis == position else 1 for axis in range(len(shape))])
    return gain


def split_up(amount, total, limit, skew):
    portions = [(1 << 20) // math.isqrt(standing ** skew) + 1 for standing in range(2, amount + 1)]
    rest, counts = total - limit - (amount - 1), [1] * (amount - 1)
    while rest > 0:
        free = [i for i in range(amount - 1) if counts[i] < limit]
        mass, budget = sum([portions[i] for i in free]), rest
        for i in free:
            extra = min(limit - counts[i], max(1, budget * portions[i] // mass), rest)
            counts[i] = counts[i] + extra
            rest = rest - extra
    return np.array([limit] + counts)


def uneven_parts(own_key, count, total, reach, skew):
    if count == 2:
        one = jax.random.randint(own_key, (), max(1, total - reach), min(reach, total - 1) + 1)
        return jnp.stack([one, total - one])
    sizes = jnp.asarray(split_up(count, total, reach, skew), jnp.int32)
    twos = (count - 1) // 2
    donor, receiver = sizes[1:1 + 2 * twos:2], sizes[2:2 + 2 * twos:2]
    slack = jnp.minimum(donor - 1, reach - receiver)
    passed = jax.random.randint(jax.random.fold_in(own_key, 1), (twos,), 0, 1 << 20) % (slack + 1)
    sizes = sizes.at[1:1 + 2 * twos:2].set(donor - passed).at[2:2 + 2 * twos:2].set(receiver + passed)
    return sizes[jax.random.permutation(jax.random.fold_in(own_key, 2), count)]


def normal_values(rng, shape, scale, reach, shards=(), held_as=jnp.bfloat16):
    values = scale * jax.random.normal(rng, shape, jnp.float32)
    if shards:
        values = values * steps_of(rng, shape, shards, -0.22, 0.18)
    return jnp.clip(values, -reach, reach).astype(held_as)


def setup_inputs(seed: int = 0) -> dict:
    seeds = jax.random.split(jax.random.key(seed), 13)
    return {
        "tokens": normal_values(seeds[0], (MB, TOKENS, D), 1.0, 6.0, ((1, 32),)),
        "cotangent": normal_values(seeds[1], (MB, TOKENS, D), 1.0, 6.0, ((1, 32),)),
        "lengths": jax.vmap(lambda own: uneven_parts(own, SEQS, STREAM, STREAM * 3 // 4, 2))(jax.random.split(seeds[2], MB * N_REP)).reshape((MB, N_REP, SEQS)).astype(jnp.int32),
        "decay_rates": jnp.clip(jnp.exp(jax.random.uniform(seeds[3], (HEADS,), jnp.float32, math.log(0.00048828125), math.log(0.05))), 0.00048828125, 0.05),
        "w_query": normal_values(seeds[4], (D, D), D ** -0.5, 0.125, ((0, 4),)),
        "w_key": normal_values(seeds[5], (D, D), D ** -0.5, 0.125, ((0, 4),)),
        "w_value": normal_values(seeds[6], (D, D), D ** -0.5, 0.125, ((0, 4),)),
        "w_gate": normal_values(seeds[7], (D, D), D ** -0.5, 0.125, ((0, 4),)),
        "w_out": normal_values(seeds[8], (D, D), D ** -0.5, 0.125, ((0, 4),)),
        "w_one": normal_values(seeds[9], (D, FF), D ** -0.5, 0.125, ((0, 4),)),
        "w_two": normal_values(seeds[10], (D, FF), D ** -0.5, 0.125, ((0, 4),)),
        "w_down": normal_values(seeds[11], (D, FF), FF ** -0.5, 0.078125, ((0, 4),)),
    }


@jax.custom_vjp
def low(v):
    return lax.optimization_barrier(v.astype(jnp.bfloat16)).astype(jnp.float32)

@jax.custom_vjp
def low_back(v):
    return v

def low_keep(v):
    return (low(v), None)

def low_pass(kept, grad):
    return (grad,)

def back_keep(v):
    return (v, None)

def back_low(kept, grad):
    return (low(grad),)
low.defvjp(low_keep, low_pass)
low_back.defvjp(back_keep, back_low)
epsilon = 1e-06
highest = lax.Precision.HIGHEST

def normed(values):
    return values * lax.rsqrt(lax.optimization_barrier(jnp.mean(values * values, axis=-1, keepdims=True)) + epsilon)

def matmul(former, latter):
    return jnp.dot(former, latter, precision=highest)

def layer(inputs, w_query, w_key, w_value, w_gate, w_out, w_one, w_two, w_down, mask):
    length = inputs.shape[0]
    hidden = low(normed(inputs))
    queries = low(jax.nn.silu(low_back(matmul(hidden, w_query))))
    keys_all = low(jax.nn.silu(low_back(matmul(hidden, w_key))))
    values_all = low(low_back(matmul(hidden, w_value)))
    gate_pre = low_back(matmul(hidden, w_gate))
    q_heads = queries.reshape(length, HEADS, HEAD_DIM)
    k_heads = keys_all.reshape(length, HEADS, HEAD_DIM)
    v_heads = values_all.reshape(length, HEADS, HEAD_DIM)
    scores = low_back(jnp.einsum('thd,shd->hts', q_heads, k_heads, precision=highest))
    weights = low(scores * mask)
    attended = jnp.einsum('hts,shd->thd', weights, v_heads, precision=highest).reshape(length, HEADS * HEAD_DIM)
    attended = low_back(attended)
    gated = low(normed(attended) * gate_pre)
    middle = inputs + low_back(matmul(gated, w_out))
    second = low(normed(middle))
    first_pre = low_back(matmul(second, w_one))
    second_pre = low_back(matmul(second, w_two))
    product = low(first_pre * second_pre)
    return middle + low_back(matmul(product, w_down.T))

def build_mask(lengths_row, decay_rates, length):
    positions = jnp.arange(length, dtype=jnp.int32)
    seq_ends = jnp.cumsum(lengths_row)
    segments = lax.optimization_barrier(jnp.sum((seq_ends[None, :] <= positions[:, None]).astype(jnp.int32), axis=1))
    gap = positions[:, None] - positions[None, :]
    allowed = (gap >= 0) & (segments[:, None] == segments[None, :])
    decayed = jnp.exp(-decay_rates[:, None, None] * jnp.maximum(gap, 0).astype(jnp.float32)[None, :, :])
    return jnp.where(allowed[None, :, :], decayed, jnp.float32(0.0))

def reference(tokens, cotangent, lengths, decay_rates, w_query, w_key, w_value, w_gate, w_out, w_one, w_two, w_down):
    group = STREAM
    width = tokens.shape[2]
    weights = tuple((w.astype(jnp.float32) for w in (w_query, w_key, w_value, w_gate, w_out, w_one, w_two, w_down)))
    streams = tokens.astype(jnp.float32).reshape(MB * N_REP, group, width)
    upstreams = cotangent.astype(jnp.float32).reshape(MB * N_REP, group, width)
    stream_lengths = lengths.reshape(MB * N_REP, SEQS)

    def one_stream(totals, inputs):
        stream, upstream, lengths_row = inputs
        mask = build_mask(lengths_row, decay_rates, group)

        def forward(source, *params):
            return layer(source, *params, mask)
        result, pullback = jax.vjp(forward, stream, *weights)
        grads = pullback(upstream)
        new_totals = tuple((summed + grad for summed, grad in zip(totals, grads[1:])))
        return (new_totals, (result.astype(jnp.bfloat16), grads[0].astype(jnp.bfloat16)))
    start_totals = tuple((jnp.zeros(w.shape, jnp.float32) for w in weights))
    totals, (results, input_grads) = lax.scan(one_stream, start_totals, (streams, upstreams, stream_lengths))
    output = results.reshape(MB, N_REP * group, width)
    input_grad = input_grads.reshape(MB, N_REP * group, width)
    return (output, input_grad, totals[0], totals[1], totals[2], totals[3], totals[4], totals[5], totals[6], totals[7])
```

```python
import functools

import jax
import jax.numpy as jnp
from jax import lax
from jax.experimental import pallas as pl
from jax.experimental.pallas import tpu as pltpu
from jax.sharding import PartitionSpec as P

HEADS = 16
HEAD_DIM = 128
STREAM = 1024
GROUP = 4
BLOCK = 256
EPSILON = 1e-06
AXES = ("rep", "shard")
LOW = jnp.bfloat16
F32 = jnp.float32


def matmul(former, latter):
    return jnp.dot(former, latter, preferred_element_type=F32)


def times_transposed(former, latter):
    return lax.dot_general(former, latter, (((1,), (1,)), ((), ())), preferred_element_type=F32)


def cross_tokens(former, latter):
    return lax.dot_general(former, latter, (((0,), (0,)), ((), ())), preferred_element_type=F32)


def masked_decay(rate, ends, first, columns):
    row = first + lax.broadcasted_iota(jnp.int32, (BLOCK, 1), 0)
    column = lax.broadcasted_iota(jnp.int32, (1, columns), 1)
    begin = jnp.zeros((BLOCK, 1), jnp.int32)
    for end in ends:
        begin = jnp.where(row >= end, end, begin)
    falling = jnp.exp(-rate * (row - first).astype(F32))
    rising = jnp.exp(rate * (column - first).astype(F32))
    allowed = (column <= row) & (column >= begin)
    return jnp.where(allowed, falling * rising, 0.0)


def attend_kernel(rates, ends, zq_ref, zk_ref, zv_ref, out_ref):
    stream, head = pl.program_id(0), pl.program_id(1)
    rate = rates[head]
    bounds = [ends[stream, i] for i in range(ends.shape[1])]
    zq, zk = zq_ref[...], zk_ref[...]
    q = (zq * jax.nn.sigmoid(zq)).astype(LOW)
    k = (zk * jax.nn.sigmoid(zk)).astype(LOW)
    v = zv_ref[...].astype(LOW)
    for first in range(0, STREAM, BLOCK):
        columns = first + BLOCK
        mask = masked_decay(rate, bounds, first, columns)
        scores = times_transposed(q[first:columns], k[:columns])
        weights = (scores * mask).astype(LOW)
        out_ref[first:columns, :] = matmul(weights, v[:columns])


def attend_back_kernel(
    rates, ends, zq_ref, zk_ref, zv_ref, do_ref, dzq_ref, dzk_ref, dzv_ref, dk_ref, dv_ref
):
    stream, head = pl.program_id(0), pl.program_id(1)
    rate = rates[head]
    bounds = [ends[stream, i] for i in range(ends.shape[1])]
    zq, zk = zq_ref[...], zk_ref[...]
    sig_q, sig_k = jax.nn.sigmoid(zq), jax.nn.sigmoid(zk)
    q = (zq * sig_q).astype(LOW)
    k = (zk * sig_k).astype(LOW)
    slope_q = sig_q * (1.0 + zq * (1.0 - sig_q))
    v = zv_ref[...].astype(LOW)
    d_o = do_ref[...]
    dk_ref[...] = jnp.zeros_like(dk_ref)
    dv_ref[...] = jnp.zeros_like(dv_ref)
    for first in range(0, STREAM, BLOCK):
        columns = first + BLOCK
        rows = slice(first, columns)
        mask = masked_decay(rate, bounds, first, columns)
        weights = (times_transposed(q[rows], k[:columns]) * mask).astype(LOW)
        d_scores = (times_transposed(d_o[rows], v[:columns]) * mask).astype(LOW)
        dzq_ref[rows, :] = (matmul(d_scores, k[:columns]) * slope_q[rows]).astype(LOW)
        dk_ref[:columns, :] += cross_tokens(d_scores, q[rows])
        dv_ref[:columns, :] += cross_tokens(weights, d_o[rows])
    dzk_ref[...] = (dk_ref[...] * (sig_k * (1.0 + zk * (1.0 - sig_k)))).astype(LOW)
    dzv_ref[...] = dv_ref[...].astype(LOW)


def head_block(offset=0):
    return pl.BlockSpec((STREAM, HEAD_DIM), lambda g, h, *_: (g, h + offset))


def attend(rates, ends, z_qk, z_vg):
    heads, streams = rates.shape[0], ends.shape[0]
    work = streams * heads * STREAM * STREAM
    return pl.pallas_call(
        attend_kernel,
        out_shape=jax.ShapeDtypeStruct((streams * STREAM, heads * HEAD_DIM), F32),
        grid_spec=pltpu.PrefetchScalarGridSpec(
            num_scalar_prefetch=2,
            grid=(streams, heads),
            in_specs=[head_block(), head_block(heads), head_block()],
            out_specs=head_block(),
        ),
        compiler_params=pltpu.CompilerParams(vmem_limit_bytes=40 << 20),
        cost_estimate=pl.CostEstimate(
            flops=4 * work * HEAD_DIM, transcendentals=work // 64,
            bytes_accessed=streams * heads * STREAM * HEAD_DIM * 16,
        ),
        name="attend",
    )(rates, ends, z_qk, z_qk, z_vg)


def attend_back(rates, ends, z_qk, z_vg, d_o):
    heads, streams = rates.shape[0], ends.shape[0]
    work = streams * heads * STREAM * STREAM
    return pl.pallas_call(
        attend_back_kernel,
        out_shape=[jax.ShapeDtypeStruct((streams * STREAM, heads * HEAD_DIM), LOW)] * 3,
        grid_spec=pltpu.PrefetchScalarGridSpec(
            num_scalar_prefetch=2,
            grid=(streams, heads),
            in_specs=[head_block(), head_block(heads), head_block(), head_block()],
            out_specs=[head_block()] * 3,
            scratch_shapes=[pltpu.VMEM((STREAM, HEAD_DIM), F32)] * 2,
        ),
        compiler_params=pltpu.CompilerParams(vmem_limit_bytes=40 << 20),
        cost_estimate=pl.CostEstimate(
            flops=10 * work * HEAD_DIM, transcendentals=work // 64,
            bytes_accessed=streams * heads * STREAM * HEAD_DIM * 20,
        ),
        name="attend_back",
    )(rates, ends, z_qk, z_qk, z_vg, d_o)


def body(reps, shards, tokens, cotangent, lengths, decay_rates, *weights):
    spread = reps // GROUP
    rep, place = lax.axis_index("rep"), lax.axis_index("shard")
    c, b, a = rep % 2, (rep // 2) % 2, rep // GROUP
    quarter = rep % GROUP
    micro, run, width = tokens.shape
    streams = micro * GROUP // shards
    per_block = STREAM // run // GROUP * streams

    def move(x, target):
        pairs = [(r * shards + s, target(r) * shards + s) for r in range(reps) for s in range(shards)]
        return lax.ppermute(x, AXES, pairs)

    def swap_c(x):
        return move(x, lambda r: r ^ 1)

    def swap_b(x):
        return move(x, lambda r: r ^ 2)

    def shift_a(x, k):
        return move(x, lambda r: (r + GROUP * k) % reps)

    def ordered(index, own, other, axis):
        return jnp.where(
            index == 0, jnp.stack([own, other], axis), jnp.stack([other, own], axis)
        )


    def origin(r, s, p):
        run_id = (r % GROUP) * per_block + p
        stream, part = run_id // shards, run_id % shards
        index = s * streams + stream if streams == 1 else s
        if streams == 1:
            batch, member = index // GROUP, index % GROUP
        else:
            batch, member = s // 2, 2 * stream + s % 2
        return (r // GROUP) * GROUP + member, part, batch

    def routes(p, batch):
        found = []
        for r in range(reps):
            for s in range(shards):
                from_r, from_s, from_batch = origin(r, s, p)
                if from_batch == batch:
                    found.append((from_r * shards + from_s, r * shards + s))
        return found

    def bring(x):
        slots = []
        for p in range(per_block):
            arrived = [lax.ppermute(x[m], AXES, routes(p, m)) for m in range(micro)]
            slots.append(functools.reduce(jnp.add, arrived))
        return jnp.concatenate(slots, axis=0)

    def bring_back(x):
        slots = x.reshape(per_block, run, width)
        batches = []
        for m in range(micro):
            arrived = [
                lax.ppermute(slots[p], AXES, [(d, o) for o, d in routes(p, m)])
                for p in range(per_block)
            ]
            batches.append(functools.reduce(jnp.add, arrived))
        return jnp.stack(batches)


    def gather_rows(x):
        both = ordered(b, x, swap_b(x), 0)
        return ordered(c, both, swap_c(both), 1).reshape(-1, x.shape[1])

    def gather_columns(x):
        both = ordered(b, x, swap_b(x), 0)
        four = ordered(c, both, swap_c(both), 1)
        return jnp.concatenate([four[i, j] for i in range(2) for j in range(2)], axis=1)

    def scatter_columns(x):
        cut = x.reshape(x.shape[0], 2, 2, -1)
        pick = functools.partial(lax.dynamic_index_in_dim, keepdims=False)
        kept = pick(cut, c, 2) + swap_c(pick(cut, 1 - c, 2).astype(LOW)).astype(F32)
        return pick(kept, b, 1) + swap_b(pick(kept, 1 - b, 1).astype(LOW)).astype(F32)

    def total(x):
        x = x + swap_c(x)
        return x + swap_b(x)

    def to_runs(x):
        cut = x.reshape(2, 2, -1, x.shape[1])
        pick = functools.partial(lax.dynamic_index_in_dim, keepdims=False)
        both = ordered(b, pick(cut, b, 0), swap_b(pick(cut, 1 - b, 0)), 0)
        four = ordered(c, pick(both, c, 1), swap_c(pick(both, 1 - c, 1)), 1)
        return bring_back(
            jnp.concatenate([four[i, j] for i in range(2) for j in range(2)], axis=1)
        )

    def own_columns(x):
        size = x.shape[1] // GROUP
        return lax.dynamic_slice_in_dim(x, quarter * size, size, 1)


    rows = weights[0].shape[0]
    part = rows // spread

    def whole(members):
        cut = [
            lax.dynamic_slice(
                w, (a * part, quarter * (w.shape[1] // GROUP)), (part, w.shape[1] // GROUP)
            )
            for w in members
        ]
        piece = jnp.concatenate(cut, axis=1) if len(cut) > 1 else cut[0]
        mine = lax.all_gather(piece, "shard", axis=0, tiled=True).reshape(shards, part, -1)
        relative = [mine] + [shift_a(mine, k) for k in range(1, spread)]
        if spread == 2:
            full = ordered(a, relative[0], relative[1], 1)
        else:
            stacked = jnp.stack(relative, 0)
            full = jnp.stack(
                [
                    lax.dynamic_index_in_dim(stacked, (a - j) % spread, 0, False)
                    for j in range(spread)
                ],
                1,
            )
        return full.reshape(shards * rows, -1)

    def by_owner(x):
        cut = x.reshape(x.shape[0], shards, spread, part)
        return [
            lax.dynamic_index_in_dim(cut, (a + k) % spread, 2, False).reshape(x.shape[0], -1)
            for k in range(spread)
        ]

    def summed(left, right):
        products = [cross_tokens(x, right).astype(LOW) for x in left]
        kept = products[0].astype(F32)
        for k in range(1, spread):
            kept = kept + shift_a(products[k], k).astype(F32)
        return lax.psum_scatter(kept.astype(LOW), "shard", scatter_dimension=0, tiled=True)

    def spread_out(x):
        relative = [x] + [shift_a(x, k) for k in range(1, spread)]
        if spread == 2:
            full = ordered(a, relative[0], relative[1], 0)
        else:
            stacked = jnp.stack(relative, 0)
            full = jnp.stack(
                [
                    lax.dynamic_index_in_dim(stacked, (a - j) % spread, 0, False)
                    for j in range(spread)
                ],
                0,
            )
        full = full.reshape(rows, -1)
        both = ordered(b, full, swap_b(full), 0)
        return ordered(c, both, swap_c(both), 1)

    def as_outputs(four, count):
        size = four.shape[3] // count
        return [
            jnp.concatenate(
                [four[i, j][:, n * size : (n + 1) * size] for i in range(2) for j in range(2)],
                axis=1,
            ).astype(F32)
            for n in range(count)
        ]


    w_query, w_key, w_value, w_gate, w_out, w_one, w_two, w_down = weights
    x_run = bring(tokens)
    x_all = gather_rows(x_run)
    w_qk = whole((w_query, w_key))
    w_vg = whole((w_value, w_gate))
    w_o = whole((w_out,))
    w_1 = whole((w_one,))
    w_2 = whole((w_two,))
    w_d = whole((w_down,))
    dy_all = gather_rows(bring(cotangent))

    heads = HEADS // GROUP
    rates = lax.dynamic_slice_in_dim(decay_rates, quarter * heads, heads, 0)
    cuts = lengths.reshape(1, -1)
    cuts = gather_rows(cuts).reshape(GROUP, micro, -1)
    if streams == 1:
        batch = place // GROUP
        chosen = lax.dynamic_slice_in_dim(cuts, place % GROUP, 1, 0)
    else:
        batch = place // 2
        chosen = lax.dynamic_index_in_dim(cuts.reshape(2, 2, micro, -1), place % 2, 1, False)
    chosen = lax.dynamic_index_in_dim(chosen, batch, 1, False)
    seq_ends = [chosen[:, 0]]
    for i in range(1, chosen.shape[1]):
        seq_ends.append(seq_ends[-1] + chosen[:, i])
    ends = jnp.stack(seq_ends, axis=1)


    x_float = x_all.astype(F32)
    x_scale = lax.rsqrt(jnp.mean(x_float * x_float, axis=-1, keepdims=True) + EPSILON)
    hidden_one = (x_float * x_scale).astype(LOW)
    z_qk = matmul(hidden_one, w_qk)
    z_vg = matmul(hidden_one, w_vg)
    attended = attend(rates, ends, z_qk, z_vg)
    gate = z_vg[:, z_vg.shape[1] // 2 :]
    o_scale = lax.rsqrt(total(jnp.sum(attended * attended, axis=-1)) / width + EPSILON)[:, None]
    o_normed = attended * o_scale
    gated = gather_columns((o_normed * gate).astype(LOW))
    x_own = own_columns(x_all).astype(F32)
    middle = x_own + matmul(gated, w_o)
    m_scale = lax.rsqrt(total(jnp.sum(middle * middle, axis=-1)) / width + EPSILON)[:, None]
    m_normed = middle * m_scale
    hidden_two = gather_columns(m_normed.astype(LOW))
    z_one = matmul(hidden_two, w_1)
    z_two = matmul(hidden_two, w_2)
    product = (z_one * z_two).astype(LOW)
    output = to_runs((middle + scatter_columns(times_transposed(product, w_d))).astype(LOW))


    g_down = summed(by_owner(dy_all), product)
    d_product = matmul(dy_all, w_d)
    d_one = (d_product * z_two).astype(LOW)
    d_two = (d_product * z_one).astype(LOW)
    second_left = by_owner(hidden_two)
    g_one = summed(second_left, d_one)
    g_two = summed(second_left, d_two)
    d_hidden = scatter_columns(times_transposed(d_one, w_1) + times_transposed(d_two, w_2))
    lean = total(jnp.sum(m_normed * d_hidden, axis=-1))[:, None] / width
    d_middle = own_columns(dy_all).astype(F32) + m_scale * (d_hidden - m_normed * lean)
    d_branch = d_middle.astype(LOW)
    d_gated = scatter_columns(times_transposed(d_branch, w_o))
    g_out = summed(by_owner(gated), d_branch)
    d_gate = (d_gated * o_normed).astype(LOW)
    d_normed = d_gated * gate
    lean = total(jnp.sum(o_normed * d_normed, axis=-1))[:, None] / width
    d_attended = (o_scale * (d_normed - o_normed * lean)).astype(LOW)
    d_query, d_key, d_value = attend_back(rates, ends, z_qk, z_vg, d_attended)
    d_qk = jnp.concatenate([d_query, d_key], axis=1)
    d_vg = jnp.concatenate([d_value, d_gate], axis=1)
    first_left = by_owner(hidden_one)
    g_qk = summed(first_left, d_qk)
    g_vg = summed(first_left, d_vg)
    d_hidden = scatter_columns(times_transposed(d_qk, w_qk) + times_transposed(d_vg, w_vg))
    x_normed = x_own * x_scale
    lean = total(jnp.sum(x_normed * d_hidden, axis=-1))[:, None] / width
    input_grad = to_runs((d_middle + x_scale * (d_hidden - x_normed * lean)).astype(LOW))

    grads = []
    for reduced, count in ((g_qk, 2), (g_vg, 2), (g_out, 1), (g_one, 1), (g_two, 1), (g_down, 1)):
        grads += as_outputs(spread_out(reduced), count)
    return (output, input_grad, *grads)


def solution(mesh):
    by_tokens = P(None, ("rep", "shard"), None)
    by_rows = P("shard", None)
    return jax.shard_map(
        functools.partial(body, mesh.shape["rep"], mesh.shape["shard"]),
        mesh=mesh,
        in_specs=(by_tokens, by_tokens, P(None, "rep", None), P(), *[by_rows] * 8),
        out_specs=(by_tokens, by_tokens, *[by_rows] * 8),
        check_vma=False,
    )
```

```python
import functools

import jax
import jax.numpy as jnp
from jax import lax
from jax.experimental import pallas as pl
from jax.experimental.pallas import tpu as pltpu
from jax.sharding import PartitionSpec as P

HEADS = 16
HEAD_DIM = 128
STREAM = 1024
GROUP = 4
BLOCK = 256
EPSILON = 1e-06
AXES = ("rep", "shard")
LOW = jnp.bfloat16
F32 = jnp.float32


def matmul(former, latter):
    return jnp.dot(former, latter, preferred_element_type=F32)


def times_transposed(former, latter):
    return lax.dot_general(former, latter, (((1,), (1,)), ((), ())), preferred_element_type=F32)


def cross_tokens(former, latter):
    return lax.dot_general(former, latter, (((0,), (0,)), ((), ())), preferred_element_type=F32)


def masked_decay(rate, ends, first, columns):
    row = first + lax.broadcasted_iota(jnp.int32, (BLOCK, 1), 0)
    column = lax.broadcasted_iota(jnp.int32, (1, columns), 1)
    begin = jnp.zeros((BLOCK, 1), jnp.int32)
    for end in ends:
        begin = jnp.where(row >= end, end, begin)
    falling = jnp.exp(-rate * (row - first).astype(F32))
    rising = jnp.exp(rate * (column - first).astype(F32))
    allowed = (column <= row) & (column >= begin)
    return jnp.where(allowed, falling * rising, 0.0)


def attend_kernel(rates, ends, zq_ref, zk_ref, zv_ref, out_ref):
    stream, head = pl.program_id(0), pl.program_id(1)
    rate = rates[head]
    bounds = [ends[stream, i] for i in range(ends.shape[1])]
    zq, zk = zq_ref[...], zk_ref[...]
    q = (zq * jax.nn.sigmoid(zq)).astype(LOW)
    k = (zk * jax.nn.sigmoid(zk)).astype(LOW)
    v = zv_ref[...].astype(LOW)
    for first in range(0, STREAM, BLOCK):
        columns = first + BLOCK
        mask = masked_decay(rate, bounds, first, columns)
        scores = times_transposed(q[first:columns], k[:columns])
        weights = (scores * mask).astype(LOW)
        out_ref[first:columns, :] = matmul(weights, v[:columns])


def attend_back_kernel(
    rates, ends, zq_ref, zk_ref, zv_ref, do_ref, dzq_ref, dzk_ref, dzv_ref, dk_ref, dv_ref
):
    stream, head = pl.program_id(0), pl.program_id(1)
    rate = rates[head]
    bounds = [ends[stream, i] for i in range(ends.shape[1])]
    zq, zk = zq_ref[...], zk_ref[...]
    sig_q, sig_k = jax.nn.sigmoid(zq), jax.nn.sigmoid(zk)
    q = (zq * sig_q).astype(LOW)
    k = (zk * sig_k).astype(LOW)
    slope_q = sig_q * (1.0 + zq * (1.0 - sig_q))
    v = zv_ref[...].astype(LOW)
    d_o = do_ref[...]
    dk_ref[...] = jnp.zeros_like(dk_ref)
    dv_ref[...] = jnp.zeros_like(dv_ref)
    for first in range(0, STREAM, BLOCK):
        columns = first + BLOCK
        rows = slice(first, columns)
        mask = masked_decay(rate, bounds, first, columns)
        weights = (times_transposed(q[rows], k[:columns]) * mask).astype(LOW)
        d_scores = (times_transposed(d_o[rows], v[:columns]) * mask).astype(LOW)
        dzq_ref[rows, :] = (matmul(d_scores, k[:columns]) * slope_q[rows]).astype(LOW)
        dk_ref[:columns, :] += cross_tokens(d_scores, q[rows])
        dv_ref[:columns, :] += cross_tokens(weights, d_o[rows])
    dzk_ref[...] = (dk_ref[...] * (sig_k * (1.0 + zk * (1.0 - sig_k)))).astype(LOW)
    dzv_ref[...] = dv_ref[...].astype(LOW)


def head_block(offset=0):
    return pl.BlockSpec((STREAM, HEAD_DIM), lambda g, h, *_: (g, h + offset))


def attend(rates, ends, z_qk, z_vg):
    heads, streams = rates.shape[0], ends.shape[0]
    work = streams * heads * STREAM * STREAM
    return pl.pallas_call(
        attend_kernel,
        out_shape=jax.ShapeDtypeStruct((streams * STREAM, heads * HEAD_DIM), F32),
        grid_spec=pltpu.PrefetchScalarGridSpec(
            num_scalar_prefetch=2,
            grid=(streams, heads),
            in_specs=[head_block(), head_block(heads), head_block()],
            out_specs=head_block(),
        ),
        compiler_params=pltpu.CompilerParams(vmem_limit_bytes=40 << 20),
        cost_estimate=pl.CostEstimate(
            flops=4 * work * HEAD_DIM, transcendentals=work // 64,
            bytes_accessed=streams * heads * STREAM * HEAD_DIM * 16,
        ),
        name="attend",
    )(rates, ends, z_qk, z_qk, z_vg)


def attend_back(rates, ends, z_qk, z_vg, d_o):
    heads, streams = rates.shape[0], ends.shape[0]
    work = streams * heads * STREAM * STREAM
    return pl.pallas_call(
        attend_back_kernel,
        out_shape=[jax.ShapeDtypeStruct((streams * STREAM, heads * HEAD_DIM), LOW)] * 3,
        grid_spec=pltpu.PrefetchScalarGridSpec(
            num_scalar_prefetch=2,
            grid=(streams, heads),
            in_specs=[head_block(), head_block(heads), head_block(), head_block()],
            out_specs=[head_block()] * 3,
            scratch_shapes=[pltpu.VMEM((STREAM, HEAD_DIM), F32)] * 2,
        ),
        compiler_params=pltpu.CompilerParams(vmem_limit_bytes=40 << 20),
        cost_estimate=pl.CostEstimate(
            flops=10 * work * HEAD_DIM, transcendentals=work // 64,
            bytes_accessed=streams * heads * STREAM * HEAD_DIM * 20,
        ),
        name="attend_back",
    )(rates, ends, z_qk, z_qk, z_vg, d_o)


def tie(*values):
    return lax.optimization_barrier(values)


def body(reps, shards, tokens, cotangent, lengths, decay_rates, *weights):
    spread = reps // GROUP
    rep, place = lax.axis_index("rep"), lax.axis_index("shard")
    c, b, a = rep % 2, (rep // 2) % 2, rep // GROUP
    quarter = 2 * c + b
    micro, run, width = tokens.shape
    half, own = width // 2, width // GROUP
    streams = micro * GROUP // shards
    per_block = STREAM // run // GROUP * streams
    rows = width // shards
    part = rows // spread
    columns = functools.partial(lax.dynamic_slice_in_dim, axis=1)

    def move(x, target):
        pairs = [(r * shards + s, target(r) * shards + s) for r in range(reps) for s in range(shards)]
        return lax.ppermute(x, AXES, pairs)

    def swap_c(x):
        return move(x, lambda r: r ^ 1)

    def swap_b(x):
        return move(x, lambda r: r ^ 2)

    def shift_a(x, k):
        return move(x, lambda r: (r + GROUP * k) % reps)

    def ordered(index, mine, other, axis):
        return jnp.where(
            index == 0,
            jnp.concatenate([mine, other], axis),
            jnp.concatenate([other, mine], axis),
        )


    def origin(r, s, p):
        run_id = (2 * (r % 2) + (r // 2) % 2) * per_block + p
        stream, piece = run_id // shards, run_id % shards
        if streams == 1:
            batch, member = s // GROUP, s % GROUP
        else:
            batch, member = s // 2, 2 * stream + s % 2
        return (r // GROUP) * GROUP + member, piece, batch

    def routes(p, batch):
        found = []
        for r in range(reps):
            for s in range(shards):
                from_r, from_s, from_batch = origin(r, s, p)
                if from_batch == batch:
                    found.append((from_r * shards + from_s, r * shards + s))
        return found

    def permuted(x):
        return jnp.concatenate(
            [
                x[:, (z * spread + k) * part : (z * spread + k + 1) * part]
                for k in range(spread)
                for z in range(shards)
            ],
            axis=1,
        )

    def natural(x):
        return jnp.concatenate(
            [
                x[:, (k * shards + z) * part : (k * shards + z + 1) * part]
                for z in range(shards)
                for k in range(spread)
            ],
            axis=1,
        )

    def bring(x):
        slots = []
        for p in range(per_block):
            arrived = [lax.ppermute(x[m], AXES, routes(p, m)) for m in range(micro)]
            slots.append(functools.reduce(jnp.add, arrived))
        return permuted(jnp.concatenate(slots, axis=0))

    def bring_back(x):
        slots = natural(x).reshape(per_block, run, width)
        batches = []
        for m in range(micro):
            arrived = [
                lax.ppermute(slots[p], AXES, [(d, o) for o, d in routes(p, m)])
                for p in range(per_block)
            ]
            batches.append(functools.reduce(jnp.add, arrived))
        return jnp.stack(batches)


    def gather_b(x):
        return ordered(b, x, swap_b(x), 1)

    def gather_c(x):
        return ordered(c, x, swap_c(x), 1)

    def gather_rows_b(x):
        return ordered(b, x, swap_b(x), 0)

    def gather_rows_c(x):
        return ordered(c, x, swap_c(x), 0)

    def total(x):
        x = x + swap_c(x)
        return x + swap_b(x)

    def fold_c(product):
        sent = swap_c(product(1 - c).astype(LOW))
        return product(c) + sent.astype(F32)

    def fold_b(x):
        sent = swap_b(columns(x, (1 - b) * own, own).astype(LOW))
        return columns(x, b * own, own) + sent.astype(F32)

    def to_runs(x):
        cut = x.reshape(2, 2, -1, own)
        pick = functools.partial(lax.dynamic_index_in_dim, keepdims=False)
        both = ordered(b, pick(cut, b, 1), swap_b(pick(cut, 1 - b, 1)), 2)
        four = ordered(c, pick(both, c, 0), swap_c(pick(both, 1 - c, 0)), 1)
        return bring_back(four)


    def own_features(w):
        count = shards * spread // GROUP
        cut = []
        for i in range(count):
            block = quarter * count + i
            cut.append(columns(w, (block % shards) * rows + (block // shards) * part, part))
        return jnp.concatenate(cut, axis=1)

    def own_units(w):
        return columns(w, quarter * (w.shape[1] // GROUP), w.shape[1] // GROUP)

    def over_shards(*members):
        cut = jnp.concatenate(members, axis=1) if len(members) > 1 else members[0]
        piece = lax.dynamic_slice_in_dim(cut, a * part, part, 0)
        return lax.all_gather(piece, "shard", axis=0, tiled=True)

    def over_spread(x):
        return [shift_a(x, k) for k in range(1, spread)]

    def by_spread(relative):
        if spread == 2:
            return ordered(a, relative[0], relative[1], 0)
        stacked = jnp.stack(relative, 0)
        pick = functools.partial(lax.dynamic_index_in_dim, axis=0, keepdims=False)
        return jnp.concatenate([pick(stacked, (a - j) % spread) for j in range(spread)], axis=0)

    def in_row_order(x):
        cut = x.reshape(spread, shards, part, -1)
        return jnp.transpose(cut, (1, 0, 2, 3)).reshape(width, -1)

    def row_half(w, h):
        return lax.dynamic_slice_in_dim(w, h * half, half, 0)


    def owned_by(x, k):
        return columns(x, ((a + k) % spread) * (width // spread), width // spread)

    def away(left, right):
        return [cross_tokens(owned_by(left, k), right).astype(LOW) for k in range(1, spread)]

    def kept(left, right):
        return cross_tokens(owned_by(left, 0), right).astype(LOW)

    def sent_a(terms):
        return [shift_a(x, k + 1) for k, x in enumerate(terms)]

    def summed(mine, arrived):
        whole = mine.astype(F32)
        for x in arrived:
            whole = whole + x.astype(F32)
        return lax.psum_scatter(whole.astype(LOW), "shard", scatter_dimension=0, tiled=True)

    def spread_out(x):
        full = by_spread([x] + over_spread(x))
        return gather_quarters(full)

    def gather_quarters(full):
        pair = ordered(b, full[None], swap_b(full)[None], 0)
        return ordered(c, pair[None], swap_c(pair)[None], 0)

    def as_outputs(four, count, unpermute):
        size = four.shape[3] // count
        found = []
        for n in range(count):
            flat = jnp.concatenate(
                [four[i, j][:, n * size : (n + 1) * size] for i in range(2) for j in range(2)],
                axis=1,
            )
            found.append((natural(flat) if unpermute else flat).astype(F32))
        return found


    w_query, w_key, w_value, w_gate, w_out, w_one, w_two, w_down = weights
    g_qk = over_shards(own_units(w_query), own_units(w_key))
    g_vg = over_shards(own_units(w_value), own_units(w_gate))
    g_o = over_shards(own_features(w_out))
    g_1 = over_shards(own_units(w_one))
    g_2 = over_shards(own_units(w_two))
    g_d = over_shards(own_units(w_down))

    heads = HEADS // GROUP
    rates = lax.dynamic_slice_in_dim(decay_rates, quarter * heads, heads, 0)
    cuts = gather_rows_c(gather_rows_b(lengths.reshape(1, -1))).reshape(GROUP, micro, -1)
    if streams == 1:
        batch = place // GROUP
        member = place % GROUP
        chosen = lax.dynamic_slice_in_dim(cuts, 2 * (member % 2) + member // 2, 1, 0)
    else:
        batch = place // 2
        chosen = lax.dynamic_index_in_dim(cuts.reshape(2, 2, micro, -1), place % 2, 0, False)
    chosen = lax.dynamic_index_in_dim(chosen, batch, 1, False)
    seq_ends = [chosen[:, 0]]
    for i in range(1, chosen.shape[1]):
        seq_ends.append(seq_ends[-1] + chosen[:, i])
    ends = jnp.stack(seq_ends, axis=1)

    x_run = bring(tokens)
    x_run, g_qk = tie(x_run, g_qk)

    x_pair = gather_rows_b(x_run)
    s_qk = over_spread(g_qk)
    x_pair, s_qk, g_vg = tie(x_pair, s_qk, g_vg)

    s_vg = over_spread(g_vg)
    x_all = gather_rows_c(x_pair)
    x_float = x_all.astype(F32)
    x_scale = lax.rsqrt(jnp.mean(x_float * x_float, axis=-1, keepdims=True) + EPSILON)
    hidden_one = (x_float * x_scale).astype(LOW)
    w_qk = by_spread([g_qk, *s_qk])
    z_qk = matmul(hidden_one, w_qk)
    z_qk, s_vg, g_o = tie(z_qk, s_vg, g_o)

    s_o = over_spread(g_o)
    w_vg = by_spread([g_vg, *s_vg])
    z_vg = matmul(hidden_one, w_vg)
    attended = attend(rates, ends, z_qk, z_vg)
    gate = z_vg[:, own:]
    o_scale = lax.rsqrt(total(jnp.sum(attended * attended, axis=-1)) / width + EPSILON)[:, None]
    o_normed = attended * o_scale
    gated = (o_normed * gate).astype(LOW)
    gated, s_o, g_1 = tie(gated, s_o, g_1)

    s_1 = over_spread(g_1)
    dy_run = bring(cotangent)
    gated = gather_b(gated)
    w_o = in_row_order(by_spread([g_o, *s_o]))
    gated, s_1, g_2, dy_run = tie(gated, s_1, g_2, dy_run)

    s_2 = over_spread(g_2)
    gated = gather_c(gated)
    x_own = columns(x_all, quarter * own, own).astype(F32)
    middle = x_own + matmul(gated, w_o)
    m_scale = lax.rsqrt(total(jnp.sum(middle * middle, axis=-1)) / width + EPSILON)[:, None]
    m_normed = middle * m_scale
    hidden_two = gather_b(m_normed.astype(LOW))
    w_1 = by_spread([g_1, *s_1])
    hidden_two, s_2, g_d = tie(hidden_two, s_2, g_d)

    s_d = over_spread(g_d)
    hidden_two = gather_c(hidden_two)
    dy_all = gather_rows_c(gather_rows_b(dy_run))
    z_one = matmul(hidden_two, w_1)
    w_2 = by_spread([g_2, *s_2])
    z_two = matmul(hidden_two, w_2)
    product = (z_one * z_two).astype(LOW)
    t_down = away(dy_all, product)
    z_one, z_two, product, t_down, s_d = tie(z_one, z_two, product, t_down, s_d)

    r_down = sent_a(t_down)
    w_d = by_spread([g_d, *s_d])
    d_product = matmul(dy_all, w_d)
    d_one = (d_product * z_two).astype(LOW)
    d_two = (d_product * z_one).astype(LOW)
    t_one = away(hidden_two, d_one)
    k_down = kept(dy_all, product)
    d_hidden = fold_c(
        lambda h: times_transposed(d_one, row_half(w_1, h)) + times_transposed(d_two, row_half(w_2, h))
    )
    d_hidden, d_one, d_two, t_one, r_down, k_down = tie(
        d_hidden, d_one, d_two, t_one, r_down, k_down
    )

    r_one = sent_a(t_one)
    f_down = summed(k_down, r_down)
    d_hidden = fold_b(d_hidden)
    k_one = kept(hidden_two, d_one)
    t_two = away(hidden_two, d_two)
    d_hidden, r_one, k_one, t_two = tie(d_hidden, r_one, k_one, t_two)

    r_two = sent_a(t_two)
    f_one = summed(k_one, r_one)
    lean = total(jnp.sum(m_normed * d_hidden, axis=-1))[:, None] / width
    dy_own = columns(dy_all, quarter * own, own).astype(F32)
    d_middle = dy_own + m_scale * (d_hidden - m_normed * lean)
    d_branch = d_middle.astype(LOW)
    d_gated = fold_b(fold_c(lambda h: times_transposed(d_branch, row_half(w_o, h))))
    k_two = kept(hidden_two, d_two)
    p_out = cross_tokens(gated, d_branch).astype(LOW).reshape(shards, spread, part, -1)
    p_out = jnp.transpose(p_out, (1, 0, 2, 3)).reshape(spread, width // spread, -1)
    t_out = [lax.dynamic_index_in_dim(p_out, (a + k) % spread, 0, False) for k in range(spread)]
    d_gated, r_two, k_two, t_out = tie(d_gated, r_two, k_two, t_out)

    r_out = sent_a(t_out[1:])
    f_two = summed(k_two, r_two)
    d_gate = (d_gated * o_normed).astype(LOW)
    d_normed = d_gated * gate
    lean = total(jnp.sum(o_normed * d_normed, axis=-1))[:, None] / width
    d_attended = (o_scale * (d_normed - o_normed * lean)).astype(LOW)
    d_query, d_key, d_value = attend_back(rates, ends, z_qk, z_vg, d_attended)
    d_qk = jnp.concatenate([d_query, d_key], axis=1)
    d_vg = jnp.concatenate([d_value, d_gate], axis=1)
    t_qk = away(hidden_one, d_qk)
    d_qk, d_vg, r_out, t_qk = tie(d_qk, d_vg, r_out, t_qk)

    r_qk = sent_a(t_qk)
    f_out = summed(t_out[0], r_out)
    t_vg = away(hidden_one, d_vg)
    r_vg = sent_a(t_vg)
    k_qk = kept(hidden_one, d_qk)
    k_vg = kept(hidden_one, d_vg)
    f_qk = summed(k_qk, r_qk)
    f_vg = summed(k_vg, r_vg)
    d_hidden = fold_b(
        fold_c(
            lambda h: times_transposed(d_qk, row_half(w_qk, h))
            + times_transposed(d_vg, row_half(w_vg, h))
        )
    )
    x_normed = x_own * x_scale
    lean = total(jnp.sum(x_normed * d_hidden, axis=-1))[:, None] / width
    input_grad = to_runs((d_middle + x_scale * (d_hidden - x_normed * lean)).astype(LOW))

    result = fold_b(fold_c(lambda h: times_transposed(product, row_half(w_d, h))))
    output = to_runs((middle + result).astype(LOW))

    grads = []
    for reduced, count in ((f_qk, 2), (f_vg, 2), (f_out, 1), (f_one, 1), (f_two, 1), (f_down, 1)):
        grads += as_outputs(spread_out(reduced), count, reduced is f_out)
    return (output, input_grad, *grads)


def solution(mesh):
    by_tokens = P(None, ("rep", "shard"), None)
    by_rows = P("shard", None)
    return jax.shard_map(
        functools.partial(body, mesh.shape["rep"], mesh.shape["shard"]),
        mesh=mesh,
        in_specs=(by_tokens, by_tokens, P(None, "rep", None), P(), *[by_rows] * 8),
        out_specs=(by_tokens, by_tokens, *[by_rows] * 8),
        check_vma=False,
    )
```

```python
import functools

import jax
import jax.numpy as jnp
from jax import lax
from jax.experimental import pallas as pl
from jax.experimental.pallas import tpu as pltpu
from jax.sharding import PartitionSpec as P

HEADS = 16
HEAD_DIM = 128
STREAM = 1024
GROUP = 4
BLOCK = 256
TILE = 256
EPSILON = 1e-06
AXES = ("rep", "shard")
LOW = jnp.bfloat16
F32 = jnp.float32


def matmul(former, latter):
    return jnp.dot(former, latter, preferred_element_type=F32)


def times_transposed(former, latter):
    return lax.dot_general(former, latter, (((1,), (1,)), ((), ())), preferred_element_type=F32)


def cross_tokens(former, latter):
    return lax.dot_general(former, latter, (((0,), (0,)), ((), ())), preferred_element_type=F32)


def masked_decay(rate, ends, first, columns):
    row = first + lax.broadcasted_iota(jnp.int32, (BLOCK, 1), 0)
    column = lax.broadcasted_iota(jnp.int32, (1, columns), 1)
    begin = jnp.zeros((BLOCK, 1), jnp.int32)
    for end in ends:
        begin = jnp.where(row >= end, end, begin)
    falling = jnp.exp(-rate * (row - first).astype(F32))
    rising = jnp.exp(rate * (column - first).astype(F32))
    allowed = (column <= row) & (column >= begin)
    return jnp.where(allowed, falling * rising, 0.0)


def attend_kernel(rates, ends, zq_ref, zk_ref, zv_ref, out_ref):
    stream, head = pl.program_id(0), pl.program_id(1)
    rate = rates[head]
    bounds = [ends[stream, i] for i in range(ends.shape[1])]
    zq, zk = zq_ref[...], zk_ref[...]
    q = (zq * jax.nn.sigmoid(zq)).astype(LOW)
    k = (zk * jax.nn.sigmoid(zk)).astype(LOW)
    v = zv_ref[...].astype(LOW)
    for first in range(0, STREAM, BLOCK):
        columns = first + BLOCK
        mask = masked_decay(rate, bounds, first, columns)
        scores = times_transposed(q[first:columns], k[:columns])
        weights = (scores * mask).astype(LOW)
        out_ref[first:columns, :] = matmul(weights, v[:columns])


def attend_back_kernel(
    rates, ends, zq_ref, zk_ref, zv_ref, do_ref, dzq_ref, dzk_ref, dzv_ref, dk_ref, dv_ref
):
    stream, head = pl.program_id(0), pl.program_id(1)
    rate = rates[head]
    bounds = [ends[stream, i] for i in range(ends.shape[1])]
    zq, zk = zq_ref[...], zk_ref[...]
    sig_q, sig_k = jax.nn.sigmoid(zq), jax.nn.sigmoid(zk)
    q = (zq * sig_q).astype(LOW)
    k = (zk * sig_k).astype(LOW)
    slope_q = sig_q * (1.0 + zq * (1.0 - sig_q))
    v = zv_ref[...].astype(LOW)
    d_o = do_ref[...]
    dk_ref[...] = jnp.zeros_like(dk_ref)
    dv_ref[...] = jnp.zeros_like(dv_ref)
    for first in range(0, STREAM, BLOCK):
        columns = first + BLOCK
        rows = slice(first, columns)
        mask = masked_decay(rate, bounds, first, columns)
        weights = (times_transposed(q[rows], k[:columns]) * mask).astype(LOW)
        d_scores = (times_transposed(d_o[rows], v[:columns]) * mask).astype(LOW)
        dzq_ref[rows, :] = (matmul(d_scores, k[:columns]) * slope_q[rows]).astype(LOW)
        dk_ref[:columns, :] += cross_tokens(d_scores, q[rows])
        dv_ref[:columns, :] += cross_tokens(weights, d_o[rows])
    dzk_ref[...] = (dk_ref[...] * (sig_k * (1.0 + zk * (1.0 - sig_k)))).astype(LOW)
    dzv_ref[...] = dv_ref[...].astype(LOW)


def head_block(offset=0):
    return pl.BlockSpec((STREAM, HEAD_DIM), lambda g, h, *_: (g, h + offset))


def attend(rates, ends, z_qk, z_vg):
    heads, streams = rates.shape[0], ends.shape[0]
    work = streams * heads * STREAM * STREAM
    return pl.pallas_call(
        attend_kernel,
        out_shape=jax.ShapeDtypeStruct((streams * STREAM, heads * HEAD_DIM), F32),
        grid_spec=pltpu.PrefetchScalarGridSpec(
            num_scalar_prefetch=2,
            grid=(streams, heads),
            in_specs=[head_block(), head_block(heads), head_block()],
            out_specs=head_block(),
        ),
        compiler_params=pltpu.CompilerParams(vmem_limit_bytes=40 << 20),
        cost_estimate=pl.CostEstimate(
            flops=4 * work * HEAD_DIM, transcendentals=work // 64,
            bytes_accessed=streams * heads * STREAM * HEAD_DIM * 16,
        ),
        name="attend",
    )(rates, ends, z_qk, z_qk, z_vg)


def attend_back(rates, ends, z_qk, z_vg, d_o):
    heads, streams = rates.shape[0], ends.shape[0]
    work = streams * heads * STREAM * STREAM
    return pl.pallas_call(
        attend_back_kernel,
        out_shape=[jax.ShapeDtypeStruct((streams * STREAM, heads * HEAD_DIM), LOW)] * 3,
        grid_spec=pltpu.PrefetchScalarGridSpec(
            num_scalar_prefetch=2,
            grid=(streams, heads),
            in_specs=[head_block(), head_block(heads), head_block(), head_block()],
            out_specs=[head_block()] * 3,
            scratch_shapes=[pltpu.VMEM((STREAM, HEAD_DIM), F32)] * 2,
        ),
        compiler_params=pltpu.CompilerParams(vmem_limit_bytes=40 << 20),
        cost_estimate=pl.CostEstimate(
            flops=10 * work * HEAD_DIM, transcendentals=work // 64,
            bytes_accessed=streams * heads * STREAM * HEAD_DIM * 20,
        ),
        name="attend_back",
    )(rates, ends, z_qk, z_qk, z_vg, d_o)


def chunk_copies(chunks, buffer, sems, turn, half=None):
    count, size = len(chunks), chunks[0].shape[0]
    copies = []
    for k, chunk in enumerate(chunks):
        index = lax.rem(turn - k + count, count)
        wanted = None
        if half is not None:
            wanted = lax.div(index, count // 2) == half
            index = lax.rem(index, count // 2)
        target = buffer.at[pl.ds(pl.multiple_of(index * size, size), size)]
        copies.append((wanted, pltpu.make_async_copy(chunk, target, sems.at[k])))
    return copies


def each(copies, act):
    for wanted, copy in copies:
        if wanted is None:
            act(copy)
        else:
            pl.when(wanted)(functools.partial(act, copy))


def start(copies):
    each(copies, lambda copy: copy.start())


def finish(copies):
    each(copies, lambda copy: copy.wait())


def estimate(flops, *arrays):
    moved = sum(x.size * x.dtype.itemsize for x in arrays)
    return pl.CostEstimate(flops=flops, transcendentals=0, bytes_accessed=moved)


def limit(mebibytes):
    return pltpu.CompilerParams(vmem_limit_bytes=mebibytes << 20)


ANYWHERE = pl.BlockSpec(memory_space=pl.ANY)


def weight_buffer(chunks, share=1):
    size = len(chunks) * chunks[0].shape[0] // share
    return [pltpu.VMEM((size, chunks[0].shape[1]), LOW), pltpu.SemaphoreType.DMA((len(chunks),))]


def tile_rows(width, column=0):
    return pl.BlockSpec((TILE, width), lambda i, *_: (i, column))


def joined_rows(width, tiles):
    own = pl.BlockSpec((TILE, width), lambda i, s: (jnp.clip(i - s[0] * tiles, 0, tiles - 1), 0))
    other = pl.BlockSpec(
        (TILE, width), lambda i, s: (jnp.clip(i - (1 - s[0]) * tiles, 0, tiles - 1), 0)
    )
    return [own, other]


def enter_kernel(tiles, blocks, project, spots, own_ref, other_ref, *refs):
    i = pl.program_id(0)
    rows = jnp.where(i // tiles == spots[0], own_ref[...], other_ref[...])
    part = rows.shape[1] // len(blocks)
    permuted = jnp.concatenate([rows[:, n * part : (n + 1) * part] for n in blocks], axis=1)
    if not project:
        all_ref, quarter_ref = refs
        all_ref[...] = permuted
        held = all_ref
    else:
        chunks, (h_ref, z_ref, scale_ref, quarter_ref, held, buffer, sems) = refs[:-7], refs[-7:]
        held[...] = permuted
        copies = chunk_copies(chunks, buffer, sems, spots[2])

        @pl.when(i == 0)
        def _():
            start(copies)

        x = rows.astype(F32)
        scale = lax.rsqrt(jnp.mean(x * x, axis=-1, keepdims=True) + EPSILON)
        scale_ref[...] = scale
        hidden = (permuted.astype(F32) * scale).astype(LOW)
        h_ref[...] = hidden

        @pl.when(i == 0)
        def _():
            finish(copies)

        z_ref[...] = matmul(hidden, buffer[...])
    size = quarter_ref.shape[1]
    quarter_ref[...] = held[:, pl.ds(pl.multiple_of(spots[1] * size, size), size)]


def enter(spots, blocks, own, other, chunks=()):
    width = own.shape[1]
    count, tiles = 2 * own.shape[0], own.shape[0] // TILE
    shape = jax.ShapeDtypeStruct
    quarter = shape((count, width // GROUP), LOW)
    if chunks:
        columns = chunks[0].shape[1]
        outs = [shape((count, width), LOW), shape((count, columns), F32), shape((count, 1), F32), quarter]
        scratch = [pltpu.VMEM((TILE, width), LOW), *weight_buffer(chunks)]
    else:
        columns, scratch = 0, []
        outs = [shape((count, width), LOW), quarter]
    return pl.pallas_call(
        functools.partial(enter_kernel, tiles, blocks, bool(chunks)),
        out_shape=outs,
        grid_spec=pltpu.PrefetchScalarGridSpec(
            num_scalar_prefetch=1,
            grid=(2 * tiles,),
            in_specs=joined_rows(width, tiles) + [ANYWHERE] * len(chunks),
            out_specs=[tile_rows(o.shape[1]) for o in outs],
            scratch_shapes=scratch,
        ),
        compiler_params=limit(40),
        cost_estimate=estimate(2 * count * width * columns, own, other, *chunks, *outs),
        name="enter",
    )(spots, own, other, *chunks)


def project_kernel(spots, h_ref, *refs):
    chunks, (z_ref, buffer, sems) = refs[:-3], refs[-3:]
    copies = chunk_copies(chunks, buffer, sems, spots[2])

    @pl.when(pl.program_id(0) == 0)
    def _():
        start(copies)
        finish(copies)

    z_ref[...] = matmul(h_ref[...], buffer[...])


def project(spots, hidden, chunks):
    count, width = hidden.shape
    out = jax.ShapeDtypeStruct((count, chunks[0].shape[1]), F32)
    return pl.pallas_call(
        project_kernel,
        out_shape=out,
        grid_spec=pltpu.PrefetchScalarGridSpec(
            num_scalar_prefetch=1,
            grid=(count // TILE,),
            in_specs=[tile_rows(width)] + [ANYWHERE] * len(chunks),
            out_specs=tile_rows(out.shape[1]),
            scratch_shapes=weight_buffer(chunks),
        ),
        compiler_params=limit(40),
        cost_estimate=estimate(2 * count * width * out.shape[1], hidden, *chunks, out),
        name="project",
    )(spots, hidden, *chunks)


def unit_kernel(spots, own_ref, other_ref, *refs):
    chunks, rest = refs[:-9], refs[-9:]
    h_ref, one_ref, two_ref, product_ref, scale_ref, first, second, sem_one, sem_two = rest
    split = len(chunks) // 2
    copies = [
        chunk_copies(chunks[:split], first, sem_one, spots[2]),
        chunk_copies(chunks[split:], second, sem_two, spots[2]),
    ]
    begins = pl.program_id(0) == 0

    @pl.when(begins)
    def _():
        start(copies[0])
        start(copies[1])

    mine, other = own_ref[...], other_ref[...]
    swapped = spots[0] == 1
    middle = jnp.concatenate(
        [jnp.where(swapped, other, mine), jnp.where(swapped, mine, other)], axis=1
    ).astype(F32)
    scale = lax.rsqrt(jnp.mean(middle * middle, axis=-1, keepdims=True) + EPSILON)
    scale_ref[...] = scale
    hidden = (middle * scale).astype(LOW)
    h_ref[...] = hidden

    @pl.when(begins)
    def _():
        finish(copies[0])

    z_one = matmul(hidden, first[...])

    @pl.when(begins)
    def _():
        finish(copies[1])

    z_two = matmul(hidden, second[...])
    one_ref[...] = z_one.astype(LOW)
    two_ref[...] = z_two.astype(LOW)
    product_ref[...] = (z_one * z_two).astype(LOW)


def gated_unit(spots, own, other, first, second):
    count, width, units = own.shape[0], 2 * own.shape[1], first[0].shape[1]
    shape = jax.ShapeDtypeStruct
    outs = [shape((count, width), LOW)] + [shape((count, units), LOW)] * 3 + [shape((count, 1), F32)]
    (buffer, sems) = weight_buffer(first)
    return pl.pallas_call(
        unit_kernel,
        out_shape=outs,
        grid_spec=pltpu.PrefetchScalarGridSpec(
            num_scalar_prefetch=1,
            grid=(count // TILE,),
            in_specs=[tile_rows(width // 2)] * 2 + [ANYWHERE] * (2 * len(first)),
            out_specs=[tile_rows(o.shape[1]) for o in outs],
            scratch_shapes=[buffer, buffer, sems, sems],
        ),
        compiler_params=limit(48),
        cost_estimate=estimate(4 * count * width * units, own, other, *first, *second, *outs),
        name="gated_unit",
    )(spots, own, other, *first, *second)


def unit_back_kernel(spots, dy_ref, one_ref, two_ref, *refs):
    chunks, (d_one_ref, d_two_ref, sum_ref, buffer, sems) = refs[:-5], refs[-5:]
    copies = chunk_copies(chunks, buffer, sems, spots[2])

    @pl.when(pl.program_id(0) == 0)
    def _():
        start(copies)
        finish(copies)

    d_product = matmul(dy_ref[...], buffer[...])
    z_one, z_two = one_ref[...].astype(F32), two_ref[...].astype(F32)
    d_one = d_product * z_two
    d_one_ref[...] = d_one.astype(LOW)
    d_two_ref[...] = (d_product * z_one).astype(LOW)
    sum_ref[...] = jnp.sum(d_one * z_one, axis=-1, keepdims=True)


def gated_unit_back(spots, dy, z_one, z_two, chunks):
    count, width, units = dy.shape[0], dy.shape[1], z_one.shape[1]
    shape = jax.ShapeDtypeStruct
    outs = [shape((count, units), LOW)] * 2 + [shape((count, 1), F32)]
    return pl.pallas_call(
        unit_back_kernel,
        out_shape=outs,
        grid_spec=pltpu.PrefetchScalarGridSpec(
            num_scalar_prefetch=1,
            grid=(count // TILE,),
            in_specs=[tile_rows(width), tile_rows(units), tile_rows(units)] + [ANYWHERE] * len(chunks),
            out_specs=[tile_rows(o.shape[1]) for o in outs],
            scratch_shapes=weight_buffer(chunks),
        ),
        compiler_params=limit(40),
        cost_estimate=estimate(2 * count * width * units, dy, z_one, z_two, *chunks, *outs),
        name="gated_unit_back",
    )(spots, dy, z_one, z_two, *chunks)


def fold_kernel(members, keeps, spots, *refs):
    values, refs = refs[:members], refs[members:]
    arrived, refs = (refs[0], refs[1:]) if keeps else (None, refs)
    outs = 2 if keeps else 1
    chunks, refs = refs[: -outs - 2 * members], refs[-outs - 2 * members :]
    outs, buffers, sems = refs[:outs], refs[outs : outs + members], refs[outs + members :]
    each_count = len(chunks) // members
    half = spots[0] if keeps else 1 - spots[0]
    begins = pl.program_id(0) == 0
    copies = [
        chunk_copies(chunks[m * each_count : (m + 1) * each_count], buffers[m], sems[m], spots[2], half)
        for m in range(members)
    ]

    @pl.when(begins)
    def _():
        for m in range(members):
            start(copies[m])

    whole = None
    for m in range(members):
        pl.when(begins)(functools.partial(finish, copies[m]))
        term = times_transposed(values[m][...], buffers[m][...])
        whole = term if whole is None else whole + term
    if not keeps:
        outs[0][...] = whole.astype(LOW)
    else:
        whole = whole + arrived[...].astype(F32)
        size = whole.shape[1] // 2
        upper = spots[3] == 1
        outs[0][...] = jnp.where(upper, whole[:, :size], whole[:, size:]).astype(LOW)
        outs[1][...] = jnp.where(upper, whole[:, size:], whole[:, :size])


def fold_half(spots, values, weights, arrived=None):
    count = values[0].shape[0]
    half = len(weights[0]) * weights[0][0].shape[0] // 2
    shape = jax.ShapeDtypeStruct
    if arrived is None:
        outs, extra = [shape((count, half), LOW)], []
    else:
        outs, extra = [shape((count, half // 2), LOW), shape((count, half // 2), F32)], [arrived]
    buffers, sems = zip(*[weight_buffer(w, 2) for w in weights])
    chunks = [x for w in weights for x in w]
    flops = sum(2 * count * half * v.shape[1] for v in values)
    found = pl.pallas_call(
        functools.partial(fold_kernel, len(values), arrived is not None),
        out_shape=outs,
        grid_spec=pltpu.PrefetchScalarGridSpec(
            num_scalar_prefetch=1,
            grid=(count // TILE,),
            in_specs=[tile_rows(v.shape[1]) for v in values]
            + [tile_rows(half)] * len(extra)
            + [ANYWHERE] * len(chunks),
            out_specs=[tile_rows(o.shape[1]) for o in outs],
            scratch_shapes=[*buffers, *sems],
        ),
        compiler_params=limit(40),
        cost_estimate=estimate(flops, *values, *extra, *chunks[: len(chunks) // 2], *outs),
        name="fold_half",
    )(spots, *values, *extra, *chunks)
    return found[0] if arrived is None else found


def place_kernel(count, spots, *refs):
    quarter = pl.program_id(0)
    cross = lax.rem(lax.div(quarter, 2) + spots[0], 2) * 2 + lax.rem(lax.rem(quarter, 2) + spots[3], 2)
    for n in range(4):

        @pl.when(cross == n)
        def _():
            size = refs[n].shape[1] // count
            for m in range(count):
                refs[4 + m][...] = refs[n][:, m * size : (m + 1) * size].astype(F32)


def place_quarters(spots, four, count):
    rows, columns = four[0].shape
    size = columns // count
    outs = [jax.ShapeDtypeStruct((rows, GROUP * size), F32)] * count
    return pl.pallas_call(
        functools.partial(place_kernel, count),
        out_shape=outs,
        grid_spec=pltpu.PrefetchScalarGridSpec(
            num_scalar_prefetch=1,
            grid=(GROUP,),
            in_specs=[pl.BlockSpec((rows, columns), lambda q, s: (0, 0))] * 4,
            out_specs=[pl.BlockSpec((rows, size), lambda q, s: (0, q))] * count,
        ),
        compiler_params=limit(40),
        cost_estimate=estimate(0, *four, *outs),
        name="place_quarters",
    )(spots, *four)


def tie(*values):
    return lax.optimization_barrier(values)


def body(reps, shards, tokens, cotangent, lengths, decay_rates, *weights):
    spread = reps // GROUP
    rep, place = lax.axis_index("rep"), lax.axis_index("shard")
    c, b, a = rep % 2, (rep // 2) % 2, rep // GROUP
    quarter = 2 * c + b
    micro, run, width = tokens.shape
    half, own = width // 2, width // GROUP
    streams = micro * GROUP // shards
    per_block = STREAM // run // GROUP * streams
    rows = width // shards
    part = rows // spread
    columns = functools.partial(lax.dynamic_slice_in_dim, axis=1)
    spots = jnp.stack([c, quarter, a, b]).astype(jnp.int32)
    blocks = [z * spread + k for k in range(spread) for z in range(shards)]

    def move(x, target):
        pairs = [(r * shards + s, target(r) * shards + s) for r in range(reps) for s in range(shards)]
        return lax.ppermute(x, AXES, pairs)

    def swap_c(x):
        return move(x, lambda r: r ^ 1)

    def swap_b(x):
        return move(x, lambda r: r ^ 2)

    def shift_a(x, k):
        return move(x, lambda r: (r + GROUP * k) % reps)

    def ordered(index, mine, other, axis):
        return jnp.where(
            index == 0,
            jnp.concatenate([mine, other], axis),
            jnp.concatenate([other, mine], axis),
        )


    def origin(r, s, p):
        run_id = (2 * (r % 2) + (r // 2) % 2) * per_block + p
        stream, piece = run_id // shards, run_id % shards
        if streams == 1:
            batch, member = s // GROUP, s % GROUP
        else:
            batch, member = s // 2, 2 * stream + s % 2
        return (r // GROUP) * GROUP + member, piece, batch

    def routes(p, batch):
        found = []
        for r in range(reps):
            for s in range(shards):
                from_r, from_s, from_batch = origin(r, s, p)
                if from_batch == batch:
                    found.append((from_r * shards + from_s, r * shards + s))
        return found

    def natural(x):
        return jnp.concatenate(
            [
                x[:, (k * shards + z) * part : (k * shards + z + 1) * part]
                for z in range(shards)
                for k in range(spread)
            ],
            axis=1,
        )

    def bring(x):
        slots = []
        for p in range(per_block):
            arrived = [lax.ppermute(x[m], AXES, routes(p, m)) for m in range(micro)]
            slots.append(functools.reduce(jnp.add, arrived))
        return jnp.concatenate(slots, axis=0)

    def bring_back(x):
        slots = natural(x).reshape(per_block, run, width)
        batches = []
        for m in range(micro):
            arrived = [
                lax.ppermute(slots[p], AXES, [(d, o) for o, d in routes(p, m)])
                for p in range(per_block)
            ]
            batches.append(functools.reduce(jnp.add, arrived))
        return jnp.stack(batches)


    def gather_b(x):
        return ordered(b, x, swap_b(x), 1)

    def gather_c(x):
        return ordered(c, x, swap_c(x), 1)

    def gather_rows_b(x):
        return ordered(b, x, swap_b(x), 0)

    def total(x):
        x = x + swap_c(x)
        return x + swap_b(x)

    def fold_c(product):
        sent = swap_c(product(1 - c).astype(LOW))
        return product(c) + sent.astype(F32)

    def fold_sent(values, members):
        return swap_c(fold_half(spots, values, members))

    def fold_kept(values, members, arrived):
        sent, mine = fold_half(spots, values, members, arrived)
        return mine, swap_b(sent)

    def fold_b(x):
        sent = swap_b(columns(x, (1 - b) * own, own).astype(LOW))
        return columns(x, b * own, own) + sent.astype(F32)

    def to_runs(x):
        cut = x.reshape(2, 2, -1, own)
        pick = functools.partial(lax.dynamic_index_in_dim, keepdims=False)
        both = ordered(b, pick(cut, b, 1), swap_b(pick(cut, 1 - b, 1)), 2)
        four = ordered(c, pick(both, c, 0), swap_c(pick(both, 1 - c, 0)), 1)
        return bring_back(four)


    def own_features(w):
        count = shards * spread // GROUP
        cut = []
        for i in range(count):
            block = quarter * count + i
            cut.append(columns(w, (block % shards) * rows + (block // shards) * part, part))
        return jnp.concatenate(cut, axis=1)

    def own_units(w):
        return columns(w, quarter * (w.shape[1] // GROUP), w.shape[1] // GROUP)

    def over_shards(*members):
        cut = jnp.concatenate(members, axis=1) if len(members) > 1 else members[0]
        piece = lax.dynamic_slice_in_dim(cut, a * part, part, 0)
        return lax.all_gather(piece, "shard", axis=0, tiled=True)

    def over_spread(x):
        return [shift_a(x, k) for k in range(1, spread)]

    def by_spread(relative):
        if spread == 2:
            return ordered(a, relative[0], relative[1], 0)
        stacked = jnp.stack(relative, 0)
        pick = functools.partial(lax.dynamic_index_in_dim, axis=0, keepdims=False)
        return jnp.concatenate([pick(stacked, (a - j) % spread) for j in range(spread)], axis=0)

    def in_row_order(x):
        cut = x.reshape(spread, shards, part, -1)
        return jnp.transpose(cut, (1, 0, 2, 3)).reshape(width, -1)

    def row_half(w, h):
        return lax.dynamic_slice_in_dim(w, h * half, half, 0)


    def owned_by(x, k):
        return columns(x, ((a + k) % spread) * (width // spread), width // spread)

    def away(left, right):
        return [cross_tokens(owned_by(left, k), right).astype(LOW) for k in range(1, spread)]

    def kept(left, right):
        return cross_tokens(owned_by(left, 0), right).astype(LOW)

    def sent_a(terms):
        return [shift_a(x, k + 1) for k, x in enumerate(terms)]

    def summed(mine, arrived):
        whole = mine.astype(F32)
        for x in arrived:
            whole = whole + x.astype(F32)
        return lax.psum_scatter(whole.astype(LOW), "shard", scatter_dimension=0, tiled=True)

    def spread_a(x):
        return by_spread([x] + over_spread(x))

    def spread_b(x):
        return (x, swap_b(x))

    def spread_c(two):
        return [*two, swap_c(two[0]), swap_c(two[1])]

    def features_in_order(four):
        pair = [ordered(b, four[n], four[n + 1], 1) for n in (0, 2)]
        return natural(ordered(c, pair[0], pair[1], 1)).astype(F32)


    w_query, w_key, w_value, w_gate, w_out, w_one, w_two, w_down = weights
    g_qk = over_shards(own_units(w_query), own_units(w_key))
    g_vg = over_shards(own_units(w_value), own_units(w_gate))
    g_o = over_shards(own_features(w_out))
    g_1 = over_shards(own_units(w_one))
    g_2 = over_shards(own_units(w_two))
    g_d = over_shards(own_units(w_down))

    heads = HEADS // GROUP
    rates = lax.dynamic_slice_in_dim(decay_rates, quarter * heads, heads, 0)
    cuts = gather_rows_b(lengths.reshape(1, -1))
    cuts = ordered(c, cuts, swap_c(cuts), 0).reshape(GROUP, micro, -1)
    if streams == 1:
        batch = place // GROUP
        member = place % GROUP
        chosen = lax.dynamic_slice_in_dim(cuts, 2 * (member % 2) + member // 2, 1, 0)
    else:
        batch = place // 2
        chosen = lax.dynamic_index_in_dim(cuts.reshape(2, 2, micro, -1), place % 2, 0, False)
    chosen = lax.dynamic_index_in_dim(chosen, batch, 1, False)
    seq_ends = [chosen[:, 0]]
    for i in range(1, chosen.shape[1]):
        seq_ends.append(seq_ends[-1] + chosen[:, i])
    ends = jnp.stack(seq_ends, axis=1)

    x_run = bring(tokens)
    x_run, g_qk = tie(x_run, g_qk)

    x_pair = gather_rows_b(x_run)
    s_qk = over_spread(g_qk)
    x_pair, s_qk, g_vg = tie(x_pair, s_qk, g_vg)

    s_vg = over_spread(g_vg)
    dy_run = bring(cotangent)
    w_qk = [g_qk, *s_qk]
    hidden_one, z_qk, x_scale, x_own = enter(spots, blocks, x_pair, swap_c(x_pair), w_qk)
    z_qk, hidden_one, s_vg, g_o, dy_run = tie(z_qk, hidden_one, s_vg, g_o, dy_run)

    s_o = over_spread(g_o)
    dy_pair = gather_rows_b(dy_run)
    w_vg = [g_vg, *s_vg]
    z_vg = project(spots, hidden_one, w_vg)
    attended = attend(rates, ends, z_qk, z_vg)
    gate = z_vg[:, own:]
    o_scale = lax.rsqrt(total(jnp.sum(attended * attended, axis=-1)) / width + EPSILON)[:, None]
    lifted = (attended * gate).astype(LOW)
    lifted, dy_pair, s_o, g_1 = tie(lifted, dy_pair, s_o, g_1)

    s_1 = over_spread(g_1)
    lifted = gather_b(lifted)
    dy_all, dy_own = enter(spots, blocks, dy_pair, swap_c(dy_pair))
    w_o = in_row_order(by_spread([g_o, *s_o]))
    lifted, s_1, g_2, dy_all, o_scale = tie(lifted, s_1, g_2, dy_all, o_scale)

    s_2 = over_spread(g_2)
    lifted = gather_c(lifted)
    branch = o_scale * matmul(lifted, w_o)
    middle = x_own.astype(F32) + branch
    low_middle = gather_b(middle.astype(LOW))
    low_middle, s_2, g_d = tie(low_middle, s_2, g_d)

    s_d = over_spread(g_d)
    w_1, w_2 = [g_1, *s_1], [g_2, *s_2]
    hidden_two, z_one, z_two, product, m_scale = gated_unit(
        spots, low_middle, swap_c(low_middle), w_1, w_2
    )
    t_down = away(dy_all, product)
    z_one, z_two, product, t_down, s_d = tie(z_one, z_two, product, t_down, s_d)

    r_down = sent_a(t_down)
    w_d = [g_d, *s_d]
    d_one, d_two, lean_m = gated_unit_back(spots, dy_all, z_one, z_two, w_d)
    arrived = fold_sent([d_one, d_two], [w_1, w_2])
    t_one = away(hidden_two, d_one)
    lean_m = total(lean_m[:, 0])
    d_one, d_two, t_one, arrived, lean_m = tie(d_one, d_two, t_one, arrived, lean_m)

    mine, crossed = fold_kept([d_one, d_two], [w_1, w_2], arrived)
    k_down = kept(dy_all, product)
    r_one = sent_a(t_one)
    t_two = away(hidden_two, d_two)
    k_one = kept(hidden_two, d_one)
    r_down, k_down, crossed, t_two = tie(r_down, k_down, crossed, t_two)

    f_down = summed(k_down, r_down)
    d_hidden = mine + crossed.astype(F32)
    m_normed = middle * m_scale
    lean = lean_m[:, None] * (2.0 / width)
    d_middle = dy_own.astype(F32) + m_scale * (d_hidden - m_normed * lean)
    d_branch = d_middle.astype(LOW)
    lean_o = total(jnp.sum(d_middle * branch, axis=-1))
    d_gated = fold_c(lambda h: times_transposed(d_branch, row_half(w_o, h)))
    r_two = sent_a(t_two)
    k_two = kept(hidden_two, d_two)
    r_one, k_one, d_gated, lean_o = tie(r_one, k_one, d_gated, lean_o)

    f_one = summed(k_one, r_one)
    d_gated = fold_b(d_gated)
    p_out = cross_tokens(lifted, (o_scale * d_middle).astype(LOW)).astype(LOW)
    p_out = jnp.transpose(p_out.reshape(shards, spread, part, -1), (1, 0, 2, 3))
    p_out = p_out.reshape(spread, width // spread, -1)
    t_out = [lax.dynamic_index_in_dim(p_out, (a + k) % spread, 0, False) for k in range(spread)]
    result = fold_sent([product], [w_d])
    d_gated, r_two, k_two, t_out, f_down, result = tie(d_gated, r_two, k_two, t_out, f_down, result)

    r_out = sent_a(t_out[1:])
    f_two = summed(k_two, r_two)
    y_down = spread_a(f_down)
    o_normed = attended * o_scale
    d_gate = (d_gated * o_normed).astype(LOW)
    lean = lean_o[:, None] / width
    d_attended = (o_scale * (d_gated * gate - o_normed * lean)).astype(LOW)
    result, result_b = fold_kept([product], [w_d], result)
    d_query, d_key, d_value = attend_back(rates, ends, z_qk, z_vg, d_attended)
    d_qk = jnp.concatenate([d_query, d_key], axis=1)
    d_vg = jnp.concatenate([d_value, d_gate], axis=1)
    t_qk = away(hidden_one, d_qk)
    d_qk, d_vg, t_qk, r_out, f_one, y_down, result_b = tie(
        d_qk, d_vg, t_qk, r_out, f_one, y_down, result_b
    )

    r_qk = sent_a(t_qk)
    f_out = summed(t_out[0], r_out)
    t_vg = away(hidden_one, d_vg)
    r_vg = sent_a(t_vg)
    arrived = fold_sent([d_qk, d_vg], [w_qk, w_vg])
    lean_x = total(
        jnp.sum(z_qk * d_qk.astype(F32), axis=-1) + jnp.sum(z_vg * d_vg.astype(F32), axis=-1)
    )
    k_qk = kept(hidden_one, d_qk)
    mine, crossed = fold_kept([d_qk, d_vg], [w_qk, w_vg], arrived)
    k_qk, r_qk, k_vg_in, f_two = tie(k_qk, r_qk, hidden_one, f_two)

    f_qk = summed(k_qk, r_qk)
    k_vg = kept(k_vg_in, d_vg)
    output = (middle + (result + result_b.astype(F32))).astype(LOW)
    d_hidden = mine + crossed.astype(F32)
    x_normed = x_own.astype(F32) * x_scale
    lean = lean_x[:, None] / width
    input_grad = (d_middle + x_scale * (d_hidden - x_normed * lean)).astype(LOW)
    k_vg, r_vg, f_one, f_two, f_out, output, input_grad = tie(
        k_vg, r_vg, f_one, f_two, f_out, output, input_grad
    )

    f_vg = summed(k_vg, r_vg)
    input_grad, output = to_runs(input_grad), to_runs(output)
    g_down = spread_c(spread_b(y_down))
    g_one = spread_c(spread_b(spread_a(f_one)))
    g_two = spread_c(spread_b(spread_a(f_two)))
    g_out = spread_c(spread_b(spread_a(f_out)))
    g_qk = spread_c(spread_b(spread_a(f_qk)))
    g_vg = spread_c(spread_b(spread_a(f_vg)))
    return (
        output,
        input_grad,
        *place_quarters(spots, g_qk, 2),
        *place_quarters(spots, g_vg, 2),
        features_in_order(g_out),
        *place_quarters(spots, g_one, 1),
        *place_quarters(spots, g_two, 1),
        *place_quarters(spots, g_down, 1),
    )


def solution(mesh):
    by_tokens = P(None, ("rep", "shard"), None)
    by_rows = P("shard", None)
    return jax.shard_map(
        functools.partial(body, mesh.shape["rep"], mesh.shape["shard"]),
        mesh=mesh,
        in_specs=(by_tokens, by_tokens, P(None, "rep", None), P(), *[by_rows] * 8),
        out_specs=(by_tokens, by_tokens, *[by_rows] * 8),
        check_vma=False,
    )
```

```python
import functools

import jax
import jax.numpy as jnp
from jax import lax
from jax.experimental import pallas as pl
from jax.experimental.pallas import tpu as pltpu
from jax.sharding import Mesh, PartitionSpec as P

HEADS = 16
HEAD_DIM = 128
STREAM = 1024
GROUP = 4
BLOCK = 256
TILE = 256
EPSILON = 1e-06
AXES = ("a", "b", "c", "shard")
OWNERS = ("a", "shard")
LOW = jnp.bfloat16
F32 = jnp.float32


def matmul(former, latter):
    return jnp.dot(former, latter, preferred_element_type=F32)


def times_transposed(former, latter):
    return lax.dot_general(former, latter, (((1,), (1,)), ((), ())), preferred_element_type=F32)


def cross_tokens(former, latter):
    return lax.dot_general(former, latter, (((0,), (0,)), ((), ())), preferred_element_type=F32)


def masked_decay(rate, ends, first, columns):
    row = first + lax.broadcasted_iota(jnp.int32, (BLOCK, 1), 0)
    column = lax.broadcasted_iota(jnp.int32, (1, columns), 1)
    begin = jnp.zeros((BLOCK, 1), jnp.int32)
    for end in ends:
        begin = jnp.where(row >= end, end, begin)
    falling = jnp.exp(-rate * (row - first).astype(F32))
    rising = jnp.exp(rate * (column - first).astype(F32))
    allowed = (column <= row) & (column >= begin)
    return jnp.where(allowed, falling * rising, 0.0)


def attend_kernel(rates, ends, zq_ref, zk_ref, zv_ref, out_ref):
    stream, head = pl.program_id(0), pl.program_id(1)
    rate = rates[head]
    bounds = [ends[stream, i] for i in range(ends.shape[1])]
    zq, zk = zq_ref[...], zk_ref[...]
    q = (zq * jax.nn.sigmoid(zq)).astype(LOW)
    k = (zk * jax.nn.sigmoid(zk)).astype(LOW)
    v = zv_ref[...].astype(LOW)
    for first in range(0, STREAM, BLOCK):
        columns = first + BLOCK
        mask = masked_decay(rate, bounds, first, columns)
        scores = times_transposed(q[first:columns], k[:columns])
        weights = (scores * mask).astype(LOW)
        out_ref[first:columns, :] = matmul(weights, v[:columns])


def attend_back_kernel(
    rates, ends, zq_ref, zk_ref, zv_ref, do_ref, dzq_ref, dzk_ref, dzv_ref, dk_ref, dv_ref
):
    stream, head = pl.program_id(0), pl.program_id(1)
    rate = rates[head]
    bounds = [ends[stream, i] for i in range(ends.shape[1])]
    zq, zk = zq_ref[...], zk_ref[...]
    sig_q, sig_k = jax.nn.sigmoid(zq), jax.nn.sigmoid(zk)
    q = (zq * sig_q).astype(LOW)
    k = (zk * sig_k).astype(LOW)
    slope_q = sig_q * (1.0 + zq * (1.0 - sig_q))
    v = zv_ref[...].astype(LOW)
    d_o = do_ref[...]
    dk_ref[...] = jnp.zeros_like(dk_ref)
    dv_ref[...] = jnp.zeros_like(dv_ref)
    for first in range(0, STREAM, BLOCK):
        columns = first + BLOCK
        rows = slice(first, columns)
        mask = masked_decay(rate, bounds, first, columns)
        weights = (times_transposed(q[rows], k[:columns]) * mask).astype(LOW)
        d_scores = (times_transposed(d_o[rows], v[:columns]) * mask).astype(LOW)
        dzq_ref[rows, :] = (matmul(d_scores, k[:columns]) * slope_q[rows]).astype(LOW)
        dk_ref[:columns, :] += cross_tokens(d_scores, q[rows])
        dv_ref[:columns, :] += cross_tokens(weights, d_o[rows])
    dzk_ref[...] = (dk_ref[...] * (sig_k * (1.0 + zk * (1.0 - sig_k)))).astype(LOW)
    dzv_ref[...] = dv_ref[...].astype(LOW)


def head_block(offset=0):
    return pl.BlockSpec((STREAM, HEAD_DIM), lambda g, h, *_: (g, h + offset))


def attend(rates, ends, z_qk, z_vg):
    heads, streams = rates.shape[0], ends.shape[0]
    work = streams * heads * STREAM * STREAM
    return pl.pallas_call(
        attend_kernel,
        out_shape=jax.ShapeDtypeStruct((streams * STREAM, heads * HEAD_DIM), F32),
        grid_spec=pltpu.PrefetchScalarGridSpec(
            num_scalar_prefetch=2,
            grid=(streams, heads),
            in_specs=[head_block(), head_block(heads), head_block()],
            out_specs=head_block(),
        ),
        compiler_params=pltpu.CompilerParams(vmem_limit_bytes=40 << 20),
        cost_estimate=pl.CostEstimate(
            flops=4 * work * HEAD_DIM, transcendentals=work // 64,
            bytes_accessed=streams * heads * STREAM * HEAD_DIM * 16,
        ),
        name="attend",
    )(rates, ends, z_qk, z_qk, z_vg)


def attend_back(rates, ends, z_qk, z_vg, d_o):
    heads, streams = rates.shape[0], ends.shape[0]
    work = streams * heads * STREAM * STREAM
    return pl.pallas_call(
        attend_back_kernel,
        out_shape=[jax.ShapeDtypeStruct((streams * STREAM, heads * HEAD_DIM), LOW)] * 3,
        grid_spec=pltpu.PrefetchScalarGridSpec(
            num_scalar_prefetch=2,
            grid=(streams, heads),
            in_specs=[head_block(), head_block(heads), head_block(), head_block()],
            out_specs=[head_block()] * 3,
            scratch_shapes=[pltpu.VMEM((STREAM, HEAD_DIM), F32)] * 2,
        ),
        compiler_params=pltpu.CompilerParams(vmem_limit_bytes=40 << 20),
        cost_estimate=pl.CostEstimate(
            flops=10 * work * HEAD_DIM, transcendentals=work // 64,
            bytes_accessed=streams * heads * STREAM * HEAD_DIM * 20,
        ),
        name="attend_back",
    )(rates, ends, z_qk, z_qk, z_vg, d_o)


def chunk_copies(chunks, buffer, sems, turn, half=None):
    count, size = len(chunks), chunks[0].shape[0]
    if count == 1:
        rows = buffer.shape[0]
        first = 0 if half is None else pl.multiple_of(half * rows, rows)
        return [(None, pltpu.make_async_copy(chunks[0].at[pl.ds(first, rows)], buffer, sems.at[0]))]
    copies = []
    for k, chunk in enumerate(chunks):
        index = lax.rem(turn - k + count, count)
        wanted = None
        if half is not None:
            wanted = lax.div(index, count // 2) == half
            index = lax.rem(index, count // 2)
        target = buffer.at[pl.ds(pl.multiple_of(index * size, size), size)]
        copies.append((wanted, pltpu.make_async_copy(chunk, target, sems.at[k])))
    return copies


def each(copies, act):
    for wanted, copy in copies:
        if wanted is None:
            act(copy)
        else:
            pl.when(wanted)(functools.partial(act, copy))


def start(copies):
    each(copies, lambda copy: copy.start())


def finish(copies):
    each(copies, lambda copy: copy.wait())


def estimate(flops, *arrays):
    moved = sum(x.size * x.dtype.itemsize for x in arrays)
    return pl.CostEstimate(flops=flops, transcendentals=0, bytes_accessed=moved)


def limit(mebibytes):
    return pltpu.CompilerParams(vmem_limit_bytes=mebibytes << 20)


ANYWHERE = pl.BlockSpec(memory_space=pl.ANY)


def weight_buffer(chunks, share=1):
    size = len(chunks) * chunks[0].shape[0] // share
    return [pltpu.VMEM((size, chunks[0].shape[1]), LOW), pltpu.SemaphoreType.DMA((len(chunks),))]


def tile_rows(width, column=0):
    return pl.BlockSpec((TILE, width), lambda i, *_: (i, column))


def joined_rows(width, tiles):
    own = pl.BlockSpec((TILE, width), lambda i, s: (jnp.clip(i - s[0] * tiles, 0, tiles - 1), 0))
    other = pl.BlockSpec(
        (TILE, width), lambda i, s: (jnp.clip(i - (1 - s[0]) * tiles, 0, tiles - 1), 0)
    )
    return [own, other]


def enter_kernel(tiles, blocks, project, spots, own_ref, other_ref, *refs):
    i = pl.program_id(0)
    rows = jnp.where(i // tiles == spots[0], own_ref[...], other_ref[...])
    part = rows.shape[1] // len(blocks)
    permuted = jnp.concatenate([rows[:, n * part : (n + 1) * part] for n in blocks], axis=1)
    if not project:
        all_ref, quarter_ref = refs
        all_ref[...] = permuted
        held = all_ref
    else:
        chunks, (h_ref, z_ref, scale_ref, quarter_ref, held, buffer, sems) = refs[:-7], refs[-7:]
        held[...] = permuted
        copies = chunk_copies(chunks, buffer, sems, spots[2])

        @pl.when(i == 0)
        def _():
            start(copies)

        x = rows.astype(F32)
        scale = lax.rsqrt(jnp.mean(x * x, axis=-1, keepdims=True) + EPSILON)
        scale_ref[...] = scale
        hidden = (permuted.astype(F32) * scale).astype(LOW)
        h_ref[...] = hidden

        @pl.when(i == 0)
        def _():
            finish(copies)

        z_ref[...] = matmul(hidden, buffer[...])
    size = quarter_ref.shape[1]
    quarter_ref[...] = held[:, pl.ds(pl.multiple_of(spots[1] * size, size), size)]


def enter(spots, blocks, own, other, chunks=()):
    width = own.shape[1]
    count, tiles = 2 * own.shape[0], own.shape[0] // TILE
    shape = jax.ShapeDtypeStruct
    quarter = shape((count, width // GROUP), LOW)
    if chunks:
        columns = chunks[0].shape[1]
        outs = [shape((count, width), LOW), shape((count, columns), F32), shape((count, 1), F32), quarter]
        scratch = [pltpu.VMEM((TILE, width), LOW), *weight_buffer(chunks)]
    else:
        columns, scratch = 0, []
        outs = [shape((count, width), LOW), quarter]
    return pl.pallas_call(
        functools.partial(enter_kernel, tiles, blocks, bool(chunks)),
        out_shape=outs,
        grid_spec=pltpu.PrefetchScalarGridSpec(
            num_scalar_prefetch=1,
            grid=(2 * tiles,),
            in_specs=joined_rows(width, tiles) + [ANYWHERE] * len(chunks),
            out_specs=[tile_rows(o.shape[1]) for o in outs],
            scratch_shapes=scratch,
        ),
        compiler_params=limit(40),
        cost_estimate=estimate(2 * count * width * columns, own, other, *chunks, *outs),
        name="enter",
    )(spots, own, other, *chunks)


def project_kernel(spots, h_ref, *refs):
    chunks, (z_ref, buffer, sems) = refs[:-3], refs[-3:]
    copies = chunk_copies(chunks, buffer, sems, spots[2])

    @pl.when(pl.program_id(0) == 0)
    def _():
        start(copies)
        finish(copies)

    z_ref[...] = matmul(h_ref[...], buffer[...])


def project(spots, hidden, chunks):
    count, width = hidden.shape
    out = jax.ShapeDtypeStruct((count, chunks[0].shape[1]), F32)
    return pl.pallas_call(
        project_kernel,
        out_shape=out,
        grid_spec=pltpu.PrefetchScalarGridSpec(
            num_scalar_prefetch=1,
            grid=(count // TILE,),
            in_specs=[tile_rows(width)] + [ANYWHERE] * len(chunks),
            out_specs=tile_rows(out.shape[1]),
            scratch_shapes=weight_buffer(chunks),
        ),
        compiler_params=limit(40),
        cost_estimate=estimate(2 * count * width * out.shape[1], hidden, *chunks, out),
        name="project",
    )(spots, hidden, *chunks)


def unit_kernel(spots, own_ref, other_ref, *refs):
    chunks, rest = refs[:-9], refs[-9:]
    h_ref, one_ref, two_ref, product_ref, scale_ref, first, second, sem_one, sem_two = rest
    split = len(chunks) // 2
    copies = [
        chunk_copies(chunks[:split], first, sem_one, spots[2]),
        chunk_copies(chunks[split:], second, sem_two, spots[2]),
    ]
    begins = pl.program_id(0) == 0

    @pl.when(begins)
    def _():
        start(copies[0])
        start(copies[1])

    mine, other = own_ref[...], other_ref[...]
    swapped = spots[0] == 1
    middle = jnp.concatenate(
        [jnp.where(swapped, other, mine), jnp.where(swapped, mine, other)], axis=1
    ).astype(F32)
    scale = lax.rsqrt(jnp.mean(middle * middle, axis=-1, keepdims=True) + EPSILON)
    scale_ref[...] = scale
    hidden = (middle * scale).astype(LOW)
    h_ref[...] = hidden

    @pl.when(begins)
    def _():
        finish(copies[0])

    z_one = matmul(hidden, first[...])

    @pl.when(begins)
    def _():
        finish(copies[1])

    z_two = matmul(hidden, second[...])
    one_ref[...] = z_one.astype(LOW)
    two_ref[...] = z_two.astype(LOW)
    product_ref[...] = (z_one * z_two).astype(LOW)


def gated_unit(spots, own, other, first, second):
    count, width, units = own.shape[0], 2 * own.shape[1], first[0].shape[1]
    shape = jax.ShapeDtypeStruct
    outs = [shape((count, width), LOW)] + [shape((count, units), LOW)] * 3 + [shape((count, 1), F32)]
    (buffer, sems) = weight_buffer(first)
    return pl.pallas_call(
        unit_kernel,
        out_shape=outs,
        grid_spec=pltpu.PrefetchScalarGridSpec(
            num_scalar_prefetch=1,
            grid=(count // TILE,),
            in_specs=[tile_rows(width // 2)] * 2 + [ANYWHERE] * (2 * len(first)),
            out_specs=[tile_rows(o.shape[1]) for o in outs],
            scratch_shapes=[buffer, buffer, sems, sems],
        ),
        compiler_params=limit(48),
        cost_estimate=estimate(4 * count * width * units, own, other, *first, *second, *outs),
        name="gated_unit",
    )(spots, own, other, *first, *second)


def unit_back_kernel(spots, dy_ref, one_ref, two_ref, *refs):
    chunks, (d_one_ref, d_two_ref, sum_ref, buffer, sems) = refs[:-5], refs[-5:]
    copies = chunk_copies(chunks, buffer, sems, spots[2])

    @pl.when(pl.program_id(0) == 0)
    def _():
        start(copies)
        finish(copies)

    d_product = matmul(dy_ref[...], buffer[...])
    z_one, z_two = one_ref[...].astype(F32), two_ref[...].astype(F32)
    d_one = d_product * z_two
    d_one_ref[...] = d_one.astype(LOW)
    d_two_ref[...] = (d_product * z_one).astype(LOW)
    sum_ref[...] = jnp.sum(d_one * z_one, axis=-1, keepdims=True)


def gated_unit_back(spots, dy, z_one, z_two, chunks):
    count, width, units = dy.shape[0], dy.shape[1], z_one.shape[1]
    shape = jax.ShapeDtypeStruct
    outs = [shape((count, units), LOW)] * 2 + [shape((count, 1), F32)]
    return pl.pallas_call(
        unit_back_kernel,
        out_shape=outs,
        grid_spec=pltpu.PrefetchScalarGridSpec(
            num_scalar_prefetch=1,
            grid=(count // TILE,),
            in_specs=[tile_rows(width), tile_rows(units), tile_rows(units)] + [ANYWHERE] * len(chunks),
            out_specs=[tile_rows(o.shape[1]) for o in outs],
            scratch_shapes=weight_buffer(chunks),
        ),
        compiler_params=limit(40),
        cost_estimate=estimate(2 * count * width * units, dy, z_one, z_two, *chunks, *outs),
        name="gated_unit_back",
    )(spots, dy, z_one, z_two, *chunks)


def fold_kernel(members, keeps, spots, *refs):
    values, refs = refs[:members], refs[members:]
    arrived, refs = (refs[0], refs[1:]) if keeps else (None, refs)
    outs = 2 if keeps else 1
    chunks, refs = refs[: -outs - 2 * members], refs[-outs - 2 * members :]
    outs, buffers, sems = refs[:outs], refs[outs : outs + members], refs[outs + members :]
    each_count = len(chunks) // members
    half = spots[0] if keeps else 1 - spots[0]
    begins = pl.program_id(0) == 0
    copies = [
        chunk_copies(chunks[m * each_count : (m + 1) * each_count], buffers[m], sems[m], spots[2], half)
        for m in range(members)
    ]

    @pl.when(begins)
    def _():
        for m in range(members):
            start(copies[m])

    whole = None
    for m in range(members):
        pl.when(begins)(functools.partial(finish, copies[m]))
        term = times_transposed(values[m][...], buffers[m][...])
        whole = term if whole is None else whole + term
    if not keeps:
        outs[0][...] = whole.astype(LOW)
    else:
        whole = whole + arrived[...].astype(F32)
        size = whole.shape[1] // 2
        upper = spots[3] == 1
        outs[0][...] = jnp.where(upper, whole[:, :size], whole[:, size:]).astype(LOW)
        outs[1][...] = jnp.where(upper, whole[:, size:], whole[:, :size])


def fold_half(spots, values, weights, arrived=None):
    count = values[0].shape[0]
    half = len(weights[0]) * weights[0][0].shape[0] // 2
    shape = jax.ShapeDtypeStruct
    if arrived is None:
        outs, extra = [shape((count, half), LOW)], []
    else:
        outs, extra = [shape((count, half // 2), LOW), shape((count, half // 2), F32)], [arrived]
    buffers, sems = zip(*[weight_buffer(w, 2) for w in weights])
    chunks = [x for w in weights for x in w]
    flops = sum(2 * count * half * v.shape[1] for v in values)
    found = pl.pallas_call(
        functools.partial(fold_kernel, len(values), arrived is not None),
        out_shape=outs,
        grid_spec=pltpu.PrefetchScalarGridSpec(
            num_scalar_prefetch=1,
            grid=(count // TILE,),
            in_specs=[tile_rows(v.shape[1]) for v in values]
            + [tile_rows(half)] * len(extra)
            + [ANYWHERE] * len(chunks),
            out_specs=[tile_rows(o.shape[1]) for o in outs],
            scratch_shapes=[*buffers, *sems],
        ),
        compiler_params=limit(40),
        cost_estimate=estimate(flops, *values, *extra, *chunks[: len(chunks) // 2], *outs),
        name="fold_half",
    )(spots, *values, *extra, *chunks)
    return found[0] if arrived is None else found


def gradient_kernel(spots, left_ref, right_ref, *refs):
    found = cross_tokens(left_ref[...], right_ref[...])
    for arrived_ref in refs[:-1]:
        found = found + arrived_ref[...].astype(F32)
    refs[-1][...] = found.astype(LOW)


def gradient_rows(spots, spread, k, left, right, arrived=()):
    count, columns = right.shape
    rows = left.shape[1] // (1 if k is None else spread)
    tiles = rows // TILE

    def block(i, s):
        return (0, i if k is None else lax.rem(s[2] + k, spread) * tiles + i)

    out = jax.ShapeDtypeStruct((rows, columns), LOW)
    return pl.pallas_call(
        gradient_kernel,
        out_shape=out,
        grid_spec=pltpu.PrefetchScalarGridSpec(
            num_scalar_prefetch=1,
            grid=(tiles,),
            in_specs=[
                pl.BlockSpec((count, TILE), block),
                pl.BlockSpec((count, columns), lambda i, s: (0, 0), pipeline_mode=pl.Buffered(1)),
            ]
            + [tile_rows(columns)] * len(arrived),
            out_specs=tile_rows(columns),
        ),
        compiler_params=limit(40),
        cost_estimate=estimate(2 * count * rows * columns, right, out, out, *arrived),
        name="gradient_rows",
    )(spots, left, right, *arrived)


def place_kernel(count, spots, *refs):
    quarter = pl.program_id(0)
    cross = lax.rem(lax.div(quarter, 2) + spots[0], 2) * 2 + lax.rem(lax.rem(quarter, 2) + spots[3], 2)
    for n in range(4):

        @pl.when(cross == n)
        def _():
            size = refs[n].shape[1] // count
            for m in range(count):
                refs[4 + m][...] = refs[n][:, m * size : (m + 1) * size].astype(F32)


def place_quarters(spots, four, count):
    rows, columns = four[0][0].shape[0], four[0][2]
    size = columns // count
    outs = [jax.ShapeDtypeStruct((rows, GROUP * size), F32)] * count

    def block(index):
        return pl.BlockSpec((rows, columns), lambda q, s: (0, index))

    return pl.pallas_call(
        functools.partial(place_kernel, count),
        out_shape=outs,
        grid_spec=pltpu.PrefetchScalarGridSpec(
            num_scalar_prefetch=1,
            grid=(GROUP,),
            in_specs=[block(index) for _, index, _ in four],
            out_specs=[pl.BlockSpec((rows, size), lambda q, s: (0, q))] * count,
        ),
        compiler_params=limit(40),
        cost_estimate=estimate(0, *[x for x, _, _ in four], *outs),
        name="place_quarters",
    )(spots, *[x for x, _, _ in four])


def tie(*values):
    return lax.optimization_barrier(values)


def body(reps, shards, tokens, cotangent, lengths, decay_rates, *weights):
    spread = reps // GROUP
    place = lax.axis_index("shard")
    a, b, c = lax.axis_index("a"), lax.axis_index("b"), lax.axis_index("c")
    quarter = 2 * c + b
    micro, run, width = tokens.shape
    half, own = width // 2, width // GROUP
    streams = micro * GROUP // shards
    per_block = STREAM // run // GROUP * streams
    rows = width // shards
    part = rows // spread
    columns = functools.partial(lax.dynamic_slice_in_dim, axis=1)
    spots = jnp.stack([c, quarter, a, b]).astype(jnp.int32)
    blocks = [z * spread + k for k in range(spread) for z in range(shards)]

    def move(x, target):
        pairs = [(r * shards + s, target(r) * shards + s) for r in range(reps) for s in range(shards)]
        return lax.ppermute(x, AXES, pairs)

    def swap_c(x):
        return move(x, lambda r: r ^ 1)

    def swap_b(x):
        return move(x, lambda r: r ^ 2)

    def shift_a(x, k):
        return move(x, lambda r: (r + GROUP * k) % reps)

    def ordered(index, mine, other, axis):
        return jnp.where(
            index == 0,
            jnp.concatenate([mine, other], axis),
            jnp.concatenate([other, mine], axis),
        )


    def origin(r, s, p):
        run_id = (2 * (r % 2) + (r // 2) % 2) * per_block + p
        stream, piece = run_id // shards, run_id % shards
        if streams == 1:
            batch, member = s // GROUP, s % GROUP
        else:
            batch, member = s // 2, 2 * stream + s % 2
        return (r // GROUP) * GROUP + member, piece, batch

    def routes(p, batch):
        found = []
        for r in range(reps):
            for s in range(shards):
                from_r, from_s, from_batch = origin(r, s, p)
                if from_batch == batch:
                    found.append((from_r * shards + from_s, r * shards + s))
        return found

    def natural(x):
        return jnp.concatenate(
            [
                x[:, (k * shards + z) * part : (k * shards + z + 1) * part]
                for z in range(shards)
                for k in range(spread)
            ],
            axis=1,
        )

    def bring(x):
        slots = []
        for p in range(per_block):
            arrived = [lax.ppermute(x[m], AXES, routes(p, m)) for m in range(micro)]
            slots.append(functools.reduce(jnp.add, arrived))
        return jnp.concatenate(slots, axis=0)

    def bring_back(x):
        slots = natural(x).reshape(per_block, run, width)
        batches = []
        for m in range(micro):
            arrived = [
                lax.ppermute(slots[p], AXES, [(d, o) for o, d in routes(p, m)])
                for p in range(per_block)
            ]
            batches.append(functools.reduce(jnp.add, arrived))
        return jnp.stack(batches)


    def gather_b(x):
        return ordered(b, x, swap_b(x), 1)

    def gather_c(x):
        return ordered(c, x, swap_c(x), 1)

    def gather_rows_b(x):
        return ordered(b, x, swap_b(x), 0)

    def total(x):
        x = x + swap_c(x)
        return x + swap_b(x)

    def fold_c(product):
        sent = swap_c(product(1 - c).astype(LOW))
        return product(c) + sent.astype(F32)

    def fold_b(x):
        sent = swap_b(columns(x, (1 - b) * own, own).astype(LOW))
        return columns(x, b * own, own) + sent.astype(F32)

    def to_runs(x):
        cut = x.reshape(2, 2, -1, own)
        pick = functools.partial(lax.dynamic_index_in_dim, keepdims=False)
        both = ordered(b, pick(cut, b, 1), swap_b(pick(cut, 1 - b, 1)), 2)
        return ordered(c, pick(both, c, 0), swap_c(pick(both, 1 - c, 0)), 1)


    def own_features(w):
        count = shards * spread // GROUP
        cut = []
        for i in range(count):
            block = quarter * count + i
            cut.append(columns(w, (block % shards) * rows + (block // shards) * part, part))
        return jnp.concatenate(cut, axis=1)

    def own_units(w):
        return columns(w, quarter * (w.shape[1] // GROUP), w.shape[1] // GROUP)

    def over_shards(*members):
        cut = jnp.concatenate(members, axis=1) if len(members) > 1 else members[0]
        piece = lax.dynamic_slice_in_dim(cut, a * part, part, 0)
        return lax.all_gather(piece, "shard", axis=0, tiled=True)

    def over_owners(w):
        piece = lax.dynamic_slice_in_dim(w, a * part, part, 0)
        return lax.all_gather(piece, OWNERS, axis=0, tiled=True)

    def over_spread(x):
        return [shift_a(x, k) for k in range(1, spread)]

    def by_spread(relative):
        if spread == 2:
            return ordered(a, relative[0], relative[1], 0)
        stacked = jnp.stack(relative, 0)
        pick = functools.partial(lax.dynamic_index_in_dim, axis=0, keepdims=False)
        return jnp.concatenate([pick(stacked, (a - j) % spread) for j in range(spread)], axis=0)

    def in_row_order(x):
        cut = x.reshape(spread, shards, part, -1)
        return jnp.transpose(cut, (1, 0, 2, 3)).reshape(width, -1)

    def row_half(w, h):
        return lax.dynamic_slice_in_dim(w, h * half, half, 0)


    def away(left, right):
        return [gradient_rows(spots, spread, k, left, right) for k in range(1, spread)]

    def sent_a(terms):
        return [shift_a(x, k + 1) for k, x in enumerate(terms)]

    def scattered(x):
        return lax.psum_scatter(x, "shard", scatter_dimension=0, tiled=True)

    def whole_rows(left, right):
        return gradient_rows(spots, spread, None, left, right)

    def scattered_all(x):
        return lax.psum_scatter(x, OWNERS, scatter_dimension=0, tiled=True)

    def summed(left, right, arrived):
        return scattered(gradient_rows(spots, spread, 0, left, right, arrived))

    def spread_a(x):
        return by_spread([x] + over_spread(x))

    def spread_b(x):
        return jnp.concatenate([x, swap_b(x)], axis=1)

    def spread_c(pair):
        other, size = swap_c(pair), pair.shape[1] // 2
        return [(pair, 0, size), (pair, 1, size), (other, 0, size), (other, 1, size)]

    def features_in_order(four):
        cut = [x[:, index * size : (index + 1) * size] for x, index, size in four]
        pair = [ordered(b, cut[n], cut[n + 1], 1) for n in (0, 2)]
        return natural(ordered(c, pair[0], pair[1], 1)).astype(F32)


    w_query, w_key, w_value, w_gate, w_out, w_one, w_two, w_down = weights
    g_qk = over_shards(own_units(w_query), own_units(w_key))
    g_vg = over_shards(own_units(w_value), own_units(w_gate))
    g_o = over_shards(own_features(w_out))
    g_1 = over_shards(own_units(w_one))
    g_2 = over_shards(own_units(w_two))
    w_d = [over_owners(own_units(w_down))]

    heads = HEADS // GROUP
    rates = lax.dynamic_slice_in_dim(decay_rates, quarter * heads, heads, 0)
    cuts = gather_rows_b(lengths.reshape(1, -1))
    cuts = ordered(c, cuts, swap_c(cuts), 0).reshape(GROUP, micro, -1)
    if streams == 1:
        batch = place // GROUP
        member = place % GROUP
        chosen = lax.dynamic_slice_in_dim(cuts, 2 * (member % 2) + member // 2, 1, 0)
    else:
        batch = place // 2
        chosen = lax.dynamic_index_in_dim(cuts.reshape(2, 2, micro, -1), place % 2, 0, False)
    chosen = lax.dynamic_index_in_dim(chosen, batch, 1, False)
    seq_ends = [chosen[:, 0]]
    for i in range(1, chosen.shape[1]):
        seq_ends.append(seq_ends[-1] + chosen[:, i])
    ends = jnp.stack(seq_ends, axis=1)

    x_run = bring(tokens)
    x_run, g_qk = tie(x_run, g_qk)

    x_pair = gather_rows_b(x_run)
    s_qk = over_spread(g_qk)
    x_pair, s_qk, g_vg = tie(x_pair, s_qk, g_vg)

    s_vg = over_spread(g_vg)
    w_qk = [g_qk, *s_qk]
    hidden_one, z_qk, x_scale, x_own = enter(spots, blocks, x_pair, swap_c(x_pair), w_qk)
    z_qk, hidden_one, s_vg, g_o, cotangent = tie(z_qk, hidden_one, s_vg, g_o, cotangent)

    s_o = over_spread(g_o)
    dy_run = bring(cotangent)
    w_vg = [g_vg, *s_vg]
    z_vg = project(spots, hidden_one, w_vg)
    attended = attend(rates, ends, z_qk, z_vg)
    gate = z_vg[:, own:]
    o_scale = lax.rsqrt(total(jnp.sum(attended * attended, axis=-1)) / width + EPSILON)[:, None]
    lifted = (attended * gate).astype(LOW)
    lifted, s_o, g_1 = tie(lifted, s_o, g_1)

    s_1 = over_spread(g_1)
    lifted = gather_c(gather_b(lifted))
    w_o = in_row_order(by_spread([g_o, *s_o]))
    branch = o_scale * matmul(lifted, w_o)
    middle = x_own.astype(F32) + branch
    low_middle = middle.astype(LOW)
    low_middle, s_1, g_2 = tie(low_middle, s_1, g_2)

    s_2 = over_spread(g_2)
    low_middle = gather_b(low_middle)
    low_middle, dy_run = tie(low_middle, dy_run)

    other_middle = swap_c(low_middle)
    dy_pair = gather_rows_b(dy_run)
    other_middle, dy_pair, s_2 = tie(other_middle, dy_pair, s_2)

    dy_all, dy_own = enter(spots, blocks, dy_pair, swap_c(dy_pair))
    w_1, w_2 = [g_1, *s_1], [g_2, *s_2]
    hidden_two, z_one, z_two, product, m_scale = gated_unit(spots, low_middle, other_middle, w_1, w_2)
    f_down = scattered_all(whole_rows(dy_all, product))
    z_one, z_two, product, w_d[0] = tie(z_one, z_two, product, w_d[0])


    d_one, d_two, lean_m = gated_unit_back(spots, dy_all, z_one, z_two, w_d)
    sent = fold_half(spots, [d_one, d_two], [w_1, w_2])
    sent, d_two, lean_m = tie(sent, d_two, lean_m)

    arrived = swap_c(sent)
    t_two = away(hidden_two, d_two)
    lean_m = total(lean_m[:, 0])
    sent, mine = fold_half(spots, [d_one, d_two], [w_1, w_2], arrived)
    sent, d_one, t_two, product = tie(sent, d_one, t_two, product)

    crossed = swap_b(sent)
    cut = [(x[: x.shape[0] // 2], x[x.shape[0] // 2 :]) for x in t_two]
    upper = sent_a([x for x, _ in cut])
    f_one = whole_rows(hidden_two, d_one)
    result = fold_half(spots, [product], [w_d])
    crossed, result, lean_m, f_one, upper = tie(crossed, result, lean_m, f_one, upper)

    f_one = scattered_all(f_one)
    d_hidden = mine + crossed.astype(F32)
    m_normed = middle * m_scale
    lean = lean_m[:, None] * (2.0 / width)
    d_middle = dy_own.astype(F32) + m_scale * (d_hidden - m_normed * lean)
    d_branch = d_middle.astype(LOW)
    lean_o = jnp.sum(d_middle * branch, axis=-1)
    sent = times_transposed(d_branch, row_half(w_o, 1 - c)).astype(LOW)
    sent, result, d_middle, lean_o = tie(sent, result, d_middle, lean_o)

    arrived = swap_c(sent)
    r_result = swap_c(result)
    lean_o = total(lean_o)
    p_out = cross_tokens(lifted, (o_scale * d_middle).astype(LOW)).astype(LOW)
    p_out = jnp.transpose(p_out.reshape(shards, spread, part, -1), (1, 0, 2, 3))
    p_out = p_out.reshape(spread, width // spread, -1)
    t_out = [lax.dynamic_index_in_dim(p_out, (a + k) % spread, 0, False) for k in range(spread)]
    d_gated = times_transposed(d_branch, row_half(w_o, c)) + arrived.astype(F32)
    sent = columns(d_gated, (1 - b) * own, own).astype(LOW)
    mine = columns(d_gated, b * own, own)
    lower = [x for _, x in cut]
    sent, mine, lower, r_result, t_out = tie(sent, mine, lower, r_result, t_out)

    crossed = swap_b(sent)
    lower = sent_a(lower)
    result, result_mine = fold_half(spots, [product], [w_d], r_result)
    crossed, result, f_down, lean_o, lower, t_out = tie(crossed, result, f_down, lean_o, lower, t_out)

    r_two = [jnp.concatenate(pair, axis=0) for pair in zip(upper, lower)]
    f_two = summed(hidden_two, d_two, r_two)
    r_out = sent_a(t_out[1:])
    result = swap_b(result)
    y_down = spread_a(f_down)
    d_gated = mine + crossed.astype(F32)
    o_normed = attended * o_scale
    d_gate = (d_gated * o_normed).astype(LOW)
    lean = lean_o[:, None] / width
    d_attended = (o_scale * (d_gated * gate - o_normed * lean)).astype(LOW)
    d_query, d_key, d_value = attend_back(rates, ends, z_qk, z_vg, d_attended)
    d_qk = jnp.concatenate([d_query, d_key], axis=1)
    d_vg = jnp.concatenate([d_value, d_gate], axis=1)
    t_qk = away(hidden_one, d_qk)
    d_qk, d_vg, t_qk, r_out, y_down = tie(d_qk, d_vg, t_qk, r_out, y_down)

    r_qk = sent_a(t_qk)
    f_out = scattered(sum([x.astype(F32) for x in r_out], t_out[0].astype(F32)).astype(LOW))
    t_vg = away(hidden_one, d_vg)
    sent = fold_half(spots, [d_qk, d_vg], [w_qk, w_vg])
    sent, t_vg, result, d_qk, d_vg = tie(sent, t_vg, result, d_qk, d_vg)

    r_vg = sent_a(t_vg)
    arrived = swap_c(sent)
    x_down = spread_b(y_down)
    lean_x = total(
        jnp.sum(z_qk * d_qk.astype(F32), axis=-1) + jnp.sum(z_vg * d_vg.astype(F32), axis=-1)
    )
    sent, mine = fold_half(spots, [d_qk, d_vg], [w_qk, w_vg], arrived)
    output = (middle + (result_mine + result.astype(F32))).astype(LOW)
    sent, mine, r_qk, d_qk, d_vg, f_one, x_down, output = tie(
        sent, mine, r_qk, d_qk, d_vg, f_one, x_down, output
    )

    crossed = swap_b(sent)
    f_qk = summed(hidden_one, d_qk, r_qk)
    x_one = spread_b(f_one)
    output = to_runs(output)
    crossed, d_vg, r_vg, x_one, f_two, lean_x, output = tie(
        crossed, d_vg, r_vg, x_one, f_two, lean_x, output
    )

    vg_rows = gradient_rows(spots, spread, 0, hidden_one, d_vg, r_vg)
    vg_rows, crossed, x_one, f_two, f_out, output = tie(
        vg_rows, crossed, x_one, f_two, f_out, output
    )

    f_vg = scattered(vg_rows)
    d_hidden = mine + crossed.astype(F32)
    x_normed = x_own.astype(F32) * x_scale
    lean = lean_x[:, None] / width
    input_grad = (d_middle + x_scale * (d_hidden - x_normed * lean)).astype(LOW)
    output = bring_back(output)
    x_two = spread_b(f_two)
    y_one = spread_a(x_one)
    y_out = spread_a(f_out)
    input_grad = to_runs(input_grad)
    y_qk = spread_a(f_qk)
    output, input_grad, x_two, y_one, y_out, y_qk, f_vg = tie(
        output, input_grad, x_two, y_one, y_out, y_qk, f_vg
    )

    y_vg = spread_a(f_vg)
    x_qk = spread_b(y_qk)
    y_vg, x_qk = tie(y_vg, x_qk)

    x_vg = spread_b(y_vg)
    input_grad = bring_back(input_grad)
    y_two = spread_a(x_two)
    x_out = spread_b(y_out)
    return (
        output,
        input_grad,
        *place_quarters(spots, spread_c(x_qk), 2),
        *place_quarters(spots, spread_c(x_vg), 2),
        features_in_order(spread_c(x_out)),
        *place_quarters(spots, spread_c(y_one), 1),
        *place_quarters(spots, spread_c(y_two), 1),
        *place_quarters(spots, spread_c(x_down), 1),
    )


def solution(mesh):
    reps, shards = mesh.shape["rep"], mesh.shape["shard"]
    devices = mesh.devices.reshape(reps // GROUP, 2, 2, shards)
    rep = ("a", "b", "c")
    by_tokens = P(None, (*rep, "shard"), None)
    by_rows = P("shard", None)
    return jax.shard_map(
        functools.partial(body, reps, shards),
        mesh=Mesh(devices, AXES),
        in_specs=(by_tokens, by_tokens, P(None, rep, None), P(), *[by_rows] * 8),
        out_specs=(by_tokens, by_tokens, *[by_rows] * 8),
        check_vma=False,
    )
```

```python
import functools

import jax
import jax.numpy as jnp
from jax import lax
from jax.experimental import pallas as pl
from jax.experimental.pallas import tpu as pltpu
from jax.sharding import Mesh, PartitionSpec as P

HEADS = 16
HEAD_DIM = 128
STREAM = 1024
GROUP = 4
BLOCK = 256
TILE = 256
EPSILON = 1e-06
AXES = ("a", "b", "c", "shard")
OWNERS = ("a", "shard")
LOW = jnp.bfloat16
F32 = jnp.float32


def matmul(former, latter):
    return jnp.dot(former, latter, preferred_element_type=F32)


def times_transposed(former, latter):
    return lax.dot_general(former, latter, (((1,), (1,)), ((), ())), preferred_element_type=F32)


def cross_tokens(former, latter):
    return lax.dot_general(former, latter, (((0,), (0,)), ((), ())), preferred_element_type=F32)


def masked_decay(rate, ends, first, columns):
    row = first + lax.broadcasted_iota(jnp.int32, (BLOCK, 1), 0)
    column = lax.broadcasted_iota(jnp.int32, (1, columns), 1)
    begin = jnp.zeros((BLOCK, 1), jnp.int32)
    for end in ends:
        begin = jnp.where(row >= end, end, begin)
    falling = jnp.exp(-rate * (row - first).astype(F32))
    rising = jnp.exp(rate * (column - first).astype(F32))
    allowed = (column <= row) & (column >= begin)
    return jnp.where(allowed, falling * rising, 0.0)


def attend_kernel(rates, ends, zq_ref, zk_ref, zv_ref, out_ref):
    stream, head = pl.program_id(0), pl.program_id(1)
    rate = rates[head]
    bounds = [ends[stream, i] for i in range(ends.shape[1])]
    zq, zk = zq_ref[...], zk_ref[...]
    q = (zq * jax.nn.sigmoid(zq)).astype(LOW)
    k = (zk * jax.nn.sigmoid(zk)).astype(LOW)
    v = zv_ref[...].astype(LOW)
    for first in range(0, STREAM, BLOCK):
        columns = first + BLOCK
        mask = masked_decay(rate, bounds, first, columns)
        scores = times_transposed(q[first:columns], k[:columns])
        weights = (scores * mask).astype(LOW)
        out_ref[first:columns, :] = matmul(weights, v[:columns])


def attend_back_kernel(
    rates, ends, zq_ref, zk_ref, zv_ref, do_ref, dzq_ref, dzk_ref, dzv_ref, dk_ref, dv_ref
):
    stream, head = pl.program_id(0), pl.program_id(1)
    rate = rates[head]
    bounds = [ends[stream, i] for i in range(ends.shape[1])]
    zq, zk = zq_ref[...], zk_ref[...]
    sig_q, sig_k = jax.nn.sigmoid(zq), jax.nn.sigmoid(zk)
    q = (zq * sig_q).astype(LOW)
    k = (zk * sig_k).astype(LOW)
    slope_q = sig_q * (1.0 + zq * (1.0 - sig_q))
    v = zv_ref[...].astype(LOW)
    d_o = do_ref[...]
    dk_ref[...] = jnp.zeros_like(dk_ref)
    dv_ref[...] = jnp.zeros_like(dv_ref)
    for first in range(0, STREAM, BLOCK):
        columns = first + BLOCK
        rows = slice(first, columns)
        mask = masked_decay(rate, bounds, first, columns)
        weights = (times_transposed(q[rows], k[:columns]) * mask).astype(LOW)
        d_scores = (times_transposed(d_o[rows], v[:columns]) * mask).astype(LOW)
        dzq_ref[rows, :] = (matmul(d_scores, k[:columns]) * slope_q[rows]).astype(LOW)
        dk_ref[:columns, :] += cross_tokens(d_scores, q[rows])
        dv_ref[:columns, :] += cross_tokens(weights, d_o[rows])
    dzk_ref[...] = (dk_ref[...] * (sig_k * (1.0 + zk * (1.0 - sig_k)))).astype(LOW)
    dzv_ref[...] = dv_ref[...].astype(LOW)


def head_block(offset=0):
    return pl.BlockSpec((STREAM, HEAD_DIM), lambda g, h, *_: (g, h + offset))


def attend(rates, ends, z_qk, z_vg):
    heads, streams = rates.shape[0], ends.shape[0]
    work = streams * heads * STREAM * STREAM
    return pl.pallas_call(
        attend_kernel,
        out_shape=jax.ShapeDtypeStruct((streams * STREAM, heads * HEAD_DIM), F32),
        grid_spec=pltpu.PrefetchScalarGridSpec(
            num_scalar_prefetch=2,
            grid=(streams, heads),
            in_specs=[head_block(), head_block(heads), head_block()],
            out_specs=head_block(),
        ),
        compiler_params=pltpu.CompilerParams(vmem_limit_bytes=40 << 20),
        cost_estimate=pl.CostEstimate(
            flops=4 * work * HEAD_DIM, transcendentals=work // 64,
            bytes_accessed=streams * heads * STREAM * HEAD_DIM * 16,
        ),
        name="attend",
    )(rates, ends, z_qk, z_qk, z_vg)


def attend_back(rates, ends, z_qk, z_vg, d_o):
    heads, streams = rates.shape[0], ends.shape[0]
    work = streams * heads * STREAM * STREAM
    return pl.pallas_call(
        attend_back_kernel,
        out_shape=[jax.ShapeDtypeStruct((streams * STREAM, heads * HEAD_DIM), LOW)] * 3,
        grid_spec=pltpu.PrefetchScalarGridSpec(
            num_scalar_prefetch=2,
            grid=(streams, heads),
            in_specs=[head_block(), head_block(heads), head_block(), head_block()],
            out_specs=[head_block()] * 3,
            scratch_shapes=[pltpu.VMEM((STREAM, HEAD_DIM), F32)] * 2,
        ),
        compiler_params=pltpu.CompilerParams(vmem_limit_bytes=40 << 20),
        cost_estimate=pl.CostEstimate(
            flops=10 * work * HEAD_DIM, transcendentals=work // 64,
            bytes_accessed=streams * heads * STREAM * HEAD_DIM * 20,
        ),
        name="attend_back",
    )(rates, ends, z_qk, z_qk, z_vg, d_o)


def chunk_copies(chunks, buffer, sems, turn, half=None):
    count, size = len(chunks), chunks[0].shape[0]
    if count == 1:
        rows = buffer.shape[0]
        first = 0 if half is None else pl.multiple_of(half * rows, rows)
        return [(None, pltpu.make_async_copy(chunks[0].at[pl.ds(first, rows)], buffer, sems.at[0]))]
    copies = []
    for k, chunk in enumerate(chunks):
        index = lax.rem(turn - k + count, count)
        wanted = None
        if half is not None:
            wanted = lax.div(index, count // 2) == half
            index = lax.rem(index, count // 2)
        target = buffer.at[pl.ds(pl.multiple_of(index * size, size), size)]
        copies.append((wanted, pltpu.make_async_copy(chunk, target, sems.at[k])))
    return copies


def each(copies, act):
    for wanted, copy in copies:
        if wanted is None:
            act(copy)
        else:
            pl.when(wanted)(functools.partial(act, copy))


def start(copies):
    each(copies, lambda copy: copy.start())


def finish(copies):
    each(copies, lambda copy: copy.wait())


def estimate(flops, *arrays):
    moved = sum(x.size * x.dtype.itemsize for x in arrays)
    return pl.CostEstimate(flops=flops, transcendentals=0, bytes_accessed=moved)


def limit(mebibytes):
    return pltpu.CompilerParams(vmem_limit_bytes=mebibytes << 20)


ANYWHERE = pl.BlockSpec(memory_space=pl.ANY)


def weight_buffer(chunks, share=1):
    size = len(chunks) * chunks[0].shape[0] // share
    return [pltpu.VMEM((size, chunks[0].shape[1]), LOW), pltpu.SemaphoreType.DMA((len(chunks),))]


def tile_rows(width, column=0):
    return pl.BlockSpec((TILE, width), lambda i, *_: (i, column))


def joined_rows(width, tiles):
    own = pl.BlockSpec((TILE, width), lambda i, s: (jnp.clip(i - s[0] * tiles, 0, tiles - 1), 0))
    other = pl.BlockSpec(
        (TILE, width), lambda i, s: (jnp.clip(i - (1 - s[0]) * tiles, 0, tiles - 1), 0)
    )
    return [own, other]


def enter_kernel(tiles, blocks, project, spots, own_ref, other_ref, *refs):
    i = pl.program_id(0)
    rows = jnp.where(i // tiles == spots[0], own_ref[...], other_ref[...])
    part = rows.shape[1] // len(blocks)
    permuted = jnp.concatenate([rows[:, n * part : (n + 1) * part] for n in blocks], axis=1)
    if not project:
        all_ref, quarter_ref = refs
        all_ref[...] = permuted
        held = all_ref
    else:
        chunks, (h_ref, z_ref, scale_ref, quarter_ref, held, buffer, sems) = refs[:-7], refs[-7:]
        held[...] = permuted
        copies = chunk_copies(chunks, buffer, sems, spots[2])

        @pl.when(i == 0)
        def _():
            start(copies)

        x = rows.astype(F32)
        scale = lax.rsqrt(jnp.mean(x * x, axis=-1, keepdims=True) + EPSILON)
        scale_ref[...] = scale
        hidden = (permuted.astype(F32) * scale).astype(LOW)
        h_ref[...] = hidden

        @pl.when(i == 0)
        def _():
            finish(copies)

        z_ref[...] = matmul(hidden, buffer[...])
    size = quarter_ref.shape[1]
    quarter_ref[...] = held[:, pl.ds(pl.multiple_of(spots[1] * size, size), size)]


def enter(spots, blocks, own, other, chunks=()):
    width = own.shape[1]
    count, tiles = 2 * own.shape[0], own.shape[0] // TILE
    shape = jax.ShapeDtypeStruct
    quarter = shape((count, width // GROUP), LOW)
    if chunks:
        columns = chunks[0].shape[1]
        outs = [shape((count, width), LOW), shape((count, columns), F32), shape((count, 1), F32), quarter]
        scratch = [pltpu.VMEM((TILE, width), LOW), *weight_buffer(chunks)]
    else:
        columns, scratch = 0, []
        outs = [shape((count, width), LOW), quarter]
    return pl.pallas_call(
        functools.partial(enter_kernel, tiles, blocks, bool(chunks)),
        out_shape=outs,
        grid_spec=pltpu.PrefetchScalarGridSpec(
            num_scalar_prefetch=1,
            grid=(2 * tiles,),
            in_specs=joined_rows(width, tiles) + [ANYWHERE] * len(chunks),
            out_specs=[tile_rows(o.shape[1]) for o in outs],
            scratch_shapes=scratch,
        ),
        compiler_params=limit(40),
        cost_estimate=estimate(2 * count * width * columns, own, other, *chunks, *outs),
        name="enter",
    )(spots, own, other, *chunks)


def project_kernel(spots, h_ref, *refs):
    chunks, (z_ref, buffer, sems) = refs[:-3], refs[-3:]
    copies = chunk_copies(chunks, buffer, sems, spots[2])

    @pl.when(pl.program_id(0) == 0)
    def _():
        start(copies)
        finish(copies)

    z_ref[...] = matmul(h_ref[...], buffer[...])


def project(spots, hidden, chunks):
    count, width = hidden.shape
    out = jax.ShapeDtypeStruct((count, chunks[0].shape[1]), F32)
    return pl.pallas_call(
        project_kernel,
        out_shape=out,
        grid_spec=pltpu.PrefetchScalarGridSpec(
            num_scalar_prefetch=1,
            grid=(count // TILE,),
            in_specs=[tile_rows(width)] + [ANYWHERE] * len(chunks),
            out_specs=tile_rows(out.shape[1]),
            scratch_shapes=weight_buffer(chunks),
        ),
        compiler_params=limit(40),
        cost_estimate=estimate(2 * count * width * out.shape[1], hidden, *chunks, out),
        name="project",
    )(spots, hidden, *chunks)


def unit_kernel(spots, own_ref, other_ref, *refs):
    chunks, rest = refs[:-9], refs[-9:]
    h_ref, one_ref, two_ref, product_ref, scale_ref, first, second, sem_one, sem_two = rest
    split = len(chunks) // 2
    copies = [
        chunk_copies(chunks[:split], first, sem_one, spots[2]),
        chunk_copies(chunks[split:], second, sem_two, spots[2]),
    ]
    begins = pl.program_id(0) == 0

    @pl.when(begins)
    def _():
        start(copies[0])
        start(copies[1])

    mine, other = own_ref[...], other_ref[...]
    swapped = spots[0] == 1
    middle = jnp.concatenate(
        [jnp.where(swapped, other, mine), jnp.where(swapped, mine, other)], axis=1
    ).astype(F32)
    scale = lax.rsqrt(jnp.mean(middle * middle, axis=-1, keepdims=True) + EPSILON)
    scale_ref[...] = scale
    hidden = (middle * scale).astype(LOW)
    h_ref[...] = hidden

    @pl.when(begins)
    def _():
        finish(copies[0])

    z_one = matmul(hidden, first[...])

    @pl.when(begins)
    def _():
        finish(copies[1])

    z_two = matmul(hidden, second[...])
    one_ref[...] = z_one.astype(LOW)
    two_ref[...] = z_two.astype(LOW)
    product_ref[...] = (z_one * z_two).astype(LOW)


def gated_unit(spots, own, other, first, second):
    count, width, units = own.shape[0], 2 * own.shape[1], first[0].shape[1]
    shape = jax.ShapeDtypeStruct
    outs = [shape((count, width), LOW)] + [shape((count, units), LOW)] * 3 + [shape((count, 1), F32)]
    (buffer, sems) = weight_buffer(first)
    return pl.pallas_call(
        unit_kernel,
        out_shape=outs,
        grid_spec=pltpu.PrefetchScalarGridSpec(
            num_scalar_prefetch=1,
            grid=(count // TILE,),
            in_specs=[tile_rows(width // 2)] * 2 + [ANYWHERE] * (2 * len(first)),
            out_specs=[tile_rows(o.shape[1]) for o in outs],
            scratch_shapes=[buffer, buffer, sems, sems],
        ),
        compiler_params=limit(48),
        cost_estimate=estimate(4 * count * width * units, own, other, *first, *second, *outs),
        name="gated_unit",
    )(spots, own, other, *first, *second)


def unit_back_kernel(spots, dy_ref, one_ref, two_ref, *refs):
    chunks, (d_one_ref, d_two_ref, sum_ref, buffer, sems) = refs[:-5], refs[-5:]
    copies = chunk_copies(chunks, buffer, sems, spots[2])

    @pl.when(pl.program_id(0) == 0)
    def _():
        start(copies)
        finish(copies)

    d_product = matmul(dy_ref[...], buffer[...])
    z_one, z_two = one_ref[...].astype(F32), two_ref[...].astype(F32)
    d_one = d_product * z_two
    d_one_ref[...] = d_one.astype(LOW)
    d_two_ref[...] = (d_product * z_one).astype(LOW)
    sum_ref[...] = jnp.sum(d_one * z_one, axis=-1, keepdims=True)


def gated_unit_back(spots, dy, z_one, z_two, chunks):
    count, width, units = dy.shape[0], dy.shape[1], z_one.shape[1]
    shape = jax.ShapeDtypeStruct
    outs = [shape((count, units), LOW)] * 2 + [shape((count, 1), F32)]
    return pl.pallas_call(
        unit_back_kernel,
        out_shape=outs,
        grid_spec=pltpu.PrefetchScalarGridSpec(
            num_scalar_prefetch=1,
            grid=(count // TILE,),
            in_specs=[tile_rows(width), tile_rows(units), tile_rows(units)] + [ANYWHERE] * len(chunks),
            out_specs=[tile_rows(o.shape[1]) for o in outs],
            scratch_shapes=weight_buffer(chunks),
        ),
        compiler_params=limit(40),
        cost_estimate=estimate(2 * count * width * units, dy, z_one, z_two, *chunks, *outs),
        name="gated_unit_back",
    )(spots, dy, z_one, z_two, *chunks)


def fold_kernel(members, keeps, spots, *refs):
    values, refs = refs[:members], refs[members:]
    arrived, refs = (refs[0], refs[1:]) if keeps else (None, refs)
    outs = 2 if keeps else 1
    chunks, refs = refs[: -outs - 2 * members], refs[-outs - 2 * members :]
    outs, buffers, sems = refs[:outs], refs[outs : outs + members], refs[outs + members :]
    each_count = len(chunks) // members
    half = spots[0] if keeps else 1 - spots[0]
    begins = pl.program_id(0) == 0
    copies = [
        chunk_copies(chunks[m * each_count : (m + 1) * each_count], buffers[m], sems[m], spots[2], half)
        for m in range(members)
    ]

    @pl.when(begins)
    def _():
        for m in range(members):
            start(copies[m])

    whole = None
    for m in range(members):
        pl.when(begins)(functools.partial(finish, copies[m]))
        term = times_transposed(values[m][...], buffers[m][...])
        whole = term if whole is None else whole + term
    if not keeps:
        outs[0][...] = whole.astype(LOW)
    else:
        whole = whole + arrived[...].astype(F32)
        size = whole.shape[1] // 2
        upper = spots[3] == 1
        outs[0][...] = jnp.where(upper, whole[:, :size], whole[:, size:]).astype(LOW)
        outs[1][...] = jnp.where(upper, whole[:, size:], whole[:, :size])


def fold_half(spots, values, weights, arrived=None):
    count = values[0].shape[0]
    half = len(weights[0]) * weights[0][0].shape[0] // 2
    shape = jax.ShapeDtypeStruct
    if arrived is None:
        outs, extra = [shape((count, half), LOW)], []
    else:
        outs, extra = [shape((count, half // 2), LOW), shape((count, half // 2), F32)], [arrived]
    buffers, sems = zip(*[weight_buffer(w, 2) for w in weights])
    chunks = [x for w in weights for x in w]
    flops = sum(2 * count * half * v.shape[1] for v in values)
    found = pl.pallas_call(
        functools.partial(fold_kernel, len(values), arrived is not None),
        out_shape=outs,
        grid_spec=pltpu.PrefetchScalarGridSpec(
            num_scalar_prefetch=1,
            grid=(count // TILE,),
            in_specs=[tile_rows(v.shape[1]) for v in values]
            + [tile_rows(half)] * len(extra)
            + [ANYWHERE] * len(chunks),
            out_specs=[tile_rows(o.shape[1]) for o in outs],
            scratch_shapes=[*buffers, *sems],
        ),
        compiler_params=limit(40),
        cost_estimate=estimate(flops, *values, *extra, *chunks[: len(chunks) // 2], *outs),
        name="fold_half",
    )(spots, *values, *extra, *chunks)
    return found[0] if arrived is None else found


def gradient_kernel(spots, left_ref, right_ref, *refs):
    found = cross_tokens(left_ref[...], right_ref[...])
    for arrived_ref in refs[:-1]:
        found = found + arrived_ref[...].astype(F32)
    refs[-1][...] = found.astype(LOW)


def gradient_rows(spots, spread, k, left, right, arrived=()):
    count, columns = right.shape
    rows = left.shape[1] // (1 if k is None else spread)
    tiles = rows // TILE

    def block(i, s):
        return (0, i if k is None else lax.rem(s[2] + k, spread) * tiles + i)

    out = jax.ShapeDtypeStruct((rows, columns), LOW)
    return pl.pallas_call(
        gradient_kernel,
        out_shape=out,
        grid_spec=pltpu.PrefetchScalarGridSpec(
            num_scalar_prefetch=1,
            grid=(tiles,),
            in_specs=[
                pl.BlockSpec((count, TILE), block),
                pl.BlockSpec((count, columns), lambda i, s: (0, 0), pipeline_mode=pl.Buffered(1)),
            ]
            + [tile_rows(columns)] * len(arrived),
            out_specs=tile_rows(columns),
        ),
        compiler_params=limit(40),
        cost_estimate=estimate(2 * count * rows * columns, right, out, out, *arrived),
        name="gradient_rows",
    )(spots, left, right, *arrived)


def place_kernel(cuts, spots, *refs):
    quarter = pl.program_id(0)
    cross = lax.rem(lax.div(quarter, 2) + spots[0], 2) * 2 + lax.rem(lax.rem(quarter, 2) + spots[3], 2)
    for n in range(4):

        @pl.when(cross == n)
        def _():
            for (first, size), out_ref in zip(cuts, refs[4:]):
                out_ref[...] = refs[n][:, first : first + size].astype(F32)


def place_quarters(spots, four, *cuts):
    rows, columns = four[0][0].shape[0], four[0][2]
    outs = [jax.ShapeDtypeStruct((rows, GROUP * size), F32) for _, size in cuts]

    def block(index):
        return pl.BlockSpec((rows, columns), lambda q, s: (0, index), pipeline_mode=pl.Buffered(1))

    return pl.pallas_call(
        functools.partial(place_kernel, cuts),
        out_shape=outs,
        grid_spec=pltpu.PrefetchScalarGridSpec(
            num_scalar_prefetch=1,
            grid=(GROUP,),
            in_specs=[block(index) for _, index, _ in four],
            out_specs=[pl.BlockSpec((rows, size), lambda q, s: (0, q)) for _, size in cuts],
        ),
        compiler_params=limit(40),
        cost_estimate=estimate(0, *[x for x, _, _ in four], *outs),
        name="place_quarters",
    )(spots, *[x for x, _, _ in four])


def tie(*values):
    return lax.optimization_barrier(values)


def body(reps, shards, tokens, cotangent, lengths, decay_rates, *weights):
    spread = reps // GROUP
    place = lax.axis_index("shard")
    a, b, c = lax.axis_index("a"), lax.axis_index("b"), lax.axis_index("c")
    quarter = 2 * c + b
    micro, run, width = tokens.shape
    half, own = width // 2, width // GROUP
    streams = micro * GROUP // shards
    per_block = STREAM // run // GROUP * streams
    rows = width // shards
    part = rows // spread
    columns = functools.partial(lax.dynamic_slice_in_dim, axis=1)
    spots = jnp.stack([c, quarter, a, b]).astype(jnp.int32)
    blocks = [z * spread + k for k in range(spread) for z in range(shards)]

    def move(x, target):
        pairs = [(r * shards + s, target(r) * shards + s) for r in range(reps) for s in range(shards)]
        return lax.ppermute(x, AXES, pairs)

    def swap_c(x):
        return move(x, lambda r: r ^ 1)

    def swap_b(x):
        return move(x, lambda r: r ^ 2)

    def joined(*parts):
        return jnp.concatenate(parts, axis=1)

    def shift_a(x, k):
        return move(x, lambda r: (r + GROUP * k) % reps)

    def ordered(index, mine, other, axis):
        return jnp.where(
            index == 0,
            jnp.concatenate([mine, other], axis),
            jnp.concatenate([other, mine], axis),
        )


    def batch_of(s):
        return s // (shards // micro)

    def origin(r, s, p):
        run_id = (2 * (r % 2) + (r // 2) % 2) * per_block + p
        stream, piece = run_id // shards, run_id % shards
        member = s % GROUP if streams == 1 else 2 * stream + s % 2
        return (r // GROUP) * GROUP + member, piece

    def routes(p):
        found = []
        for r in range(reps):
            for s in range(shards):
                from_r, from_s = origin(r, s, p ^ batch_of(s))
                found.append((from_r * shards + from_s, r * shards + s))
        return found

    def natural(x):
        return jnp.concatenate(
            [
                x[:, (k * shards + z) * part : (k * shards + z + 1) * part]
                for z in range(shards)
                for k in range(spread)
            ],
            axis=1,
        )

    def bring(x):
        arrived = [
            lax.ppermute(lax.dynamic_index_in_dim(x, (place + p) % 2, 0, False), AXES, routes(p))
            for p in range(2)
        ]
        return ordered(batch_of(place), *arrived, 0)

    def bring_back(x):
        slots = natural(x).reshape(2, run, width)
        arrived = [
            lax.ppermute(
                lax.dynamic_index_in_dim(slots, (batch_of(place) + p) % 2, 0, False),
                AXES,
                [(to, origin) for origin, to in routes(p)],
            )
            for p in range(2)
        ]
        return ordered(place % 2, arrived[0][None], arrived[1][None], 0)


    def gather_b(x):
        return ordered(b, x, swap_b(x), 1)

    def gather_c(x):
        return ordered(c, x, swap_c(x), 1)

    def gather_rows_b(x):
        return ordered(b, x, swap_b(x), 0)

    def total(x):
        x = x + swap_c(x)
        return x + swap_b(x)

    def fold_c(product):
        sent = swap_c(product(1 - c).astype(LOW))
        return product(c) + sent.astype(F32)

    def fold_b(x):
        sent = swap_b(columns(x, (1 - b) * own, own).astype(LOW))
        return columns(x, b * own, own) + sent.astype(F32)

    def to_runs(x):
        cut = x.reshape(2, 2, -1, own)
        pick = functools.partial(lax.dynamic_index_in_dim, keepdims=False)
        both = ordered(b, pick(cut, b, 1), swap_b(pick(cut, 1 - b, 1)), 2)
        return ordered(c, pick(both, c, 0), swap_c(pick(both, 1 - c, 0)), 1)


    def own_features(w):
        count = shards * spread // GROUP
        cut = []
        for i in range(count):
            block = quarter * count + i
            cut.append(columns(w, (block % shards) * rows + (block // shards) * part, part))
        return jnp.concatenate(cut, axis=1)

    def own_units(w):
        return columns(w, quarter * (w.shape[1] // GROUP), w.shape[1] // GROUP)

    def over_shards(*members):
        cut = jnp.concatenate(members, axis=1) if len(members) > 1 else members[0]
        piece = lax.dynamic_slice_in_dim(cut, a * part, part, 0)
        return lax.all_gather(piece, "shard", axis=0, tiled=True)

    def over_owners(w):
        piece = lax.dynamic_slice_in_dim(w, a * part, part, 0)
        return lax.all_gather(piece, OWNERS, axis=0, tiled=True)

    def over_spread(x):
        return [shift_a(x, k) for k in range(1, spread)]

    def by_spread(relative):
        if spread == 2:
            return ordered(a, relative[0], relative[1], 0)
        stacked = jnp.stack(relative, 0)
        pick = functools.partial(lax.dynamic_index_in_dim, axis=0, keepdims=False)
        return jnp.concatenate([pick(stacked, (a - j) % spread) for j in range(spread)], axis=0)

    def in_row_order(x):
        cut = x.reshape(spread, shards, part, -1)
        return jnp.transpose(cut, (1, 0, 2, 3)).reshape(width, -1)

    def row_half(w, h):
        return lax.dynamic_slice_in_dim(w, h * half, half, 0)


    def away(left, right):
        return [gradient_rows(spots, spread, k, left, right) for k in range(1, spread)]

    def sent_a(terms):
        return [shift_a(x, k + 1) for k, x in enumerate(terms)]

    def scattered(x):
        return lax.psum_scatter(x, "shard", scatter_dimension=0, tiled=True)

    def whole_rows(left, right):
        return gradient_rows(spots, spread, None, left, right)

    def scattered_all(x):
        return lax.psum_scatter(x, OWNERS, scatter_dimension=0, tiled=True)

    def summed(left, right, arrived):
        return scattered(gradient_rows(spots, spread, 0, left, right, arrived))

    def spread_a(x):
        return by_spread([x] + over_spread(x))

    def spread_b(x):
        return jnp.concatenate([x, swap_b(x)], axis=1)

    def spread_c(pair):
        other, size = swap_c(pair), pair.shape[1] // 2
        return [(pair, 0, size), (pair, 1, size), (other, 0, size), (other, 1, size)]

    def features_in_order(four, first, size):
        cut = [x[:, index * full + first : index * full + first + size] for x, index, full in four]
        pair = [ordered(b, cut[n], cut[n + 1], 1) for n in (0, 2)]
        return natural(ordered(c, pair[0], pair[1], 1)).astype(F32)


    w_query, w_key, w_value, w_gate, w_out, w_one, w_two, w_down = weights
    g_qk = over_shards(own_units(w_query), own_units(w_key))
    g_vg = over_shards(own_units(w_value), own_units(w_gate))
    g_o = over_shards(own_features(w_out))
    g_1 = over_shards(own_units(w_one))
    g_2 = over_shards(own_units(w_two))
    w_d = [over_owners(own_units(w_down))]

    heads = HEADS // GROUP
    rates = lax.dynamic_slice_in_dim(decay_rates, quarter * heads, heads, 0)
    cuts = gather_rows_b(lengths.reshape(1, -1))
    cuts = ordered(c, cuts, swap_c(cuts), 0).reshape(GROUP, micro, -1)
    if streams == 1:
        batch = place // GROUP
        member = place % GROUP
        chosen = lax.dynamic_slice_in_dim(cuts, 2 * (member % 2) + member // 2, 1, 0)
    else:
        batch = place // 2
        chosen = lax.dynamic_index_in_dim(cuts.reshape(2, 2, micro, -1), place % 2, 0, False)
    chosen = lax.dynamic_index_in_dim(chosen, batch, 1, False)
    seq_ends = [chosen[:, 0]]
    for i in range(1, chosen.shape[1]):
        seq_ends.append(seq_ends[-1] + chosen[:, i])
    ends = jnp.stack(seq_ends, axis=1)

    x_run = bring(tokens)
    x_run, g_qk = tie(x_run, g_qk)

    x_pair = gather_rows_b(x_run)
    s_qk = over_spread(g_qk)
    x_pair, s_qk, g_vg = tie(x_pair, s_qk, g_vg)

    s_vg = over_spread(g_vg)
    w_qk = [g_qk, *s_qk]
    hidden_one, z_qk, x_scale, x_own = enter(spots, blocks, x_pair, swap_c(x_pair), w_qk)
    z_qk, hidden_one, s_vg, g_o = tie(z_qk, hidden_one, s_vg, g_o)

    s_o = over_spread(g_o)
    w_vg = [g_vg, *s_vg]
    z_vg = project(spots, hidden_one, w_vg)
    attended = attend(rates, ends, z_qk, z_vg)
    gate = z_vg[:, own:]
    o_scale = lax.rsqrt(total(jnp.sum(attended * attended, axis=-1)) / width + EPSILON)[:, None]
    lifted = (attended * gate).astype(LOW)
    lifted, s_o, g_1, cotangent = tie(lifted, s_o, g_1, cotangent)

    s_1 = over_spread(g_1)
    lifted = gather_b(lifted)
    lifted, s_1, g_2, o_scale, cotangent = tie(lifted, s_1, g_2, o_scale, cotangent)

    s_2 = over_spread(g_2)
    dy_run = bring(cotangent)
    lifted = gather_c(lifted)
    w_o = in_row_order(by_spread([g_o, *s_o]))
    branch = o_scale * matmul(lifted, w_o)
    middle = x_own.astype(F32) + branch
    low_middle = gather_b(middle.astype(LOW))
    low_middle, s_2, dy_run = tie(low_middle, s_2, dy_run)

    other_middle = swap_c(low_middle)
    dy_pair = gather_rows_b(dy_run)
    w_1, w_2 = [g_1, *s_1], [g_2, *s_2]
    hidden_two, z_one, z_two, product, m_scale = gated_unit(spots, low_middle, other_middle, w_1, w_2)
    z_one, z_two, product, dy_pair = tie(z_one, z_two, product, dy_pair)

    dy_all, dy_own = enter(spots, blocks, dy_pair, swap_c(dy_pair))
    f_down = whole_rows(dy_all, product)
    z_one, z_two, product, f_down, w_d[0] = tie(z_one, z_two, product, f_down, w_d[0])


    f_down = scattered_all(f_down)
    d_one, d_two, lean_m = gated_unit_back(spots, dy_all, z_one, z_two, w_d)
    sent = fold_half(spots, [d_one, d_two], [w_1, w_2])
    sent, d_two, lean_m = tie(sent, d_two, lean_m)

    arrived = swap_c(sent)
    t_two = away(hidden_two, d_two)
    lean_m = total(lean_m[:, 0])
    sent, mine = fold_half(spots, [d_one, d_two], [w_1, w_2], arrived)
    sent, d_one, t_two, product, lean_m = tie(sent, d_one, t_two, product, lean_m)

    crossed = swap_b(sent)
    cut = [(x[: x.shape[0] // 2], x[x.shape[0] // 2 :]) for x in t_two]
    upper = sent_a([x for x, _ in cut])
    f_one = whole_rows(hidden_two, d_one)
    result = fold_half(spots, [product], [w_d])
    crossed, result, f_one, upper = tie(crossed, result, f_one, upper)

    f_one = scattered_all(f_one)
    d_hidden = mine + crossed.astype(F32)
    m_normed = middle * m_scale
    lean = lean_m[:, None] * (2.0 / width)
    d_middle = dy_own.astype(F32) + m_scale * (d_hidden - m_normed * lean)
    d_branch = d_middle.astype(LOW)
    lean_o = jnp.sum(d_middle * branch, axis=-1)
    sent = times_transposed(d_branch, row_half(w_o, 1 - c)).astype(LOW)
    sent, result, d_middle, lean_o = tie(sent, result, d_middle, lean_o)

    arrived = swap_c(sent)
    r_result = swap_c(result)
    lean_o = total(lean_o)
    p_out = cross_tokens(lifted, (o_scale * d_middle).astype(LOW)).astype(LOW)
    p_out = jnp.transpose(p_out.reshape(shards, spread, part, -1), (1, 0, 2, 3))
    p_out = p_out.reshape(spread, width // spread, -1)
    t_out = [lax.dynamic_index_in_dim(p_out, (a + k) % spread, 0, False) for k in range(spread)]
    d_gated = times_transposed(d_branch, row_half(w_o, c)) + arrived.astype(F32)
    sent = columns(d_gated, (1 - b) * own, own).astype(LOW)
    mine = columns(d_gated, b * own, own)
    lower = [x for _, x in cut]
    sent, mine, lower, r_result, t_out, lean_o = tie(sent, mine, lower, r_result, t_out, lean_o)

    crossed = swap_b(sent)
    lower = sent_a(lower)
    result, result_mine = fold_half(spots, [product], [w_d], r_result)
    r_two = [jnp.concatenate(pair, axis=0) for pair in zip(upper, lower)]
    crossed, result, r_two, t_out, f_down = tie(crossed, result, r_two, t_out, f_down)

    f_two = gradient_rows(spots, spread, 0, hidden_two, d_two, r_two)
    r_out = sent_a(t_out[1:])
    result = swap_b(result)
    y_down = spread_a(f_down)
    o_normed = attended * o_scale
    d_gated = mine + crossed.astype(F32)
    d_gate = (d_gated * o_normed).astype(LOW)
    lean = lean_o[:, None] / width
    d_attended = (o_scale * (d_gated * gate - o_normed * lean)).astype(LOW)
    d_query, d_key, d_value = attend_back(rates, ends, z_qk, z_vg, d_attended)
    d_qk = joined(d_query, d_key)
    d_vg = joined(d_value, d_gate)
    t_qk = away(hidden_one, d_qk)
    d_qk, d_vg, t_qk, f_two, r_out, result, y_down = tie(d_qk, d_vg, t_qk, f_two, r_out, result, y_down)

    r_qk = sent_a(t_qk)
    f_two = scattered(f_two)
    f_out = scattered(sum([x.astype(F32) for x in r_out], t_out[0].astype(F32)).astype(LOW))
    output = to_runs((middle + (result_mine + result.astype(F32))).astype(LOW))
    t_vg = away(hidden_one, d_vg)
    sent = fold_half(spots, [d_qk, d_vg], [w_qk, w_vg])
    sent, t_vg, d_qk, d_vg = tie(sent, t_vg, d_qk, d_vg)

    arrived = swap_c(sent)
    lean_x = total(
        jnp.sum(z_qk * d_qk.astype(F32), axis=-1) + jnp.sum(z_vg * d_vg.astype(F32), axis=-1)
    )
    sent, mine = fold_half(spots, [d_qk, d_vg], [w_qk, w_vg], arrived)
    sent, mine, r_qk, t_vg, f_one, output, lean_x, y_down = tie(
        sent, mine, r_qk, t_vg, f_one, output, lean_x, y_down
    )

    crossed = swap_b(sent)
    r_vg = sent_a(t_vg)
    f_qk = scattered(gradient_rows(spots, spread, 0, hidden_one, d_qk, r_qk))
    output = bring_back(output)
    x_one = spread_b(f_one)
    crossed, d_vg, r_vg, x_one, output, y_down = tie(crossed, d_vg, r_vg, x_one, output, y_down)

    f_vg = gradient_rows(spots, spread, 0, hidden_one, d_vg, r_vg)
    f_vg, crossed, x_one, f_two, f_out, y_down = tie(f_vg, crossed, x_one, f_two, f_out, y_down)

    f_vg = scattered(f_vg)
    d_hidden = mine + crossed.astype(F32)
    x_normed = x_own.astype(F32) * x_scale
    lean = lean_x[:, None] / width
    input_grad = to_runs((d_middle + x_scale * (d_hidden - x_normed * lean)).astype(LOW))
    x_down = spread_b(y_down)
    y_one = spread_a(x_one)
    x_two = spread_b(f_two)
    y_oqk = spread_a(joined(f_out, f_qk))
    input_grad, x_down, y_one, x_two, y_oqk, f_vg = tie(input_grad, x_down, y_one, x_two, y_oqk, f_vg)

    y_vg = spread_a(f_vg)
    x_oqk = spread_b(y_oqk)
    y_vg, x_oqk = tie(y_vg, x_oqk)

    four_vg = spread_c(spread_b(y_vg))
    input_grad = bring_back(input_grad)
    four_two = spread_c(spread_a(x_two))
    four_one = spread_c(y_one)
    four_down = spread_c(x_down)
    four_oqk = spread_c(x_oqk)
    units = f_one.shape[1]
    g_query, g_key = place_quarters(spots, four_oqk, (own, own), (2 * own, own))
    g_value, g_gate = place_quarters(spots, four_vg, (0, own), (own, own))
    [g_one] = place_quarters(spots, four_one, (0, units))
    [g_two] = place_quarters(spots, four_two, (0, units))
    [g_down] = place_quarters(spots, four_down, (0, units))
    g_out = features_in_order(four_oqk, 0, own)
    return output, input_grad, g_query, g_key, g_value, g_gate, g_out, g_one, g_two, g_down


def solution(mesh):
    reps, shards = mesh.shape["rep"], mesh.shape["shard"]
    devices = mesh.devices.reshape(reps // GROUP, 2, 2, shards)
    rep = ("a", "b", "c")
    by_tokens = P(None, (*rep, "shard"), None)
    by_rows = P("shard", None)
    return jax.shard_map(
        functools.partial(body, reps, shards),
        mesh=Mesh(devices, AXES),
        in_specs=(by_tokens, by_tokens, P(None, rep, None), P(), *[by_rows] * 8),
        out_specs=(by_tokens, by_tokens, *[by_rows] * 8),
        check_vma=False,
    )
```

```python
import functools

import jax
import jax.numpy as jnp
from jax import lax
from jax.experimental import pallas as pl
from jax.experimental.pallas import tpu as pltpu
from jax.sharding import Mesh, PartitionSpec as P

HEADS = 16
HEAD_DIM = 128
STREAM = 1024
GROUP = 4
BLOCK = 256
TILE = 256
EPSILON = 1e-06
AXES = ("a", "b", "c", "shard")
OWNERS = ("a", "shard")
LOW = jnp.bfloat16
F32 = jnp.float32


def matmul(former, latter):
    return jnp.dot(former, latter, preferred_element_type=F32)


def times_transposed(former, latter):
    return lax.dot_general(former, latter, (((1,), (1,)), ((), ())), preferred_element_type=F32)


def cross_tokens(former, latter):
    return lax.dot_general(former, latter, (((0,), (0,)), ((), ())), preferred_element_type=F32)


def masked_decay(rate, ends, first, columns):
    row = first + lax.broadcasted_iota(jnp.int32, (BLOCK, 1), 0)
    column = lax.broadcasted_iota(jnp.int32, (1, columns), 1)
    begin = jnp.zeros((BLOCK, 1), jnp.int32)
    for end in ends:
        begin = jnp.where(row >= end, end, begin)
    falling = jnp.exp(-rate * (row - first).astype(F32))
    rising = jnp.exp(rate * (column - first).astype(F32))
    allowed = (column <= row) & (column >= begin)
    return jnp.where(allowed, falling * rising, 0.0)


def attend_kernel(rates, ends, zq_ref, zk_ref, zv_ref, out_ref):
    stream, head = pl.program_id(0), pl.program_id(1)
    rate = rates[head]
    bounds = [ends[stream, i] for i in range(ends.shape[1])]
    zq, zk = zq_ref[...], zk_ref[...]
    q = (zq * jax.nn.sigmoid(zq)).astype(LOW)
    k = (zk * jax.nn.sigmoid(zk)).astype(LOW)
    v = zv_ref[...].astype(LOW)
    for first in range(0, STREAM, BLOCK):
        columns = first + BLOCK
        mask = masked_decay(rate, bounds, first, columns)
        scores = times_transposed(q[first:columns], k[:columns])
        weights = (scores * mask).astype(LOW)
        out_ref[first:columns, :] = matmul(weights, v[:columns])


def attend_back_kernel(
    rates, ends, zq_ref, zk_ref, zv_ref, do_ref, dzq_ref, dzk_ref, dzv_ref, dk_ref, dv_ref
):
    stream, head = pl.program_id(0), pl.program_id(1)
    rate = rates[head]
    bounds = [ends[stream, i] for i in range(ends.shape[1])]
    zq, zk = zq_ref[...], zk_ref[...]
    sig_q, sig_k = jax.nn.sigmoid(zq), jax.nn.sigmoid(zk)
    q = (zq * sig_q).astype(LOW)
    k = (zk * sig_k).astype(LOW)
    slope_q = sig_q * (1.0 + zq * (1.0 - sig_q))
    v = zv_ref[...].astype(LOW)
    d_o = do_ref[...]
    dk_ref[...] = jnp.zeros_like(dk_ref)
    dv_ref[...] = jnp.zeros_like(dv_ref)
    for first in range(0, STREAM, BLOCK):
        columns = first + BLOCK
        rows = slice(first, columns)
        mask = masked_decay(rate, bounds, first, columns)
        weights = (times_transposed(q[rows], k[:columns]) * mask).astype(LOW)
        d_scores = (times_transposed(d_o[rows], v[:columns]) * mask).astype(LOW)
        dzq_ref[rows, :] = (matmul(d_scores, k[:columns]) * slope_q[rows]).astype(LOW)
        dk_ref[:columns, :] += cross_tokens(d_scores, q[rows])
        dv_ref[:columns, :] += cross_tokens(weights, d_o[rows])
    dzk_ref[...] = (dk_ref[...] * (sig_k * (1.0 + zk * (1.0 - sig_k)))).astype(LOW)
    dzv_ref[...] = dv_ref[...].astype(LOW)


def head_block(offset=0):
    return pl.BlockSpec((STREAM, HEAD_DIM), lambda g, h, *_: (g, h + offset))


def attend(rates, ends, z_qk, z_vg):
    heads, streams = rates.shape[0], ends.shape[0]
    work = streams * heads * STREAM * STREAM
    return pl.pallas_call(
        attend_kernel,
        out_shape=jax.ShapeDtypeStruct((streams * STREAM, heads * HEAD_DIM), F32),
        grid_spec=pltpu.PrefetchScalarGridSpec(
            num_scalar_prefetch=2,
            grid=(streams, heads),
            in_specs=[head_block(), head_block(heads), head_block()],
            out_specs=head_block(),
        ),
        compiler_params=pltpu.CompilerParams(vmem_limit_bytes=40 << 20),
        cost_estimate=pl.CostEstimate(
            flops=4 * work * HEAD_DIM, transcendentals=work // 64,
            bytes_accessed=streams * heads * STREAM * HEAD_DIM * 16,
        ),
        name="attend",
    )(rates, ends, z_qk, z_qk, z_vg)


def attend_back(rates, ends, z_qk, z_vg, d_o):
    heads, streams = rates.shape[0], ends.shape[0]
    work = streams * heads * STREAM * STREAM
    return pl.pallas_call(
        attend_back_kernel,
        out_shape=[jax.ShapeDtypeStruct((streams * STREAM, heads * HEAD_DIM), LOW)] * 3,
        grid_spec=pltpu.PrefetchScalarGridSpec(
            num_scalar_prefetch=2,
            grid=(streams, heads),
            in_specs=[head_block(), head_block(heads), head_block(), head_block()],
            out_specs=[head_block()] * 3,
            scratch_shapes=[pltpu.VMEM((STREAM, HEAD_DIM), F32)] * 2,
        ),
        compiler_params=pltpu.CompilerParams(vmem_limit_bytes=40 << 20),
        cost_estimate=pl.CostEstimate(
            flops=10 * work * HEAD_DIM, transcendentals=work // 64,
            bytes_accessed=streams * heads * STREAM * HEAD_DIM * 20,
        ),
        name="attend_back",
    )(rates, ends, z_qk, z_qk, z_vg, d_o)


def chunk_copies(chunks, buffer, sems, turn, half=None):
    count, size = len(chunks), chunks[0].shape[0]
    if count == 1:
        rows = buffer.shape[0]
        first = 0 if half is None else pl.multiple_of(half * rows, rows)
        return [(None, pltpu.make_async_copy(chunks[0].at[pl.ds(first, rows)], buffer, sems.at[0]))]
    copies = []
    for k, chunk in enumerate(chunks):
        index = lax.rem(turn - k + count, count)
        wanted = None
        if half is not None:
            wanted = lax.div(index, count // 2) == half
            index = lax.rem(index, count // 2)
        target = buffer.at[pl.ds(pl.multiple_of(index * size, size), size)]
        copies.append((wanted, pltpu.make_async_copy(chunk, target, sems.at[k])))
    return copies


def each(copies, act):
    for wanted, copy in copies:
        if wanted is None:
            act(copy)
        else:
            pl.when(wanted)(functools.partial(act, copy))


def start(copies):
    each(copies, lambda copy: copy.start())


def finish(copies):
    each(copies, lambda copy: copy.wait())


def estimate(flops, *arrays):
    moved = sum(x.size * x.dtype.itemsize for x in arrays)
    return pl.CostEstimate(flops=flops, transcendentals=0, bytes_accessed=moved)


def limit(mebibytes):
    return pltpu.CompilerParams(vmem_limit_bytes=mebibytes << 20)


ANYWHERE = pl.BlockSpec(memory_space=pl.ANY)


def weight_buffer(chunks, share=1):
    size = len(chunks) * chunks[0].shape[0] // share
    return [pltpu.VMEM((size, chunks[0].shape[1]), LOW), pltpu.SemaphoreType.DMA((len(chunks),))]


def tile_rows(width, column=0):
    return pl.BlockSpec((TILE, width), lambda i, *_: (i, column))


def joined_rows(width, tiles):
    spec = pl.BlockSpec((TILE, width), lambda i, s: (i // (2 * tiles) * tiles + i % tiles, 0))
    return [spec, spec]


def enter_kernel(tiles, blocks, project, spots, own_ref, other_ref, *refs):
    i = pl.program_id(0)
    mine = lax.rem(lax.div(i, tiles), 2) == spots[0]
    rows = jnp.where(mine, own_ref[...], other_ref[...])
    part = rows.shape[1] // len(blocks)
    permuted = jnp.concatenate([rows[:, n * part : (n + 1) * part] for n in blocks], axis=1)
    if not project:
        all_ref, quarter_ref = refs
        all_ref[...] = permuted
        held = all_ref
    else:
        chunks, (h_ref, z_ref, scale_ref, quarter_ref, held, buffer, sems) = refs[:-7], refs[-7:]
        held[...] = permuted
        copies = chunk_copies(chunks, buffer, sems, spots[2])

        @pl.when(i == 0)
        def _():
            start(copies)

        x = rows.astype(F32)
        scale = lax.rsqrt(jnp.mean(x * x, axis=-1, keepdims=True) + EPSILON)
        scale_ref[...] = scale
        hidden = (permuted.astype(F32) * scale).astype(LOW)
        h_ref[...] = hidden

        @pl.when(i == 0)
        def _():
            finish(copies)

        z_ref[...] = matmul(hidden, buffer[...])
    size = quarter_ref.shape[1]
    quarter_ref[...] = held[:, pl.ds(pl.multiple_of(spots[1] * size, size), size)]


def enter(spots, blocks, own, other, chunks=()):
    width = own.shape[1]
    count, tiles = 2 * own.shape[0], own.shape[0] // TILE // 2
    shape = jax.ShapeDtypeStruct
    quarter = shape((count, width // GROUP), LOW)
    if chunks:
        columns = chunks[0].shape[1]
        outs = [shape((count, width), LOW), shape((count, columns), F32), shape((count, 1), F32), quarter]
        scratch = [pltpu.VMEM((TILE, width), LOW), *weight_buffer(chunks)]
    else:
        columns, scratch = 0, []
        outs = [shape((count, width), LOW), quarter]
    return pl.pallas_call(
        functools.partial(enter_kernel, tiles, blocks, bool(chunks)),
        out_shape=outs,
        grid_spec=pltpu.PrefetchScalarGridSpec(
            num_scalar_prefetch=1,
            grid=(count // TILE,),
            in_specs=joined_rows(width, tiles) + [ANYWHERE] * len(chunks),
            out_specs=[tile_rows(o.shape[1]) for o in outs],
            scratch_shapes=scratch,
        ),
        compiler_params=limit(40),
        cost_estimate=estimate(2 * count * width * columns, own, other, *chunks, *outs),
        name="enter",
    )(spots, own, other, *chunks)


def project_kernel(spots, h_ref, *refs):
    chunks, (z_ref, buffer, sems) = refs[:-3], refs[-3:]
    copies = chunk_copies(chunks, buffer, sems, spots[2])

    @pl.when(pl.program_id(0) == 0)
    def _():
        start(copies)
        finish(copies)

    z_ref[...] = matmul(h_ref[...], buffer[...])


def project(spots, hidden, chunks):
    count, width = hidden.shape
    out = jax.ShapeDtypeStruct((count, chunks[0].shape[1]), F32)
    return pl.pallas_call(
        project_kernel,
        out_shape=out,
        grid_spec=pltpu.PrefetchScalarGridSpec(
            num_scalar_prefetch=1,
            grid=(count // TILE,),
            in_specs=[tile_rows(width)] + [ANYWHERE] * len(chunks),
            out_specs=tile_rows(out.shape[1]),
            scratch_shapes=weight_buffer(chunks),
        ),
        compiler_params=limit(40),
        cost_estimate=estimate(2 * count * width * out.shape[1], hidden, *chunks, out),
        name="project",
    )(spots, hidden, *chunks)


def unit_kernel(spots, own_ref, other_ref, *refs):
    chunks, rest = refs[:-9], refs[-9:]
    h_ref, one_ref, two_ref, product_ref, scale_ref, first, second, sem_one, sem_two = rest
    split = len(chunks) // 2
    copies = [
        chunk_copies(chunks[:split], first, sem_one, spots[2]),
        chunk_copies(chunks[split:], second, sem_two, spots[2]),
    ]
    begins = pl.program_id(0) == 0

    @pl.when(begins)
    def _():
        start(copies[0])
        start(copies[1])

    mine, other = own_ref[...], other_ref[...]
    swapped = spots[0] == 1
    middle = jnp.concatenate(
        [jnp.where(swapped, other, mine), jnp.where(swapped, mine, other)], axis=1
    ).astype(F32)
    scale = lax.rsqrt(jnp.mean(middle * middle, axis=-1, keepdims=True) + EPSILON)
    scale_ref[...] = scale
    hidden = (middle * scale).astype(LOW)
    h_ref[...] = hidden

    @pl.when(begins)
    def _():
        finish(copies[0])

    z_one = matmul(hidden, first[...])

    @pl.when(begins)
    def _():
        finish(copies[1])

    z_two = matmul(hidden, second[...])
    one_ref[...] = z_one.astype(LOW)
    two_ref[...] = z_two.astype(LOW)
    product_ref[...] = (z_one * z_two).astype(LOW)


def gated_unit(spots, own, other, first, second):
    count, width, units = own.shape[0], 2 * own.shape[1], first[0].shape[1]
    shape = jax.ShapeDtypeStruct
    outs = [shape((count, width), LOW)] + [shape((count, units), LOW)] * 3 + [shape((count, 1), F32)]
    (buffer, sems) = weight_buffer(first)
    return pl.pallas_call(
        unit_kernel,
        out_shape=outs,
        grid_spec=pltpu.PrefetchScalarGridSpec(
            num_scalar_prefetch=1,
            grid=(count // TILE,),
            in_specs=[tile_rows(width // 2)] * 2 + [ANYWHERE] * (2 * len(first)),
            out_specs=[tile_rows(o.shape[1]) for o in outs],
            scratch_shapes=[buffer, buffer, sems, sems],
        ),
        compiler_params=limit(48),
        cost_estimate=estimate(4 * count * width * units, own, other, *first, *second, *outs),
        name="gated_unit",
    )(spots, own, other, *first, *second)


def unit_back_kernel(spots, dy_ref, one_ref, two_ref, *refs):
    chunks, (d_one_ref, d_two_ref, sum_ref, buffer, sems) = refs[:-5], refs[-5:]
    copies = chunk_copies(chunks, buffer, sems, spots[2])

    @pl.when(pl.program_id(0) == 0)
    def _():
        start(copies)
        finish(copies)

    d_product = matmul(dy_ref[...], buffer[...])
    z_one, z_two = one_ref[...].astype(F32), two_ref[...].astype(F32)
    d_one = d_product * z_two
    d_one_ref[...] = d_one.astype(LOW)
    d_two_ref[...] = (d_product * z_one).astype(LOW)
    sum_ref[...] = jnp.sum(d_one * z_one, axis=-1, keepdims=True)


def gated_unit_back(spots, dy, z_one, z_two, chunks):
    count, width, units = dy.shape[0], dy.shape[1], z_one.shape[1]
    shape = jax.ShapeDtypeStruct
    outs = [shape((count, units), LOW)] * 2 + [shape((count, 1), F32)]
    return pl.pallas_call(
        unit_back_kernel,
        out_shape=outs,
        grid_spec=pltpu.PrefetchScalarGridSpec(
            num_scalar_prefetch=1,
            grid=(count // TILE,),
            in_specs=[tile_rows(width), tile_rows(units), tile_rows(units)] + [ANYWHERE] * len(chunks),
            out_specs=[tile_rows(o.shape[1]) for o in outs],
            scratch_shapes=weight_buffer(chunks),
        ),
        compiler_params=limit(40),
        cost_estimate=estimate(2 * count * width * units, dy, z_one, z_two, *chunks, *outs),
        name="gated_unit_back",
    )(spots, dy, z_one, z_two, *chunks)


def fold_kernel(members, keeps, spots, *refs):
    values, refs = refs[:members], refs[members:]
    arrived, refs = (refs[0], refs[1:]) if keeps else (None, refs)
    outs = 2 if keeps else 1
    chunks, refs = refs[: -outs - 2 * members], refs[-outs - 2 * members :]
    outs, buffers, sems = refs[:outs], refs[outs : outs + members], refs[outs + members :]
    each_count = len(chunks) // members
    half = spots[0] if keeps else 1 - spots[0]
    begins = pl.program_id(0) == 0
    copies = [
        chunk_copies(chunks[m * each_count : (m + 1) * each_count], buffers[m], sems[m], spots[2], half)
        for m in range(members)
    ]

    @pl.when(begins)
    def _():
        for m in range(members):
            start(copies[m])

    whole = None
    for m in range(members):
        pl.when(begins)(functools.partial(finish, copies[m]))
        term = times_transposed(values[m][...], buffers[m][...])
        whole = term if whole is None else whole + term
    if not keeps:
        outs[0][...] = whole.astype(LOW)
    else:
        whole = whole + arrived[...].astype(F32)
        size = whole.shape[1] // 2
        upper = spots[3] == 1
        outs[0][...] = jnp.where(upper, whole[:, :size], whole[:, size:]).astype(LOW)
        outs[1][...] = jnp.where(upper, whole[:, size:], whole[:, :size])


def fold_half(spots, values, weights, arrived=None):
    count = values[0].shape[0]
    half = len(weights[0]) * weights[0][0].shape[0] // 2
    shape = jax.ShapeDtypeStruct
    if arrived is None:
        outs, extra = [shape((count, half), LOW)], []
    else:
        outs, extra = [shape((count, half // 2), LOW), shape((count, half // 2), F32)], [arrived]
    buffers, sems = zip(*[weight_buffer(w, 2) for w in weights])
    chunks = [x for w in weights for x in w]
    flops = sum(2 * count * half * v.shape[1] for v in values)
    found = pl.pallas_call(
        functools.partial(fold_kernel, len(values), arrived is not None),
        out_shape=outs,
        grid_spec=pltpu.PrefetchScalarGridSpec(
            num_scalar_prefetch=1,
            grid=(count // TILE,),
            in_specs=[tile_rows(v.shape[1]) for v in values]
            + [tile_rows(half)] * len(extra)
            + [ANYWHERE] * len(chunks),
            out_specs=[tile_rows(o.shape[1]) for o in outs],
            scratch_shapes=[*buffers, *sems],
        ),
        compiler_params=limit(40),
        cost_estimate=estimate(flops, *values, *extra, *chunks[: len(chunks) // 2], *outs),
        name="fold_half",
    )(spots, *values, *extra, *chunks)
    return found[0] if arrived is None else found


def gradient_kernel(spots, left_ref, right_ref, *refs):
    found = cross_tokens(left_ref[...], right_ref[...])
    for arrived_ref in refs[:-1]:
        found = found + arrived_ref[...].astype(F32)
    refs[-1][...] = found.astype(LOW)


def gradient_rows(spots, spread, k, left, right, arrived=()):
    count, columns = right.shape
    rows = left.shape[1] // (1 if k is None else spread)
    tiles = rows // TILE

    def block(i, s):
        return (0, i if k is None else lax.rem(s[2] + k, spread) * tiles + i)

    out = jax.ShapeDtypeStruct((rows, columns), LOW)
    return pl.pallas_call(
        gradient_kernel,
        out_shape=out,
        grid_spec=pltpu.PrefetchScalarGridSpec(
            num_scalar_prefetch=1,
            grid=(tiles,),
            in_specs=[
                pl.BlockSpec((count, TILE), block),
                pl.BlockSpec((count, columns), lambda i, s: (0, 0), pipeline_mode=pl.Buffered(1)),
            ]
            + [tile_rows(columns)] * len(arrived),
            out_specs=tile_rows(columns),
        ),
        compiler_params=limit(40),
        cost_estimate=estimate(2 * count * rows * columns, right, out, out, *arrived),
        name="gradient_rows",
    )(spots, left, right, *arrived)


def place_kernel(cuts, spots, *refs):
    quarter = pl.program_id(0)
    cross = lax.rem(lax.div(quarter, 2) + spots[0], 2) * 2 + lax.rem(lax.rem(quarter, 2) + spots[3], 2)
    for n in range(4):

        @pl.when(cross == n)
        def _():
            for (first, size), out_ref in zip(cuts, refs[4:]):
                out_ref[...] = refs[n][:, first : first + size].astype(F32)


def place_quarters(spots, four, *cuts):
    rows, columns = four[0][0].shape[0], four[0][2]
    outs = [jax.ShapeDtypeStruct((rows, GROUP * size), F32) for _, size in cuts]

    def block(index):
        return pl.BlockSpec((rows, columns), lambda q, s: (0, index), pipeline_mode=pl.Buffered(1))

    return pl.pallas_call(
        functools.partial(place_kernel, cuts),
        out_shape=outs,
        grid_spec=pltpu.PrefetchScalarGridSpec(
            num_scalar_prefetch=1,
            grid=(GROUP,),
            in_specs=[block(index) for _, index, _ in four],
            out_specs=[pl.BlockSpec((rows, size), lambda q, s: (0, q)) for _, size in cuts],
        ),
        compiler_params=limit(40),
        cost_estimate=estimate(0, *[x for x, _, _ in four], *outs),
        name="place_quarters",
    )(spots, *[x for x, _, _ in four])


def tie(*values):
    return lax.optimization_barrier(values)


def body(reps, shards, tokens, cotangent, lengths, decay_rates, *weights):
    spread = reps // GROUP
    place = lax.axis_index("shard")
    a, b, c = lax.axis_index("a"), lax.axis_index("b"), lax.axis_index("c")
    quarter = 2 * c + b
    micro, run, width = tokens.shape
    half, own = width // 2, width // GROUP
    streams = micro * GROUP // shards
    per_block = STREAM // run // GROUP * streams
    rows = width // shards
    part = rows // spread
    columns = functools.partial(lax.dynamic_slice_in_dim, axis=1)
    spots = jnp.stack([c, quarter, a, b]).astype(jnp.int32)
    blocks = [z * spread + k for k in range(spread) for z in range(shards)]

    def move(x, target):
        pairs = [(r * shards + s, target(r) * shards + s) for r in range(reps) for s in range(shards)]
        return lax.ppermute(x, AXES, pairs)

    def swap_c(x):
        return move(x, lambda r: r ^ 1)

    def swap_b(x):
        return move(x, lambda r: r ^ 2)

    def joined(*parts):
        return jnp.concatenate(parts, axis=1)

    def shift_a(x, k):
        return move(x, lambda r: (r + GROUP * k) % reps)

    def ordered(index, mine, other, axis):
        return jnp.where(
            index == 0,
            jnp.concatenate([mine, other], axis),
            jnp.concatenate([other, mine], axis),
        )


    def batch_of(s):
        return s // (shards // micro)

    def origin(r, s, p):
        run_id = (r % GROUP) * per_block + p
        stream, piece = run_id // shards, run_id % shards
        member = s % GROUP if streams == 1 else 2 * stream + s % 2
        return (r // GROUP) * GROUP + member, piece

    def routes(p):
        found = []
        for r in range(reps):
            for s in range(shards):
                from_r, from_s = origin(r, s, p ^ batch_of(s))
                found.append((from_r * shards + from_s, r * shards + s))
        return found

    def natural(x):
        return jnp.concatenate(
            [
                x[:, (k * shards + z) * part : (k * shards + z + 1) * part]
                for z in range(shards)
                for k in range(spread)
            ],
            axis=1,
        )

    def bring(x):
        arrived = [
            lax.ppermute(lax.dynamic_index_in_dim(x, (place + p) % 2, 0, False), AXES, routes(p))
            for p in range(2)
        ]
        return ordered(batch_of(place), *arrived, 0)

    def bring_back(x):
        slots = natural(x).reshape(2, run, width)
        arrived = [
            lax.ppermute(
                lax.dynamic_index_in_dim(slots, (batch_of(place) + p) % 2, 0, False),
                AXES,
                [(to, origin) for origin, to in routes(p)],
            )
            for p in range(2)
        ]
        return ordered(place % 2, arrived[0][None], arrived[1][None], 0)


    def gather_b(x):
        return ordered(b, x, swap_b(x), 1)

    def gather_c(x):
        return ordered(c, x, swap_c(x), 1)

    def gather_rows_b(x):
        return ordered(b, x, swap_b(x), 0)

    def total(x):
        x = x + swap_c(x)
        return x + swap_b(x)

    def fold_c(product):
        sent = swap_c(product(1 - c).astype(LOW))
        return product(c) + sent.astype(F32)

    def fold_b(x):
        sent = swap_b(columns(x, (1 - b) * own, own).astype(LOW))
        return columns(x, b * own, own) + sent.astype(F32)

    def to_runs(x):
        cut = x.reshape(2, 2, -1, own)
        pick = functools.partial(lax.dynamic_index_in_dim, keepdims=False)
        both = ordered(b, pick(cut, b, 0), swap_b(pick(cut, 1 - b, 0)), 2)
        return ordered(c, pick(both, c, 0), swap_c(pick(both, 1 - c, 0)), 1)


    def own_features(w):
        count = shards * spread // GROUP
        cut = []
        for i in range(count):
            block = quarter * count + i
            cut.append(columns(w, (block % shards) * rows + (block // shards) * part, part))
        return jnp.concatenate(cut, axis=1)

    def own_units(w):
        return columns(w, quarter * (w.shape[1] // GROUP), w.shape[1] // GROUP)

    def over_shards(*members):
        cut = jnp.concatenate(members, axis=1) if len(members) > 1 else members[0]
        piece = lax.dynamic_slice_in_dim(cut, a * part, part, 0)
        return lax.all_gather(piece, "shard", axis=0, tiled=True)

    def over_owners(w):
        piece = lax.dynamic_slice_in_dim(w, a * part, part, 0)
        return lax.all_gather(piece, OWNERS, axis=0, tiled=True)

    def over_spread(x):
        return [shift_a(x, k) for k in range(1, spread)]

    def by_spread(relative):
        if spread == 2:
            return ordered(a, relative[0], relative[1], 0)
        stacked = jnp.stack(relative, 0)
        pick = functools.partial(lax.dynamic_index_in_dim, axis=0, keepdims=False)
        return jnp.concatenate([pick(stacked, (a - j) % spread) for j in range(spread)], axis=0)

    def in_row_order(x):
        cut = x.reshape(spread, shards, part, -1)
        return jnp.transpose(cut, (1, 0, 2, 3)).reshape(width, -1)

    def row_half(w, h):
        return lax.dynamic_slice_in_dim(w, h * half, half, 0)


    def away(left, right):
        return [gradient_rows(spots, spread, k, left, right) for k in range(1, spread)]

    def in_two(terms):
        middles = [x.shape[0] // 2 for x in terms]
        return [x[:m] for x, m in zip(terms, middles)], [x[m:] for x, m in zip(terms, middles)]

    def stacked(upper, lower):
        return [jnp.concatenate(pair, axis=0) for pair in zip(upper, lower)]

    def sent_a(terms):
        return [shift_a(x, k + 1) for k, x in enumerate(terms)]

    def scattered(x):
        return lax.psum_scatter(x, "shard", scatter_dimension=0, tiled=True)

    def whole_rows(left, right):
        return gradient_rows(spots, spread, None, left, right)

    def scattered_all(x):
        return lax.psum_scatter(x, OWNERS, scatter_dimension=0, tiled=True)

    def summed(left, right, arrived):
        return scattered(gradient_rows(spots, spread, 0, left, right, arrived))

    def spread_a(x):
        return by_spread([x] + over_spread(x))

    def spread_b(x):
        return jnp.concatenate([x, swap_b(x)], axis=1)

    def spread_c(pair):
        other, size = swap_c(pair), pair.shape[1] // 2
        return [(pair, 0, size), (pair, 1, size), (other, 0, size), (other, 1, size)]

    def features_in_order(four, first, size):
        cut = [x[:, index * full + first : index * full + first + size] for x, index, full in four]
        pair = [ordered(b, cut[n], cut[n + 1], 1) for n in (0, 2)]
        return natural(ordered(c, pair[0], pair[1], 1)).astype(F32)


    w_query, w_key, w_value, w_gate, w_out, w_one, w_two, w_down = weights
    g_qk = over_shards(own_units(w_query), own_units(w_key))
    g_vg = over_shards(own_units(w_value), own_units(w_gate))
    g_o = over_shards(own_features(w_out))
    g_1 = over_shards(own_units(w_one))
    g_2 = over_shards(own_units(w_two))
    w_d = [over_owners(own_units(w_down))]

    heads = HEADS // GROUP
    rates = lax.dynamic_slice_in_dim(decay_rates, quarter * heads, heads, 0)
    cuts = gather_rows_b(lengths.reshape(1, -1))
    cuts = ordered(c, cuts, swap_c(cuts), 0).reshape(GROUP, micro, -1)
    if streams == 1:
        batch = place // GROUP
        member = place % GROUP
        chosen = lax.dynamic_slice_in_dim(cuts, 2 * (member % 2) + member // 2, 1, 0)
    else:
        batch = place // 2
        chosen = lax.dynamic_index_in_dim(cuts.reshape(2, 2, micro, -1), place % 2, 0, False)
    chosen = lax.dynamic_index_in_dim(chosen, batch, 1, False)
    seq_ends = [chosen[:, 0]]
    for i in range(1, chosen.shape[1]):
        seq_ends.append(seq_ends[-1] + chosen[:, i])
    ends = jnp.stack(seq_ends, axis=1)

    x_run = bring(tokens)
    x_run, g_qk = tie(x_run, g_qk)

    x_pair = gather_rows_b(x_run)
    s_qk = over_spread(g_qk)
    x_pair, s_qk, g_vg = tie(x_pair, s_qk, g_vg)

    s_vg = over_spread(g_vg)
    w_qk = [g_qk, *s_qk]
    hidden_one, z_qk, x_scale, x_own = enter(spots, blocks, x_pair, swap_c(x_pair), w_qk)
    z_qk, hidden_one, s_vg, g_o = tie(z_qk, hidden_one, s_vg, g_o)

    s_o = over_spread(g_o)
    w_vg = [g_vg, *s_vg]
    z_vg = project(spots, hidden_one, w_vg)
    attended = attend(rates, ends, z_qk, z_vg)
    gate = z_vg[:, own:]
    o_scale = lax.rsqrt(total(jnp.sum(attended * attended, axis=-1)) / width + EPSILON)[:, None]
    lifted = (attended * gate).astype(LOW)
    lifted, s_o, g_1, cotangent = tie(lifted, s_o, g_1, cotangent)

    s_1 = over_spread(g_1)
    lifted = gather_b(lifted)
    lifted, s_1, g_2, o_scale, cotangent = tie(lifted, s_1, g_2, o_scale, cotangent)

    s_2 = over_spread(g_2)
    dy_run = bring(cotangent)
    lifted = gather_c(lifted)
    w_o = in_row_order(by_spread([g_o, *s_o]))
    branch = o_scale * matmul(lifted, w_o)
    middle = x_own.astype(F32) + branch
    low_middle = gather_b(middle.astype(LOW))
    low_middle, s_2, dy_run = tie(low_middle, s_2, dy_run)

    other_middle = swap_c(low_middle)
    dy_other = swap_b(dy_run)
    w_1, w_2 = [g_1, *s_1], [g_2, *s_2]
    hidden_two, z_one, z_two, product, m_scale = gated_unit(spots, low_middle, other_middle, w_1, w_2)
    z_one, z_two, product, dy_other = tie(z_one, z_two, product, dy_other)

    dy_pair = ordered(b, dy_run, dy_other, 0)
    dy_all, dy_own = enter(spots, blocks, dy_pair, swap_c(dy_pair))
    f_down = whole_rows(dy_all, product)
    z_one, z_two, product, f_down, w_d[0] = tie(z_one, z_two, product, f_down, w_d[0])


    f_down = scattered_all(f_down)
    d_one, d_two, lean_m = gated_unit_back(spots, dy_all, z_one, z_two, w_d)
    sent = fold_half(spots, [d_one, d_two], [w_1, w_2])
    sent, d_two, lean_m = tie(sent, d_two, lean_m)

    arrived = swap_c(sent)
    t_two = away(hidden_two, d_two)
    lean_m = total(lean_m[:, 0])
    sent, mine = fold_half(spots, [d_one, d_two], [w_1, w_2], arrived)
    sent, d_one, t_two, product, lean_m = tie(sent, d_one, t_two, product, lean_m)

    crossed = swap_b(sent)
    upper, lower = in_two(t_two)
    upper = sent_a(upper)
    f_one = whole_rows(hidden_two, d_one)
    result = fold_half(spots, [product], [w_d])
    crossed, result, f_one, upper, f_down = tie(crossed, result, f_one, upper, f_down)

    f_one = scattered_all(f_one)
    d_hidden = mine + crossed.astype(F32)
    m_normed = middle * m_scale
    lean = lean_m[:, None] * (2.0 / width)
    d_middle = dy_own.astype(F32) + m_scale * (d_hidden - m_normed * lean)
    d_branch = d_middle.astype(LOW)
    lean_o = jnp.sum(d_middle * branch, axis=-1)
    sent = times_transposed(d_branch, row_half(w_o, 1 - c)).astype(LOW)
    sent, result, d_middle, lean_o = tie(sent, result, d_middle, lean_o)

    arrived = swap_c(sent)
    r_result = swap_c(result)
    y_down = spread_a(f_down)
    lean_o = total(lean_o)
    p_out = cross_tokens(lifted, (o_scale * d_middle).astype(LOW)).astype(LOW)
    p_out = jnp.transpose(p_out.reshape(shards, spread, part, -1), (1, 0, 2, 3))
    p_out = p_out.reshape(spread, width // spread, -1)
    t_out = [lax.dynamic_index_in_dim(p_out, (a + k) % spread, 0, False) for k in range(spread)]
    d_gated = times_transposed(d_branch, row_half(w_o, c)) + arrived.astype(F32)
    sent = columns(d_gated, (1 - b) * own, own).astype(LOW)
    mine = columns(d_gated, b * own, own)
    sent, mine, r_result, t_out, lean_o, y_down = tie(sent, mine, r_result, t_out, lean_o, y_down)

    crossed = swap_b(sent)
    r_out = sent_a(t_out[1:])
    result, result_mine = fold_half(spots, [product], [w_d], r_result)
    crossed, result, r_out, lower = tie(crossed, result, r_out, lower)

    lower = sent_a(lower)
    result = swap_b(result)
    f_out = scattered(sum([x.astype(F32) for x in r_out], t_out[0].astype(F32)).astype(LOW))
    o_normed = attended * o_scale
    d_gated = mine + crossed.astype(F32)
    d_gate = (d_gated * o_normed).astype(LOW)
    lean = lean_o[:, None] / width
    d_attended = (o_scale * (d_gated * gate - o_normed * lean)).astype(LOW)
    d_query, d_key, d_value = attend_back(rates, ends, z_qk, z_vg, d_attended)
    d_qk = joined(d_query, d_key)
    d_vg = joined(d_value, d_gate)
    t_qk = away(hidden_one, d_qk)
    d_qk, d_vg, t_qk, lower, result = tie(d_qk, d_vg, t_qk, lower, result)

    upper_qk, lower_qk = in_two(t_qk)
    upper_qk = sent_a(upper_qk)
    f_two = gradient_rows(spots, spread, 0, hidden_two, d_two, stacked(upper, lower))
    output = to_runs((middle + (result_mine + result.astype(F32))).astype(LOW))
    t_vg = away(hidden_one, d_vg)
    sent = fold_half(spots, [d_qk, d_vg], [w_qk, w_vg])
    sent, t_vg, d_qk, d_vg, f_two, output, upper_qk, lower_qk = tie(
        sent, t_vg, d_qk, d_vg, f_two, output, upper_qk, lower_qk
    )

    f_two = scattered(f_two)
    lower_qk = sent_a(lower_qk)
    arrived = swap_c(sent)
    lean_x = total(
        jnp.sum(z_qk * d_qk.astype(F32), axis=-1) + jnp.sum(z_vg * d_vg.astype(F32), axis=-1)
    )
    sent, mine = fold_half(spots, [d_qk, d_vg], [w_qk, w_vg], arrived)
    sent, mine, lower_qk, t_vg, f_one, lean_x, y_down = tie(
        sent, mine, lower_qk, t_vg, f_one, lean_x, y_down
    )

    crossed = swap_b(sent)
    r_vg = sent_a(t_vg)
    f_qk = scattered(gradient_rows(spots, spread, 0, hidden_one, d_qk, stacked(upper_qk, lower_qk)))
    output = bring_back(output)
    x_one = spread_b(f_one)
    crossed, d_vg, r_vg, x_one, output, y_down = tie(crossed, d_vg, r_vg, x_one, output, y_down)

    f_vg = gradient_rows(spots, spread, 0, hidden_one, d_vg, r_vg)
    f_vg, crossed, x_one, f_two, f_out, y_down = tie(f_vg, crossed, x_one, f_two, f_out, y_down)

    f_vg = scattered(f_vg)
    d_hidden = mine + crossed.astype(F32)
    x_normed = x_own.astype(F32) * x_scale
    lean = lean_x[:, None] / width
    input_grad = to_runs((d_middle + x_scale * (d_hidden - x_normed * lean)).astype(LOW))
    x_down = spread_b(y_down)
    y_one = spread_a(x_one)
    x_two = spread_b(f_two)
    y_oqk = spread_a(joined(f_out, f_qk))
    input_grad, x_down, y_one, x_two, y_oqk, f_vg = tie(input_grad, x_down, y_one, x_two, y_oqk, f_vg)

    y_vg = spread_a(f_vg)
    x_oqk = spread_b(y_oqk)
    y_vg, x_oqk = tie(y_vg, x_oqk)

    four_vg = spread_c(spread_b(y_vg))
    input_grad = bring_back(input_grad)
    four_two = spread_c(spread_a(x_two))
    four_one = spread_c(y_one)
    four_down = spread_c(x_down)
    four_oqk = spread_c(x_oqk)
    units = f_one.shape[1]
    g_query, g_key = place_quarters(spots, four_oqk, (own, own), (2 * own, own))
    g_value, g_gate = place_quarters(spots, four_vg, (0, own), (own, own))
    [g_one] = place_quarters(spots, four_one, (0, units))
    [g_two] = place_quarters(spots, four_two, (0, units))
    [g_down] = place_quarters(spots, four_down, (0, units))
    g_out = features_in_order(four_oqk, 0, own)
    return output, input_grad, g_query, g_key, g_value, g_gate, g_out, g_one, g_two, g_down


def solution(mesh):
    reps, shards = mesh.shape["rep"], mesh.shape["shard"]
    devices = mesh.devices.reshape(reps // GROUP, 2, 2, shards)
    rep = ("a", "b", "c")
    by_tokens = P(None, (*rep, "shard"), None)
    by_rows = P("shard", None)
    return jax.shard_map(
        functools.partial(body, reps, shards),
        mesh=Mesh(devices, AXES),
        in_specs=(by_tokens, by_tokens, P(None, rep, None), P(), *[by_rows] * 8),
        out_specs=(by_tokens, by_tokens, *[by_rows] * 8),
        check_vma=False,
    )
```

```python
import functools

import jax
import jax.numpy as jnp
from jax import lax
from jax.experimental import pallas as pl
from jax.experimental.pallas import tpu as pltpu
from jax.sharding import Mesh, PartitionSpec as P

HEADS = 16
HEAD_DIM = 128
STREAM = 1024
GROUP = 4
BLOCK = 256
TILE = 256
EPSILON = 1e-06
AXES = ("a", "b", "c", "shard")
OWNERS = ("a", "shard")
LOW = jnp.bfloat16
F32 = jnp.float32


def matmul(former, latter):
    return jnp.dot(former, latter, preferred_element_type=F32)


def times_transposed(former, latter):
    return lax.dot_general(former, latter, (((1,), (1,)), ((), ())), preferred_element_type=F32)


def cross_tokens(former, latter):
    return lax.dot_general(former, latter, (((0,), (0,)), ((), ())), preferred_element_type=F32)


def masked_decay(rate, ends, first, columns):
    row = first + lax.broadcasted_iota(jnp.int32, (BLOCK, 1), 0)
    column = lax.broadcasted_iota(jnp.int32, (1, columns), 1)
    begin = jnp.zeros((BLOCK, 1), jnp.int32)
    for end in ends:
        begin = jnp.where(row >= end, end, begin)
    falling = jnp.exp(-rate * (row - first).astype(F32))
    rising = jnp.exp(rate * (column - first).astype(F32))
    allowed = (column <= row) & (column >= begin)
    return jnp.where(allowed, falling * rising, 0.0)


def attend_kernel(rates, ends, zq_ref, zk_ref, zv_ref, out_ref):
    stream, head = pl.program_id(0), pl.program_id(1)
    rate = rates[head]
    bounds = [ends[stream, i] for i in range(ends.shape[1])]
    zq, zk = zq_ref[...], zk_ref[...]
    q = (zq * jax.nn.sigmoid(zq)).astype(LOW)
    k = (zk * jax.nn.sigmoid(zk)).astype(LOW)
    v = zv_ref[...].astype(LOW)
    for first in range(0, STREAM, BLOCK):
        columns = first + BLOCK
        mask = masked_decay(rate, bounds, first, columns)
        scores = times_transposed(q[first:columns], k[:columns])
        weights = (scores * mask).astype(LOW)
        out_ref[first:columns, :] = matmul(weights, v[:columns])


def attend_back_kernel(
    rates, ends, zq_ref, zk_ref, zv_ref, do_ref, dzq_ref, dzk_ref, dzv_ref, dk_ref, dv_ref
):
    stream, head = pl.program_id(0), pl.program_id(1)
    rate = rates[head]
    bounds = [ends[stream, i] for i in range(ends.shape[1])]
    zq, zk = zq_ref[...], zk_ref[...]
    sig_q, sig_k = jax.nn.sigmoid(zq), jax.nn.sigmoid(zk)
    q = (zq * sig_q).astype(LOW)
    k = (zk * sig_k).astype(LOW)
    slope_q = sig_q * (1.0 + zq * (1.0 - sig_q))
    v = zv_ref[...].astype(LOW)
    d_o = do_ref[...]
    dk_ref[...] = jnp.zeros_like(dk_ref)
    dv_ref[...] = jnp.zeros_like(dv_ref)
    for first in range(0, STREAM, BLOCK):
        columns = first + BLOCK
        rows = slice(first, columns)
        mask = masked_decay(rate, bounds, first, columns)
        weights = (times_transposed(q[rows], k[:columns]) * mask).astype(LOW)
        d_scores = (times_transposed(d_o[rows], v[:columns]) * mask).astype(LOW)
        dzq_ref[rows, :] = (matmul(d_scores, k[:columns]) * slope_q[rows]).astype(LOW)
        dk_ref[:columns, :] += cross_tokens(d_scores, q[rows])
        dv_ref[:columns, :] += cross_tokens(weights, d_o[rows])
    dzk_ref[...] = (dk_ref[...] * (sig_k * (1.0 + zk * (1.0 - sig_k)))).astype(LOW)
    dzv_ref[...] = dv_ref[...].astype(LOW)


def head_block(offset=0):
    return pl.BlockSpec((STREAM, HEAD_DIM), lambda g, h, *_: (g, h + offset))


def attend(rates, ends, z_qk, z_vg):
    heads, streams = rates.shape[0], ends.shape[0]
    work = streams * heads * STREAM * STREAM
    return pl.pallas_call(
        attend_kernel,
        out_shape=jax.ShapeDtypeStruct((streams * STREAM, heads * HEAD_DIM), F32),
        grid_spec=pltpu.PrefetchScalarGridSpec(
            num_scalar_prefetch=2,
            grid=(streams, heads),
            in_specs=[head_block(), head_block(heads), head_block()],
            out_specs=head_block(),
        ),
        compiler_params=pltpu.CompilerParams(vmem_limit_bytes=40 << 20),
        cost_estimate=pl.CostEstimate(
            flops=4 * work * HEAD_DIM, transcendentals=work // 64,
            bytes_accessed=streams * heads * STREAM * HEAD_DIM * 16,
        ),
        name="attend",
    )(rates, ends, z_qk, z_qk, z_vg)


def attend_back(rates, ends, z_qk, z_vg, d_o):
    heads, streams = rates.shape[0], ends.shape[0]
    work = streams * heads * STREAM * STREAM
    return pl.pallas_call(
        attend_back_kernel,
        out_shape=[jax.ShapeDtypeStruct((streams * STREAM, heads * HEAD_DIM), LOW)] * 3,
        grid_spec=pltpu.PrefetchScalarGridSpec(
            num_scalar_prefetch=2,
            grid=(streams, heads),
            in_specs=[head_block(), head_block(heads), head_block(), head_block()],
            out_specs=[head_block()] * 3,
            scratch_shapes=[pltpu.VMEM((STREAM, HEAD_DIM), F32)] * 2,
        ),
        compiler_params=pltpu.CompilerParams(vmem_limit_bytes=40 << 20),
        cost_estimate=pl.CostEstimate(
            flops=10 * work * HEAD_DIM, transcendentals=work // 64,
            bytes_accessed=streams * heads * STREAM * HEAD_DIM * 20,
        ),
        name="attend_back",
    )(rates, ends, z_qk, z_qk, z_vg, d_o)


def chunk_copies(chunks, buffer, sems, turn, half=None):
    count, size = len(chunks), chunks[0].shape[0]
    if count == 1:
        rows = buffer.shape[0]
        first = 0 if half is None else pl.multiple_of(half * rows, rows)
        return [(None, pltpu.make_async_copy(chunks[0].at[pl.ds(first, rows)], buffer, sems.at[0]))]
    copies = []
    for k, chunk in enumerate(chunks):
        index = lax.rem(turn - k + count, count)
        wanted = None
        if half is not None:
            wanted = lax.div(index, count // 2) == half
            index = lax.rem(index, count // 2)
        target = buffer.at[pl.ds(pl.multiple_of(index * size, size), size)]
        copies.append((wanted, pltpu.make_async_copy(chunk, target, sems.at[k])))
    return copies


def each(copies, act):
    for wanted, copy in copies:
        if wanted is None:
            act(copy)
        else:
            pl.when(wanted)(functools.partial(act, copy))


def start(copies):
    each(copies, lambda copy: copy.start())


def finish(copies):
    each(copies, lambda copy: copy.wait())


def estimate(flops, *arrays):
    moved = sum(x.size * x.dtype.itemsize for x in arrays)
    return pl.CostEstimate(flops=flops, transcendentals=0, bytes_accessed=moved)


def limit(mebibytes):
    return pltpu.CompilerParams(vmem_limit_bytes=mebibytes << 20)


ANYWHERE = pl.BlockSpec(memory_space=pl.ANY)


def weight_buffer(chunks, share=1):
    size = len(chunks) * chunks[0].shape[0] // share
    return [pltpu.VMEM((size, chunks[0].shape[1]), LOW), pltpu.SemaphoreType.DMA((len(chunks),))]


def tile_rows(width, column=0):
    return pl.BlockSpec((TILE, width), lambda i, *_: (i, column))


def joined_rows(width, tiles):
    spec = pl.BlockSpec((TILE, width), lambda i, s: (i // (2 * tiles) * tiles + i % tiles, 0))
    return [spec, spec]


def enter_kernel(tiles, blocks, project, spots, own_ref, other_ref, *refs):
    i = pl.program_id(0)
    mine = lax.rem(lax.div(i, tiles), 2) == spots[0]
    rows = jnp.where(mine, own_ref[...], other_ref[...])
    part = rows.shape[1] // len(blocks)
    permuted = jnp.concatenate([rows[:, n * part : (n + 1) * part] for n in blocks], axis=1)
    if not project:
        all_ref, quarter_ref = refs
        all_ref[...] = permuted
        held = all_ref
    else:
        chunks, (h_ref, z_ref, scale_ref, quarter_ref, held, buffer, sems) = refs[:-7], refs[-7:]
        held[...] = permuted
        copies = chunk_copies(chunks, buffer, sems, spots[2])

        @pl.when(i == 0)
        def _():
            start(copies)

        x = rows.astype(F32)
        scale = lax.rsqrt(jnp.mean(x * x, axis=-1, keepdims=True) + EPSILON)
        scale_ref[...] = scale
        hidden = (permuted.astype(F32) * scale).astype(LOW)
        h_ref[...] = hidden

        @pl.when(i == 0)
        def _():
            finish(copies)

        z_ref[...] = matmul(hidden, buffer[...])
    size = quarter_ref.shape[1]
    quarter_ref[...] = held[:, pl.ds(pl.multiple_of(spots[1] * size, size), size)]


def enter(spots, blocks, own, other, chunks=()):
    width = own.shape[1]
    count, tiles = 2 * own.shape[0], own.shape[0] // TILE // 2
    shape = jax.ShapeDtypeStruct
    quarter = shape((count, width // GROUP), LOW)
    if chunks:
        columns = chunks[0].shape[1]
        outs = [shape((count, width), LOW), shape((count, columns), F32), shape((count, 1), F32), quarter]
        scratch = [pltpu.VMEM((TILE, width), LOW), *weight_buffer(chunks)]
    else:
        columns, scratch = 0, []
        outs = [shape((count, width), LOW), quarter]
    return pl.pallas_call(
        functools.partial(enter_kernel, tiles, blocks, bool(chunks)),
        out_shape=outs,
        grid_spec=pltpu.PrefetchScalarGridSpec(
            num_scalar_prefetch=1,
            grid=(count // TILE,),
            in_specs=joined_rows(width, tiles) + [ANYWHERE] * len(chunks),
            out_specs=[tile_rows(o.shape[1]) for o in outs],
            scratch_shapes=scratch,
        ),
        compiler_params=limit(40),
        cost_estimate=estimate(2 * count * width * columns, own, other, *chunks, *outs),
        name="enter",
    )(spots, own, other, *chunks)


def project_kernel(spots, h_ref, *refs):
    chunks, (z_ref, buffer, sems) = refs[:-3], refs[-3:]
    copies = chunk_copies(chunks, buffer, sems, spots[2])

    @pl.when(pl.program_id(0) == 0)
    def _():
        start(copies)
        finish(copies)

    z_ref[...] = matmul(h_ref[...], buffer[...])


def project(spots, hidden, chunks):
    count, width = hidden.shape
    out = jax.ShapeDtypeStruct((count, chunks[0].shape[1]), F32)
    return pl.pallas_call(
        project_kernel,
        out_shape=out,
        grid_spec=pltpu.PrefetchScalarGridSpec(
            num_scalar_prefetch=1,
            grid=(count // TILE,),
            in_specs=[tile_rows(width)] + [ANYWHERE] * len(chunks),
            out_specs=tile_rows(out.shape[1]),
            scratch_shapes=weight_buffer(chunks),
        ),
        compiler_params=limit(40),
        cost_estimate=estimate(2 * count * width * out.shape[1], hidden, *chunks, out),
        name="project",
    )(spots, hidden, *chunks)


def unit_kernel(spots, own_ref, other_ref, *refs):
    chunks, rest = refs[:-9], refs[-9:]
    h_ref, one_ref, two_ref, product_ref, scale_ref, first, second, sem_one, sem_two = rest
    split = len(chunks) // 2
    copies = [
        chunk_copies(chunks[:split], first, sem_one, spots[2]),
        chunk_copies(chunks[split:], second, sem_two, spots[2]),
    ]
    begins = pl.program_id(0) == 0

    @pl.when(begins)
    def _():
        start(copies[0])
        start(copies[1])

    mine, other = own_ref[...], other_ref[...]
    swapped = spots[0] == 1
    middle = jnp.concatenate(
        [jnp.where(swapped, other, mine), jnp.where(swapped, mine, other)], axis=1
    ).astype(F32)
    scale = lax.rsqrt(jnp.mean(middle * middle, axis=-1, keepdims=True) + EPSILON)
    scale_ref[...] = scale
    hidden = (middle * scale).astype(LOW)
    h_ref[...] = hidden

    @pl.when(begins)
    def _():
        finish(copies[0])

    z_one = matmul(hidden, first[...])

    @pl.when(begins)
    def _():
        finish(copies[1])

    z_two = matmul(hidden, second[...])
    one_ref[...] = z_one.astype(LOW)
    two_ref[...] = z_two.astype(LOW)
    product_ref[...] = (z_one * z_two).astype(LOW)


def gated_unit(spots, own, other, first, second):
    count, width, units = own.shape[0], 2 * own.shape[1], first[0].shape[1]
    shape = jax.ShapeDtypeStruct
    outs = [shape((count, width), LOW)] + [shape((count, units), LOW)] * 3 + [shape((count, 1), F32)]
    (buffer, sems) = weight_buffer(first)
    return pl.pallas_call(
        unit_kernel,
        out_shape=outs,
        grid_spec=pltpu.PrefetchScalarGridSpec(
            num_scalar_prefetch=1,
            grid=(count // TILE,),
            in_specs=[tile_rows(width // 2)] * 2 + [ANYWHERE] * (2 * len(first)),
            out_specs=[tile_rows(o.shape[1]) for o in outs],
            scratch_shapes=[buffer, buffer, sems, sems],
        ),
        compiler_params=limit(48),
        cost_estimate=estimate(4 * count * width * units, own, other, *first, *second, *outs),
        name="gated_unit",
    )(spots, own, other, *first, *second)


def unit_back_kernel(spots, dy_ref, one_ref, two_ref, *refs):
    chunks, (d_one_ref, d_two_ref, sum_ref, buffer, sems) = refs[:-5], refs[-5:]
    copies = chunk_copies(chunks, buffer, sems, spots[2])

    @pl.when(pl.program_id(0) == 0)
    def _():
        start(copies)
        finish(copies)

    d_product = matmul(dy_ref[...], buffer[...])
    z_one, z_two = one_ref[...].astype(F32), two_ref[...].astype(F32)
    d_one = d_product * z_two
    d_one_ref[...] = d_one.astype(LOW)
    d_two_ref[...] = (d_product * z_one).astype(LOW)
    sum_ref[...] = jnp.sum(d_one * z_one, axis=-1, keepdims=True)


def gated_unit_back(spots, dy, z_one, z_two, chunks):
    count, width, units = dy.shape[0], dy.shape[1], z_one.shape[1]
    shape = jax.ShapeDtypeStruct
    outs = [shape((count, units), LOW)] * 2 + [shape((count, 1), F32)]
    return pl.pallas_call(
        unit_back_kernel,
        out_shape=outs,
        grid_spec=pltpu.PrefetchScalarGridSpec(
            num_scalar_prefetch=1,
            grid=(count // TILE,),
            in_specs=[tile_rows(width), tile_rows(units), tile_rows(units)] + [ANYWHERE] * len(chunks),
            out_specs=[tile_rows(o.shape[1]) for o in outs],
            scratch_shapes=weight_buffer(chunks),
        ),
        compiler_params=limit(40),
        cost_estimate=estimate(2 * count * width * units, dy, z_one, z_two, *chunks, *outs),
        name="gated_unit_back",
    )(spots, dy, z_one, z_two, *chunks)


def fold_kernel(members, keeps, spots, *refs):
    values, refs = refs[:members], refs[members:]
    arrived, refs = (refs[0], refs[1:]) if keeps else (None, refs)
    outs = 2 if keeps else 1
    chunks, refs = refs[: -outs - 2 * members], refs[-outs - 2 * members :]
    outs, buffers, sems = refs[:outs], refs[outs : outs + members], refs[outs + members :]
    each_count = len(chunks) // members
    half = spots[0] if keeps else 1 - spots[0]
    begins = pl.program_id(0) == 0
    copies = [
        chunk_copies(chunks[m * each_count : (m + 1) * each_count], buffers[m], sems[m], spots[2], half)
        for m in range(members)
    ]

    @pl.when(begins)
    def _():
        for m in range(members):
            start(copies[m])

    whole = None
    for m in range(members):
        pl.when(begins)(functools.partial(finish, copies[m]))
        term = times_transposed(values[m][...], buffers[m][...])
        whole = term if whole is None else whole + term
    if not keeps:
        outs[0][...] = whole.astype(LOW)
    else:
        whole = whole + arrived[...].astype(F32)
        size = whole.shape[1] // 2
        upper = spots[3] == 1
        outs[0][...] = jnp.where(upper, whole[:, :size], whole[:, size:]).astype(LOW)
        outs[1][...] = jnp.where(upper, whole[:, size:], whole[:, :size])


def fold_half(spots, values, weights, arrived=None):
    count = values[0].shape[0]
    half = len(weights[0]) * weights[0][0].shape[0] // 2
    shape = jax.ShapeDtypeStruct
    if arrived is None:
        outs, extra = [shape((count, half), LOW)], []
    else:
        outs, extra = [shape((count, half // 2), LOW), shape((count, half // 2), F32)], [arrived]
    buffers, sems = zip(*[weight_buffer(w, 2) for w in weights])
    chunks = [x for w in weights for x in w]
    flops = sum(2 * count * half * v.shape[1] for v in values)
    found = pl.pallas_call(
        functools.partial(fold_kernel, len(values), arrived is not None),
        out_shape=outs,
        grid_spec=pltpu.PrefetchScalarGridSpec(
            num_scalar_prefetch=1,
            grid=(count // TILE,),
            in_specs=[tile_rows(v.shape[1]) for v in values]
            + [tile_rows(half)] * len(extra)
            + [ANYWHERE] * len(chunks),
            out_specs=[tile_rows(o.shape[1]) for o in outs],
            scratch_shapes=[*buffers, *sems],
        ),
        compiler_params=limit(40),
        cost_estimate=estimate(flops, *values, *extra, *chunks[: len(chunks) // 2], *outs),
        name="fold_half",
    )(spots, *values, *extra, *chunks)
    return found[0] if arrived is None else found


def gradient_kernel(spots, left_ref, right_ref, *refs):
    found = cross_tokens(left_ref[...], right_ref[...])
    for arrived_ref in refs[:-1]:
        found = found + arrived_ref[...].astype(F32)
    refs[-1][...] = found.astype(LOW)


def gradient_rows(spots, spread, k, left, right, arrived=()):
    count, columns = right.shape
    rows = left.shape[1] // (1 if k is None else spread)
    tiles = rows // TILE

    def block(i, s):
        return (0, i if k is None else lax.rem(s[2] + k, spread) * tiles + i)

    out = jax.ShapeDtypeStruct((rows, columns), LOW)
    return pl.pallas_call(
        gradient_kernel,
        out_shape=out,
        grid_spec=pltpu.PrefetchScalarGridSpec(
            num_scalar_prefetch=1,
            grid=(tiles,),
            in_specs=[
                pl.BlockSpec((count, TILE), block),
                pl.BlockSpec((count, columns), lambda i, s: (0, 0), pipeline_mode=pl.Buffered(1)),
            ]
            + [tile_rows(columns)] * len(arrived),
            out_specs=tile_rows(columns),
        ),
        compiler_params=limit(40),
        cost_estimate=estimate(2 * count * rows * columns, right, out, out, *arrived),
        name="gradient_rows",
    )(spots, left, right, *arrived)


def place_kernel(cuts, spots, *refs):
    quarter = pl.program_id(0)
    cross = lax.rem(lax.div(quarter, 2) + spots[0], 2) * 2 + lax.rem(lax.rem(quarter, 2) + spots[3], 2)
    for n in range(4):

        @pl.when(cross == n)
        def _():
            for (first, size), out_ref in zip(cuts, refs[4:]):
                out_ref[...] = refs[n][:, first : first + size].astype(F32)


def place_quarters(spots, pairs, *cuts):
    rows, columns = pairs[0].shape[0], pairs[0].shape[1] // 2
    outs = [jax.ShapeDtypeStruct((rows, GROUP * size), F32) for _, size in cuts]

    def block(index):
        return pl.BlockSpec((rows, columns), lambda q, s: (0, index), pipeline_mode=pl.Buffered(1))

    return pl.pallas_call(
        functools.partial(place_kernel, cuts),
        out_shape=outs,
        grid_spec=pltpu.PrefetchScalarGridSpec(
            num_scalar_prefetch=1,
            grid=(GROUP,),
            in_specs=[block(0), block(1), block(0), block(1)],
            out_specs=[pl.BlockSpec((rows, size), lambda q, s: (0, q)) for _, size in cuts],
        ),
        compiler_params=limit(40),
        cost_estimate=estimate(0, *pairs, *outs),
        name="place_quarters",
    )(spots, pairs[0], pairs[0], pairs[1], pairs[1])


def tie(*values):
    return lax.optimization_barrier(values)


def body(reps, shards, tokens, cotangent, lengths, decay_rates, *weights):
    spread = reps // GROUP
    place = lax.axis_index("shard")
    a, b, c = lax.axis_index("a"), lax.axis_index("b"), lax.axis_index("c")
    quarter = 2 * c + b
    micro, run, width = tokens.shape
    half, own = width // 2, width // GROUP
    streams = micro * GROUP // shards
    per_block = STREAM // run // GROUP * streams
    rows = width // shards
    part = rows // spread
    columns = functools.partial(lax.dynamic_slice_in_dim, axis=1)
    spots = jnp.stack([c, quarter, a, b]).astype(jnp.int32)
    blocks = [z * spread + k for k in range(spread) for z in range(shards)]

    def move(x, target):
        pairs = [(r * shards + s, target(r) * shards + s) for r in range(reps) for s in range(shards)]
        return lax.ppermute(x, AXES, pairs)

    def swap_c(x):
        return move(x, lambda r: r ^ 1)

    def swap_b(x):
        return move(x, lambda r: r ^ 2)

    def joined(*parts):
        return jnp.concatenate(parts, axis=1)

    def shift_a(x, k):
        return move(x, lambda r: (r + GROUP * k) % reps)

    def ordered(index, mine, other, axis):
        return jnp.where(
            index == 0,
            jnp.concatenate([mine, other], axis),
            jnp.concatenate([other, mine], axis),
        )


    def batch_of(s):
        return s // (shards // micro)

    def origin(r, s, p):
        run_id = (r % GROUP) * per_block + p
        stream, piece = run_id // shards, run_id % shards
        member = s % GROUP if streams == 1 else 2 * stream + s % 2
        return (r // GROUP) * GROUP + member, piece

    def routes(p):
        found = []
        for r in range(reps):
            for s in range(shards):
                from_r, from_s = origin(r, s, p ^ batch_of(s))
                found.append((from_r * shards + from_s, r * shards + s))
        return found

    def natural(x):
        return jnp.concatenate(
            [
                x[:, (k * shards + z) * part : (k * shards + z + 1) * part]
                for z in range(shards)
                for k in range(spread)
            ],
            axis=1,
        )

    def bring(x):
        arrived = [
            lax.ppermute(lax.dynamic_index_in_dim(x, (place + p) % 2, 0, False), AXES, routes(p))
            for p in range(2)
        ]
        return ordered(batch_of(place), *arrived, 0)

    def bring_back(x):
        slots = natural(x).reshape(2, run, width)
        arrived = [
            lax.ppermute(
                lax.dynamic_index_in_dim(slots, (batch_of(place) + p) % 2, 0, False),
                AXES,
                [(to, origin) for origin, to in routes(p)],
            )
            for p in range(2)
        ]
        return ordered(place % 2, arrived[0][None], arrived[1][None], 0)


    def gather_b(x):
        return ordered(b, x, swap_b(x), 1)

    def gather_c(x):
        return ordered(c, x, swap_c(x), 1)

    def gather_rows_b(x):
        return ordered(b, x, swap_b(x), 0)

    def total(x):
        x = x + swap_c(x)
        return x + swap_b(x)

    def fold_c(product):
        sent = swap_c(product(1 - c).astype(LOW))
        return product(c) + sent.astype(F32)

    def fold_b(x):
        sent = swap_b(columns(x, (1 - b) * own, own).astype(LOW))
        return columns(x, b * own, own) + sent.astype(F32)

    def to_runs(x):
        cut = x.reshape(2, 2, -1, own)
        pick = functools.partial(lax.dynamic_index_in_dim, keepdims=False)
        both = ordered(b, pick(cut, b, 0), swap_b(pick(cut, 1 - b, 0)), 2)
        return ordered(c, pick(both, c, 0), swap_c(pick(both, 1 - c, 0)), 1)


    def own_features(w):
        count = shards * spread // GROUP
        cut = []
        for i in range(count):
            block = quarter * count + i
            cut.append(columns(w, (block % shards) * rows + (block // shards) * part, part))
        return jnp.concatenate(cut, axis=1)

    def own_units(w):
        return columns(w, quarter * (w.shape[1] // GROUP), w.shape[1] // GROUP)

    def over_shards(*members):
        cut = jnp.concatenate(members, axis=1) if len(members) > 1 else members[0]
        piece = lax.dynamic_slice_in_dim(cut, a * part, part, 0)
        return lax.all_gather(piece, "shard", axis=0, tiled=True)

    def over_owners(w):
        piece = lax.dynamic_slice_in_dim(w, a * part, part, 0)
        return lax.all_gather(piece, OWNERS, axis=0, tiled=True)

    def over_spread(x):
        return [shift_a(x, k) for k in range(1, spread)]

    def by_spread(relative):
        if spread == 2:
            return ordered(a, relative[0], relative[1], 0)
        stacked = jnp.stack(relative, 0)
        pick = functools.partial(lax.dynamic_index_in_dim, axis=0, keepdims=False)
        return jnp.concatenate([pick(stacked, (a - j) % spread) for j in range(spread)], axis=0)

    def in_row_order(x):
        cut = x.reshape(spread, shards, part, -1)
        return jnp.transpose(cut, (1, 0, 2, 3)).reshape(width, -1)

    def row_half(w, h):
        return lax.dynamic_slice_in_dim(w, h * half, half, 0)


    def away(left, right):
        return [gradient_rows(spots, spread, k, left, right) for k in range(1, spread)]

    def pieces(terms, *eighths):
        marks = [0, *eighths, 8]
        return [
            [x[x.shape[0] * i // 8 : x.shape[0] * j // 8] for x in terms]
            for i, j in zip(marks[:-1], marks[1:])
        ]

    def stacked(*arrived):
        return [jnp.concatenate(cut, axis=0) for cut in zip(*arrived)]

    def sent_a(terms):
        return [shift_a(x, k + 1) for k, x in enumerate(terms)]

    def scattered(x):
        return lax.psum_scatter(x, "shard", scatter_dimension=0, tiled=True)

    def kept(left, right, *arrived):
        return gradient_rows(spots, spread, 0, left, right, stacked(*arrived))

    def spread_a(x):
        return by_spread([x] + over_spread(x))

    def spread_b(x):
        return jnp.concatenate([x, swap_b(x)], axis=1)

    def spread_c(pair):
        return pair, swap_c(pair)

    def features_in_order(pairs, first, size):
        full = pairs[0].shape[1] // 2
        cut = [x[:, i * full + first : i * full + first + size] for x in pairs for i in range(2)]
        pair = [ordered(b, cut[n], cut[n + 1], 1) for n in (0, 2)]
        return natural(ordered(c, pair[0], pair[1], 1)).astype(F32)


    w_query, w_key, w_value, w_gate, w_out, w_one, w_two, w_down = weights
    g_qk = over_shards(own_units(w_query), own_units(w_key))
    g_vg = over_shards(own_units(w_value), own_units(w_gate))
    g_o = over_shards(own_features(w_out))
    g_1 = over_shards(own_units(w_one))
    g_2 = over_shards(own_units(w_two))
    w_d = [over_owners(own_units(w_down))]

    heads = HEADS // GROUP
    rates = lax.dynamic_slice_in_dim(decay_rates, quarter * heads, heads, 0)
    cuts = gather_rows_b(lengths.reshape(1, -1))
    cuts = ordered(c, cuts, swap_c(cuts), 0).reshape(GROUP, micro, -1)
    if streams == 1:
        batch = place // GROUP
        member = place % GROUP
        chosen = lax.dynamic_slice_in_dim(cuts, 2 * (member % 2) + member // 2, 1, 0)
    else:
        batch = place // 2
        chosen = lax.dynamic_index_in_dim(cuts.reshape(2, 2, micro, -1), place % 2, 0, False)
    chosen = lax.dynamic_index_in_dim(chosen, batch, 1, False)
    seq_ends = [chosen[:, 0]]
    for i in range(1, chosen.shape[1]):
        seq_ends.append(seq_ends[-1] + chosen[:, i])
    ends = jnp.stack(seq_ends, axis=1)

    x_run = bring(tokens)
    x_run, g_qk = tie(x_run, g_qk)

    x_pair = gather_rows_b(x_run)
    s_qk = over_spread(g_qk)
    x_pair, s_qk, g_vg = tie(x_pair, s_qk, g_vg)

    s_vg = over_spread(g_vg)
    w_qk = [g_qk, *s_qk]
    hidden_one, z_qk, x_scale, x_own = enter(spots, blocks, x_pair, swap_c(x_pair), w_qk)
    z_qk, hidden_one, s_vg, g_o = tie(z_qk, hidden_one, s_vg, g_o)

    s_o = over_spread(g_o)
    w_vg = [g_vg, *s_vg]
    z_vg = project(spots, hidden_one, w_vg)
    attended = attend(rates, ends, z_qk, z_vg)
    gate = z_vg[:, own:]
    o_scale = lax.rsqrt(total(jnp.sum(attended * attended, axis=-1)) / width + EPSILON)[:, None]
    lifted = (attended * gate).astype(LOW)
    lifted, s_o, g_1, cotangent = tie(lifted, s_o, g_1, cotangent)

    s_1 = over_spread(g_1)
    lifted = gather_b(lifted)
    lifted, s_1, g_2, o_scale, cotangent = tie(lifted, s_1, g_2, o_scale, cotangent)

    s_2 = over_spread(g_2)
    dy_run = bring(cotangent)
    lifted = gather_c(lifted)
    w_o = in_row_order(by_spread([g_o, *s_o]))
    branch = o_scale * matmul(lifted, w_o)
    middle = x_own.astype(F32) + branch
    low_middle = gather_b(middle.astype(LOW))
    low_middle, s_2, dy_run = tie(low_middle, s_2, dy_run)

    other_middle = swap_c(low_middle)
    dy_other = swap_b(dy_run)
    w_1, w_2 = [g_1, *s_1], [g_2, *s_2]
    hidden_two, z_one, z_two, product, m_scale = gated_unit(spots, low_middle, other_middle, w_1, w_2)
    z_one, z_two, product, dy_other = tie(z_one, z_two, product, dy_other)

    dy_pair = ordered(b, dy_run, dy_other, 0)
    dy_all, dy_own = enter(spots, blocks, dy_pair, swap_c(dy_pair))
    t_down = away(dy_all, product)
    z_one, z_two, product, t_down, w_d[0] = tie(z_one, z_two, product, t_down, w_d[0])


    down_a, down_b = pieces(t_down, 6)
    down_a = sent_a(down_a)
    d_one, d_two, lean_m = gated_unit_back(spots, dy_all, z_one, z_two, w_d)
    sent = fold_half(spots, [d_one, d_two], [w_1, w_2])
    sent, d_one, d_two, lean_m, down_a = tie(sent, d_one, d_two, lean_m, down_a)

    arrived = swap_c(sent)
    down_b = sent_a(down_b)
    t_one = away(hidden_two, d_one)
    lean_m = total(lean_m[:, 0])
    sent, mine = fold_half(spots, [d_one, d_two], [w_1, w_2], arrived)
    sent, d_two, t_one, product, lean_m, down_b = tie(sent, d_two, t_one, product, lean_m, down_b)

    crossed = swap_b(sent)
    one_a, one_b = pieces(t_one, 6)
    one_a = sent_a(one_a)
    f_down = kept(dy_all, product, down_a, down_b)
    t_two = away(hidden_two, d_two)
    result = fold_half(spots, [product], [w_d])
    crossed, result, f_down, t_two, one_a = tie(crossed, result, f_down, t_two, one_a)

    f_down = scattered(f_down)
    one_b = sent_a(one_b)
    two_a, two_b = pieces(t_two, 3)
    two_a = sent_a(two_a)
    d_hidden = mine + crossed.astype(F32)
    m_normed = middle * m_scale
    lean = lean_m[:, None] * (2.0 / width)
    d_middle = dy_own.astype(F32) + m_scale * (d_hidden - m_normed * lean)
    d_branch = d_middle.astype(LOW)
    lean_o = jnp.sum(d_middle * branch, axis=-1)
    sent = times_transposed(d_branch, row_half(w_o, 1 - c)).astype(LOW)
    sent, result, d_middle, lean_o = tie(sent, result, d_middle, lean_o)

    arrived = swap_c(sent)
    r_result = swap_c(result)
    lean_o = total(lean_o)
    p_out = cross_tokens(lifted, (o_scale * d_middle).astype(LOW)).astype(LOW)
    p_out = jnp.transpose(p_out.reshape(shards, spread, part, -1), (1, 0, 2, 3))
    p_out = p_out.reshape(spread, width // spread, -1)
    t_out = [lax.dynamic_index_in_dim(p_out, (a + k) % spread, 0, False) for k in range(spread)]
    d_gated = times_transposed(d_branch, row_half(w_o, c)) + arrived.astype(F32)
    sent = columns(d_gated, (1 - b) * own, own).astype(LOW)
    mine = columns(d_gated, b * own, own)
    sent, mine, d_one, r_result, t_out, lean_o, one_b, two_a = tie(
        sent, mine, d_one, r_result, t_out, lean_o, one_b, two_a
    )

    crossed = swap_b(sent)
    two_b = sent_a(two_b)
    f_one = kept(hidden_two, d_one, one_a, one_b)
    result, result_mine = fold_half(spots, [product], [w_d], r_result)
    crossed, result, f_one, f_down, two_b = tie(crossed, result, f_one, f_down, two_b)

    f_one = scattered(f_one)
    r_out = sent_a(t_out[1:])
    y_down = spread_a(f_down)
    result = swap_b(result)
    f_two = kept(hidden_two, d_two, two_a, two_b)
    o_normed = attended * o_scale
    d_gated = mine + crossed.astype(F32)
    d_gate = (d_gated * o_normed).astype(LOW)
    lean = lean_o[:, None] / width
    d_attended = (o_scale * (d_gated * gate - o_normed * lean)).astype(LOW)
    d_query, d_key, d_value = attend_back(rates, ends, z_qk, z_vg, d_attended)
    d_qk = joined(d_query, d_key)
    d_vg = joined(d_value, d_gate)
    t_qk = away(hidden_one, d_qk)
    d_qk, d_vg, t_qk, f_two, r_out, y_down, result = tie(d_qk, d_vg, t_qk, f_two, r_out, y_down, result)

    f_two = scattered(f_two)
    qk_a, qk_b = pieces(t_qk, 4)
    qk_a = sent_a(qk_a)
    output = to_runs((middle + (result_mine + result.astype(F32))).astype(LOW))
    x_down = swap_b(y_down)
    y_one = over_spread(f_one)
    t_vg = away(hidden_one, d_vg)
    sent = fold_half(spots, [d_qk, d_vg], [w_qk, w_vg])
    sent, t_vg, d_qk, d_vg, output, qk_a, x_down, y_one = tie(
        sent, t_vg, d_qk, d_vg, output, qk_a, x_down, y_one
    )

    f_out = scattered(sum([x.astype(F32) for x in r_out], t_out[0].astype(F32)).astype(LOW))
    arrived = swap_c(sent)
    qk_b = sent_a(qk_b)
    x_down = joined(y_down, x_down)
    y_one = by_spread([f_one, *y_one])
    x_one = swap_b(y_one)
    lean_x = total(
        jnp.sum(z_qk * d_qk.astype(F32), axis=-1) + jnp.sum(z_vg * d_vg.astype(F32), axis=-1)
    )
    sent, mine = fold_half(spots, [d_qk, d_vg], [w_qk, w_vg], arrived)
    sent, mine, qk_b, t_vg, lean_x, x_one = tie(sent, mine, qk_b, t_vg, lean_x, x_one)

    crossed = swap_b(sent)
    r_vg = sent_a(t_vg)
    f_qk = scattered(kept(hidden_one, d_qk, qk_a, qk_b))
    output = bring_back(output)
    four_down = spread_c(x_down)
    crossed, d_vg, r_vg, output, f_two, four_down = tie(crossed, d_vg, r_vg, output, f_two, four_down)

    f_vg = kept(hidden_one, d_vg, r_vg)
    x_one = joined(y_one, x_one)
    f_vg, crossed, f_two, f_out, x_one = tie(f_vg, crossed, f_two, f_out, x_one)

    f_vg = scattered(f_vg)
    d_hidden = mine + crossed.astype(F32)
    x_normed = x_own.astype(F32) * x_scale
    lean = lean_x[:, None] / width
    input_grad = to_runs((d_middle + x_scale * (d_hidden - x_normed * lean)).astype(LOW))
    f_oqk = joined(f_out, f_qk)
    x_oqk = swap_b(f_oqk)
    y_two = over_spread(f_two)
    four_one = spread_c(x_one)
    units = f_one.shape[1]
    [g_down] = place_quarters(spots, four_down, (0, units))
    [g_one] = place_quarters(spots, four_one, (0, units))
    input_grad, x_oqk, y_two, f_vg, g_down, g_one = tie(input_grad, x_oqk, y_two, f_vg, g_down, g_one)

    x_vg = spread_b(f_vg)
    y_two = by_spread([f_two, *y_two])
    y_oqk = spread_a(joined(f_oqk, x_oqk))
    x_vg, y_oqk = tie(x_vg, y_oqk)

    four_vg = spread_c(spread_a(x_vg))
    input_grad = bring_back(input_grad)
    four_two = spread_c(spread_b(y_two))
    four_oqk = spread_c(y_oqk)
    g_query, g_key = place_quarters(spots, four_oqk, (own, own), (2 * own, own))
    g_value, g_gate = place_quarters(spots, four_vg, (0, own), (own, own))
    [g_two] = place_quarters(spots, four_two, (0, units))
    g_out = features_in_order(four_oqk, 0, own)
    return output, input_grad, g_query, g_key, g_value, g_gate, g_out, g_one, g_two, g_down


def solution(mesh):
    reps, shards = mesh.shape["rep"], mesh.shape["shard"]
    devices = mesh.devices.reshape(reps // GROUP, 2, 2, shards)
    rep = ("a", "b", "c")
    by_tokens = P(None, (*rep, "shard"), None)
    by_rows = P("shard", None)
    return jax.shard_map(
        functools.partial(body, reps, shards),
        mesh=Mesh(devices, AXES),
        in_specs=(by_tokens, by_tokens, P(None, rep, None), P(), *[by_rows] * 8),
        out_specs=(by_tokens, by_tokens, *[by_rows] * 8),
        check_vma=False,
    )
```

```python
import functools

import jax
import jax.numpy as jnp
from jax import lax
from jax.experimental import pallas as pl
from jax.experimental.pallas import tpu as pltpu
from jax.sharding import Mesh, PartitionSpec as P

HEADS = 16
HEAD_DIM = 128
STREAM = 1024
GROUP = 4
BLOCK = 256
TILE = 256
EPSILON = 1e-06
AXES = ("a", "b", "c", "shard")
OWNERS = ("a", "shard")
LOW = jnp.bfloat16
F32 = jnp.float32


def matmul(former, latter):
    return jnp.dot(former, latter, preferred_element_type=F32)


def times_transposed(former, latter):
    return lax.dot_general(former, latter, (((1,), (1,)), ((), ())), preferred_element_type=F32)


def cross_tokens(former, latter):
    return lax.dot_general(former, latter, (((0,), (0,)), ((), ())), preferred_element_type=F32)


def masked_decay(rate, ends, first, columns):
    row = first + lax.broadcasted_iota(jnp.int32, (BLOCK, 1), 0)
    column = lax.broadcasted_iota(jnp.int32, (1, columns), 1)
    begin = jnp.zeros((BLOCK, 1), jnp.int32)
    for end in ends:
        begin = jnp.where(row >= end, end, begin)
    falling = jnp.exp(-rate * (row - first).astype(F32))
    rising = jnp.exp(rate * (column - first).astype(F32))
    allowed = (column <= row) & (column >= begin)
    return jnp.where(allowed, falling * rising, 0.0)


def attend_kernel(rates, ends, zq_ref, zk_ref, zv_ref, out_ref):
    stream, head = pl.program_id(0), pl.program_id(1)
    rate = rates[head]
    bounds = [ends[stream, i] for i in range(ends.shape[1])]
    zq, zk = zq_ref[...], zk_ref[...]
    q = (zq * jax.nn.sigmoid(zq)).astype(LOW)
    k = (zk * jax.nn.sigmoid(zk)).astype(LOW)
    v = zv_ref[...].astype(LOW)
    for first in range(0, STREAM, BLOCK):
        columns = first + BLOCK
        mask = masked_decay(rate, bounds, first, columns)
        scores = times_transposed(q[first:columns], k[:columns])
        weights = (scores * mask).astype(LOW)
        out_ref[first:columns, :] = matmul(weights, v[:columns])


def attend_back_kernel(
    rates, ends, zq_ref, zk_ref, zv_ref, do_ref, dzq_ref, dzk_ref, dzv_ref, dk_ref, dv_ref
):
    stream, head = pl.program_id(0), pl.program_id(1)
    rate = rates[head]
    bounds = [ends[stream, i] for i in range(ends.shape[1])]
    zq, zk = zq_ref[...], zk_ref[...]
    sig_q, sig_k = jax.nn.sigmoid(zq), jax.nn.sigmoid(zk)
    q = (zq * sig_q).astype(LOW)
    k = (zk * sig_k).astype(LOW)
    slope_q = sig_q * (1.0 + zq * (1.0 - sig_q))
    v = zv_ref[...].astype(LOW)
    d_o = do_ref[...]
    dk_ref[...] = jnp.zeros_like(dk_ref)
    dv_ref[...] = jnp.zeros_like(dv_ref)
    for first in range(0, STREAM, BLOCK):
        columns = first + BLOCK
        rows = slice(first, columns)
        mask = masked_decay(rate, bounds, first, columns)
        weights = (times_transposed(q[rows], k[:columns]) * mask).astype(LOW)
        d_scores = (times_transposed(d_o[rows], v[:columns]) * mask).astype(LOW)
        dzq_ref[rows, :] = (matmul(d_scores, k[:columns]) * slope_q[rows]).astype(LOW)
        dk_ref[:columns, :] += cross_tokens(d_scores, q[rows])
        dv_ref[:columns, :] += cross_tokens(weights, d_o[rows])
    dzk_ref[...] = (dk_ref[...] * (sig_k * (1.0 + zk * (1.0 - sig_k)))).astype(LOW)
    dzv_ref[...] = dv_ref[...].astype(LOW)


def head_block(offset=0):
    return pl.BlockSpec((STREAM, HEAD_DIM), lambda g, h, *_: (g, h + offset))


def attend(rates, ends, z_qk, z_vg):
    heads, streams = rates.shape[0], ends.shape[0]
    work = streams * heads * STREAM * STREAM
    return pl.pallas_call(
        attend_kernel,
        out_shape=jax.ShapeDtypeStruct((streams * STREAM, heads * HEAD_DIM), F32),
        grid_spec=pltpu.PrefetchScalarGridSpec(
            num_scalar_prefetch=2,
            grid=(streams, heads),
            in_specs=[head_block(), head_block(heads), head_block()],
            out_specs=head_block(),
        ),
        compiler_params=pltpu.CompilerParams(vmem_limit_bytes=40 << 20),
        cost_estimate=pl.CostEstimate(
            flops=4 * work * HEAD_DIM, transcendentals=work // 64,
            bytes_accessed=streams * heads * STREAM * HEAD_DIM * 16,
        ),
        name="attend",
    )(rates, ends, z_qk, z_qk, z_vg)


def attend_back(rates, ends, z_qk, z_vg, d_o):
    heads, streams = rates.shape[0], ends.shape[0]
    work = streams * heads * STREAM * STREAM
    return pl.pallas_call(
        attend_back_kernel,
        out_shape=[jax.ShapeDtypeStruct((streams * STREAM, heads * HEAD_DIM), LOW)] * 3,
        grid_spec=pltpu.PrefetchScalarGridSpec(
            num_scalar_prefetch=2,
            grid=(streams, heads),
            in_specs=[head_block(), head_block(heads), head_block(), head_block()],
            out_specs=[head_block()] * 3,
            scratch_shapes=[pltpu.VMEM((STREAM, HEAD_DIM), F32)] * 2,
        ),
        compiler_params=pltpu.CompilerParams(vmem_limit_bytes=40 << 20),
        cost_estimate=pl.CostEstimate(
            flops=10 * work * HEAD_DIM, transcendentals=work // 64,
            bytes_accessed=streams * heads * STREAM * HEAD_DIM * 20,
        ),
        name="attend_back",
    )(rates, ends, z_qk, z_qk, z_vg, d_o)


def chunk_copies(chunks, buffer, sems, turn, half=None):
    count, size = len(chunks), chunks[0].shape[0]
    if count == 1:
        rows = buffer.shape[0]
        first = 0 if half is None else pl.multiple_of(half * rows, rows)
        return [(None, pltpu.make_async_copy(chunks[0].at[pl.ds(first, rows)], buffer, sems.at[0]))]
    copies = []
    for k, chunk in enumerate(chunks):
        index = lax.rem(turn - k + count, count)
        wanted = None
        if half is not None:
            wanted = lax.div(index, count // 2) == half
            index = lax.rem(index, count // 2)
        target = buffer.at[pl.ds(pl.multiple_of(index * size, size), size)]
        copies.append((wanted, pltpu.make_async_copy(chunk, target, sems.at[k])))
    return copies


def each(copies, act):
    for wanted, copy in copies:
        if wanted is None:
            act(copy)
        else:
            pl.when(wanted)(functools.partial(act, copy))


def start(copies):
    each(copies, lambda copy: copy.start())


def finish(copies):
    each(copies, lambda copy: copy.wait())


def estimate(flops, *arrays):
    moved = sum(x.size * x.dtype.itemsize for x in arrays)
    return pl.CostEstimate(flops=flops, transcendentals=0, bytes_accessed=moved)


def limit(mebibytes):
    return pltpu.CompilerParams(vmem_limit_bytes=mebibytes << 20)


ANYWHERE = pl.BlockSpec(memory_space=pl.ANY)


def weight_buffer(chunks, share=1):
    size = len(chunks) * chunks[0].shape[0] // share
    return [pltpu.VMEM((size, chunks[0].shape[1]), LOW), pltpu.SemaphoreType.DMA((len(chunks),))]


def tile_rows(width, column=0):
    return pl.BlockSpec((TILE, width), lambda i, *_: (i, column))


def joined_rows(width, tiles):
    spec = pl.BlockSpec((TILE, width), lambda i, s: (i // (2 * tiles) * tiles + i % tiles, 0))
    return [spec, spec]


def enter_kernel(tiles, blocks, project, spots, own_ref, other_ref, *refs):
    i = pl.program_id(0)
    mine = lax.rem(lax.div(i, tiles), 2) == spots[0]
    rows = jnp.where(mine, own_ref[...], other_ref[...])
    part = rows.shape[1] // len(blocks)
    permuted = jnp.concatenate([rows[:, n * part : (n + 1) * part] for n in blocks], axis=1)
    if not project:
        all_ref, quarter_ref = refs
        all_ref[...] = permuted
        held = all_ref
    else:
        chunks, (h_ref, z_ref, scale_ref, quarter_ref, held, buffer, sems) = refs[:-7], refs[-7:]
        held[...] = permuted
        copies = chunk_copies(chunks, buffer, sems, spots[2])

        @pl.when(i == 0)
        def _():
            start(copies)

        x = rows.astype(F32)
        scale = lax.rsqrt(jnp.mean(x * x, axis=-1, keepdims=True) + EPSILON)
        scale_ref[...] = scale
        hidden = (permuted.astype(F32) * scale).astype(LOW)
        h_ref[...] = hidden

        @pl.when(i == 0)
        def _():
            finish(copies)

        z_ref[...] = matmul(hidden, buffer[...])
    size = quarter_ref.shape[1]
    quarter_ref[...] = held[:, pl.ds(pl.multiple_of(spots[1] * size, size), size)]


def enter(spots, blocks, own, other, chunks=()):
    width = own.shape[1]
    count, tiles = 2 * own.shape[0], own.shape[0] // TILE // 2
    shape = jax.ShapeDtypeStruct
    quarter = shape((count, width // GROUP), LOW)
    if chunks:
        columns = chunks[0].shape[1]
        outs = [shape((count, width), LOW), shape((count, columns), F32), shape((count, 1), F32), quarter]
        scratch = [pltpu.VMEM((TILE, width), LOW), *weight_buffer(chunks)]
    else:
        columns, scratch = 0, []
        outs = [shape((count, width), LOW), quarter]
    return pl.pallas_call(
        functools.partial(enter_kernel, tiles, blocks, bool(chunks)),
        out_shape=outs,
        grid_spec=pltpu.PrefetchScalarGridSpec(
            num_scalar_prefetch=1,
            grid=(count // TILE,),
            in_specs=joined_rows(width, tiles) + [ANYWHERE] * len(chunks),
            out_specs=[tile_rows(o.shape[1]) for o in outs],
            scratch_shapes=scratch,
        ),
        compiler_params=limit(40),
        cost_estimate=estimate(2 * count * width * columns, own, other, *chunks, *outs),
        name="enter",
    )(spots, own, other, *chunks)


def project_kernel(spots, h_ref, *refs):
    chunks, (z_ref, buffer, sems) = refs[:-3], refs[-3:]
    copies = chunk_copies(chunks, buffer, sems, spots[2])

    @pl.when(pl.program_id(0) == 0)
    def _():
        start(copies)
        finish(copies)

    z_ref[...] = matmul(h_ref[...], buffer[...])


def project(spots, hidden, chunks):
    count, width = hidden.shape
    out = jax.ShapeDtypeStruct((count, chunks[0].shape[1]), F32)
    return pl.pallas_call(
        project_kernel,
        out_shape=out,
        grid_spec=pltpu.PrefetchScalarGridSpec(
            num_scalar_prefetch=1,
            grid=(count // TILE,),
            in_specs=[tile_rows(width)] + [ANYWHERE] * len(chunks),
            out_specs=tile_rows(out.shape[1]),
            scratch_shapes=weight_buffer(chunks),
        ),
        compiler_params=limit(40),
        cost_estimate=estimate(2 * count * width * out.shape[1], hidden, *chunks, out),
        name="project",
    )(spots, hidden, *chunks)


def unit_kernel(spots, own_ref, other_ref, *refs):
    chunks, rest = refs[:-9], refs[-9:]
    h_ref, one_ref, two_ref, product_ref, scale_ref, first, second, sem_one, sem_two = rest
    split = len(chunks) // 2
    copies = [
        chunk_copies(chunks[:split], first, sem_one, spots[2]),
        chunk_copies(chunks[split:], second, sem_two, spots[2]),
    ]
    begins = pl.program_id(0) == 0

    @pl.when(begins)
    def _():
        start(copies[0])
        start(copies[1])

    mine, other = own_ref[...], other_ref[...]
    swapped = spots[0] == 1
    middle = jnp.concatenate(
        [jnp.where(swapped, other, mine), jnp.where(swapped, mine, other)], axis=1
    ).astype(F32)
    scale = lax.rsqrt(jnp.mean(middle * middle, axis=-1, keepdims=True) + EPSILON)
    scale_ref[...] = scale
    hidden = (middle * scale).astype(LOW)
    h_ref[...] = hidden

    @pl.when(begins)
    def _():
        finish(copies[0])

    z_one = matmul(hidden, first[...])

    @pl.when(begins)
    def _():
        finish(copies[1])

    z_two = matmul(hidden, second[...])
    one_ref[...] = z_one.astype(LOW)
    two_ref[...] = z_two.astype(LOW)
    product_ref[...] = (z_one * z_two).astype(LOW)


def gated_unit(spots, own, other, first, second):
    count, width, units = own.shape[0], 2 * own.shape[1], first[0].shape[1]
    shape = jax.ShapeDtypeStruct
    outs = [shape((count, width), LOW)] + [shape((count, units), LOW)] * 3 + [shape((count, 1), F32)]
    (buffer, sems) = weight_buffer(first)
    return pl.pallas_call(
        unit_kernel,
        out_shape=outs,
        grid_spec=pltpu.PrefetchScalarGridSpec(
            num_scalar_prefetch=1,
            grid=(count // TILE,),
            in_specs=[tile_rows(width // 2)] * 2 + [ANYWHERE] * (2 * len(first)),
            out_specs=[tile_rows(o.shape[1]) for o in outs],
            scratch_shapes=[buffer, buffer, sems, sems],
        ),
        compiler_params=limit(48),
        cost_estimate=estimate(4 * count * width * units, own, other, *first, *second, *outs),
        name="gated_unit",
    )(spots, own, other, *first, *second)


def unit_back_kernel(spots, dy_ref, one_ref, two_ref, *refs):
    chunks, (d_one_ref, d_two_ref, sum_ref, buffer, sems) = refs[:-5], refs[-5:]
    copies = chunk_copies(chunks, buffer, sems, spots[2])

    @pl.when(pl.program_id(0) == 0)
    def _():
        start(copies)
        finish(copies)

    d_product = matmul(dy_ref[...], buffer[...])
    z_one, z_two = one_ref[...].astype(F32), two_ref[...].astype(F32)
    d_one = d_product * z_two
    d_one_ref[...] = d_one.astype(LOW)
    d_two_ref[...] = (d_product * z_one).astype(LOW)
    sum_ref[...] = jnp.sum(d_one * z_one, axis=-1, keepdims=True)


def gated_unit_back(spots, dy, z_one, z_two, chunks):
    count, width, units = dy.shape[0], dy.shape[1], z_one.shape[1]
    shape = jax.ShapeDtypeStruct
    outs = [shape((count, units), LOW)] * 2 + [shape((count, 1), F32)]
    return pl.pallas_call(
        unit_back_kernel,
        out_shape=outs,
        grid_spec=pltpu.PrefetchScalarGridSpec(
            num_scalar_prefetch=1,
            grid=(count // TILE,),
            in_specs=[tile_rows(width), tile_rows(units), tile_rows(units)] + [ANYWHERE] * len(chunks),
            out_specs=[tile_rows(o.shape[1]) for o in outs],
            scratch_shapes=weight_buffer(chunks),
        ),
        compiler_params=limit(40),
        cost_estimate=estimate(2 * count * width * units, dy, z_one, z_two, *chunks, *outs),
        name="gated_unit_back",
    )(spots, dy, z_one, z_two, *chunks)


def fold_kernel(members, keeps, spots, *refs):
    values, refs = refs[:members], refs[members:]
    arrived, refs = (refs[0], refs[1:]) if keeps else (None, refs)
    outs = 2 if keeps else 1
    chunks, refs = refs[: -outs - 2 * members], refs[-outs - 2 * members :]
    outs, buffers, sems = refs[:outs], refs[outs : outs + members], refs[outs + members :]
    each_count = len(chunks) // members
    half = spots[0] if keeps else 1 - spots[0]
    begins = pl.program_id(0) == 0
    copies = [
        chunk_copies(chunks[m * each_count : (m + 1) * each_count], buffers[m], sems[m], spots[2], half)
        for m in range(members)
    ]

    @pl.when(begins)
    def _():
        for m in range(members):
            start(copies[m])

    whole = None
    for m in range(members):
        pl.when(begins)(functools.partial(finish, copies[m]))
        term = times_transposed(values[m][...], buffers[m][...])
        whole = term if whole is None else whole + term
    if not keeps:
        outs[0][...] = whole.astype(LOW)
    else:
        whole = whole + arrived[...].astype(F32)
        size = whole.shape[1] // 2
        upper = spots[3] == 1
        outs[0][...] = jnp.where(upper, whole[:, :size], whole[:, size:]).astype(LOW)
        outs[1][...] = jnp.where(upper, whole[:, size:], whole[:, :size])


def fold_half(spots, values, weights, arrived=None):
    count = values[0].shape[0]
    half = len(weights[0]) * weights[0][0].shape[0] // 2
    shape = jax.ShapeDtypeStruct
    if arrived is None:
        outs, extra = [shape((count, half), LOW)], []
    else:
        outs, extra = [shape((count, half // 2), LOW), shape((count, half // 2), F32)], [arrived]
    buffers, sems = zip(*[weight_buffer(w, 2) for w in weights])
    chunks = [x for w in weights for x in w]
    flops = sum(2 * count * half * v.shape[1] for v in values)
    found = pl.pallas_call(
        functools.partial(fold_kernel, len(values), arrived is not None),
        out_shape=outs,
        grid_spec=pltpu.PrefetchScalarGridSpec(
            num_scalar_prefetch=1,
            grid=(count // TILE,),
            in_specs=[tile_rows(v.shape[1]) for v in values]
            + [tile_rows(half)] * len(extra)
            + [ANYWHERE] * len(chunks),
            out_specs=[tile_rows(o.shape[1]) for o in outs],
            scratch_shapes=[*buffers, *sems],
        ),
        compiler_params=limit(40),
        cost_estimate=estimate(flops, *values, *extra, *chunks[: len(chunks) // 2], *outs),
        name="fold_half",
    )(spots, *values, *extra, *chunks)
    return found[0] if arrived is None else found


def gradient_kernel(spots, left_ref, right_ref, *refs):
    found = cross_tokens(left_ref[...], right_ref[...])
    for arrived_ref in refs[:-1]:
        found = found + arrived_ref[...].astype(F32)
    refs[-1][...] = found.astype(LOW)


def gradient_rows(spots, spread, k, left, right, arrived=()):
    count, columns = right.shape
    rows = left.shape[1] // (1 if k is None else spread)
    tiles = rows // TILE

    def block(i, s):
        return (0, i if k is None else lax.rem(s[2] + k, spread) * tiles + i)

    out = jax.ShapeDtypeStruct((rows, columns), LOW)
    return pl.pallas_call(
        gradient_kernel,
        out_shape=out,
        grid_spec=pltpu.PrefetchScalarGridSpec(
            num_scalar_prefetch=1,
            grid=(tiles,),
            in_specs=[
                pl.BlockSpec((count, TILE), block),
                pl.BlockSpec((count, columns), lambda i, s: (0, 0), pipeline_mode=pl.Buffered(1)),
            ]
            + [tile_rows(columns)] * len(arrived),
            out_specs=tile_rows(columns),
        ),
        compiler_params=limit(40),
        cost_estimate=estimate(2 * count * rows * columns, right, out, out, *arrived),
        name="gradient_rows",
    )(spots, left, right, *arrived)


def place_kernel(cuts, spots, *refs):
    quarter = pl.program_id(0)
    cross = lax.rem(lax.div(quarter, 2) + spots[0], 2) * 2 + lax.rem(lax.rem(quarter, 2) + spots[3], 2)
    for n in range(4):

        @pl.when(cross == n)
        def _():
            for (first, size), out_ref in zip(cuts, refs[4:]):
                out_ref[...] = refs[n][:, first : first + size].astype(F32)


def place_quarters(spots, pairs, *cuts):
    rows, columns = pairs[0].shape[0], pairs[0].shape[1] // 2
    outs = [jax.ShapeDtypeStruct((rows, GROUP * size), F32) for _, size in cuts]

    def block(index):
        return pl.BlockSpec((rows, columns), lambda q, s: (0, index), pipeline_mode=pl.Buffered(1))

    return pl.pallas_call(
        functools.partial(place_kernel, cuts),
        out_shape=outs,
        grid_spec=pltpu.PrefetchScalarGridSpec(
            num_scalar_prefetch=1,
            grid=(GROUP,),
            in_specs=[block(0), block(1), block(0), block(1)],
            out_specs=[pl.BlockSpec((rows, size), lambda q, s: (0, q)) for _, size in cuts],
        ),
        compiler_params=limit(40),
        cost_estimate=estimate(0, *pairs, *outs),
        name="place_quarters",
    )(spots, pairs[0], pairs[0], pairs[1], pairs[1])


def tie(*values):
    return lax.optimization_barrier(values)


def body(reps, shards, tokens, cotangent, lengths, decay_rates, *weights):
    spread = reps // GROUP
    place = lax.axis_index("shard")
    a, b, c = lax.axis_index("a"), lax.axis_index("b"), lax.axis_index("c")
    quarter = 2 * c + b
    micro, run, width = tokens.shape
    half, own = width // 2, width // GROUP
    streams = micro * GROUP // shards
    per_block = STREAM // run // GROUP * streams
    rows = width // shards
    part = rows // spread
    columns = functools.partial(lax.dynamic_slice_in_dim, axis=1)
    spots = jnp.stack([c, quarter, a, b]).astype(jnp.int32)
    blocks = [z * spread + k for k in range(spread) for z in range(shards)]

    def move(x, target):
        pairs = [(r * shards + s, target(r) * shards + s) for r in range(reps) for s in range(shards)]
        return lax.ppermute(x, AXES, pairs)

    def swap_c(x):
        return move(x, lambda r: r ^ 1)

    def swap_b(x):
        return move(x, lambda r: r ^ 2)

    def joined(*parts):
        return jnp.concatenate(parts, axis=1)

    def shift_a(x, k):
        return move(x, lambda r: (r + GROUP * k) % reps)

    def ordered(index, mine, other, axis):
        return jnp.where(
            index == 0,
            jnp.concatenate([mine, other], axis),
            jnp.concatenate([other, mine], axis),
        )


    def batch_of(s):
        return s // (shards // micro)

    def origin(r, s, p):
        run_id = (r % GROUP) * per_block + p
        stream, piece = run_id // shards, run_id % shards
        member = s % GROUP if streams == 1 else 2 * stream + s % 2
        return (r // GROUP) * GROUP + member, piece

    def routes(p):
        found = []
        for r in range(reps):
            for s in range(shards):
                from_r, from_s = origin(r, s, p ^ batch_of(s))
                found.append((from_r * shards + from_s, r * shards + s))
        return found

    def natural(x):
        return jnp.concatenate(
            [
                x[:, (k * shards + z) * part : (k * shards + z + 1) * part]
                for z in range(shards)
                for k in range(spread)
            ],
            axis=1,
        )

    def bring(x):
        arrived = [
            lax.ppermute(lax.dynamic_index_in_dim(x, (place + p) % 2, 0, False), AXES, routes(p))
            for p in range(2)
        ]
        return ordered(batch_of(place), *arrived, 0)

    def send_back(x):
        slots = natural(x).reshape(2, run, width)
        return [
            lax.ppermute(
                lax.dynamic_index_in_dim(slots, (batch_of(place) + p) % 2, 0, False),
                AXES,
                [(to, origin) for origin, to in routes(p)],
            )
            for p in range(2)
        ]

    def as_batches(arrived):
        return ordered(place % 2, arrived[0][None], arrived[1][None], 0)


    def gather_b(x):
        return ordered(b, x, swap_b(x), 1)

    def gather_c(x):
        return ordered(c, x, swap_c(x), 1)

    def gather_rows_b(x):
        return ordered(b, x, swap_b(x), 0)

    def total(x):
        x = x + swap_c(x)
        return x + swap_b(x)

    def fold_c(product):
        sent = swap_c(product(1 - c).astype(LOW))
        return product(c) + sent.astype(F32)

    def fold_b(x):
        sent = swap_b(columns(x, (1 - b) * own, own).astype(LOW))
        return columns(x, b * own, own) + sent.astype(F32)


    pick = functools.partial(lax.dynamic_index_in_dim, keepdims=False)

    def away_b(x):
        cut = x.reshape(2, 2, -1, own)
        return pick(cut, b, 0), swap_b(pick(cut, 1 - b, 0))

    def away_c(mine, arrived):
        both = ordered(b, mine, arrived, 2)
        return pick(both, c, 0), swap_c(pick(both, 1 - c, 0))

    def to_runs(x):
        return ordered(c, *away_c(*away_b(x)), 1)


    def own_features(w):
        count = shards * spread // GROUP
        cut = []
        for i in range(count):
            block = quarter * count + i
            cut.append(columns(w, (block % shards) * rows + (block // shards) * part, part))
        return jnp.concatenate(cut, axis=1)

    def own_units(w):
        return columns(w, quarter * (w.shape[1] // GROUP), w.shape[1] // GROUP)

    def over_shards(*members):
        cut = jnp.concatenate(members, axis=1) if len(members) > 1 else members[0]
        piece = lax.dynamic_slice_in_dim(cut, a * part, part, 0)
        return lax.all_gather(piece, "shard", axis=0, tiled=True)

    def over_owners(w):
        piece = lax.dynamic_slice_in_dim(w, a * part, part, 0)
        return lax.all_gather(piece, OWNERS, axis=0, tiled=True)

    def over_spread(x):
        return [shift_a(x, k) for k in range(1, spread)]

    def by_spread(relative):
        if spread == 2:
            return ordered(a, relative[0], relative[1], 0)
        stacked = jnp.stack(relative, 0)
        pick = functools.partial(lax.dynamic_index_in_dim, axis=0, keepdims=False)
        return jnp.concatenate([pick(stacked, (a - j) % spread) for j in range(spread)], axis=0)

    def in_row_order(x):
        cut = x.reshape(spread, shards, part, -1)
        return jnp.transpose(cut, (1, 0, 2, 3)).reshape(width, -1)

    def row_half(w, h):
        return lax.dynamic_slice_in_dim(w, h * half, half, 0)


    def away(left, right):
        return [gradient_rows(spots, spread, k, left, right) for k in range(1, spread)]

    def pieces(terms, *eighths):
        marks = [0, *eighths, 8]
        return [
            [x[x.shape[0] * i // 8 : x.shape[0] * j // 8] for x in terms]
            for i, j in zip(marks[:-1], marks[1:])
        ]

    def stacked(*arrived):
        return [jnp.concatenate(cut, axis=0) for cut in zip(*arrived)]

    def sent_a(terms):
        return [shift_a(x, k + 1) for k, x in enumerate(terms)]

    def scattered(x):
        return lax.psum_scatter(x, "shard", scatter_dimension=0, tiled=True)

    def kept(left, right, *arrived):
        return gradient_rows(spots, spread, 0, left, right, stacked(*arrived))

    def spread_a(x):
        return by_spread([x] + over_spread(x))

    def spread_b(x):
        return jnp.concatenate([x, swap_b(x)], axis=1)

    def spread_c(pair):
        return pair, swap_c(pair)

    def features_in_order(pairs, first, size):
        full = pairs[0].shape[1] // 2
        cut = [x[:, i * full + first : i * full + first + size] for x in pairs for i in range(2)]
        pair = [ordered(b, cut[n], cut[n + 1], 1) for n in (0, 2)]
        return natural(ordered(c, pair[0], pair[1], 1)).astype(F32)


    w_query, w_key, w_value, w_gate, w_out, w_one, w_two, w_down = weights
    g_qk = over_shards(own_units(w_query), own_units(w_key))
    g_vg = over_shards(own_units(w_value), own_units(w_gate))
    g_o = over_shards(own_features(w_out))
    g_1 = over_shards(own_units(w_one))
    g_2 = over_shards(own_units(w_two))
    w_d = [over_owners(own_units(w_down))]

    heads = HEADS // GROUP
    rates = lax.dynamic_slice_in_dim(decay_rates, quarter * heads, heads, 0)
    cuts = gather_rows_b(lengths.reshape(1, -1))
    cuts = ordered(c, cuts, swap_c(cuts), 0).reshape(GROUP, micro, -1)
    if streams == 1:
        batch = place // GROUP
        member = place % GROUP
        chosen = lax.dynamic_slice_in_dim(cuts, 2 * (member % 2) + member // 2, 1, 0)
    else:
        batch = place // 2
        chosen = lax.dynamic_index_in_dim(cuts.reshape(2, 2, micro, -1), place % 2, 0, False)
    chosen = lax.dynamic_index_in_dim(chosen, batch, 1, False)
    seq_ends = [chosen[:, 0]]
    for i in range(1, chosen.shape[1]):
        seq_ends.append(seq_ends[-1] + chosen[:, i])
    ends = jnp.stack(seq_ends, axis=1)

    x_run = bring(tokens)
    x_run, g_qk = tie(x_run, g_qk)

    x_pair = gather_rows_b(x_run)
    s_qk = over_spread(g_qk)
    x_pair, s_qk, g_vg = tie(x_pair, s_qk, g_vg)

    s_vg = over_spread(g_vg)
    w_qk = [g_qk, *s_qk]
    hidden_one, z_qk, x_scale, x_own = enter(spots, blocks, x_pair, swap_c(x_pair), w_qk)
    z_qk, hidden_one, s_vg, g_o = tie(z_qk, hidden_one, s_vg, g_o)

    s_o = over_spread(g_o)
    w_vg = [g_vg, *s_vg]
    z_vg = project(spots, hidden_one, w_vg)
    attended = attend(rates, ends, z_qk, z_vg)
    gate = z_vg[:, own:]
    o_scale = lax.rsqrt(total(jnp.sum(attended * attended, axis=-1)) / width + EPSILON)[:, None]
    lifted = (attended * gate).astype(LOW)
    lifted, s_o, g_1, cotangent = tie(lifted, s_o, g_1, cotangent)

    s_1 = over_spread(g_1)
    lifted = gather_b(lifted)
    lifted, s_1, g_2, o_scale, cotangent = tie(lifted, s_1, g_2, o_scale, cotangent)

    s_2 = over_spread(g_2)
    dy_run = bring(cotangent)
    lifted = gather_c(lifted)
    w_o = in_row_order(by_spread([g_o, *s_o]))
    branch = o_scale * matmul(lifted, w_o)
    middle = x_own.astype(F32) + branch
    low_middle = gather_b(middle.astype(LOW))
    low_middle, s_2, dy_run = tie(low_middle, s_2, dy_run)

    other_middle = swap_c(low_middle)
    dy_other = swap_b(dy_run)
    w_1, w_2 = [g_1, *s_1], [g_2, *s_2]
    hidden_two, z_one, z_two, product, m_scale = gated_unit(spots, low_middle, other_middle, w_1, w_2)
    z_one, z_two, product, dy_other = tie(z_one, z_two, product, dy_other)

    dy_pair = ordered(b, dy_run, dy_other, 0)
    dy_all, dy_own = enter(spots, blocks, dy_pair, swap_c(dy_pair))
    t_down = away(dy_all, product)
    z_one, z_two, product, t_down, w_d[0] = tie(z_one, z_two, product, t_down, w_d[0])


    down_a, down_b = pieces(t_down, 6)
    down_a = sent_a(down_a)
    d_one, d_two, lean_m = gated_unit_back(spots, dy_all, z_one, z_two, w_d)
    sent = fold_half(spots, [d_one, d_two], [w_1, w_2])
    sent, d_one, d_two, lean_m, down_a = tie(sent, d_one, d_two, lean_m, down_a)

    arrived = swap_c(sent)
    down_b = sent_a(down_b)
    t_one = away(hidden_two, d_one)
    result = fold_half(spots, [product], [w_d])
    lean_m = total(lean_m[:, 0])
    arrived, result, t_one = tie(arrived, result, t_one)

    r_result = swap_c(result)
    one_a, one_b = pieces(t_one, 2)
    one_a = sent_a(one_a)
    sent, mine = fold_half(spots, [d_one, d_two], [w_1, w_2], arrived)
    sent, d_two, one_a, one_b, product, lean_m, down_b, r_result = tie(
        sent, d_two, one_a, one_b, product, lean_m, down_b, r_result
    )

    crossed = swap_b(sent)
    one_b = sent_a(one_b)
    f_down = kept(dy_all, product, down_a, down_b)
    t_two = away(hidden_two, d_two)
    result, result_mine = fold_half(spots, [product], [w_d], r_result)
    crossed, result, f_down, t_two, one_b = tie(crossed, result, f_down, t_two, one_b)

    f_down = scattered(f_down)
    two_a, two_b = pieces(t_two, 5)
    two_a = sent_a(two_a)
    result_b = swap_b(result)
    d_hidden = mine + crossed.astype(F32)
    m_normed = middle * m_scale
    lean = lean_m[:, None] * (2.0 / width)
    d_middle = dy_own.astype(F32) + m_scale * (d_hidden - m_normed * lean)
    d_branch = d_middle.astype(LOW)
    lean_o = jnp.sum(d_middle * branch, axis=-1)
    sent = times_transposed(d_branch, row_half(w_o, 1 - c)).astype(LOW)
    sent, d_middle, lean_o = tie(sent, d_middle, lean_o)

    arrived = swap_c(sent)
    lean_o = total(lean_o)
    p_out = cross_tokens(lifted, (o_scale * d_middle).astype(LOW)).astype(LOW)
    p_out = jnp.transpose(p_out.reshape(shards, spread, part, -1), (1, 0, 2, 3))
    p_out = p_out.reshape(spread, width // spread, -1)
    t_out = [lax.dynamic_index_in_dim(p_out, (a + k) % spread, 0, False) for k in range(spread)]
    d_gated = times_transposed(d_branch, row_half(w_o, c)) + arrived.astype(F32)
    sent = columns(d_gated, (1 - b) * own, own).astype(LOW)
    mine = columns(d_gated, b * own, own)
    sent, mine, d_one, result_b, t_out, lean_o, two_a = tie(
        sent, mine, d_one, result_b, t_out, lean_o, two_a
    )

    crossed = swap_b(sent)
    two_b = sent_a(two_b)
    r_out = sent_a(t_out[1:])
    f_one = kept(hidden_two, d_one, one_a, one_b)
    output = (middle + (result_mine + result_b.astype(F32))).astype(LOW)
    crossed, output, f_one, f_down, two_b, r_out = tie(crossed, output, f_one, f_down, two_b, r_out)

    f_one = scattered(f_one)
    f_out = scattered(sum([x.astype(F32) for x in r_out], t_out[0].astype(F32)).astype(LOW))
    y_down = over_spread(f_down)
    f_two = kept(hidden_two, d_two, two_a, two_b)
    output, out_b = away_b(output)
    o_normed = attended * o_scale
    d_gated = mine + crossed.astype(F32)
    d_gate = (d_gated * o_normed).astype(LOW)
    lean = lean_o[:, None] / width
    d_attended = (o_scale * (d_gated * gate - o_normed * lean)).astype(LOW)
    d_query, d_key, d_value = attend_back(rates, ends, z_qk, z_vg, d_attended)
    d_qk = joined(d_query, d_key)
    d_vg = joined(d_value, d_gate)
    t_qk = away(hidden_one, d_qk)
    d_qk, d_vg, t_qk, f_two, y_down, out_b = tie(d_qk, d_vg, t_qk, f_two, y_down, out_b)

    f_two = scattered(f_two)
    y_down = by_spread([f_down, *y_down])
    qk_a, qk_b = pieces(t_qk, 4)
    qk_a = sent_a(qk_a)
    output, out_c = away_c(output, out_b)
    x_down = swap_b(y_down)
    y_one = over_spread(f_one)
    t_vg = away(hidden_one, d_vg)
    sent = fold_half(spots, [d_qk, d_vg], [w_qk, w_vg])
    sent, t_vg, d_qk, d_vg, out_c, qk_a, x_down, y_one, f_out = tie(
        sent, t_vg, d_qk, d_vg, out_c, qk_a, x_down, y_one, f_out
    )

    arrived = swap_c(sent)
    output = send_back(ordered(c, output, out_c, 1))
    qk_b = sent_a(qk_b)
    x_down = joined(y_down, x_down)
    y_one = by_spread([f_one, *y_one])
    x_one = swap_b(y_one)
    lean_x = jnp.sum(z_qk * d_qk.astype(F32), axis=-1) + jnp.sum(z_vg * d_vg.astype(F32), axis=-1)
    sent, mine = fold_half(spots, [d_qk, d_vg], [w_qk, w_vg], arrived)
    sent, mine, qk_b, t_vg, lean_x, x_one, output = tie(sent, mine, qk_b, t_vg, lean_x, x_one, output)

    crossed = swap_b(sent)
    lean_x = total(lean_x)
    r_vg = sent_a(t_vg)
    f_qk = scattered(kept(hidden_one, d_qk, qk_a, qk_b))
    four_down = spread_c(x_down)
    crossed, d_vg, r_vg, lean_x, f_two, four_down = tie(crossed, d_vg, r_vg, lean_x, f_two, four_down)

    f_vg = kept(hidden_one, d_vg, r_vg)
    x_one = joined(y_one, x_one)
    f_vg, crossed, f_two, f_out, x_one = tie(f_vg, crossed, f_two, f_out, x_one)

    f_vg = scattered(f_vg)
    d_hidden = mine + crossed.astype(F32)
    x_normed = x_own.astype(F32) * x_scale
    lean = lean_x[:, None] / width
    input_grad = to_runs((d_middle + x_scale * (d_hidden - x_normed * lean)).astype(LOW))
    f_oqk = joined(f_out, f_qk)
    x_oqk = swap_b(f_oqk)
    y_two = over_spread(f_two)
    four_one = spread_c(x_one)
    units = f_one.shape[1]
    [g_down] = place_quarters(spots, four_down, (0, units))
    [g_one] = place_quarters(spots, four_one, (0, units))
    input_grad, x_oqk, y_two, f_vg, g_down, g_one = tie(input_grad, x_oqk, y_two, f_vg, g_down, g_one)

    x_vg = spread_b(f_vg)
    y_two = by_spread([f_two, *y_two])
    y_oqk = spread_a(joined(f_oqk, x_oqk))
    x_vg, y_oqk = tie(x_vg, y_oqk)

    four_vg = spread_c(spread_a(x_vg))
    input_grad = send_back(input_grad)
    four_two = spread_c(spread_b(y_two))
    four_oqk = spread_c(y_oqk)
    g_query, g_key = place_quarters(spots, four_oqk, (own, own), (2 * own, own))
    g_value, g_gate = place_quarters(spots, four_vg, (0, own), (own, own))
    [g_two] = place_quarters(spots, four_two, (0, units))
    g_out = features_in_order(four_oqk, 0, own)
    output, input_grad = as_batches(output), as_batches(input_grad)
    return output, input_grad, g_query, g_key, g_value, g_gate, g_out, g_one, g_two, g_down


def solution(mesh):
    reps, shards = mesh.shape["rep"], mesh.shape["shard"]
    devices = mesh.devices.reshape(reps // GROUP, 2, 2, shards)
    rep = ("a", "b", "c")
    by_tokens = P(None, (*rep, "shard"), None)
    by_rows = P("shard", None)
    return jax.shard_map(
        functools.partial(body, reps, shards),
        mesh=Mesh(devices, AXES),
        in_specs=(by_tokens, by_tokens, P(None, rep, None), P(), *[by_rows] * 8),
        out_specs=(by_tokens, by_tokens, *[by_rows] * 8),
        check_vma=False,
    )
```

```python
import functools

import jax
import jax.numpy as jnp
from jax import lax
from jax.experimental import pallas as pl
from jax.experimental.pallas import tpu as pltpu
from jax.sharding import Mesh, PartitionSpec as P

HEADS = 16
HEAD_DIM = 128
STREAM = 1024
GROUP = 4
BLOCK = 256
TILE = 256
EPSILON = 1e-06
AXES = ("a", "b", "c", "shard")
OWNERS = ("a", "shard")
LOW = jnp.bfloat16
F32 = jnp.float32


def matmul(former, latter):
    return jnp.dot(former, latter, preferred_element_type=F32)


def times_transposed(former, latter):
    return lax.dot_general(former, latter, (((1,), (1,)), ((), ())), preferred_element_type=F32)


def cross_tokens(former, latter):
    return lax.dot_general(former, latter, (((0,), (0,)), ((), ())), preferred_element_type=F32)


def masked_decay(rate, ends, first, columns):
    row = first + lax.broadcasted_iota(jnp.int32, (BLOCK, 1), 0)
    column = lax.broadcasted_iota(jnp.int32, (1, columns), 1)
    begin = jnp.zeros((BLOCK, 1), jnp.int32)
    for end in ends:
        begin = jnp.where(row >= end, end, begin)
    falling = jnp.exp(-rate * (row - first).astype(F32))
    rising = jnp.exp(rate * (column - first).astype(F32))
    allowed = (column <= row) & (column >= begin)
    return jnp.where(allowed, falling * rising, 0.0)


def attend_kernel(rates, ends, zq_ref, zk_ref, zv_ref, out_ref):
    stream, head = pl.program_id(0), pl.program_id(1)
    rate = rates[head]
    bounds = [ends[stream, i] for i in range(ends.shape[1])]
    zq, zk = zq_ref[...], zk_ref[...]
    q = (zq * jax.nn.sigmoid(zq)).astype(LOW)
    k = (zk * jax.nn.sigmoid(zk)).astype(LOW)
    v = zv_ref[...].astype(LOW)
    for first in range(0, STREAM, BLOCK):
        columns = first + BLOCK
        mask = masked_decay(rate, bounds, first, columns)
        scores = times_transposed(q[first:columns], k[:columns])
        weights = (scores * mask).astype(LOW)
        out_ref[first:columns, :] = matmul(weights, v[:columns])


def attend_back_kernel(
    rates, ends, zq_ref, zk_ref, zv_ref, do_ref, dzq_ref, dzk_ref, dzv_ref, dk_ref, dv_ref
):
    stream, head = pl.program_id(0), pl.program_id(1)
    rate = rates[head]
    bounds = [ends[stream, i] for i in range(ends.shape[1])]
    zq, zk = zq_ref[...], zk_ref[...]
    sig_q, sig_k = jax.nn.sigmoid(zq), jax.nn.sigmoid(zk)
    q = (zq * sig_q).astype(LOW)
    k = (zk * sig_k).astype(LOW)
    slope_q = sig_q * (1.0 + zq * (1.0 - sig_q))
    v = zv_ref[...].astype(LOW)
    d_o = do_ref[...]
    dk_ref[...] = jnp.zeros_like(dk_ref)
    dv_ref[...] = jnp.zeros_like(dv_ref)
    for first in range(0, STREAM, BLOCK):
        columns = first + BLOCK
        rows = slice(first, columns)
        mask = masked_decay(rate, bounds, first, columns)
        weights = (times_transposed(q[rows], k[:columns]) * mask).astype(LOW)
        d_scores = (times_transposed(d_o[rows], v[:columns]) * mask).astype(LOW)
        dzq_ref[rows, :] = (matmul(d_scores, k[:columns]) * slope_q[rows]).astype(LOW)
        dk_ref[:columns, :] += cross_tokens(d_scores, q[rows])
        dv_ref[:columns, :] += cross_tokens(weights, d_o[rows])
    dzk_ref[...] = (dk_ref[...] * (sig_k * (1.0 + zk * (1.0 - sig_k)))).astype(LOW)
    dzv_ref[...] = dv_ref[...].astype(LOW)


def head_block(offset=0):
    return pl.BlockSpec((STREAM, HEAD_DIM), lambda g, h, *_: (g, h + offset))


def attend(rates, ends, z_qk, z_vg):
    heads, streams = rates.shape[0], ends.shape[0]
    work = streams * heads * STREAM * STREAM
    return pl.pallas_call(
        attend_kernel,
        out_shape=jax.ShapeDtypeStruct((streams * STREAM, heads * HEAD_DIM), F32),
        grid_spec=pltpu.PrefetchScalarGridSpec(
            num_scalar_prefetch=2,
            grid=(streams, heads),
            in_specs=[head_block(), head_block(heads), head_block()],
            out_specs=head_block(),
        ),
        compiler_params=pltpu.CompilerParams(vmem_limit_bytes=40 << 20),
        cost_estimate=pl.CostEstimate(
            flops=4 * work * HEAD_DIM, transcendentals=work // 64,
            bytes_accessed=streams * heads * STREAM * HEAD_DIM * 16,
        ),
        name="attend",
    )(rates, ends, z_qk, z_qk, z_vg)


def attend_back(rates, ends, z_qk, z_vg, d_o):
    heads, streams = rates.shape[0], ends.shape[0]
    work = streams * heads * STREAM * STREAM
    return pl.pallas_call(
        attend_back_kernel,
        out_shape=[jax.ShapeDtypeStruct((streams * STREAM, heads * HEAD_DIM), LOW)] * 3,
        grid_spec=pltpu.PrefetchScalarGridSpec(
            num_scalar_prefetch=2,
            grid=(streams, heads),
            in_specs=[head_block(), head_block(heads), head_block(), head_block()],
            out_specs=[head_block()] * 3,
            scratch_shapes=[pltpu.VMEM((STREAM, HEAD_DIM), F32)] * 2,
        ),
        compiler_params=pltpu.CompilerParams(vmem_limit_bytes=40 << 20),
        cost_estimate=pl.CostEstimate(
            flops=10 * work * HEAD_DIM, transcendentals=work // 64,
            bytes_accessed=streams * heads * STREAM * HEAD_DIM * 20,
        ),
        name="attend_back",
    )(rates, ends, z_qk, z_qk, z_vg, d_o)


def chunk_copies(chunks, buffer, sems, turn, half=None):
    count, size = len(chunks), chunks[0].shape[0]
    if count == 1:
        rows = buffer.shape[0]
        first = 0 if half is None else pl.multiple_of(half * rows, rows)
        return [(None, pltpu.make_async_copy(chunks[0].at[pl.ds(first, rows)], buffer, sems.at[0]))]
    copies = []
    for k, chunk in enumerate(chunks):
        index = lax.rem(turn - k + count, count)
        wanted = None
        if half is not None:
            wanted = lax.div(index, count // 2) == half
            index = lax.rem(index, count // 2)
        target = buffer.at[pl.ds(pl.multiple_of(index * size, size), size)]
        copies.append((wanted, pltpu.make_async_copy(chunk, target, sems.at[k])))
    return copies


def each(copies, act):
    for wanted, copy in copies:
        if wanted is None:
            act(copy)
        else:
            pl.when(wanted)(functools.partial(act, copy))


def start(copies):
    each(copies, lambda copy: copy.start())


def finish(copies):
    each(copies, lambda copy: copy.wait())


def estimate(flops, *arrays):
    moved = sum(x.size * x.dtype.itemsize for x in arrays)
    return pl.CostEstimate(flops=flops, transcendentals=0, bytes_accessed=moved)


def limit(mebibytes):
    return pltpu.CompilerParams(vmem_limit_bytes=mebibytes << 20)


ANYWHERE = pl.BlockSpec(memory_space=pl.ANY)


def weight_buffer(chunks, share=1):
    size = len(chunks) * chunks[0].shape[0] // share
    return [pltpu.VMEM((size, chunks[0].shape[1]), LOW), pltpu.SemaphoreType.DMA((len(chunks),))]


def tile_rows(width, column=0):
    return pl.BlockSpec((TILE, width), lambda i, *_: (i, column))


def joined_rows(width, tiles):
    spec = pl.BlockSpec((TILE, width), lambda i, s: (i // (2 * tiles) * tiles + i % tiles, 0))
    return [spec, spec]


def enter_kernel(tiles, blocks, project, spots, own_ref, other_ref, *refs):
    i = pl.program_id(0)
    mine = lax.rem(lax.div(i, tiles), 2) == spots[0]
    rows = jnp.where(mine, own_ref[...], other_ref[...])
    part = rows.shape[1] // len(blocks)
    permuted = jnp.concatenate([rows[:, n * part : (n + 1) * part] for n in blocks], axis=1)
    if not project:
        all_ref, quarter_ref = refs
        all_ref[...] = permuted
        held = all_ref
    else:
        chunks, (h_ref, z_ref, scale_ref, quarter_ref, held, buffer, sems) = refs[:-7], refs[-7:]
        held[...] = permuted
        copies = chunk_copies(chunks, buffer, sems, spots[2])

        @pl.when(i == 0)
        def _():
            start(copies)

        x = rows.astype(F32)
        scale = lax.rsqrt(jnp.mean(x * x, axis=-1, keepdims=True) + EPSILON)
        scale_ref[...] = scale
        hidden = (permuted.astype(F32) * scale).astype(LOW)
        h_ref[...] = hidden

        @pl.when(i == 0)
        def _():
            finish(copies)

        z_ref[...] = matmul(hidden, buffer[...])
    size = quarter_ref.shape[1]
    quarter_ref[...] = held[:, pl.ds(pl.multiple_of(spots[1] * size, size), size)]


def enter(spots, blocks, own, other, chunks=()):
    width = own.shape[1]
    count, tiles = 2 * own.shape[0], own.shape[0] // TILE // 2
    shape = jax.ShapeDtypeStruct
    quarter = shape((count, width // GROUP), LOW)
    if chunks:
        columns = chunks[0].shape[1]
        outs = [shape((count, width), LOW), shape((count, columns), F32), shape((count, 1), F32), quarter]
        scratch = [pltpu.VMEM((TILE, width), LOW), *weight_buffer(chunks)]
    else:
        columns, scratch = 0, []
        outs = [shape((count, width), LOW), quarter]
    return pl.pallas_call(
        functools.partial(enter_kernel, tiles, blocks, bool(chunks)),
        out_shape=outs,
        grid_spec=pltpu.PrefetchScalarGridSpec(
            num_scalar_prefetch=1,
            grid=(count // TILE,),
            in_specs=joined_rows(width, tiles) + [ANYWHERE] * len(chunks),
            out_specs=[tile_rows(o.shape[1]) for o in outs],
            scratch_shapes=scratch,
        ),
        compiler_params=limit(40),
        cost_estimate=estimate(2 * count * width * columns, own, other, *chunks, *outs),
        name="enter",
    )(spots, own, other, *chunks)


def project_kernel(spots, h_ref, *refs):
    chunks, (z_ref, buffer, sems) = refs[:-3], refs[-3:]
    copies = chunk_copies(chunks, buffer, sems, spots[2])

    @pl.when(pl.program_id(0) == 0)
    def _():
        start(copies)
        finish(copies)

    z_ref[...] = matmul(h_ref[...], buffer[...])


def project(spots, hidden, chunks):
    count, width = hidden.shape
    out = jax.ShapeDtypeStruct((count, chunks[0].shape[1]), F32)
    return pl.pallas_call(
        project_kernel,
        out_shape=out,
        grid_spec=pltpu.PrefetchScalarGridSpec(
            num_scalar_prefetch=1,
            grid=(count // TILE,),
            in_specs=[tile_rows(width)] + [ANYWHERE] * len(chunks),
            out_specs=tile_rows(out.shape[1]),
            scratch_shapes=weight_buffer(chunks),
        ),
        compiler_params=limit(40),
        cost_estimate=estimate(2 * count * width * out.shape[1], hidden, *chunks, out),
        name="project",
    )(spots, hidden, *chunks)


def unit_kernel(spots, own_ref, other_ref, *refs):
    chunks, rest = refs[:-9], refs[-9:]
    h_ref, one_ref, two_ref, product_ref, scale_ref, first, second, sem_one, sem_two = rest
    split = len(chunks) // 2
    copies = [
        chunk_copies(chunks[:split], first, sem_one, spots[2]),
        chunk_copies(chunks[split:], second, sem_two, spots[2]),
    ]
    begins = pl.program_id(0) == 0

    @pl.when(begins)
    def _():
        start(copies[0])
        start(copies[1])

    mine, other = own_ref[...], other_ref[...]
    swapped = spots[0] == 1
    middle = jnp.concatenate(
        [jnp.where(swapped, other, mine), jnp.where(swapped, mine, other)], axis=1
    ).astype(F32)
    scale = lax.rsqrt(jnp.mean(middle * middle, axis=-1, keepdims=True) + EPSILON)
    scale_ref[...] = scale
    hidden = (middle * scale).astype(LOW)
    h_ref[...] = hidden

    @pl.when(begins)
    def _():
        finish(copies[0])

    z_one = matmul(hidden, first[...])

    @pl.when(begins)
    def _():
        finish(copies[1])

    z_two = matmul(hidden, second[...])
    one_ref[...] = z_one.astype(LOW)
    two_ref[...] = z_two.astype(LOW)
    product_ref[...] = (z_one * z_two).astype(LOW)


def gated_unit(spots, own, other, first, second):
    count, width, units = own.shape[0], 2 * own.shape[1], first[0].shape[1]
    shape = jax.ShapeDtypeStruct
    outs = [shape((count, width), LOW)] + [shape((count, units), LOW)] * 3 + [shape((count, 1), F32)]
    (buffer, sems) = weight_buffer(first)
    return pl.pallas_call(
        unit_kernel,
        out_shape=outs,
        grid_spec=pltpu.PrefetchScalarGridSpec(
            num_scalar_prefetch=1,
            grid=(count // TILE,),
            in_specs=[tile_rows(width // 2)] * 2 + [ANYWHERE] * (2 * len(first)),
            out_specs=[tile_rows(o.shape[1]) for o in outs],
            scratch_shapes=[buffer, buffer, sems, sems],
        ),
        compiler_params=limit(48),
        cost_estimate=estimate(4 * count * width * units, own, other, *first, *second, *outs),
        name="gated_unit",
    )(spots, own, other, *first, *second)


def unit_back_kernel(spots, dy_ref, one_ref, two_ref, *refs):
    chunks, (d_one_ref, d_two_ref, sum_ref, buffer, sems) = refs[:-5], refs[-5:]
    copies = chunk_copies(chunks, buffer, sems, spots[2])

    @pl.when(pl.program_id(0) == 0)
    def _():
        start(copies)
        finish(copies)

    d_product = matmul(dy_ref[...], buffer[...])
    z_one, z_two = one_ref[...].astype(F32), two_ref[...].astype(F32)
    d_one = d_product * z_two
    d_one_ref[...] = d_one.astype(LOW)
    d_two_ref[...] = (d_product * z_one).astype(LOW)
    sum_ref[...] = jnp.sum(d_one * z_one, axis=-1, keepdims=True)


def gated_unit_back(spots, dy, z_one, z_two, chunks):
    count, width, units = dy.shape[0], dy.shape[1], z_one.shape[1]
    shape = jax.ShapeDtypeStruct
    outs = [shape((count, units), LOW)] * 2 + [shape((count, 1), F32)]
    return pl.pallas_call(
        unit_back_kernel,
        out_shape=outs,
        grid_spec=pltpu.PrefetchScalarGridSpec(
            num_scalar_prefetch=1,
            grid=(count // TILE,),
            in_specs=[tile_rows(width), tile_rows(units), tile_rows(units)] + [ANYWHERE] * len(chunks),
            out_specs=[tile_rows(o.shape[1]) for o in outs],
            scratch_shapes=weight_buffer(chunks),
        ),
        compiler_params=limit(40),
        cost_estimate=estimate(2 * count * width * units, dy, z_one, z_two, *chunks, *outs),
        name="gated_unit_back",
    )(spots, dy, z_one, z_two, *chunks)


def fold_kernel(members, keeps, spots, *refs):
    values, refs = refs[:members], refs[members:]
    arrived, refs = (refs[0], refs[1:]) if keeps else (None, refs)
    outs = 2 if keeps else 1
    chunks, refs = refs[: -outs - 2 * members], refs[-outs - 2 * members :]
    outs, buffers, sems = refs[:outs], refs[outs : outs + members], refs[outs + members :]
    each_count = len(chunks) // members
    half = spots[0] if keeps else 1 - spots[0]
    begins = pl.program_id(0) == 0
    copies = [
        chunk_copies(chunks[m * each_count : (m + 1) * each_count], buffers[m], sems[m], spots[2], half)
        for m in range(members)
    ]

    @pl.when(begins)
    def _():
        for m in range(members):
            start(copies[m])

    whole = None
    for m in range(members):
        pl.when(begins)(functools.partial(finish, copies[m]))
        term = times_transposed(values[m][...], buffers[m][...])
        whole = term if whole is None else whole + term
    if not keeps:
        outs[0][...] = whole.astype(LOW)
    else:
        whole = whole + arrived[...].astype(F32)
        size = whole.shape[1] // 2
        upper = spots[3] == 1
        outs[0][...] = jnp.where(upper, whole[:, :size], whole[:, size:]).astype(LOW)
        outs[1][...] = jnp.where(upper, whole[:, size:], whole[:, :size])


def fold_half(spots, values, weights, arrived=None):
    count = values[0].shape[0]
    half = len(weights[0]) * weights[0][0].shape[0] // 2
    shape = jax.ShapeDtypeStruct
    if arrived is None:
        outs, extra = [shape((count, half), LOW)], []
    else:
        outs, extra = [shape((count, half // 2), LOW), shape((count, half // 2), F32)], [arrived]
    buffers, sems = zip(*[weight_buffer(w, 2) for w in weights])
    chunks = [x for w in weights for x in w]
    flops = sum(2 * count * half * v.shape[1] for v in values)
    found = pl.pallas_call(
        functools.partial(fold_kernel, len(values), arrived is not None),
        out_shape=outs,
        grid_spec=pltpu.PrefetchScalarGridSpec(
            num_scalar_prefetch=1,
            grid=(count // TILE,),
            in_specs=[tile_rows(v.shape[1]) for v in values]
            + [tile_rows(half)] * len(extra)
            + [ANYWHERE] * len(chunks),
            out_specs=[tile_rows(o.shape[1]) for o in outs],
            scratch_shapes=[*buffers, *sems],
        ),
        compiler_params=limit(40),
        cost_estimate=estimate(flops, *values, *extra, *chunks[: len(chunks) // 2], *outs),
        name="fold_half",
    )(spots, *values, *extra, *chunks)
    return found[0] if arrived is None else found


def gradient_kernel(spots, left_ref, right_ref, *refs):
    found = cross_tokens(left_ref[...], right_ref[...])
    for arrived_ref in refs[:-1]:
        found = found + arrived_ref[...].astype(F32)
    refs[-1][...] = found.astype(LOW)


def gradient_rows(spots, spread, k, left, right, arrived=()):
    count, columns = right.shape
    rows = left.shape[1] // (1 if k is None else spread)
    tiles = rows // TILE

    def block(i, s):
        return (0, i if k is None else lax.rem(s[2] + k, spread) * tiles + i)

    out = jax.ShapeDtypeStruct((rows, columns), LOW)
    return pl.pallas_call(
        gradient_kernel,
        out_shape=out,
        grid_spec=pltpu.PrefetchScalarGridSpec(
            num_scalar_prefetch=1,
            grid=(tiles,),
            in_specs=[
                pl.BlockSpec((count, TILE), block),
                pl.BlockSpec((count, columns), lambda i, s: (0, 0), pipeline_mode=pl.Buffered(1)),
            ]
            + [tile_rows(columns)] * len(arrived),
            out_specs=tile_rows(columns),
        ),
        compiler_params=limit(40),
        cost_estimate=estimate(2 * count * rows * columns, right, out, out, *arrived),
        name="gradient_rows",
    )(spots, left, right, *arrived)


def place_kernel(cuts, spots, *refs):
    quarter = pl.program_id(0)
    cross = lax.rem(lax.div(quarter, 2) + spots[0], 2) * 2 + lax.rem(lax.rem(quarter, 2) + spots[3], 2)
    for n in range(4):

        @pl.when(cross == n)
        def _():
            for (first, size), out_ref in zip(cuts, refs[4:]):
                out_ref[...] = refs[n][:, first : first + size].astype(F32)


def place_quarters(spots, pairs, *cuts):
    rows, columns = pairs[0].shape[0], pairs[0].shape[1] // 2
    outs = [jax.ShapeDtypeStruct((rows, GROUP * size), F32) for _, size in cuts]

    def block(index):
        return pl.BlockSpec((rows, columns), lambda q, s: (0, index), pipeline_mode=pl.Buffered(1))

    return pl.pallas_call(
        functools.partial(place_kernel, cuts),
        out_shape=outs,
        grid_spec=pltpu.PrefetchScalarGridSpec(
            num_scalar_prefetch=1,
            grid=(GROUP,),
            in_specs=[block(0), block(1), block(0), block(1)],
            out_specs=[pl.BlockSpec((rows, size), lambda q, s: (0, q)) for _, size in cuts],
        ),
        compiler_params=limit(40),
        cost_estimate=estimate(0, *pairs, *outs),
        name="place_quarters",
    )(spots, pairs[0], pairs[0], pairs[1], pairs[1])


def tie(*values):
    return lax.optimization_barrier(values)


def body(reps, shards, tokens, cotangent, lengths, decay_rates, *weights):
    spread = reps // GROUP
    place = lax.axis_index("shard")
    a, b, c = lax.axis_index("a"), lax.axis_index("b"), lax.axis_index("c")
    quarter = 2 * c + b
    micro, run, width = tokens.shape
    half, own = width // 2, width // GROUP
    streams = micro * GROUP // shards
    per_block = STREAM // run // GROUP * streams
    rows = width // shards
    part = rows // spread
    columns = functools.partial(lax.dynamic_slice_in_dim, axis=1)
    spots = jnp.stack([c, quarter, a, b]).astype(jnp.int32)
    blocks = [z * spread + k for k in range(spread) for z in range(shards)]

    def move(x, target):
        pairs = [(r * shards + s, target(r) * shards + s) for r in range(reps) for s in range(shards)]
        return lax.ppermute(x, AXES, pairs)

    def swap_c(x):
        return move(x, lambda r: r ^ 1)

    def swap_b(x):
        return move(x, lambda r: r ^ 2)

    def joined(*parts):
        return jnp.concatenate(parts, axis=1)

    def shift_a(x, k):
        return move(x, lambda r: (r + GROUP * k) % reps)

    def ordered(index, mine, other, axis):
        return jnp.where(
            index == 0,
            jnp.concatenate([mine, other], axis),
            jnp.concatenate([other, mine], axis),
        )


    def batch_of(s):
        return s // (shards // micro)

    def origin(r, s, p):
        run_id = (r % GROUP) * per_block + p
        stream, piece = run_id // shards, run_id % shards
        member = s % GROUP if streams == 1 else 2 * stream + s % 2
        return (r // GROUP) * GROUP + member, piece

    def routes(p):
        found = []
        for r in range(reps):
            for s in range(shards):
                from_r, from_s = origin(r, s, p ^ batch_of(s))
                found.append((from_r * shards + from_s, r * shards + s))
        return found

    def natural(x):
        return jnp.concatenate(
            [
                x[:, (k * shards + z) * part : (k * shards + z + 1) * part]
                for z in range(shards)
                for k in range(spread)
            ],
            axis=1,
        )

    def bring(x):
        arrived = [
            lax.ppermute(lax.dynamic_index_in_dim(x, (place + p) % 2, 0, False), AXES, routes(p))
            for p in range(2)
        ]
        return ordered(batch_of(place), *arrived, 0)

    def send_back(x):
        slots = natural(x).reshape(2, run, width)
        return [
            lax.ppermute(
                lax.dynamic_index_in_dim(slots, (batch_of(place) + p) % 2, 0, False),
                AXES,
                [(to, origin) for origin, to in routes(p)],
            )
            for p in range(2)
        ]

    def as_batches(arrived):
        return ordered(place % 2, arrived[0][None], arrived[1][None], 0)


    def gather_b(x):
        return ordered(b, x, swap_b(x), 1)

    def gather_c(x):
        return ordered(c, x, swap_c(x), 1)

    def gather_rows_b(x):
        return ordered(b, x, swap_b(x), 0)

    def total(x):
        x = x + swap_c(x)
        return x + swap_b(x)

    def fold_c(product):
        sent = swap_c(product(1 - c).astype(LOW))
        return product(c) + sent.astype(F32)

    def fold_b(x):
        sent = swap_b(columns(x, (1 - b) * own, own).astype(LOW))
        return columns(x, b * own, own) + sent.astype(F32)


    pick = functools.partial(lax.dynamic_index_in_dim, keepdims=False)

    def away_b(x):
        cut = x.reshape(2, 2, -1, own)
        return pick(cut, b, 0), swap_b(pick(cut, 1 - b, 0))

    def away_c(mine, arrived):
        both = ordered(b, mine, arrived, 2)
        return pick(both, c, 0), swap_c(pick(both, 1 - c, 0))

    def to_runs(x):
        return ordered(c, *away_c(*away_b(x)), 1)


    def own_features(w):
        count = shards * spread // GROUP
        cut = []
        for i in range(count):
            block = quarter * count + i
            cut.append(columns(w, (block % shards) * rows + (block // shards) * part, part))
        return jnp.concatenate(cut, axis=1)

    def own_units(w):
        return columns(w, quarter * (w.shape[1] // GROUP), w.shape[1] // GROUP)

    def over_shards(*members):
        cut = jnp.concatenate(members, axis=1) if len(members) > 1 else members[0]
        piece = lax.dynamic_slice_in_dim(cut, a * part, part, 0)
        return lax.all_gather(piece, "shard", axis=0, tiled=True)

    def over_owners(w):
        piece = lax.dynamic_slice_in_dim(w, a * part, part, 0)
        return lax.all_gather(piece, OWNERS, axis=0, tiled=True)

    def over_spread(x):
        return [shift_a(x, k) for k in range(1, spread)]

    def by_spread(relative):
        if spread == 2:
            return ordered(a, relative[0], relative[1], 0)
        stacked = jnp.stack(relative, 0)
        pick = functools.partial(lax.dynamic_index_in_dim, axis=0, keepdims=False)
        return jnp.concatenate([pick(stacked, (a - j) % spread) for j in range(spread)], axis=0)

    def in_row_order(x):
        cut = x.reshape(spread, shards, part, -1)
        return jnp.transpose(cut, (1, 0, 2, 3)).reshape(width, -1)

    def row_half(w, h):
        return lax.dynamic_slice_in_dim(w, h * half, half, 0)


    def away(left, right):
        return [gradient_rows(spots, spread, k, left, right) for k in range(1, spread)]

    def pieces(terms, *eighths):
        marks = [0, *eighths, 8]
        return [
            [x[x.shape[0] * i // 8 : x.shape[0] * j // 8] for x in terms]
            for i, j in zip(marks[:-1], marks[1:])
        ]

    def stacked(*arrived):
        return [jnp.concatenate(cut, axis=0) for cut in zip(*arrived)]

    def sent_a(terms):
        return [shift_a(x, k + 1) for k, x in enumerate(terms)]

    def scattered(x):
        return lax.psum_scatter(x, "shard", scatter_dimension=0, tiled=True)

    def kept(left, right, *arrived):
        return gradient_rows(spots, spread, 0, left, right, stacked(*arrived))

    def spread_a(x):
        return by_spread([x] + over_spread(x))

    def spread_b(x):
        return jnp.concatenate([x, swap_b(x)], axis=1)

    def spread_c(pair):
        return pair, swap_c(pair)

    def features_in_order(pairs, first, size):
        full = pairs[0].shape[1] // 2
        cut = [x[:, i * full + first : i * full + first + size] for x in pairs for i in range(2)]
        pair = [ordered(b, cut[n], cut[n + 1], 1) for n in (0, 2)]
        return natural(ordered(c, pair[0], pair[1], 1)).astype(F32)


    w_query, w_key, w_value, w_gate, w_out, w_one, w_two, w_down = weights
    g_qk = over_shards(own_units(w_query), own_units(w_key))
    g_vg = over_shards(own_units(w_value), own_units(w_gate))
    g_o = over_shards(own_features(w_out))
    g_1 = over_shards(own_units(w_one))
    g_2 = over_shards(own_units(w_two))
    w_d = [over_owners(own_units(w_down))]

    heads = HEADS // GROUP
    rates = lax.dynamic_slice_in_dim(decay_rates, quarter * heads, heads, 0)
    cuts = gather_rows_b(lengths.reshape(1, -1))
    cuts = ordered(c, cuts, swap_c(cuts), 0).reshape(GROUP, micro, -1)
    if streams == 1:
        batch = place // GROUP
        member = place % GROUP
        chosen = lax.dynamic_slice_in_dim(cuts, 2 * (member % 2) + member // 2, 1, 0)
    else:
        batch = place // 2
        chosen = lax.dynamic_index_in_dim(cuts.reshape(2, 2, micro, -1), place % 2, 0, False)
    chosen = lax.dynamic_index_in_dim(chosen, batch, 1, False)
    seq_ends = [chosen[:, 0]]
    for i in range(1, chosen.shape[1]):
        seq_ends.append(seq_ends[-1] + chosen[:, i])
    ends = jnp.stack(seq_ends, axis=1)

    x_run = bring(tokens)
    x_run, g_qk = tie(x_run, g_qk)

    x_pair = gather_rows_b(x_run)
    s_qk = over_spread(g_qk)
    x_pair, s_qk, g_vg = tie(x_pair, s_qk, g_vg)

    s_vg = over_spread(g_vg)
    w_qk = [g_qk, *s_qk]
    hidden_one, z_qk, x_scale, x_own = enter(spots, blocks, x_pair, swap_c(x_pair), w_qk)
    z_qk, hidden_one, s_vg, g_o = tie(z_qk, hidden_one, s_vg, g_o)

    s_o = over_spread(g_o)
    w_vg = [g_vg, *s_vg]
    z_vg = project(spots, hidden_one, w_vg)
    attended = attend(rates, ends, z_qk, z_vg)
    gate = z_vg[:, own:]
    o_scale = lax.rsqrt(total(jnp.sum(attended * attended, axis=-1)) / width + EPSILON)[:, None]
    lifted = (attended * gate).astype(LOW)
    lifted, s_o, g_1, cotangent = tie(lifted, s_o, g_1, cotangent)

    s_1 = over_spread(g_1)
    lifted = gather_b(lifted)
    lifted, s_1, g_2, o_scale, cotangent = tie(lifted, s_1, g_2, o_scale, cotangent)

    s_2 = over_spread(g_2)
    dy_run = bring(cotangent)
    lifted = gather_c(lifted)
    w_o = in_row_order(by_spread([g_o, *s_o]))
    branch = o_scale * matmul(lifted, w_o)
    middle = x_own.astype(F32) + branch
    low_middle = gather_b(middle.astype(LOW))
    low_middle, s_2, dy_run = tie(low_middle, s_2, dy_run)

    other_middle = swap_c(low_middle)
    dy_other = swap_b(dy_run)
    w_1, w_2 = [g_1, *s_1], [g_2, *s_2]
    hidden_two, z_one, z_two, product, m_scale = gated_unit(spots, low_middle, other_middle, w_1, w_2)
    z_one, z_two, product, dy_other = tie(z_one, z_two, product, dy_other)

    dy_pair = ordered(b, dy_run, dy_other, 0)
    dy_all, dy_own = enter(spots, blocks, dy_pair, swap_c(dy_pair))
    t_down = away(dy_all, product)
    z_one, z_two, product, t_down, w_d[0] = tie(z_one, z_two, product, t_down, w_d[0])


    down_a, down_b = pieces(t_down, 6)
    down_a = sent_a(down_a)
    d_one, d_two, lean_m = gated_unit_back(spots, dy_all, z_one, z_two, w_d)
    sent = fold_half(spots, [d_one, d_two], [w_1, w_2])
    sent, d_one, d_two, lean_m, down_a = tie(sent, d_one, d_two, lean_m, down_a)

    arrived = swap_c(sent)
    down_b = sent_a(down_b)
    t_one = away(hidden_two, d_one)
    result = fold_half(spots, [product], [w_d])
    lean_m = total(lean_m[:, 0])
    arrived, result, t_one = tie(arrived, result, t_one)

    r_result = swap_c(result)
    one_a, one_b = pieces(t_one, 2)
    one_a = sent_a(one_a)
    sent, mine = fold_half(spots, [d_one, d_two], [w_1, w_2], arrived)
    sent, d_two, one_a, one_b, product, lean_m, down_b, r_result = tie(
        sent, d_two, one_a, one_b, product, lean_m, down_b, r_result
    )

    crossed = swap_b(sent)
    one_b = sent_a(one_b)
    f_down = kept(dy_all, product, down_a, down_b)
    t_two = away(hidden_two, d_two)
    result, result_mine = fold_half(spots, [product], [w_d], r_result)
    crossed, result, f_down, t_two, one_b = tie(crossed, result, f_down, t_two, one_b)

    f_down = scattered(f_down)
    two_a, two_b = pieces(t_two, 5)
    two_a = sent_a(two_a)
    result_b = swap_b(result)
    d_hidden = mine + crossed.astype(F32)
    m_normed = middle * m_scale
    lean = lean_m[:, None] * (2.0 / width)
    d_middle = dy_own.astype(F32) + m_scale * (d_hidden - m_normed * lean)
    d_branch = d_middle.astype(LOW)
    lean_o = jnp.sum(d_middle * branch, axis=-1)
    sent = times_transposed(d_branch, row_half(w_o, 1 - c)).astype(LOW)
    sent, d_middle, lean_o = tie(sent, d_middle, lean_o)

    arrived = swap_c(sent)
    lean_o = lean_o + swap_c(lean_o)
    p_out = cross_tokens(lifted, (o_scale * d_middle).astype(LOW)).astype(LOW)
    p_out = jnp.transpose(p_out.reshape(shards, spread, part, -1), (1, 0, 2, 3))
    p_out = p_out.reshape(spread, width // spread, -1)
    t_out = [lax.dynamic_index_in_dim(p_out, (a + k) % spread, 0, False) for k in range(spread)]
    d_gated = times_transposed(d_branch, row_half(w_o, c)) + arrived.astype(F32)
    sent = columns(d_gated, (1 - b) * own, own).astype(LOW)
    mine = columns(d_gated, b * own, own)
    sent, mine, d_one, result_b, t_out, lean_o, two_a = tie(
        sent, mine, d_one, result_b, t_out, lean_o, two_a
    )

    crossed = swap_b(sent)
    lean_b = swap_b(lean_o)
    two_b = sent_a(two_b)
    f_one = kept(hidden_two, d_one, one_a, one_b)
    output = (middle + (result_mine + result_b.astype(F32))).astype(LOW)
    crossed, output, f_one, f_down, two_b, t_out, lean_b = tie(
        crossed, output, f_one, f_down, two_b, t_out, lean_b
    )

    f_one = scattered(f_one)
    r_out = sent_a(t_out[1:])
    y_down = over_spread(f_down)
    f_two = kept(hidden_two, d_two, two_a, two_b)
    output, out_b = away_b(output)
    o_normed = attended * o_scale
    d_gated = mine + crossed.astype(F32)
    d_gate = (d_gated * o_normed).astype(LOW)
    lean = (lean_o + lean_b)[:, None] / width
    d_attended = (o_scale * (d_gated * gate - o_normed * lean)).astype(LOW)
    d_query, d_key, d_value = attend_back(rates, ends, z_qk, z_vg, d_attended)
    d_qk = joined(d_query, d_key)
    d_vg = joined(d_value, d_gate)
    t_qk = away(hidden_one, d_qk)
    d_qk, d_vg, t_qk, f_two, y_down, out_b, r_out = tie(d_qk, d_vg, t_qk, f_two, y_down, out_b, r_out)

    f_two = scattered(f_two)
    f_out = scattered(sum([x.astype(F32) for x in r_out], t_out[0].astype(F32)).astype(LOW))
    y_down = by_spread([f_down, *y_down])
    qk_a, qk_b = pieces(t_qk, 4)
    qk_a = sent_a(qk_a)
    output, out_c = away_c(output, out_b)
    x_down = swap_b(y_down)
    y_one = over_spread(f_one)
    t_vg = away(hidden_one, d_vg)
    sent = fold_half(spots, [d_qk, d_vg], [w_qk, w_vg])
    sent, t_vg, d_qk, d_vg, out_c, qk_a, x_down, y_one = tie(
        sent, t_vg, d_qk, d_vg, out_c, qk_a, x_down, y_one
    )

    arrived = swap_c(sent)
    output = send_back(ordered(c, output, out_c, 1))
    qk_b = sent_a(qk_b)
    x_down = joined(y_down, x_down)
    y_one = by_spread([f_one, *y_one])
    x_one = swap_b(y_one)
    lean_x = jnp.sum(z_qk * d_qk.astype(F32), axis=-1) + jnp.sum(z_vg * d_vg.astype(F32), axis=-1)
    sent, mine = fold_half(spots, [d_qk, d_vg], [w_qk, w_vg], arrived)
    lean_x = lean_x + swap_c(lean_x)
    sent, mine, qk_b, t_vg, lean_x, x_one, output = tie(sent, mine, qk_b, t_vg, lean_x, x_one, output)

    crossed = swap_b(sent)
    lean_b = swap_b(lean_x)
    r_vg = sent_a(t_vg)
    f_qk = scattered(kept(hidden_one, d_qk, qk_a, qk_b))
    four_down = spread_c(x_down)
    crossed, d_vg, r_vg, lean_b, f_two, four_down = tie(crossed, d_vg, r_vg, lean_b, f_two, four_down)

    f_vg = kept(hidden_one, d_vg, r_vg)
    x_one = joined(y_one, x_one)
    f_vg, crossed, f_two, f_out, x_one = tie(f_vg, crossed, f_two, f_out, x_one)

    f_vg = scattered(f_vg)
    d_hidden = mine + crossed.astype(F32)
    x_normed = x_own.astype(F32) * x_scale
    lean = (lean_x + lean_b)[:, None] / width
    input_grad = to_runs((d_middle + x_scale * (d_hidden - x_normed * lean)).astype(LOW))
    f_oqk = joined(f_out, f_qk)
    x_oqk = swap_b(f_oqk)
    y_two = over_spread(f_two)
    four_one = spread_c(x_one)
    units = f_one.shape[1]
    [g_down] = place_quarters(spots, four_down, (0, units))
    [g_one] = place_quarters(spots, four_one, (0, units))
    input_grad, x_oqk, y_two, f_vg, g_down, g_one = tie(input_grad, x_oqk, y_two, f_vg, g_down, g_one)

    y_vg = over_spread(f_vg)
    f_oqk = joined(f_oqk, x_oqk)
    y_oqk = over_spread(f_oqk)
    y_two = by_spread([f_two, *y_two])
    x_two = swap_b(y_two)
    input_grad = send_back(input_grad)
    y_vg, y_oqk, x_two, input_grad = tie(y_vg, y_oqk, x_two, input_grad)

    four_vg = spread_c(spread_b(by_spread([f_vg, *y_vg])))
    four_two = spread_c(joined(y_two, x_two))
    four_oqk = spread_c(by_spread([f_oqk, *y_oqk]))
    g_query, g_key = place_quarters(spots, four_oqk, (own, own), (2 * own, own))
    g_value, g_gate = place_quarters(spots, four_vg, (0, own), (own, own))
    [g_two] = place_quarters(spots, four_two, (0, units))
    g_out = features_in_order(four_oqk, 0, own)
    output, input_grad = as_batches(output), as_batches(input_grad)
    return output, input_grad, g_query, g_key, g_value, g_gate, g_out, g_one, g_two, g_down


def solution(mesh):
    reps, shards = mesh.shape["rep"], mesh.shape["shard"]
    devices = mesh.devices.reshape(reps // GROUP, 2, 2, shards)
    rep = ("a", "b", "c")
    by_tokens = P(None, (*rep, "shard"), None)
    by_rows = P("shard", None)
    return jax.shard_map(
        functools.partial(body, reps, shards),
        mesh=Mesh(devices, AXES),
        in_specs=(by_tokens, by_tokens, P(None, rep, None), P(), *[by_rows] * 8),
        out_specs=(by_tokens, by_tokens, *[by_rows] * 8),
        check_vma=False,
    )
```

```python
import functools

import jax
import jax.numpy as jnp
from jax import lax
from jax.experimental import pallas as pl
from jax.experimental.pallas import tpu as pltpu
from jax.sharding import Mesh, PartitionSpec as P

HEADS = 16
HEAD_DIM = 128
STREAM = 1024
GROUP = 4
BLOCK = 256
TILE = 256
EPSILON = 1e-06
AXES = ("a", "b", "c", "shard")
OWNERS = ("a", "shard")
LOW = jnp.bfloat16
F32 = jnp.float32


def matmul(former, latter):
    return jnp.dot(former, latter, preferred_element_type=F32)


def times_transposed(former, latter):
    return lax.dot_general(former, latter, (((1,), (1,)), ((), ())), preferred_element_type=F32)


def cross_tokens(former, latter):
    return lax.dot_general(former, latter, (((0,), (0,)), ((), ())), preferred_element_type=F32)


def masked_decay(rate, ends, first, columns):
    row = first + lax.broadcasted_iota(jnp.int32, (BLOCK, 1), 0)
    column = lax.broadcasted_iota(jnp.int32, (1, columns), 1)
    begin = jnp.zeros((BLOCK, 1), jnp.int32)
    for end in ends:
        begin = jnp.where(row >= end, end, begin)
    falling = jnp.exp(-rate * (row - first).astype(F32))
    rising = jnp.exp(rate * (column - first).astype(F32))
    allowed = (column <= row) & (column >= begin)
    return jnp.where(allowed, falling * rising, 0.0)


def attend_kernel(rates, ends, zq_ref, zk_ref, zv_ref, out_ref):
    stream, head = pl.program_id(0), pl.program_id(1)
    rate = rates[head]
    bounds = [ends[stream, i] for i in range(ends.shape[1])]
    zq, zk = zq_ref[...], zk_ref[...]
    q = (zq * jax.nn.sigmoid(zq)).astype(LOW)
    k = (zk * jax.nn.sigmoid(zk)).astype(LOW)
    v = zv_ref[...].astype(LOW)
    for first in range(0, STREAM, BLOCK):
        columns = first + BLOCK
        mask = masked_decay(rate, bounds, first, columns)
        scores = times_transposed(q[first:columns], k[:columns])
        weights = (scores * mask).astype(LOW)
        out_ref[first:columns, :] = matmul(weights, v[:columns])


def attend_back_kernel(
    rates, ends, zq_ref, zk_ref, zv_ref, do_ref, dzq_ref, dzk_ref, dzv_ref, dk_ref, dv_ref
):
    stream, head = pl.program_id(0), pl.program_id(1)
    rate = rates[head]
    bounds = [ends[stream, i] for i in range(ends.shape[1])]
    zq, zk = zq_ref[...], zk_ref[...]
    sig_q, sig_k = jax.nn.sigmoid(zq), jax.nn.sigmoid(zk)
    q = (zq * sig_q).astype(LOW)
    k = (zk * sig_k).astype(LOW)
    slope_q = sig_q * (1.0 + zq * (1.0 - sig_q))
    v = zv_ref[...].astype(LOW)
    d_o = do_ref[...]
    dk_ref[...] = jnp.zeros_like(dk_ref)
    dv_ref[...] = jnp.zeros_like(dv_ref)
    for first in range(0, STREAM, BLOCK):
        columns = first + BLOCK
        rows = slice(first, columns)
        mask = masked_decay(rate, bounds, first, columns)
        weights = (times_transposed(q[rows], k[:columns]) * mask).astype(LOW)
        d_scores = (times_transposed(d_o[rows], v[:columns]) * mask).astype(LOW)
        dzq_ref[rows, :] = (matmul(d_scores, k[:columns]) * slope_q[rows]).astype(LOW)
        dk_ref[:columns, :] += cross_tokens(d_scores, q[rows])
        dv_ref[:columns, :] += cross_tokens(weights, d_o[rows])
    dzk_ref[...] = (dk_ref[...] * (sig_k * (1.0 + zk * (1.0 - sig_k)))).astype(LOW)
    dzv_ref[...] = dv_ref[...].astype(LOW)


def head_block(offset=0):
    return pl.BlockSpec((STREAM, HEAD_DIM), lambda g, h, *_: (g, h + offset))


def attend(rates, ends, z_qk, z_vg):
    heads, streams = rates.shape[0], ends.shape[0]
    work = streams * heads * STREAM * STREAM
    return pl.pallas_call(
        attend_kernel,
        out_shape=jax.ShapeDtypeStruct((streams * STREAM, heads * HEAD_DIM), F32),
        grid_spec=pltpu.PrefetchScalarGridSpec(
            num_scalar_prefetch=2,
            grid=(streams, heads),
            in_specs=[head_block(), head_block(heads), head_block()],
            out_specs=head_block(),
        ),
        compiler_params=pltpu.CompilerParams(vmem_limit_bytes=40 << 20),
        cost_estimate=pl.CostEstimate(
            flops=4 * work * HEAD_DIM, transcendentals=work // 64,
            bytes_accessed=streams * heads * STREAM * HEAD_DIM * 16,
        ),
        name="attend",
    )(rates, ends, z_qk, z_qk, z_vg)


def attend_back(rates, ends, z_qk, z_vg, d_o):
    heads, streams = rates.shape[0], ends.shape[0]
    work = streams * heads * STREAM * STREAM
    return pl.pallas_call(
        attend_back_kernel,
        out_shape=[jax.ShapeDtypeStruct((streams * STREAM, heads * HEAD_DIM), LOW)] * 3,
        grid_spec=pltpu.PrefetchScalarGridSpec(
            num_scalar_prefetch=2,
            grid=(streams, heads),
            in_specs=[head_block(), head_block(heads), head_block(), head_block()],
            out_specs=[head_block()] * 3,
            scratch_shapes=[pltpu.VMEM((STREAM, HEAD_DIM), F32)] * 2,
        ),
        compiler_params=pltpu.CompilerParams(vmem_limit_bytes=40 << 20),
        cost_estimate=pl.CostEstimate(
            flops=10 * work * HEAD_DIM, transcendentals=work // 64,
            bytes_accessed=streams * heads * STREAM * HEAD_DIM * 20,
        ),
        name="attend_back",
    )(rates, ends, z_qk, z_qk, z_vg, d_o)


def chunk_copies(chunks, buffer, sems, turn, half=None):
    count, size = len(chunks), chunks[0].shape[0]
    if count == 1:
        rows = buffer.shape[0]
        first = 0 if half is None else pl.multiple_of(half * rows, rows)
        return [(None, pltpu.make_async_copy(chunks[0].at[pl.ds(first, rows)], buffer, sems.at[0]))]
    copies = []
    for k, chunk in enumerate(chunks):
        index = lax.rem(turn - k + count, count)
        wanted = None
        if half is not None:
            wanted = lax.div(index, count // 2) == half
            index = lax.rem(index, count // 2)
        target = buffer.at[pl.ds(pl.multiple_of(index * size, size), size)]
        copies.append((wanted, pltpu.make_async_copy(chunk, target, sems.at[k])))
    return copies


def each(copies, act):
    for wanted, copy in copies:
        if wanted is None:
            act(copy)
        else:
            pl.when(wanted)(functools.partial(act, copy))


def start(copies):
    each(copies, lambda copy: copy.start())


def finish(copies):
    each(copies, lambda copy: copy.wait())


def estimate(flops, *arrays):
    moved = sum(x.size * x.dtype.itemsize for x in arrays)
    return pl.CostEstimate(flops=flops, transcendentals=0, bytes_accessed=moved)


def limit(mebibytes):
    return pltpu.CompilerParams(vmem_limit_bytes=mebibytes << 20)


ANYWHERE = pl.BlockSpec(memory_space=pl.ANY)


def weight_buffer(chunks, share=1):
    size = len(chunks) * chunks[0].shape[0] // share
    return [pltpu.VMEM((size, chunks[0].shape[1]), LOW), pltpu.SemaphoreType.DMA((len(chunks),))]


def tile_rows(width, column=0):
    return pl.BlockSpec((TILE, width), lambda i, *_: (i, column))


def joined_rows(width, tiles):
    spec = pl.BlockSpec((TILE, width), lambda i, s: (i // (2 * tiles) * tiles + i % tiles, 0))
    return [spec, spec]


def enter_kernel(tiles, blocks, project, spots, own_ref, other_ref, *refs):
    i = pl.program_id(0)
    mine = lax.rem(lax.div(i, tiles), 2) == spots[0]
    rows = jnp.where(mine, own_ref[...], other_ref[...])
    part = rows.shape[1] // len(blocks)
    permuted = jnp.concatenate([rows[:, n * part : (n + 1) * part] for n in blocks], axis=1)
    if not project:
        all_ref, quarter_ref = refs
        all_ref[...] = permuted
        held = all_ref
    else:
        chunks, (h_ref, z_ref, scale_ref, quarter_ref, held, buffer, sems) = refs[:-7], refs[-7:]
        held[...] = permuted
        copies = chunk_copies(chunks, buffer, sems, spots[2])

        @pl.when(i == 0)
        def _():
            start(copies)

        x = rows.astype(F32)
        scale = lax.rsqrt(jnp.mean(x * x, axis=-1, keepdims=True) + EPSILON)
        scale_ref[...] = scale
        hidden = (permuted.astype(F32) * scale).astype(LOW)
        h_ref[...] = hidden

        @pl.when(i == 0)
        def _():
            finish(copies)

        z_ref[...] = matmul(hidden, buffer[...])
    size = quarter_ref.shape[1]
    quarter_ref[...] = held[:, pl.ds(pl.multiple_of(spots[1] * size, size), size)]


def enter(spots, blocks, own, other, chunks=()):
    width = own.shape[1]
    count, tiles = 2 * own.shape[0], own.shape[0] // TILE // 2
    shape = jax.ShapeDtypeStruct
    quarter = shape((count, width // GROUP), LOW)
    if chunks:
        columns = chunks[0].shape[1]
        outs = [shape((count, width), LOW), shape((count, columns), F32), shape((count, 1), F32), quarter]
        scratch = [pltpu.VMEM((TILE, width), LOW), *weight_buffer(chunks)]
    else:
        columns, scratch = 0, []
        outs = [shape((count, width), LOW), quarter]
    return pl.pallas_call(
        functools.partial(enter_kernel, tiles, blocks, bool(chunks)),
        out_shape=outs,
        grid_spec=pltpu.PrefetchScalarGridSpec(
            num_scalar_prefetch=1,
            grid=(count // TILE,),
            in_specs=joined_rows(width, tiles) + [ANYWHERE] * len(chunks),
            out_specs=[tile_rows(o.shape[1]) for o in outs],
            scratch_shapes=scratch,
        ),
        compiler_params=limit(40),
        cost_estimate=estimate(2 * count * width * columns, own, other, *chunks, *outs),
        name="enter",
    )(spots, own, other, *chunks)


def project_kernel(spots, h_ref, *refs):
    chunks, (z_ref, buffer, sems) = refs[:-3], refs[-3:]
    copies = chunk_copies(chunks, buffer, sems, spots[2])

    @pl.when(pl.program_id(0) == 0)
    def _():
        start(copies)
        finish(copies)

    z_ref[...] = matmul(h_ref[...], buffer[...])


def project(spots, hidden, chunks):
    count, width = hidden.shape
    out = jax.ShapeDtypeStruct((count, chunks[0].shape[1]), F32)
    return pl.pallas_call(
        project_kernel,
        out_shape=out,
        grid_spec=pltpu.PrefetchScalarGridSpec(
            num_scalar_prefetch=1,
            grid=(count // TILE,),
            in_specs=[tile_rows(width)] + [ANYWHERE] * len(chunks),
            out_specs=tile_rows(out.shape[1]),
            scratch_shapes=weight_buffer(chunks),
        ),
        compiler_params=limit(40),
        cost_estimate=estimate(2 * count * width * out.shape[1], hidden, *chunks, out),
        name="project",
    )(spots, hidden, *chunks)


def unit_kernel(spots, own_ref, other_ref, *refs):
    chunks, rest = refs[:-9], refs[-9:]
    h_ref, one_ref, two_ref, product_ref, scale_ref, first, second, sem_one, sem_two = rest
    split = len(chunks) // 2
    copies = [
        chunk_copies(chunks[:split], first, sem_one, spots[2]),
        chunk_copies(chunks[split:], second, sem_two, spots[2]),
    ]
    begins = pl.program_id(0) == 0

    @pl.when(begins)
    def _():
        start(copies[0])
        start(copies[1])

    mine, other = own_ref[...], other_ref[...]
    swapped = spots[0] == 1
    middle = jnp.concatenate(
        [jnp.where(swapped, other, mine), jnp.where(swapped, mine, other)], axis=1
    ).astype(F32)
    scale = lax.rsqrt(jnp.mean(middle * middle, axis=-1, keepdims=True) + EPSILON)
    scale_ref[...] = scale
    hidden = (middle * scale).astype(LOW)
    h_ref[...] = hidden

    @pl.when(begins)
    def _():
        finish(copies[0])

    z_one = matmul(hidden, first[...])

    @pl.when(begins)
    def _():
        finish(copies[1])

    z_two = matmul(hidden, second[...])
    one_ref[...] = z_one.astype(LOW)
    two_ref[...] = z_two.astype(LOW)
    product_ref[...] = (z_one * z_two).astype(LOW)


def gated_unit(spots, own, other, first, second):
    count, width, units = own.shape[0], 2 * own.shape[1], first[0].shape[1]
    shape = jax.ShapeDtypeStruct
    outs = [shape((count, width), LOW)] + [shape((count, units), LOW)] * 3 + [shape((count, 1), F32)]
    (buffer, sems) = weight_buffer(first)
    return pl.pallas_call(
        unit_kernel,
        out_shape=outs,
        grid_spec=pltpu.PrefetchScalarGridSpec(
            num_scalar_prefetch=1,
            grid=(count // TILE,),
            in_specs=[tile_rows(width // 2)] * 2 + [ANYWHERE] * (2 * len(first)),
            out_specs=[tile_rows(o.shape[1]) for o in outs],
            scratch_shapes=[buffer, buffer, sems, sems],
        ),
        compiler_params=limit(48),
        cost_estimate=estimate(4 * count * width * units, own, other, *first, *second, *outs),
        name="gated_unit",
    )(spots, own, other, *first, *second)


def unit_back_kernel(spots, dy_ref, one_ref, two_ref, *refs):
    chunks, (d_one_ref, d_two_ref, sum_ref, buffer, sems) = refs[:-5], refs[-5:]
    copies = chunk_copies(chunks, buffer, sems, spots[2])

    @pl.when(pl.program_id(0) == 0)
    def _():
        start(copies)
        finish(copies)

    d_product = matmul(dy_ref[...], buffer[...])
    z_one, z_two = one_ref[...].astype(F32), two_ref[...].astype(F32)
    d_one = d_product * z_two
    d_one_ref[...] = d_one.astype(LOW)
    d_two_ref[...] = (d_product * z_one).astype(LOW)
    sum_ref[...] = jnp.sum(d_one * z_one, axis=-1, keepdims=True)


def gated_unit_back(spots, dy, z_one, z_two, chunks):
    count, width, units = dy.shape[0], dy.shape[1], z_one.shape[1]
    shape = jax.ShapeDtypeStruct
    outs = [shape((count, units), LOW)] * 2 + [shape((count, 1), F32)]
    return pl.pallas_call(
        unit_back_kernel,
        out_shape=outs,
        grid_spec=pltpu.PrefetchScalarGridSpec(
            num_scalar_prefetch=1,
            grid=(count // TILE,),
            in_specs=[tile_rows(width), tile_rows(units), tile_rows(units)] + [ANYWHERE] * len(chunks),
            out_specs=[tile_rows(o.shape[1]) for o in outs],
            scratch_shapes=weight_buffer(chunks),
        ),
        compiler_params=limit(40),
        cost_estimate=estimate(2 * count * width * units, dy, z_one, z_two, *chunks, *outs),
        name="gated_unit_back",
    )(spots, dy, z_one, z_two, *chunks)


def fold_kernel(members, keeps, spots, *refs):
    values, refs = refs[:members], refs[members:]
    arrived, refs = (refs[0], refs[1:]) if keeps else (None, refs)
    outs = 2 if keeps else 1
    chunks, refs = refs[: -outs - 2 * members], refs[-outs - 2 * members :]
    outs, buffers, sems = refs[:outs], refs[outs : outs + members], refs[outs + members :]
    each_count = len(chunks) // members
    half = spots[0] if keeps else 1 - spots[0]
    begins = pl.program_id(0) == 0
    copies = [
        chunk_copies(chunks[m * each_count : (m + 1) * each_count], buffers[m], sems[m], spots[2], half)
        for m in range(members)
    ]

    @pl.when(begins)
    def _():
        for m in range(members):
            start(copies[m])

    whole = None
    for m in range(members):
        pl.when(begins)(functools.partial(finish, copies[m]))
        term = times_transposed(values[m][...], buffers[m][...])
        whole = term if whole is None else whole + term
    if not keeps:
        outs[0][...] = whole.astype(LOW)
    else:
        whole = whole + arrived[...].astype(F32)
        size = whole.shape[1] // 2
        upper = spots[3] == 1
        outs[0][...] = jnp.where(upper, whole[:, :size], whole[:, size:]).astype(LOW)
        outs[1][...] = jnp.where(upper, whole[:, size:], whole[:, :size])


def fold_half(spots, values, weights, arrived=None):
    count = values[0].shape[0]
    half = len(weights[0]) * weights[0][0].shape[0] // 2
    shape = jax.ShapeDtypeStruct
    if arrived is None:
        outs, extra = [shape((count, half), LOW)], []
    else:
        outs, extra = [shape((count, half // 2), LOW), shape((count, half // 2), F32)], [arrived]
    buffers, sems = zip(*[weight_buffer(w, 2) for w in weights])
    chunks = [x for w in weights for x in w]
    flops = sum(2 * count * half * v.shape[1] for v in values)
    found = pl.pallas_call(
        functools.partial(fold_kernel, len(values), arrived is not None),
        out_shape=outs,
        grid_spec=pltpu.PrefetchScalarGridSpec(
            num_scalar_prefetch=1,
            grid=(count // TILE,),
            in_specs=[tile_rows(v.shape[1]) for v in values]
            + [tile_rows(half)] * len(extra)
            + [ANYWHERE] * len(chunks),
            out_specs=[tile_rows(o.shape[1]) for o in outs],
            scratch_shapes=[*buffers, *sems],
        ),
        compiler_params=limit(40),
        cost_estimate=estimate(flops, *values, *extra, *chunks[: len(chunks) // 2], *outs),
        name="fold_half",
    )(spots, *values, *extra, *chunks)
    return found[0] if arrived is None else found


def gradient_kernel(spots, left_ref, right_ref, *refs):
    found = cross_tokens(left_ref[...], right_ref[...])
    for arrived_ref in refs[:-1]:
        found = found + arrived_ref[...].astype(F32)
    refs[-1][...] = found.astype(LOW)


def gradient_rows(spots, spread, k, left, right, arrived=()):
    count, columns = right.shape
    rows = left.shape[1] // (1 if k is None else spread)
    tiles = rows // TILE

    def block(i, s):
        return (0, i if k is None else lax.rem(s[2] + k, spread) * tiles + i)

    out = jax.ShapeDtypeStruct((rows, columns), LOW)
    return pl.pallas_call(
        gradient_kernel,
        out_shape=out,
        grid_spec=pltpu.PrefetchScalarGridSpec(
            num_scalar_prefetch=1,
            grid=(tiles,),
            in_specs=[
                pl.BlockSpec((count, TILE), block),
                pl.BlockSpec((count, columns), lambda i, s: (0, 0), pipeline_mode=pl.Buffered(1)),
            ]
            + [tile_rows(columns)] * len(arrived),
            out_specs=tile_rows(columns),
        ),
        compiler_params=limit(40),
        cost_estimate=estimate(2 * count * rows * columns, right, out, out, *arrived),
        name="gradient_rows",
    )(spots, left, right, *arrived)


def place_kernel(cuts, spots, *refs):
    quarter = pl.program_id(0)
    cross = lax.rem(lax.div(quarter, 2) + spots[0], 2) * 2 + lax.rem(lax.rem(quarter, 2) + spots[3], 2)
    for n in range(4):

        @pl.when(cross == n)
        def _():
            for (first, size), out_ref in zip(cuts, refs[4:]):
                out_ref[...] = refs[n][:, first : first + size].astype(F32)


def place_quarters(spots, pairs, *cuts):
    rows, columns = pairs[0].shape[0], pairs[0].shape[1] // 2
    outs = [jax.ShapeDtypeStruct((rows, GROUP * size), F32) for _, size in cuts]

    def block(index):
        return pl.BlockSpec((rows, columns), lambda q, s: (0, index), pipeline_mode=pl.Buffered(1))

    return pl.pallas_call(
        functools.partial(place_kernel, cuts),
        out_shape=outs,
        grid_spec=pltpu.PrefetchScalarGridSpec(
            num_scalar_prefetch=1,
            grid=(GROUP,),
            in_specs=[block(0), block(1), block(0), block(1)],
            out_specs=[pl.BlockSpec((rows, size), lambda q, s: (0, q)) for _, size in cuts],
        ),
        compiler_params=limit(40),
        cost_estimate=estimate(0, *pairs, *outs),
        name="place_quarters",
    )(spots, pairs[0], pairs[0], pairs[1], pairs[1])


def tie(*values):
    return lax.optimization_barrier(values)


def body(reps, shards, tokens, cotangent, lengths, decay_rates, *weights):
    spread = reps // GROUP
    place = lax.axis_index("shard")
    a, b, c = lax.axis_index("a"), lax.axis_index("b"), lax.axis_index("c")
    quarter = 2 * c + b
    micro, run, width = tokens.shape
    half, own = width // 2, width // GROUP
    streams = micro * GROUP // shards
    per_block = STREAM // run // GROUP * streams
    rows = width // shards
    part = rows // spread
    columns = functools.partial(lax.dynamic_slice_in_dim, axis=1)
    spots = jnp.stack([c, quarter, a, b]).astype(jnp.int32)
    blocks = [z * spread + k for k in range(spread) for z in range(shards)]

    def move(x, target):
        pairs = [(r * shards + s, target(r) * shards + s) for r in range(reps) for s in range(shards)]
        return lax.ppermute(x, AXES, pairs)

    def swap_c(x):
        return move(x, lambda r: r ^ 1)

    def swap_b(x):
        return move(x, lambda r: r ^ 2)

    def joined(*parts):
        return jnp.concatenate(parts, axis=1)

    def shift_a(x, k):
        return move(x, lambda r: (r + GROUP * k) % reps)

    def ordered(index, mine, other, axis):
        return jnp.where(
            index == 0,
            jnp.concatenate([mine, other], axis),
            jnp.concatenate([other, mine], axis),
        )


    def batch_of(s):
        return s // (shards // micro)

    def origin(r, s, p):
        run_id = (r % GROUP) * per_block + p
        stream, piece = run_id // shards, run_id % shards
        member = s % GROUP if streams == 1 else 2 * stream + s % 2
        return (r // GROUP) * GROUP + member, piece

    def routes(p):
        found = []
        for r in range(reps):
            for s in range(shards):
                from_r, from_s = origin(r, s, p ^ batch_of(s))
                found.append((from_r * shards + from_s, r * shards + s))
        return found

    def natural(x):
        return jnp.concatenate(
            [
                x[:, (k * shards + z) * part : (k * shards + z + 1) * part]
                for z in range(shards)
                for k in range(spread)
            ],
            axis=1,
        )

    def bring(x):
        arrived = [
            lax.ppermute(lax.dynamic_index_in_dim(x, (place + p) % 2, 0, False), AXES, routes(p))
            for p in range(2)
        ]
        return ordered(batch_of(place), *arrived, 0)

    def send_back(x):
        slots = natural(x).reshape(2, run, width)
        return [
            lax.ppermute(
                lax.dynamic_index_in_dim(slots, (batch_of(place) + p) % 2, 0, False),
                AXES,
                [(to, origin) for origin, to in routes(p)],
            )
            for p in range(2)
        ]

    def as_batches(arrived):
        return ordered(place % 2, arrived[0][None], arrived[1][None], 0)


    def gather_b(x):
        return ordered(b, x, swap_b(x), 1)

    def gather_c(x):
        return ordered(c, x, swap_c(x), 1)

    def gather_rows_b(x):
        return ordered(b, x, swap_b(x), 0)

    def total(x):
        x = x + swap_c(x)
        return x + swap_b(x)

    def fold_c(product):
        sent = swap_c(product(1 - c).astype(LOW))
        return product(c) + sent.astype(F32)

    def fold_b(x):
        sent = swap_b(columns(x, (1 - b) * own, own).astype(LOW))
        return columns(x, b * own, own) + sent.astype(F32)


    pick = functools.partial(lax.dynamic_index_in_dim, keepdims=False)

    def away_b(x):
        cut = x.reshape(2, 2, -1, own)
        return pick(cut, b, 0), swap_b(pick(cut, 1 - b, 0))

    def away_c(mine, arrived):
        both = ordered(b, mine, arrived, 2)
        return pick(both, c, 0), swap_c(pick(both, 1 - c, 0))

    def to_runs(x):
        return ordered(c, *away_c(*away_b(x)), 1)


    def own_features(w):
        count = shards * spread // GROUP
        cut = []
        for i in range(count):
            block = quarter * count + i
            cut.append(columns(w, (block % shards) * rows + (block // shards) * part, part))
        return jnp.concatenate(cut, axis=1)

    def own_units(w):
        return columns(w, quarter * (w.shape[1] // GROUP), w.shape[1] // GROUP)

    def over_shards(*members):
        cut = jnp.concatenate(members, axis=1) if len(members) > 1 else members[0]
        piece = lax.dynamic_slice_in_dim(cut, a * part, part, 0)
        return lax.all_gather(piece, "shard", axis=0, tiled=True)

    def over_owners(w):
        piece = lax.dynamic_slice_in_dim(w, a * part, part, 0)
        return lax.all_gather(piece, OWNERS, axis=0, tiled=True)

    def over_spread(x):
        return [shift_a(x, k) for k in range(1, spread)]

    def by_spread(relative):
        if spread == 2:
            return ordered(a, relative[0], relative[1], 0)
        stacked = jnp.stack(relative, 0)
        pick = functools.partial(lax.dynamic_index_in_dim, axis=0, keepdims=False)
        return jnp.concatenate([pick(stacked, (a - j) % spread) for j in range(spread)], axis=0)

    def in_row_order(x):
        cut = x.reshape(spread, shards, part, -1)
        return jnp.transpose(cut, (1, 0, 2, 3)).reshape(width, -1)

    def row_half(w, h):
        return lax.dynamic_slice_in_dim(w, h * half, half, 0)


    def away(left, right):
        return [gradient_rows(spots, spread, k, left, right) for k in range(1, spread)]

    def in_two(terms):
        middles = [x.shape[0] // 2 for x in terms]
        return [x[:m] for x, m in zip(terms, middles)], [x[m:] for x, m in zip(terms, middles)]

    def stacked(upper, lower):
        return [jnp.concatenate(pair, axis=0) for pair in zip(upper, lower)]

    def sent_a(terms):
        return [shift_a(x, k + 1) for k, x in enumerate(terms)]

    def scattered(x):
        return lax.psum_scatter(x, "shard", scatter_dimension=0, tiled=True)

    def whole_rows(left, right):
        return gradient_rows(spots, spread, None, left, right)

    def scattered_all(x):
        return lax.psum_scatter(x, OWNERS, scatter_dimension=0, tiled=True)

    def summed(left, right, arrived):
        return scattered(gradient_rows(spots, spread, 0, left, right, arrived))

    def spread_a(x):
        return by_spread([x] + over_spread(x))

    def spread_b(x):
        return jnp.concatenate([x, swap_b(x)], axis=1)

    def spread_c(pair):
        return pair, swap_c(pair)

    def features_in_order(pairs, first, size):
        full = pairs[0].shape[1] // 2
        cut = [x[:, i * full + first : i * full + first + size] for x in pairs for i in range(2)]
        pair = [ordered(b, cut[n], cut[n + 1], 1) for n in (0, 2)]
        return natural(ordered(c, pair[0], pair[1], 1)).astype(F32)


    w_query, w_key, w_value, w_gate, w_out, w_one, w_two, w_down = weights
    g_qk = over_shards(own_units(w_query), own_units(w_key))
    g_vg = over_shards(own_units(w_value), own_units(w_gate))
    g_o = over_shards(own_features(w_out))
    g_1 = over_shards(own_units(w_one))
    g_2 = over_shards(own_units(w_two))
    w_d = [over_owners(own_units(w_down))]

    heads = HEADS // GROUP
    rates = lax.dynamic_slice_in_dim(decay_rates, quarter * heads, heads, 0)
    cuts = gather_rows_b(lengths.reshape(1, -1))
    cuts = ordered(c, cuts, swap_c(cuts), 0).reshape(GROUP, micro, -1)
    if streams == 1:
        batch = place // GROUP
        member = place % GROUP
        chosen = lax.dynamic_slice_in_dim(cuts, 2 * (member % 2) + member // 2, 1, 0)
    else:
        batch = place // 2
        chosen = lax.dynamic_index_in_dim(cuts.reshape(2, 2, micro, -1), place % 2, 0, False)
    chosen = lax.dynamic_index_in_dim(chosen, batch, 1, False)
    seq_ends = [chosen[:, 0]]
    for i in range(1, chosen.shape[1]):
        seq_ends.append(seq_ends[-1] + chosen[:, i])
    ends = jnp.stack(seq_ends, axis=1)

    x_run = bring(tokens)
    x_run, g_qk = tie(x_run, g_qk)

    x_pair = gather_rows_b(x_run)
    s_qk = over_spread(g_qk)
    x_pair, s_qk, g_vg = tie(x_pair, s_qk, g_vg)

    s_vg = over_spread(g_vg)
    w_qk = [g_qk, *s_qk]
    hidden_one, z_qk, x_scale, x_own = enter(spots, blocks, x_pair, swap_c(x_pair), w_qk)
    z_qk, hidden_one, s_vg, g_o = tie(z_qk, hidden_one, s_vg, g_o)

    s_o = over_spread(g_o)
    w_vg = [g_vg, *s_vg]
    z_vg = project(spots, hidden_one, w_vg)
    attended = attend(rates, ends, z_qk, z_vg)
    gate = z_vg[:, own:]
    o_scale = lax.rsqrt(total(jnp.sum(attended * attended, axis=-1)) / width + EPSILON)[:, None]
    lifted = (attended * gate).astype(LOW)
    lifted, s_o, g_1, cotangent = tie(lifted, s_o, g_1, cotangent)

    s_1 = over_spread(g_1)
    lifted = gather_b(lifted)
    lifted, s_1, g_2, o_scale, cotangent = tie(lifted, s_1, g_2, o_scale, cotangent)

    s_2 = over_spread(g_2)
    dy_run = bring(cotangent)
    lifted = gather_c(lifted)
    w_o = in_row_order(by_spread([g_o, *s_o]))
    branch = o_scale * matmul(lifted, w_o)
    middle = x_own.astype(F32) + branch
    low_middle = gather_b(middle.astype(LOW))
    low_middle, s_2, dy_run = tie(low_middle, s_2, dy_run)

    other_middle = swap_c(low_middle)
    dy_other = swap_b(dy_run)
    w_1, w_2 = [g_1, *s_1], [g_2, *s_2]
    hidden_two, z_one, z_two, product, m_scale = gated_unit(spots, low_middle, other_middle, w_1, w_2)
    z_one, z_two, product, dy_other = tie(z_one, z_two, product, dy_other)

    dy_pair = ordered(b, dy_run, dy_other, 0)
    dy_all, dy_own = enter(spots, blocks, dy_pair, swap_c(dy_pair))
    f_down = whole_rows(dy_all, product)
    z_one, z_two, product, f_down, w_d[0] = tie(z_one, z_two, product, f_down, w_d[0])


    f_down = scattered_all(f_down)
    d_one, d_two, lean_m = gated_unit_back(spots, dy_all, z_one, z_two, w_d)
    sent = fold_half(spots, [d_one, d_two], [w_1, w_2])
    sent, d_two, lean_m = tie(sent, d_two, lean_m)

    arrived = swap_c(sent)
    t_two = away(hidden_two, d_two)
    lean_m = total(lean_m[:, 0])
    sent, mine = fold_half(spots, [d_one, d_two], [w_1, w_2], arrived)
    sent, d_one, t_two, product, lean_m = tie(sent, d_one, t_two, product, lean_m)

    crossed = swap_b(sent)
    upper, lower = in_two(t_two)
    upper = sent_a(upper)
    f_one = whole_rows(hidden_two, d_one)
    result = fold_half(spots, [product], [w_d])
    crossed, result, f_one, upper, f_down = tie(crossed, result, f_one, upper, f_down)

    f_one = scattered_all(f_one)
    d_hidden = mine + crossed.astype(F32)
    m_normed = middle * m_scale
    lean = lean_m[:, None] * (2.0 / width)
    d_middle = dy_own.astype(F32) + m_scale * (d_hidden - m_normed * lean)
    d_branch = d_middle.astype(LOW)
    lean_o = jnp.sum(d_middle * branch, axis=-1)
    sent = times_transposed(d_branch, row_half(w_o, 1 - c)).astype(LOW)
    sent, result, d_middle, lean_o = tie(sent, result, d_middle, lean_o)

    arrived = swap_c(sent)
    r_result = swap_c(result)
    y_down = spread_a(f_down)
    lean_o = lean_o + swap_c(lean_o)
    p_out = cross_tokens(lifted, (o_scale * d_middle).astype(LOW)).astype(LOW)
    p_out = jnp.transpose(p_out.reshape(shards, spread, part, -1), (1, 0, 2, 3))
    p_out = p_out.reshape(spread, width // spread, -1)
    t_out = [lax.dynamic_index_in_dim(p_out, (a + k) % spread, 0, False) for k in range(spread)]
    d_gated = times_transposed(d_branch, row_half(w_o, c)) + arrived.astype(F32)
    sent = columns(d_gated, (1 - b) * own, own).astype(LOW)
    mine = columns(d_gated, b * own, own)
    sent, mine, r_result, t_out, lean_o, y_down = tie(sent, mine, r_result, t_out, lean_o, y_down)

    crossed = swap_b(sent)
    lean_b = swap_b(lean_o)
    r_out = sent_a(t_out[1:])
    result, result_mine = fold_half(spots, [product], [w_d], r_result)
    crossed, result, r_out, lower, lean_b = tie(crossed, result, r_out, lower, lean_b)

    lower = sent_a(lower)
    result = swap_b(result)
    f_out = scattered(sum([x.astype(F32) for x in r_out], t_out[0].astype(F32)).astype(LOW))
    o_normed = attended * o_scale
    d_gated = mine + crossed.astype(F32)
    d_gate = (d_gated * o_normed).astype(LOW)
    lean = (lean_o + lean_b)[:, None] / width
    d_attended = (o_scale * (d_gated * gate - o_normed * lean)).astype(LOW)
    d_query, d_key, d_value = attend_back(rates, ends, z_qk, z_vg, d_attended)
    d_qk = joined(d_query, d_key)
    d_vg = joined(d_value, d_gate)
    t_qk = away(hidden_one, d_qk)
    d_qk, d_vg, t_qk, lower, result = tie(d_qk, d_vg, t_qk, lower, result)

    upper_qk, lower_qk = in_two(t_qk)
    upper_qk = sent_a(upper_qk)
    f_two = gradient_rows(spots, spread, 0, hidden_two, d_two, stacked(upper, lower))
    output = to_runs((middle + (result_mine + result.astype(F32))).astype(LOW))
    t_vg = away(hidden_one, d_vg)
    sent = fold_half(spots, [d_qk, d_vg], [w_qk, w_vg])
    sent, t_vg, d_qk, d_vg, f_two, output, upper_qk, lower_qk = tie(
        sent, t_vg, d_qk, d_vg, f_two, output, upper_qk, lower_qk
    )

    f_two = scattered(f_two)
    lower_qk = sent_a(lower_qk)
    x_down = swap_b(y_down)
    y_one = over_spread(f_one)
    arrived = swap_c(sent)
    lean_x = jnp.sum(z_qk * d_qk.astype(F32), axis=-1) + jnp.sum(z_vg * d_vg.astype(F32), axis=-1)
    sent, mine = fold_half(spots, [d_qk, d_vg], [w_qk, w_vg], arrived)
    lean_x = lean_x + swap_c(lean_x)
    sent, mine, lower_qk, t_vg, lean_x, x_down, y_one = tie(
        sent, mine, lower_qk, t_vg, lean_x, x_down, y_one
    )

    crossed = swap_b(sent)
    lean_b = swap_b(lean_x)
    r_vg = sent_a(t_vg)
    f_qk = scattered(gradient_rows(spots, spread, 0, hidden_one, d_qk, stacked(upper_qk, lower_qk)))
    four_down = spread_c(joined(y_down, x_down))
    crossed, d_vg, r_vg, lean_b, four_down = tie(crossed, d_vg, r_vg, lean_b, four_down)

    f_vg = gradient_rows(spots, spread, 0, hidden_one, d_vg, r_vg)
    f_vg, crossed, f_two, f_out = tie(f_vg, crossed, f_two, f_out)

    f_vg = scattered(f_vg)
    d_hidden = mine + crossed.astype(F32)
    x_normed = x_own.astype(F32) * x_scale
    lean = (lean_x + lean_b)[:, None] / width
    input_grad = to_runs((d_middle + x_scale * (d_hidden - x_normed * lean)).astype(LOW))
    y_one = by_spread([f_one, *y_one])
    x_one = swap_b(y_one)
    f_oqk = joined(f_out, f_qk)
    y_two = over_spread(f_two)
    y_oqk = over_spread(f_oqk)
    units = f_one.shape[1]
    [g_down] = place_quarters(spots, four_down, (0, units))
    input_grad, x_one, y_two, y_oqk, f_vg, g_down = tie(input_grad, x_one, y_two, y_oqk, f_vg, g_down)

    x_vg = swap_b(f_vg)
    four_one = spread_c(joined(y_one, x_one))
    x_vg, four_one = tie(x_vg, four_one)

    f_vg = joined(f_vg, x_vg)
    y_vg = over_spread(f_vg)
    y_two = by_spread([f_two, *y_two])
    x_two = swap_b(y_two)
    y_oqk = by_spread([f_oqk, *y_oqk])
    x_oqk = swap_b(y_oqk)
    output, input_grad = send_back(output), send_back(input_grad)
    [g_one] = place_quarters(spots, four_one, (0, units))
    y_vg, x_two, x_oqk, g_one = tie(y_vg, x_two, x_oqk, g_one)

    four_vg = spread_c(by_spread([f_vg, *y_vg]))
    four_two = spread_c(joined(y_two, x_two))
    four_oqk = spread_c(joined(y_oqk, x_oqk))
    g_query, g_key = place_quarters(spots, four_oqk, (own, own), (2 * own, own))
    g_value, g_gate = place_quarters(spots, four_vg, (0, own), (own, own))
    [g_two] = place_quarters(spots, four_two, (0, units))
    g_out = features_in_order(four_oqk, 0, own)
    output, input_grad = as_batches(output), as_batches(input_grad)
    return output, input_grad, g_query, g_key, g_value, g_gate, g_out, g_one, g_two, g_down


def solution(mesh):
    reps, shards = mesh.shape["rep"], mesh.shape["shard"]
    devices = mesh.devices.reshape(reps // GROUP, 2, 2, shards)
    rep = ("a", "b", "c")
    by_tokens = P(None, (*rep, "shard"), None)
    by_rows = P("shard", None)
    return jax.shard_map(
        functools.partial(body, reps, shards),
        mesh=Mesh(devices, AXES),
        in_specs=(by_tokens, by_tokens, P(None, rep, None), P(), *[by_rows] * 8),
        out_specs=(by_tokens, by_tokens, *[by_rows] * 8),
        check_vma=False,
    )
```

```python
import functools

import jax
import jax.numpy as jnp
from jax import lax
from jax.experimental import pallas as pl
from jax.experimental.pallas import tpu as pltpu
from jax.sharding import Mesh, PartitionSpec as P

HEADS = 16
HEAD_DIM = 128
STREAM = 1024
GROUP = 4
BLOCK = 256
TILE = 256
EPSILON = 1e-06
AXES = ("a", "b", "c", "shard")
OWNERS = ("a", "shard")
LOW = jnp.bfloat16
F32 = jnp.float32


def matmul(former, latter):
    return jnp.dot(former, latter, preferred_element_type=F32)


def times_transposed(former, latter):
    return lax.dot_general(former, latter, (((1,), (1,)), ((), ())), preferred_element_type=F32)


def cross_tokens(former, latter):
    return lax.dot_general(former, latter, (((0,), (0,)), ((), ())), preferred_element_type=F32)


def masked_decay(rate, ends, first, columns):
    row = first + lax.broadcasted_iota(jnp.int32, (BLOCK, 1), 0)
    column = lax.broadcasted_iota(jnp.int32, (1, columns), 1)
    begin = jnp.zeros((BLOCK, 1), jnp.int32)
    for end in ends:
        begin = jnp.where(row >= end, end, begin)
    falling = jnp.exp(-rate * (row - first).astype(F32))
    rising = jnp.exp(rate * (column - first).astype(F32))
    allowed = (column <= row) & (column >= begin)
    return jnp.where(allowed, falling * rising, 0.0)


def attend_kernel(rates, ends, zq_ref, zk_ref, zv_ref, out_ref):
    stream, head = pl.program_id(0), pl.program_id(1)
    rate = rates[head]
    bounds = [ends[stream, i] for i in range(ends.shape[1])]
    zq, zk = zq_ref[...], zk_ref[...]
    q = (zq * jax.nn.sigmoid(zq)).astype(LOW)
    k = (zk * jax.nn.sigmoid(zk)).astype(LOW)
    v = zv_ref[...].astype(LOW)
    for first in range(0, STREAM, BLOCK):
        columns = first + BLOCK
        mask = masked_decay(rate, bounds, first, columns)
        scores = times_transposed(q[first:columns], k[:columns])
        weights = (scores * mask).astype(LOW)
        out_ref[first:columns, :] = matmul(weights, v[:columns])


def attend_back_kernel(
    rates, ends, zq_ref, zk_ref, zv_ref, do_ref, dzq_ref, dzk_ref, dzv_ref, dk_ref, dv_ref
):
    stream, head = pl.program_id(0), pl.program_id(1)
    rate = rates[head]
    bounds = [ends[stream, i] for i in range(ends.shape[1])]
    zq, zk = zq_ref[...], zk_ref[...]
    sig_q, sig_k = jax.nn.sigmoid(zq), jax.nn.sigmoid(zk)
    q = (zq * sig_q).astype(LOW)
    k = (zk * sig_k).astype(LOW)
    slope_q = sig_q * (1.0 + zq * (1.0 - sig_q))
    v = zv_ref[...].astype(LOW)
    d_o = do_ref[...]
    dk_ref[...] = jnp.zeros_like(dk_ref)
    dv_ref[...] = jnp.zeros_like(dv_ref)
    for first in range(0, STREAM, BLOCK):
        columns = first + BLOCK
        rows = slice(first, columns)
        mask = masked_decay(rate, bounds, first, columns)
        weights = (times_transposed(q[rows], k[:columns]) * mask).astype(LOW)
        d_scores = (times_transposed(d_o[rows], v[:columns]) * mask).astype(LOW)
        dzq_ref[rows, :] = (matmul(d_scores, k[:columns]) * slope_q[rows]).astype(LOW)
        dk_ref[:columns, :] += cross_tokens(d_scores, q[rows])
        dv_ref[:columns, :] += cross_tokens(weights, d_o[rows])
    dzk_ref[...] = (dk_ref[...] * (sig_k * (1.0 + zk * (1.0 - sig_k)))).astype(LOW)
    dzv_ref[...] = dv_ref[...].astype(LOW)


def head_block(offset=0):
    return pl.BlockSpec((STREAM, HEAD_DIM), lambda g, h, *_: (g, h + offset))


def attend(rates, ends, z_qk, z_vg):
    heads, streams = rates.shape[0], ends.shape[0]
    work = streams * heads * STREAM * STREAM
    return pl.pallas_call(
        attend_kernel,
        out_shape=jax.ShapeDtypeStruct((streams * STREAM, heads * HEAD_DIM), F32),
        grid_spec=pltpu.PrefetchScalarGridSpec(
            num_scalar_prefetch=2,
            grid=(streams, heads),
            in_specs=[head_block(), head_block(heads), head_block()],
            out_specs=head_block(),
        ),
        compiler_params=pltpu.CompilerParams(vmem_limit_bytes=40 << 20),
        cost_estimate=pl.CostEstimate(
            flops=4 * work * HEAD_DIM, transcendentals=work // 64,
            bytes_accessed=streams * heads * STREAM * HEAD_DIM * 16,
        ),
        name="attend",
    )(rates, ends, z_qk, z_qk, z_vg)


def attend_back(rates, ends, z_qk, z_vg, d_o):
    heads, streams = rates.shape[0], ends.shape[0]
    work = streams * heads * STREAM * STREAM
    return pl.pallas_call(
        attend_back_kernel,
        out_shape=[jax.ShapeDtypeStruct((streams * STREAM, heads * HEAD_DIM), LOW)] * 3,
        grid_spec=pltpu.PrefetchScalarGridSpec(
            num_scalar_prefetch=2,
            grid=(streams, heads),
            in_specs=[head_block(), head_block(heads), head_block(), head_block()],
            out_specs=[head_block()] * 3,
            scratch_shapes=[pltpu.VMEM((STREAM, HEAD_DIM), F32)] * 2,
        ),
        compiler_params=pltpu.CompilerParams(vmem_limit_bytes=40 << 20),
        cost_estimate=pl.CostEstimate(
            flops=10 * work * HEAD_DIM, transcendentals=work // 64,
            bytes_accessed=streams * heads * STREAM * HEAD_DIM * 20,
        ),
        name="attend_back",
    )(rates, ends, z_qk, z_qk, z_vg, d_o)


def chunk_copies(chunks, buffer, sems, turn, half=None):
    count, size = len(chunks), chunks[0].shape[0]
    if count == 1:
        rows = buffer.shape[0]
        first = 0 if half is None else pl.multiple_of(half * rows, rows)
        return [(None, pltpu.make_async_copy(chunks[0].at[pl.ds(first, rows)], buffer, sems.at[0]))]
    copies = []
    for k, chunk in enumerate(chunks):
        index = lax.rem(turn - k + count, count)
        wanted = None
        if half is not None:
            wanted = lax.div(index, count // 2) == half
            index = lax.rem(index, count // 2)
        target = buffer.at[pl.ds(pl.multiple_of(index * size, size), size)]
        copies.append((wanted, pltpu.make_async_copy(chunk, target, sems.at[k])))
    return copies


def each(copies, act):
    for wanted, copy in copies:
        if wanted is None:
            act(copy)
        else:
            pl.when(wanted)(functools.partial(act, copy))


def start(copies):
    each(copies, lambda copy: copy.start())


def finish(copies):
    each(copies, lambda copy: copy.wait())


def estimate(flops, *arrays):
    moved = sum(x.size * x.dtype.itemsize for x in arrays)
    return pl.CostEstimate(flops=flops, transcendentals=0, bytes_accessed=moved)


def limit(mebibytes):
    return pltpu.CompilerParams(vmem_limit_bytes=mebibytes << 20)


ANYWHERE = pl.BlockSpec(memory_space=pl.ANY)


def weight_buffer(chunks, share=1):
    size = len(chunks) * chunks[0].shape[0] // share
    return [pltpu.VMEM((size, chunks[0].shape[1]), LOW), pltpu.SemaphoreType.DMA((len(chunks),))]


def tile_rows(width, column=0):
    return pl.BlockSpec((TILE, width), lambda i, *_: (i, column))


def joined_rows(width, tiles):
    spec = pl.BlockSpec((TILE, width), lambda i, s: (i // (2 * tiles) * tiles + i % tiles, 0))
    return [spec, spec]


def enter_kernel(tiles, blocks, project, spots, own_ref, other_ref, *refs):
    i = pl.program_id(0)
    mine = lax.rem(lax.div(i, tiles), 2) == spots[0]
    rows = jnp.where(mine, own_ref[...], other_ref[...])
    part = rows.shape[1] // len(blocks)
    permuted = jnp.concatenate([rows[:, n * part : (n + 1) * part] for n in blocks], axis=1)
    if not project:
        all_ref, quarter_ref = refs
        all_ref[...] = permuted
        held = all_ref
    else:
        chunks, (h_ref, z_ref, scale_ref, quarter_ref, held, buffer, sems) = refs[:-7], refs[-7:]
        held[...] = permuted
        copies = chunk_copies(chunks, buffer, sems, spots[2])

        @pl.when(i == 0)
        def _():
            start(copies)

        x = rows.astype(F32)
        scale = lax.rsqrt(jnp.mean(x * x, axis=-1, keepdims=True) + EPSILON)
        scale_ref[...] = scale
        hidden = (permuted.astype(F32) * scale).astype(LOW)
        h_ref[...] = hidden

        @pl.when(i == 0)
        def _():
            finish(copies)

        z_ref[...] = matmul(hidden, buffer[...])
    size = quarter_ref.shape[1]
    quarter_ref[...] = held[:, pl.ds(pl.multiple_of(spots[1] * size, size), size)]


def enter(spots, blocks, own, other, chunks=()):
    width = own.shape[1]
    count, tiles = 2 * own.shape[0], own.shape[0] // TILE // 2
    shape = jax.ShapeDtypeStruct
    quarter = shape((count, width // GROUP), LOW)
    if chunks:
        columns = chunks[0].shape[1]
        outs = [shape((count, width), LOW), shape((count, columns), F32), shape((count, 1), F32), quarter]
        scratch = [pltpu.VMEM((TILE, width), LOW), *weight_buffer(chunks)]
    else:
        columns, scratch = 0, []
        outs = [shape((count, width), LOW), quarter]
    return pl.pallas_call(
        functools.partial(enter_kernel, tiles, blocks, bool(chunks)),
        out_shape=outs,
        grid_spec=pltpu.PrefetchScalarGridSpec(
            num_scalar_prefetch=1,
            grid=(count // TILE,),
            in_specs=joined_rows(width, tiles) + [ANYWHERE] * len(chunks),
            out_specs=[tile_rows(o.shape[1]) for o in outs],
            scratch_shapes=scratch,
        ),
        compiler_params=limit(40),
        cost_estimate=estimate(2 * count * width * columns, own, other, *chunks, *outs),
        name="enter",
    )(spots, own, other, *chunks)


def project_kernel(spots, h_ref, *refs):
    chunks, (z_ref, buffer, sems) = refs[:-3], refs[-3:]
    copies = chunk_copies(chunks, buffer, sems, spots[2])

    @pl.when(pl.program_id(0) == 0)
    def _():
        start(copies)
        finish(copies)

    z_ref[...] = matmul(h_ref[...], buffer[...])


def project(spots, hidden, chunks):
    count, width = hidden.shape
    out = jax.ShapeDtypeStruct((count, chunks[0].shape[1]), F32)
    return pl.pallas_call(
        project_kernel,
        out_shape=out,
        grid_spec=pltpu.PrefetchScalarGridSpec(
            num_scalar_prefetch=1,
            grid=(count // TILE,),
            in_specs=[tile_rows(width)] + [ANYWHERE] * len(chunks),
            out_specs=tile_rows(out.shape[1]),
            scratch_shapes=weight_buffer(chunks),
        ),
        compiler_params=limit(40),
        cost_estimate=estimate(2 * count * width * out.shape[1], hidden, *chunks, out),
        name="project",
    )(spots, hidden, *chunks)


def unit_kernel(spots, own_ref, other_ref, *refs):
    chunks, rest = refs[:-9], refs[-9:]
    h_ref, one_ref, two_ref, product_ref, scale_ref, first, second, sem_one, sem_two = rest
    split = len(chunks) // 2
    copies = [
        chunk_copies(chunks[:split], first, sem_one, spots[2]),
        chunk_copies(chunks[split:], second, sem_two, spots[2]),
    ]
    begins = pl.program_id(0) == 0

    @pl.when(begins)
    def _():
        start(copies[0])
        start(copies[1])

    mine, other = own_ref[...], other_ref[...]
    swapped = spots[0] == 1
    middle = jnp.concatenate(
        [jnp.where(swapped, other, mine), jnp.where(swapped, mine, other)], axis=1
    ).astype(F32)
    scale = lax.rsqrt(jnp.mean(middle * middle, axis=-1, keepdims=True) + EPSILON)
    scale_ref[...] = scale
    hidden = (middle * scale).astype(LOW)
    h_ref[...] = hidden

    @pl.when(begins)
    def _():
        finish(copies[0])

    z_one = matmul(hidden, first[...])

    @pl.when(begins)
    def _():
        finish(copies[1])

    z_two = matmul(hidden, second[...])
    one_ref[...] = z_one.astype(LOW)
    two_ref[...] = z_two.astype(LOW)
    product_ref[...] = (z_one * z_two).astype(LOW)


def gated_unit(spots, own, other, first, second):
    count, width, units = own.shape[0], 2 * own.shape[1], first[0].shape[1]
    shape = jax.ShapeDtypeStruct
    outs = [shape((count, width), LOW)] + [shape((count, units), LOW)] * 3 + [shape((count, 1), F32)]
    (buffer, sems) = weight_buffer(first)
    return pl.pallas_call(
        unit_kernel,
        out_shape=outs,
        grid_spec=pltpu.PrefetchScalarGridSpec(
            num_scalar_prefetch=1,
            grid=(count // TILE,),
            in_specs=[tile_rows(width // 2)] * 2 + [ANYWHERE] * (2 * len(first)),
            out_specs=[tile_rows(o.shape[1]) for o in outs],
            scratch_shapes=[buffer, buffer, sems, sems],
        ),
        compiler_params=limit(48),
        cost_estimate=estimate(4 * count * width * units, own, other, *first, *second, *outs),
        name="gated_unit",
    )(spots, own, other, *first, *second)


def unit_back_kernel(spots, dy_ref, one_ref, two_ref, *refs):
    chunks, (d_one_ref, d_two_ref, sum_ref, buffer, sems) = refs[:-5], refs[-5:]
    copies = chunk_copies(chunks, buffer, sems, spots[2])

    @pl.when(pl.program_id(0) == 0)
    def _():
        start(copies)
        finish(copies)

    d_product = matmul(dy_ref[...], buffer[...])
    z_one, z_two = one_ref[...].astype(F32), two_ref[...].astype(F32)
    d_one = d_product * z_two
    d_one_ref[...] = d_one.astype(LOW)
    d_two_ref[...] = (d_product * z_one).astype(LOW)
    sum_ref[...] = jnp.sum(d_one * z_one, axis=-1, keepdims=True)


def gated_unit_back(spots, dy, z_one, z_two, chunks):
    count, width, units = dy.shape[0], dy.shape[1], z_one.shape[1]
    shape = jax.ShapeDtypeStruct
    outs = [shape((count, units), LOW)] * 2 + [shape((count, 1), F32)]
    return pl.pallas_call(
        unit_back_kernel,
        out_shape=outs,
        grid_spec=pltpu.PrefetchScalarGridSpec(
            num_scalar_prefetch=1,
            grid=(count // TILE,),
            in_specs=[tile_rows(width), tile_rows(units), tile_rows(units)] + [ANYWHERE] * len(chunks),
            out_specs=[tile_rows(o.shape[1]) for o in outs],
            scratch_shapes=weight_buffer(chunks),
        ),
        compiler_params=limit(40),
        cost_estimate=estimate(2 * count * width * units, dy, z_one, z_two, *chunks, *outs),
        name="gated_unit_back",
    )(spots, dy, z_one, z_two, *chunks)


def fold_kernel(members, keeps, spots, *refs):
    values, refs = refs[:members], refs[members:]
    arrived, refs = (refs[0], refs[1:]) if keeps else (None, refs)
    outs = 2 if keeps else 1
    chunks, refs = refs[: -outs - 2 * members], refs[-outs - 2 * members :]
    outs, buffers, sems = refs[:outs], refs[outs : outs + members], refs[outs + members :]
    each_count = len(chunks) // members
    half = spots[0] if keeps else 1 - spots[0]
    begins = pl.program_id(0) == 0
    copies = [
        chunk_copies(chunks[m * each_count : (m + 1) * each_count], buffers[m], sems[m], spots[2], half)
        for m in range(members)
    ]

    @pl.when(begins)
    def _():
        for m in range(members):
            start(copies[m])

    whole = None
    for m in range(members):
        pl.when(begins)(functools.partial(finish, copies[m]))
        term = times_transposed(values[m][...], buffers[m][...])
        whole = term if whole is None else whole + term
    if not keeps:
        outs[0][...] = whole.astype(LOW)
    else:
        whole = whole + arrived[...].astype(F32)
        size = whole.shape[1] // 2
        upper = spots[3] == 1
        outs[0][...] = jnp.where(upper, whole[:, :size], whole[:, size:]).astype(LOW)
        outs[1][...] = jnp.where(upper, whole[:, size:], whole[:, :size])


def fold_half(spots, values, weights, arrived=None):
    count = values[0].shape[0]
    half = len(weights[0]) * weights[0][0].shape[0] // 2
    shape = jax.ShapeDtypeStruct
    if arrived is None:
        outs, extra = [shape((count, half), LOW)], []
    else:
        outs, extra = [shape((count, half // 2), LOW), shape((count, half // 2), F32)], [arrived]
    buffers, sems = zip(*[weight_buffer(w, 2) for w in weights])
    chunks = [x for w in weights for x in w]
    flops = sum(2 * count * half * v.shape[1] for v in values)
    found = pl.pallas_call(
        functools.partial(fold_kernel, len(values), arrived is not None),
        out_shape=outs,
        grid_spec=pltpu.PrefetchScalarGridSpec(
            num_scalar_prefetch=1,
            grid=(count // TILE,),
            in_specs=[tile_rows(v.shape[1]) for v in values]
            + [tile_rows(half)] * len(extra)
            + [ANYWHERE] * len(chunks),
            out_specs=[tile_rows(o.shape[1]) for o in outs],
            scratch_shapes=[*buffers, *sems],
        ),
        compiler_params=limit(40),
        cost_estimate=estimate(flops, *values, *extra, *chunks[: len(chunks) // 2], *outs),
        name="fold_half",
    )(spots, *values, *extra, *chunks)
    return found[0] if arrived is None else found


def gradient_kernel(spots, left_ref, right_ref, *refs):
    found = cross_tokens(left_ref[...], right_ref[...])
    for arrived_ref in refs[:-1]:
        found = found + arrived_ref[...].astype(F32)
    refs[-1][...] = found.astype(LOW)


def gradient_rows(spots, spread, k, left, right, arrived=()):
    count, columns = right.shape
    rows = left.shape[1] // (1 if k is None else spread)
    tiles = rows // TILE

    def block(i, s):
        return (0, i if k is None else lax.rem(s[2] + k, spread) * tiles + i)

    out = jax.ShapeDtypeStruct((rows, columns), LOW)
    return pl.pallas_call(
        gradient_kernel,
        out_shape=out,
        grid_spec=pltpu.PrefetchScalarGridSpec(
            num_scalar_prefetch=1,
            grid=(tiles,),
            in_specs=[
                pl.BlockSpec((count, TILE), block),
                pl.BlockSpec((count, columns), lambda i, s: (0, 0), pipeline_mode=pl.Buffered(1)),
            ]
            + [tile_rows(columns)] * len(arrived),
            out_specs=tile_rows(columns),
        ),
        compiler_params=limit(40),
        cost_estimate=estimate(2 * count * rows * columns, right, out, out, *arrived),
        name="gradient_rows",
    )(spots, left, right, *arrived)


def place_kernel(cuts, spots, *refs):
    quarter = pl.program_id(0)
    cross = lax.rem(lax.div(quarter, 2) + spots[0], 2) * 2 + lax.rem(lax.rem(quarter, 2) + spots[3], 2)
    for n in range(4):

        @pl.when(cross == n)
        def _():
            for (first, size), out_ref in zip(cuts, refs[4:]):
                out_ref[...] = refs[n][:, first : first + size].astype(F32)


def place_quarters(spots, pairs, *cuts):
    rows, columns = pairs[0].shape[0], pairs[0].shape[1] // 2
    outs = [jax.ShapeDtypeStruct((rows, GROUP * size), F32) for _, size in cuts]

    def block(index):
        return pl.BlockSpec((rows, columns), lambda q, s: (0, index), pipeline_mode=pl.Buffered(1))

    return pl.pallas_call(
        functools.partial(place_kernel, cuts),
        out_shape=outs,
        grid_spec=pltpu.PrefetchScalarGridSpec(
            num_scalar_prefetch=1,
            grid=(GROUP,),
            in_specs=[block(0), block(1), block(0), block(1)],
            out_specs=[pl.BlockSpec((rows, size), lambda q, s: (0, q)) for _, size in cuts],
        ),
        compiler_params=limit(40),
        cost_estimate=estimate(0, *pairs, *outs),
        name="place_quarters",
    )(spots, pairs[0], pairs[0], pairs[1], pairs[1])


def tie(*values):
    return lax.optimization_barrier(values)


def body(reps, shards, tokens, cotangent, lengths, decay_rates, *weights):
    spread = reps // GROUP
    place = lax.axis_index("shard")
    a, b, c = lax.axis_index("a"), lax.axis_index("b"), lax.axis_index("c")
    quarter = 2 * c + b
    micro, run, width = tokens.shape
    half, own = width // 2, width // GROUP
    streams = micro * GROUP // shards
    per_block = STREAM // run // GROUP * streams
    rows = width // shards
    part = rows // spread
    columns = functools.partial(lax.dynamic_slice_in_dim, axis=1)
    spots = jnp.stack([c, quarter, a, b]).astype(jnp.int32)
    blocks = [z * spread + k for k in range(spread) for z in range(shards)]

    def move(x, target):
        pairs = [(r * shards + s, target(r) * shards + s) for r in range(reps) for s in range(shards)]
        return lax.ppermute(x, AXES, pairs)

    def swap_c(x):
        return move(x, lambda r: r ^ 1)

    def swap_b(x):
        return move(x, lambda r: r ^ 2)

    def joined(*parts):
        return jnp.concatenate(parts, axis=1)

    def shift_a(x, k):
        return move(x, lambda r: (r + GROUP * k) % reps)

    def ordered(index, mine, other, axis):
        return jnp.where(
            index == 0,
            jnp.concatenate([mine, other], axis),
            jnp.concatenate([other, mine], axis),
        )


    def batch_of(s):
        return s // (shards // micro)

    def origin(r, s, p):
        run_id = (r % GROUP) * per_block + p
        stream, piece = run_id // shards, run_id % shards
        member = s % GROUP if streams == 1 else 2 * stream + s % 2
        return (r // GROUP) * GROUP + member, piece

    def routes(p):
        found = []
        for r in range(reps):
            for s in range(shards):
                from_r, from_s = origin(r, s, p ^ batch_of(s))
                found.append((from_r * shards + from_s, r * shards + s))
        return found

    def natural(x):
        return jnp.concatenate(
            [
                x[:, (k * shards + z) * part : (k * shards + z + 1) * part]
                for z in range(shards)
                for k in range(spread)
            ],
            axis=1,
        )

    def bring(x):
        arrived = [
            lax.ppermute(lax.dynamic_index_in_dim(x, (place + p) % 2, 0, False), AXES, routes(p))
            for p in range(2)
        ]
        return ordered(batch_of(place), *arrived, 0)

    def send_back(x):
        slots = natural(x).reshape(2, run, width)
        return [
            lax.ppermute(
                lax.dynamic_index_in_dim(slots, (batch_of(place) + p) % 2, 0, False),
                AXES,
                [(to, origin) for origin, to in routes(p)],
            )
            for p in range(2)
        ]

    def as_batches(arrived):
        return ordered(place % 2, arrived[0][None], arrived[1][None], 0)


    def gather_b(x):
        return ordered(b, x, swap_b(x), 1)

    def gather_c(x):
        return ordered(c, x, swap_c(x), 1)

    def gather_rows_b(x):
        return ordered(b, x, swap_b(x), 0)

    def total(x):
        x = x + swap_c(x)
        return x + swap_b(x)

    def fold_c(product):
        sent = swap_c(product(1 - c).astype(LOW))
        return product(c) + sent.astype(F32)

    def fold_b(x):
        sent = swap_b(columns(x, (1 - b) * own, own).astype(LOW))
        return columns(x, b * own, own) + sent.astype(F32)


    pick = functools.partial(lax.dynamic_index_in_dim, keepdims=False)

    def away_b(x):
        cut = x.reshape(2, 2, -1, own)
        return pick(cut, b, 0), swap_b(pick(cut, 1 - b, 0))

    def away_c(mine, arrived):
        both = ordered(b, mine, arrived, 2)
        return pick(both, c, 0), swap_c(pick(both, 1 - c, 0))

    def to_runs(x):
        return ordered(c, *away_c(*away_b(x)), 1)


    def own_features(w):
        count = shards * spread // GROUP
        cut = []
        for i in range(count):
            block = quarter * count + i
            cut.append(columns(w, (block % shards) * rows + (block // shards) * part, part))
        return jnp.concatenate(cut, axis=1)

    def own_units(w):
        return columns(w, quarter * (w.shape[1] // GROUP), w.shape[1] // GROUP)

    def over_shards(*members):
        cut = jnp.concatenate(members, axis=1) if len(members) > 1 else members[0]
        piece = lax.dynamic_slice_in_dim(cut, a * part, part, 0)
        return lax.all_gather(piece, "shard", axis=0, tiled=True)

    def over_owners(w):
        piece = lax.dynamic_slice_in_dim(w, a * part, part, 0)
        return lax.all_gather(piece, OWNERS, axis=0, tiled=True)

    def over_spread(x):
        return [shift_a(x, k) for k in range(1, spread)]

    def by_spread(relative):
        if spread == 2:
            return ordered(a, relative[0], relative[1], 0)
        stacked = jnp.stack(relative, 0)
        pick = functools.partial(lax.dynamic_index_in_dim, axis=0, keepdims=False)
        return jnp.concatenate([pick(stacked, (a - j) % spread) for j in range(spread)], axis=0)

    def in_row_order(x):
        cut = x.reshape(spread, shards, part, -1)
        return jnp.transpose(cut, (1, 0, 2, 3)).reshape(width, -1)

    def row_half(w, h):
        return lax.dynamic_slice_in_dim(w, h * half, half, 0)


    def away(left, right):
        return [gradient_rows(spots, spread, k, left, right) for k in range(1, spread)]

    def in_two(terms):
        middles = [x.shape[0] // 2 for x in terms]
        return [x[:m] for x, m in zip(terms, middles)], [x[m:] for x, m in zip(terms, middles)]

    def stacked(upper, lower):
        return [jnp.concatenate(pair, axis=0) for pair in zip(upper, lower)]

    def sent_a(terms):
        return [shift_a(x, k + 1) for k, x in enumerate(terms)]

    def scattered(x):
        return lax.psum_scatter(x, "shard", scatter_dimension=0, tiled=True)

    def whole_rows(left, right):
        return gradient_rows(spots, spread, None, left, right)

    def scattered_all(x):
        return lax.psum_scatter(x, OWNERS, scatter_dimension=0, tiled=True)

    def summed(left, right, arrived):
        return scattered(gradient_rows(spots, spread, 0, left, right, arrived))

    def spread_a(x):
        return by_spread([x] + over_spread(x))

    def spread_b(x):
        return jnp.concatenate([x, swap_b(x)], axis=1)

    def spread_c(pair):
        return pair, swap_c(pair)

    def features_in_order(pairs, first, size):
        full = pairs[0].shape[1] // 2
        cut = [x[:, i * full + first : i * full + first + size] for x in pairs for i in range(2)]
        pair = [ordered(b, cut[n], cut[n + 1], 1) for n in (0, 2)]
        return natural(ordered(c, pair[0], pair[1], 1)).astype(F32)


    w_query, w_key, w_value, w_gate, w_out, w_one, w_two, w_down = weights
    g_qk = over_shards(own_units(w_query), own_units(w_key))
    g_vg = over_shards(own_units(w_value), own_units(w_gate))
    g_o = over_shards(own_features(w_out))
    g_1 = over_shards(own_units(w_one))
    g_2 = over_shards(own_units(w_two))
    w_d = [over_owners(own_units(w_down))]

    heads = HEADS // GROUP
    rates = lax.dynamic_slice_in_dim(decay_rates, quarter * heads, heads, 0)
    cuts = gather_rows_b(lengths.reshape(1, -1))
    cuts = ordered(c, cuts, swap_c(cuts), 0).reshape(GROUP, micro, -1)
    if streams == 1:
        batch = place // GROUP
        member = place % GROUP
        chosen = lax.dynamic_slice_in_dim(cuts, 2 * (member % 2) + member // 2, 1, 0)
    else:
        batch = place // 2
        chosen = lax.dynamic_index_in_dim(cuts.reshape(2, 2, micro, -1), place % 2, 0, False)
    chosen = lax.dynamic_index_in_dim(chosen, batch, 1, False)
    seq_ends = [chosen[:, 0]]
    for i in range(1, chosen.shape[1]):
        seq_ends.append(seq_ends[-1] + chosen[:, i])
    ends = jnp.stack(seq_ends, axis=1)

    x_run = bring(tokens)
    x_run, g_qk = tie(x_run, g_qk)

    x_pair = gather_rows_b(x_run)
    s_qk = over_spread(g_qk)
    x_pair, s_qk, g_vg = tie(x_pair, s_qk, g_vg)

    s_vg = over_spread(g_vg)
    w_qk = [g_qk, *s_qk]
    hidden_one, z_qk, x_scale, x_own = enter(spots, blocks, x_pair, swap_c(x_pair), w_qk)
    z_qk, hidden_one, s_vg, g_o = tie(z_qk, hidden_one, s_vg, g_o)

    s_o = over_spread(g_o)
    w_vg = [g_vg, *s_vg]
    z_vg = project(spots, hidden_one, w_vg)
    attended = attend(rates, ends, z_qk, z_vg)
    gate = z_vg[:, own:]
    o_scale = lax.rsqrt(total(jnp.sum(attended * attended, axis=-1)) / width + EPSILON)[:, None]
    lifted = (attended * gate).astype(LOW)
    lifted, s_o, g_1, cotangent = tie(lifted, s_o, g_1, cotangent)

    s_1 = over_spread(g_1)
    lifted = gather_b(lifted)
    lifted, s_1, g_2, o_scale, cotangent = tie(lifted, s_1, g_2, o_scale, cotangent)

    s_2 = over_spread(g_2)
    dy_run = bring(cotangent)
    lifted = gather_c(lifted)
    w_o = in_row_order(by_spread([g_o, *s_o]))
    branch = o_scale * matmul(lifted, w_o)
    middle = x_own.astype(F32) + branch
    low_middle = gather_b(middle.astype(LOW))
    low_middle, s_2, dy_run = tie(low_middle, s_2, dy_run)

    other_middle = swap_c(low_middle)
    dy_other = swap_b(dy_run)
    w_1, w_2 = [g_1, *s_1], [g_2, *s_2]
    hidden_two, z_one, z_two, product, m_scale = gated_unit(spots, low_middle, other_middle, w_1, w_2)
    z_one, z_two, product, dy_other = tie(z_one, z_two, product, dy_other)

    dy_pair = ordered(b, dy_run, dy_other, 0)
    dy_all, dy_own = enter(spots, blocks, dy_pair, swap_c(dy_pair))
    f_down = whole_rows(dy_all, product)
    z_one, z_two, product, f_down, w_d[0] = tie(z_one, z_two, product, f_down, w_d[0])


    f_down = scattered_all(f_down)
    d_one, d_two, lean_m = gated_unit_back(spots, dy_all, z_one, z_two, w_d)
    sent = fold_half(spots, [d_one, d_two], [w_1, w_2])
    sent, d_two, lean_m = tie(sent, d_two, lean_m)

    arrived = swap_c(sent)
    t_two = away(hidden_two, d_two)
    lean_m = lean_m[:, 0]
    lean_c = swap_c(lean_m)
    sent, mine = fold_half(spots, [d_one, d_two], [w_1, w_2], arrived)
    sent, d_one, t_two, product, lean_c = tie(sent, d_one, t_two, product, lean_c)

    crossed = swap_b(sent)
    lean_m = lean_m + lean_c
    lean_b = swap_b(lean_m)
    upper, lower = in_two(t_two)
    upper = sent_a(upper)
    f_one = whole_rows(hidden_two, d_one)
    result = fold_half(spots, [product], [w_d])
    crossed, result, f_one, upper, f_down, lean_b = tie(crossed, result, f_one, upper, f_down, lean_b)

    f_one = scattered_all(f_one)
    d_hidden = mine + crossed.astype(F32)
    m_normed = middle * m_scale
    lean = (lean_m + lean_b)[:, None] * (2.0 / width)
    d_middle = dy_own.astype(F32) + m_scale * (d_hidden - m_normed * lean)
    d_branch = d_middle.astype(LOW)
    lean_o = jnp.sum(d_middle * branch, axis=-1)
    sent = times_transposed(d_branch, row_half(w_o, 1 - c)).astype(LOW)
    sent, result, d_middle, lean_o = tie(sent, result, d_middle, lean_o)

    arrived = swap_c(sent)
    r_result = swap_c(result)
    y_down = spread_a(f_down)
    lean_o = lean_o + swap_c(lean_o)
    p_out = cross_tokens(lifted, (o_scale * d_middle).astype(LOW)).astype(LOW)
    p_out = jnp.transpose(p_out.reshape(shards, spread, part, -1), (1, 0, 2, 3))
    p_out = p_out.reshape(spread, width // spread, -1)
    t_out = [lax.dynamic_index_in_dim(p_out, (a + k) % spread, 0, False) for k in range(spread)]
    d_gated = times_transposed(d_branch, row_half(w_o, c)) + arrived.astype(F32)
    sent = columns(d_gated, (1 - b) * own, own).astype(LOW)
    mine = columns(d_gated, b * own, own)
    sent, mine, r_result, t_out, lean_o, y_down = tie(sent, mine, r_result, t_out, lean_o, y_down)

    crossed = swap_b(sent)
    lean_b = swap_b(lean_o)
    r_out = sent_a(t_out[1:])
    result, result_mine = fold_half(spots, [product], [w_d], r_result)
    crossed, result, r_out, lower, lean_b = tie(crossed, result, r_out, lower, lean_b)

    lower = sent_a(lower)
    result = swap_b(result)
    f_out = scattered(sum([x.astype(F32) for x in r_out], t_out[0].astype(F32)).astype(LOW))
    o_normed = attended * o_scale
    d_gated = mine + crossed.astype(F32)
    d_gate = (d_gated * o_normed).astype(LOW)
    lean = (lean_o + lean_b)[:, None] / width
    d_attended = (o_scale * (d_gated * gate - o_normed * lean)).astype(LOW)
    d_query, d_key, d_value = attend_back(rates, ends, z_qk, z_vg, d_attended)
    d_qk = joined(d_query, d_key)
    d_vg = joined(d_value, d_gate)
    t_qk = away(hidden_one, d_qk)
    d_qk, d_vg, t_qk, lower, result = tie(d_qk, d_vg, t_qk, lower, result)

    upper_qk, lower_qk = in_two(t_qk)
    upper_qk = sent_a(upper_qk)
    f_two = gradient_rows(spots, spread, 0, hidden_two, d_two, stacked(upper, lower))
    output = to_runs((middle + (result_mine + result.astype(F32))).astype(LOW))
    t_vg = away(hidden_one, d_vg)
    sent = fold_half(spots, [d_qk, d_vg], [w_qk, w_vg])
    sent, t_vg, d_qk, d_vg, f_two, output, upper_qk, lower_qk = tie(
        sent, t_vg, d_qk, d_vg, f_two, output, upper_qk, lower_qk
    )

    f_two = scattered(f_two)
    lower_qk = sent_a(lower_qk)
    x_down = swap_b(y_down)
    y_one = over_spread(f_one)
    arrived = swap_c(sent)
    lean_x = jnp.sum(z_qk * d_qk.astype(F32), axis=-1) + jnp.sum(z_vg * d_vg.astype(F32), axis=-1)
    sent, mine = fold_half(spots, [d_qk, d_vg], [w_qk, w_vg], arrived)
    lean_x = lean_x + swap_c(lean_x)
    sent, mine, lower_qk, t_vg, lean_x, x_down, y_one = tie(
        sent, mine, lower_qk, t_vg, lean_x, x_down, y_one
    )

    crossed = swap_b(sent)
    lean_b = swap_b(lean_x)
    r_vg = sent_a(t_vg)
    f_qk = scattered(gradient_rows(spots, spread, 0, hidden_one, d_qk, stacked(upper_qk, lower_qk)))
    four_down = spread_c(joined(y_down, x_down))
    crossed, d_vg, r_vg, lean_b, four_down = tie(crossed, d_vg, r_vg, lean_b, four_down)

    f_vg = gradient_rows(spots, spread, 0, hidden_one, d_vg, r_vg)
    f_vg, crossed, f_two, f_out = tie(f_vg, crossed, f_two, f_out)

    f_vg = scattered(f_vg)
    d_hidden = mine + crossed.astype(F32)
    x_normed = x_own.astype(F32) * x_scale
    lean = (lean_x + lean_b)[:, None] / width
    input_grad = to_runs((d_middle + x_scale * (d_hidden - x_normed * lean)).astype(LOW))
    output = send_back(output)
    y_one = by_spread([f_one, *y_one])
    x_one = swap_b(y_one)
    f_oqk = joined(f_out, f_qk)
    x_oqk = swap_b(f_oqk)
    y_two = over_spread(f_two)
    units = f_one.shape[1]
    [g_down] = place_quarters(spots, four_down, (0, units))
    input_grad, output, x_one, y_two, x_oqk, f_vg, g_down = tie(
        input_grad, output, x_one, y_two, x_oqk, f_vg, g_down
    )

    x_vg = swap_b(f_vg)
    four_one = spread_c(joined(y_one, x_one))
    x_vg, four_one = tie(x_vg, four_one)

    f_vg = joined(f_vg, x_vg)
    y_vg = over_spread(f_vg)
    y_two = by_spread([f_two, *y_two])
    x_two = swap_b(y_two)
    f_oqk = joined(f_oqk, x_oqk)
    y_oqk = over_spread(f_oqk)
    input_grad = send_back(input_grad)
    [g_one] = place_quarters(spots, four_one, (0, units))
    y_vg, x_two, y_oqk, input_grad, g_one = tie(y_vg, x_two, y_oqk, input_grad, g_one)

    four_vg = spread_c(by_spread([f_vg, *y_vg]))
    four_two = spread_c(joined(y_two, x_two))
    four_oqk = spread_c(by_spread([f_oqk, *y_oqk]))
    g_query, g_key = place_quarters(spots, four_oqk, (own, own), (2 * own, own))
    g_value, g_gate = place_quarters(spots, four_vg, (0, own), (own, own))
    [g_two] = place_quarters(spots, four_two, (0, units))
    g_out = features_in_order(four_oqk, 0, own)
    output, input_grad = as_batches(output), as_batches(input_grad)
    return output, input_grad, g_query, g_key, g_value, g_gate, g_out, g_one, g_two, g_down


def solution(mesh):
    reps, shards = mesh.shape["rep"], mesh.shape["shard"]
    devices = mesh.devices.reshape(reps // GROUP, 2, 2, shards)
    rep = ("a", "b", "c")
    by_tokens = P(None, (*rep, "shard"), None)
    by_rows = P("shard", None)
    return jax.shard_map(
        functools.partial(body, reps, shards),
        mesh=Mesh(devices, AXES),
        in_specs=(by_tokens, by_tokens, P(None, rep, None), P(), *[by_rows] * 8),
        out_specs=(by_tokens, by_tokens, *[by_rows] * 8),
        check_vma=False,
    )
```

```python
import functools

import jax
import jax.numpy as jnp
from jax import lax
from jax.experimental import pallas as pl
from jax.experimental.pallas import tpu as pltpu
from jax.sharding import Mesh, PartitionSpec as P

HEADS = 16
HEAD_DIM = 128
STREAM = 1024
GROUP = 4
BLOCK = 256
TILE = 256
EPSILON = 1e-06
AXES = ("a", "b", "c", "shard")
OWNERS = ("a", "shard")
LOW = jnp.bfloat16
F32 = jnp.float32


def matmul(former, latter):
    return jnp.dot(former, latter, preferred_element_type=F32)


def times_transposed(former, latter):
    return lax.dot_general(former, latter, (((1,), (1,)), ((), ())), preferred_element_type=F32)


def cross_tokens(former, latter):
    return lax.dot_general(former, latter, (((0,), (0,)), ((), ())), preferred_element_type=F32)


def masked_decay(rate, ends, first, columns):
    row = first + lax.broadcasted_iota(jnp.int32, (BLOCK, 1), 0)
    column = lax.broadcasted_iota(jnp.int32, (1, columns), 1)
    begin = jnp.zeros((BLOCK, 1), jnp.int32)
    for end in ends:
        begin = jnp.where(row >= end, end, begin)
    falling = jnp.exp(-rate * (row - first).astype(F32))
    rising = jnp.exp(rate * (column - first).astype(F32))
    allowed = (column <= row) & (column >= begin)
    return jnp.where(allowed, falling * rising, 0.0)


def attend_kernel(rates, ends, zq_ref, zk_ref, zv_ref, out_ref):
    stream, head = pl.program_id(0), pl.program_id(1)
    rate = rates[head]
    bounds = [ends[stream, i] for i in range(ends.shape[1])]
    zq, zk = zq_ref[...], zk_ref[...]
    q = (zq * jax.nn.sigmoid(zq)).astype(LOW)
    k = (zk * jax.nn.sigmoid(zk)).astype(LOW)
    v = zv_ref[...].astype(LOW)
    for first in range(0, STREAM, BLOCK):
        columns = first + BLOCK
        mask = masked_decay(rate, bounds, first, columns)
        scores = times_transposed(q[first:columns], k[:columns])
        weights = (scores * mask).astype(LOW)
        out_ref[first:columns, :] = matmul(weights, v[:columns])


def attend_back_kernel(
    rates, ends, zq_ref, zk_ref, zv_ref, do_ref, dzq_ref, dzk_ref, dzv_ref, dk_ref, dv_ref
):
    stream, head = pl.program_id(0), pl.program_id(1)
    rate = rates[head]
    bounds = [ends[stream, i] for i in range(ends.shape[1])]
    zq, zk = zq_ref[...], zk_ref[...]
    sig_q, sig_k = jax.nn.sigmoid(zq), jax.nn.sigmoid(zk)
    q = (zq * sig_q).astype(LOW)
    k = (zk * sig_k).astype(LOW)
    slope_q = sig_q * (1.0 + zq * (1.0 - sig_q))
    v = zv_ref[...].astype(LOW)
    d_o = do_ref[...]
    dk_ref[...] = jnp.zeros_like(dk_ref)
    dv_ref[...] = jnp.zeros_like(dv_ref)
    for first in range(0, STREAM, BLOCK):
        columns = first + BLOCK
        rows = slice(first, columns)
        mask = masked_decay(rate, bounds, first, columns)
        weights = (times_transposed(q[rows], k[:columns]) * mask).astype(LOW)
        d_scores = (times_transposed(d_o[rows], v[:columns]) * mask).astype(LOW)
        dzq_ref[rows, :] = (matmul(d_scores, k[:columns]) * slope_q[rows]).astype(LOW)
        dk_ref[:columns, :] += cross_tokens(d_scores, q[rows])
        dv_ref[:columns, :] += cross_tokens(weights, d_o[rows])
    dzk_ref[...] = (dk_ref[...] * (sig_k * (1.0 + zk * (1.0 - sig_k)))).astype(LOW)
    dzv_ref[...] = dv_ref[...].astype(LOW)


def head_block(offset=0):
    return pl.BlockSpec((STREAM, HEAD_DIM), lambda g, h, *_: (g, h + offset))


def attend(rates, ends, z_qk, z_vg):
    heads, streams = rates.shape[0], ends.shape[0]
    work = streams * heads * STREAM * STREAM
    return pl.pallas_call(
        attend_kernel,
        out_shape=jax.ShapeDtypeStruct((streams * STREAM, heads * HEAD_DIM), F32),
        grid_spec=pltpu.PrefetchScalarGridSpec(
            num_scalar_prefetch=2,
            grid=(streams, heads),
            in_specs=[head_block(), head_block(heads), head_block()],
            out_specs=head_block(),
        ),
        compiler_params=pltpu.CompilerParams(vmem_limit_bytes=40 << 20),
        cost_estimate=pl.CostEstimate(
            flops=4 * work * HEAD_DIM, transcendentals=work // 64,
            bytes_accessed=streams * heads * STREAM * HEAD_DIM * 16,
        ),
        name="attend",
    )(rates, ends, z_qk, z_qk, z_vg)


def attend_back(rates, ends, z_qk, z_vg, d_o):
    heads, streams = rates.shape[0], ends.shape[0]
    work = streams * heads * STREAM * STREAM
    return pl.pallas_call(
        attend_back_kernel,
        out_shape=[jax.ShapeDtypeStruct((streams * STREAM, heads * HEAD_DIM), LOW)] * 3,
        grid_spec=pltpu.PrefetchScalarGridSpec(
            num_scalar_prefetch=2,
            grid=(streams, heads),
            in_specs=[head_block(), head_block(heads), head_block(), head_block()],
            out_specs=[head_block()] * 3,
            scratch_shapes=[pltpu.VMEM((STREAM, HEAD_DIM), F32)] * 2,
        ),
        compiler_params=pltpu.CompilerParams(vmem_limit_bytes=40 << 20),
        cost_estimate=pl.CostEstimate(
            flops=10 * work * HEAD_DIM, transcendentals=work // 64,
            bytes_accessed=streams * heads * STREAM * HEAD_DIM * 20,
        ),
        name="attend_back",
    )(rates, ends, z_qk, z_qk, z_vg, d_o)


def chunk_copies(chunks, buffer, sems, turn, half=None):
    count, size = len(chunks), chunks[0].shape[0]
    if count == 1:
        rows = buffer.shape[0]
        first = 0 if half is None else pl.multiple_of(half * rows, rows)
        return [(None, pltpu.make_async_copy(chunks[0].at[pl.ds(first, rows)], buffer, sems.at[0]))]
    copies = []
    for k, chunk in enumerate(chunks):
        index = lax.rem(turn - k + count, count)
        wanted = None
        if half is not None:
            wanted = lax.div(index, count // 2) == half
            index = lax.rem(index, count // 2)
        target = buffer.at[pl.ds(pl.multiple_of(index * size, size), size)]
        copies.append((wanted, pltpu.make_async_copy(chunk, target, sems.at[k])))
    return copies


def each(copies, act):
    for wanted, copy in copies:
        if wanted is None:
            act(copy)
        else:
            pl.when(wanted)(functools.partial(act, copy))


def start(copies):
    each(copies, lambda copy: copy.start())


def finish(copies):
    each(copies, lambda copy: copy.wait())


def estimate(flops, *arrays):
    moved = sum(x.size * x.dtype.itemsize for x in arrays)
    return pl.CostEstimate(flops=flops, transcendentals=0, bytes_accessed=moved)


def limit(mebibytes):
    return pltpu.CompilerParams(vmem_limit_bytes=mebibytes << 20)


ANYWHERE = pl.BlockSpec(memory_space=pl.ANY)


def weight_buffer(chunks, share=1):
    size = len(chunks) * chunks[0].shape[0] // share
    return [pltpu.VMEM((size, chunks[0].shape[1]), LOW), pltpu.SemaphoreType.DMA((len(chunks),))]


def tile_rows(width, column=0):
    return pl.BlockSpec((TILE, width), lambda i, *_: (i, column))


def joined_rows(width, tiles):
    spec = pl.BlockSpec((TILE, width), lambda i, s: (i // (2 * tiles) * tiles + i % tiles, 0))
    return [spec, spec]


def enter_kernel(tiles, blocks, project, spots, own_ref, other_ref, *refs):
    i = pl.program_id(0)
    mine = lax.rem(lax.div(i, tiles), 2) == spots[0]
    rows = jnp.where(mine, own_ref[...], other_ref[...])
    part = rows.shape[1] // len(blocks)
    permuted = jnp.concatenate([rows[:, n * part : (n + 1) * part] for n in blocks], axis=1)
    if not project:
        all_ref, quarter_ref = refs
        all_ref[...] = permuted
        held = all_ref
    else:
        chunks, (h_ref, z_ref, scale_ref, quarter_ref, held, buffer, sems) = refs[:-7], refs[-7:]
        held[...] = permuted
        copies = chunk_copies(chunks, buffer, sems, spots[2])

        @pl.when(i == 0)
        def _():
            start(copies)

        x = rows.astype(F32)
        scale = lax.rsqrt(jnp.mean(x * x, axis=-1, keepdims=True) + EPSILON)
        scale_ref[...] = scale
        hidden = (permuted.astype(F32) * scale).astype(LOW)
        h_ref[...] = hidden

        @pl.when(i == 0)
        def _():
            finish(copies)

        z_ref[...] = matmul(hidden, buffer[...])
    size = quarter_ref.shape[1]
    quarter_ref[...] = held[:, pl.ds(pl.multiple_of(spots[1] * size, size), size)]


def enter(spots, blocks, own, other, chunks=()):
    width = own.shape[1]
    count, tiles = 2 * own.shape[0], own.shape[0] // TILE // 2
    shape = jax.ShapeDtypeStruct
    quarter = shape((count, width // GROUP), LOW)
    if chunks:
        columns = chunks[0].shape[1]
        outs = [shape((count, width), LOW), shape((count, columns), F32), shape((count, 1), F32), quarter]
        scratch = [pltpu.VMEM((TILE, width), LOW), *weight_buffer(chunks)]
    else:
        columns, scratch = 0, []
        outs = [shape((count, width), LOW), quarter]
    return pl.pallas_call(
        functools.partial(enter_kernel, tiles, blocks, bool(chunks)),
        out_shape=outs,
        grid_spec=pltpu.PrefetchScalarGridSpec(
            num_scalar_prefetch=1,
            grid=(count // TILE,),
            in_specs=joined_rows(width, tiles) + [ANYWHERE] * len(chunks),
            out_specs=[tile_rows(o.shape[1]) for o in outs],
            scratch_shapes=scratch,
        ),
        compiler_params=limit(40),
        cost_estimate=estimate(2 * count * width * columns, own, other, *chunks, *outs),
        name="enter",
    )(spots, own, other, *chunks)


def project_kernel(spots, h_ref, *refs):
    chunks, (z_ref, buffer, sems) = refs[:-3], refs[-3:]
    copies = chunk_copies(chunks, buffer, sems, spots[2])

    @pl.when(pl.program_id(0) == 0)
    def _():
        start(copies)
        finish(copies)

    z_ref[...] = matmul(h_ref[...], buffer[...])


def project(spots, hidden, chunks):
    count, width = hidden.shape
    out = jax.ShapeDtypeStruct((count, chunks[0].shape[1]), F32)
    return pl.pallas_call(
        project_kernel,
        out_shape=out,
        grid_spec=pltpu.PrefetchScalarGridSpec(
            num_scalar_prefetch=1,
            grid=(count // TILE,),
            in_specs=[tile_rows(width)] + [ANYWHERE] * len(chunks),
            out_specs=tile_rows(out.shape[1]),
            scratch_shapes=weight_buffer(chunks),
        ),
        compiler_params=limit(40),
        cost_estimate=estimate(2 * count * width * out.shape[1], hidden, *chunks, out),
        name="project",
    )(spots, hidden, *chunks)


def unit_kernel(spots, own_ref, other_ref, *refs):
    chunks, rest = refs[:-9], refs[-9:]
    h_ref, one_ref, two_ref, product_ref, scale_ref, first, second, sem_one, sem_two = rest
    split = len(chunks) // 2
    copies = [
        chunk_copies(chunks[:split], first, sem_one, spots[2]),
        chunk_copies(chunks[split:], second, sem_two, spots[2]),
    ]
    begins = pl.program_id(0) == 0

    @pl.when(begins)
    def _():
        start(copies[0])
        start(copies[1])

    mine, other = own_ref[...], other_ref[...]
    swapped = spots[0] == 1
    middle = jnp.concatenate(
        [jnp.where(swapped, other, mine), jnp.where(swapped, mine, other)], axis=1
    ).astype(F32)
    scale = lax.rsqrt(jnp.mean(middle * middle, axis=-1, keepdims=True) + EPSILON)
    scale_ref[...] = scale
    hidden = (middle * scale).astype(LOW)
    h_ref[...] = hidden

    @pl.when(begins)
    def _():
        finish(copies[0])

    z_one = matmul(hidden, first[...])

    @pl.when(begins)
    def _():
        finish(copies[1])

    z_two = matmul(hidden, second[...])
    one_ref[...] = z_one.astype(LOW)
    two_ref[...] = z_two.astype(LOW)
    product_ref[...] = (z_one * z_two).astype(LOW)


def gated_unit(spots, own, other, first, second):
    count, width, units = own.shape[0], 2 * own.shape[1], first[0].shape[1]
    shape = jax.ShapeDtypeStruct
    outs = [shape((count, width), LOW)] + [shape((count, units), LOW)] * 3 + [shape((count, 1), F32)]
    (buffer, sems) = weight_buffer(first)
    return pl.pallas_call(
        unit_kernel,
        out_shape=outs,
        grid_spec=pltpu.PrefetchScalarGridSpec(
            num_scalar_prefetch=1,
            grid=(count // TILE,),
            in_specs=[tile_rows(width // 2)] * 2 + [ANYWHERE] * (2 * len(first)),
            out_specs=[tile_rows(o.shape[1]) for o in outs],
            scratch_shapes=[buffer, buffer, sems, sems],
        ),
        compiler_params=limit(48),
        cost_estimate=estimate(4 * count * width * units, own, other, *first, *second, *outs),
        name="gated_unit",
    )(spots, own, other, *first, *second)


def unit_back_kernel(spots, dy_ref, one_ref, two_ref, *refs):
    chunks, (d_one_ref, d_two_ref, sum_ref, buffer, sems) = refs[:-5], refs[-5:]
    copies = chunk_copies(chunks, buffer, sems, spots[2])

    @pl.when(pl.program_id(0) == 0)
    def _():
        start(copies)
        finish(copies)

    d_product = matmul(dy_ref[...], buffer[...])
    z_one, z_two = one_ref[...].astype(F32), two_ref[...].astype(F32)
    d_one = d_product * z_two
    d_one_ref[...] = d_one.astype(LOW)
    d_two_ref[...] = (d_product * z_one).astype(LOW)
    sum_ref[...] = jnp.sum(d_one * z_one, axis=-1, keepdims=True)


def gated_unit_back(spots, dy, z_one, z_two, chunks):
    count, width, units = dy.shape[0], dy.shape[1], z_one.shape[1]
    shape = jax.ShapeDtypeStruct
    outs = [shape((count, units), LOW)] * 2 + [shape((count, 1), F32)]
    return pl.pallas_call(
        unit_back_kernel,
        out_shape=outs,
        grid_spec=pltpu.PrefetchScalarGridSpec(
            num_scalar_prefetch=1,
            grid=(count // TILE,),
            in_specs=[tile_rows(width), tile_rows(units), tile_rows(units)] + [ANYWHERE] * len(chunks),
            out_specs=[tile_rows(o.shape[1]) for o in outs],
            scratch_shapes=weight_buffer(chunks),
        ),
        compiler_params=limit(40),
        cost_estimate=estimate(2 * count * width * units, dy, z_one, z_two, *chunks, *outs),
        name="gated_unit_back",
    )(spots, dy, z_one, z_two, *chunks)


def fold_kernel(members, keeps, spots, *refs):
    values, refs = refs[:members], refs[members:]
    arrived, refs = (refs[0], refs[1:]) if keeps else (None, refs)
    outs = 2 if keeps else 1
    chunks, refs = refs[: -outs - 2 * members], refs[-outs - 2 * members :]
    outs, buffers, sems = refs[:outs], refs[outs : outs + members], refs[outs + members :]
    each_count = len(chunks) // members
    half = spots[0] if keeps else 1 - spots[0]
    begins = pl.program_id(0) == 0
    copies = [
        chunk_copies(chunks[m * each_count : (m + 1) * each_count], buffers[m], sems[m], spots[2], half)
        for m in range(members)
    ]

    @pl.when(begins)
    def _():
        for m in range(members):
            start(copies[m])

    whole = None
    for m in range(members):
        pl.when(begins)(functools.partial(finish, copies[m]))
        term = times_transposed(values[m][...], buffers[m][...])
        whole = term if whole is None else whole + term
    if not keeps:
        outs[0][...] = whole.astype(LOW)
    else:
        whole = whole + arrived[...].astype(F32)
        size = whole.shape[1] // 2
        upper = spots[3] == 1
        outs[0][...] = jnp.where(upper, whole[:, :size], whole[:, size:]).astype(LOW)
        outs[1][...] = jnp.where(upper, whole[:, size:], whole[:, :size])


def fold_half(spots, values, weights, arrived=None):
    count = values[0].shape[0]
    half = len(weights[0]) * weights[0][0].shape[0] // 2
    shape = jax.ShapeDtypeStruct
    if arrived is None:
        outs, extra = [shape((count, half), LOW)], []
    else:
        outs, extra = [shape((count, half // 2), LOW), shape((count, half // 2), F32)], [arrived]
    buffers, sems = zip(*[weight_buffer(w, 2) for w in weights])
    chunks = [x for w in weights for x in w]
    flops = sum(2 * count * half * v.shape[1] for v in values)
    found = pl.pallas_call(
        functools.partial(fold_kernel, len(values), arrived is not None),
        out_shape=outs,
        grid_spec=pltpu.PrefetchScalarGridSpec(
            num_scalar_prefetch=1,
            grid=(count // TILE,),
            in_specs=[tile_rows(v.shape[1]) for v in values]
            + [tile_rows(half)] * len(extra)
            + [ANYWHERE] * len(chunks),
            out_specs=[tile_rows(o.shape[1]) for o in outs],
            scratch_shapes=[*buffers, *sems],
        ),
        compiler_params=limit(40),
        cost_estimate=estimate(flops, *values, *extra, *chunks[: len(chunks) // 2], *outs),
        name="fold_half",
    )(spots, *values, *extra, *chunks)
    return found[0] if arrived is None else found


def gradient_kernel(spots, left_ref, right_ref, *refs):
    found = cross_tokens(left_ref[...], right_ref[...])
    for arrived_ref in refs[:-1]:
        found = found + arrived_ref[...].astype(F32)
    refs[-1][...] = found.astype(LOW)


def gradient_rows(spots, spread, k, left, right, arrived=()):
    count, columns = right.shape
    rows = left.shape[1] // (1 if k is None else spread)
    tiles = rows // TILE

    def block(i, s):
        return (0, i if k is None else lax.rem(s[2] + k, spread) * tiles + i)

    out = jax.ShapeDtypeStruct((rows, columns), LOW)
    return pl.pallas_call(
        gradient_kernel,
        out_shape=out,
        grid_spec=pltpu.PrefetchScalarGridSpec(
            num_scalar_prefetch=1,
            grid=(tiles,),
            in_specs=[
                pl.BlockSpec((count, TILE), block),
                pl.BlockSpec((count, columns), lambda i, s: (0, 0), pipeline_mode=pl.Buffered(1)),
            ]
            + [tile_rows(columns)] * len(arrived),
            out_specs=tile_rows(columns),
        ),
        compiler_params=limit(40),
        cost_estimate=estimate(2 * count * rows * columns, right, out, out, *arrived),
        name="gradient_rows",
    )(spots, left, right, *arrived)


def place_kernel(cuts, spots, *refs):
    quarter = pl.program_id(0)
    cross = lax.rem(lax.div(quarter, 2) + spots[0], 2) * 2 + lax.rem(lax.rem(quarter, 2) + spots[3], 2)
    for n in range(4):

        @pl.when(cross == n)
        def _():
            for (first, size), out_ref in zip(cuts, refs[4:]):
                out_ref[...] = refs[n][:, first : first + size].astype(F32)


def place_quarters(spots, pairs, *cuts):
    rows, columns = pairs[0].shape[0], pairs[0].shape[1] // 2
    outs = [jax.ShapeDtypeStruct((rows, GROUP * size), F32) for _, size in cuts]

    def block(index):
        return pl.BlockSpec((rows, columns), lambda q, s: (0, index), pipeline_mode=pl.Buffered(1))

    return pl.pallas_call(
        functools.partial(place_kernel, cuts),
        out_shape=outs,
        grid_spec=pltpu.PrefetchScalarGridSpec(
            num_scalar_prefetch=1,
            grid=(GROUP,),
            in_specs=[block(0), block(1), block(0), block(1)],
            out_specs=[pl.BlockSpec((rows, size), lambda q, s: (0, q)) for _, size in cuts],
        ),
        compiler_params=limit(40),
        cost_estimate=estimate(0, *pairs, *outs),
        name="place_quarters",
    )(spots, pairs[0], pairs[0], pairs[1], pairs[1])


def tie(*values):
    return lax.optimization_barrier(values)


def body(reps, shards, tokens, cotangent, lengths, decay_rates, *weights):
    spread = reps // GROUP
    place = lax.axis_index("shard")
    a, b, c = lax.axis_index("a"), lax.axis_index("b"), lax.axis_index("c")
    quarter = 2 * c + b
    micro, run, width = tokens.shape
    half, own = width // 2, width // GROUP
    streams = micro * GROUP // shards
    per_block = STREAM // run // GROUP * streams
    rows = width // shards
    part = rows // spread
    columns = functools.partial(lax.dynamic_slice_in_dim, axis=1)
    spots = jnp.stack([c, quarter, a, b]).astype(jnp.int32)
    blocks = [z * spread + k for k in range(spread) for z in range(shards)]

    def move(x, target):
        pairs = [(r * shards + s, target(r) * shards + s) for r in range(reps) for s in range(shards)]
        return lax.ppermute(x, AXES, pairs)

    def swap_c(x):
        return move(x, lambda r: r ^ 1)

    def swap_b(x):
        return move(x, lambda r: r ^ 2)

    def joined(*parts):
        return jnp.concatenate(parts, axis=1)

    def shift_a(x, k):
        return move(x, lambda r: (r + GROUP * k) % reps)

    def ordered(index, mine, other, axis):
        return jnp.where(
            index == 0,
            jnp.concatenate([mine, other], axis),
            jnp.concatenate([other, mine], axis),
        )


    def batch_of(s):
        return s // (shards // micro)

    def origin(r, s, p):
        run_id = (r % GROUP) * per_block + p
        stream, piece = run_id // shards, run_id % shards
        member = s % GROUP if streams == 1 else 2 * stream + s % 2
        return (r // GROUP) * GROUP + member, piece

    def routes(p):
        found = []
        for r in range(reps):
            for s in range(shards):
                from_r, from_s = origin(r, s, p ^ batch_of(s))
                found.append((from_r * shards + from_s, r * shards + s))
        return found

    def natural(x):
        return jnp.concatenate(
            [
                x[:, (k * shards + z) * part : (k * shards + z + 1) * part]
                for z in range(shards)
                for k in range(spread)
            ],
            axis=1,
        )

    def bring(x):
        arrived = [
            lax.ppermute(lax.dynamic_index_in_dim(x, (place + p) % 2, 0, False), AXES, routes(p))
            for p in range(2)
        ]
        return ordered(batch_of(place), *arrived, 0)

    def back_slots(x):
        slots = natural(x).reshape(2, run, width)
        return [
            lax.dynamic_index_in_dim(slots, (batch_of(place) + p) % 2, 0, False) for p in range(2)
        ]

    def send_slot(x, p):
        return lax.ppermute(x, AXES, [(to, origin) for origin, to in routes(p)])

    def send_back(x):
        return [send_slot(slot, p) for p, slot in enumerate(back_slots(x))]

    def as_batches(arrived):
        return ordered(place % 2, arrived[0][None], arrived[1][None], 0)


    def gather_b(x):
        return ordered(b, x, swap_b(x), 1)

    def gather_c(x):
        return ordered(c, x, swap_c(x), 1)

    def gather_rows_b(x):
        return ordered(b, x, swap_b(x), 0)

    def total(x):
        x = x + swap_c(x)
        return x + swap_b(x)

    def fold_c(product):
        sent = swap_c(product(1 - c).astype(LOW))
        return product(c) + sent.astype(F32)

    def fold_b(x):
        sent = swap_b(columns(x, (1 - b) * own, own).astype(LOW))
        return columns(x, b * own, own) + sent.astype(F32)


    pick = functools.partial(lax.dynamic_index_in_dim, keepdims=False)

    def away_b(x):
        cut = x.reshape(2, 2, -1, own)
        return pick(cut, b, 0), swap_b(pick(cut, 1 - b, 0))

    def away_c(mine, arrived):
        both = ordered(b, mine, arrived, 2)
        return pick(both, c, 0), swap_c(pick(both, 1 - c, 0))

    def to_runs(x):
        return ordered(c, *away_c(*away_b(x)), 1)


    def own_features(w):
        count = shards * spread // GROUP
        cut = []
        for i in range(count):
            block = quarter * count + i
            cut.append(columns(w, (block % shards) * rows + (block // shards) * part, part))
        return jnp.concatenate(cut, axis=1)

    def own_units(w):
        return columns(w, quarter * (w.shape[1] // GROUP), w.shape[1] // GROUP)

    def over_shards(*members):
        cut = jnp.concatenate(members, axis=1) if len(members) > 1 else members[0]
        piece = lax.dynamic_slice_in_dim(cut, a * part, part, 0)
        return lax.all_gather(piece, "shard", axis=0, tiled=True)

    def over_owners(w):
        piece = lax.dynamic_slice_in_dim(w, a * part, part, 0)
        return lax.all_gather(piece, OWNERS, axis=0, tiled=True)

    def over_spread(x):
        return [shift_a(x, k) for k in range(1, spread)]

    def by_spread(relative):
        if spread == 2:
            return ordered(a, relative[0], relative[1], 0)
        stacked = jnp.stack(relative, 0)
        pick = functools.partial(lax.dynamic_index_in_dim, axis=0, keepdims=False)
        return jnp.concatenate([pick(stacked, (a - j) % spread) for j in range(spread)], axis=0)

    def in_row_order(x):
        cut = x.reshape(spread, shards, part, -1)
        return jnp.transpose(cut, (1, 0, 2, 3)).reshape(width, -1)

    def row_half(w, h):
        return lax.dynamic_slice_in_dim(w, h * half, half, 0)


    def away(left, right):
        return [gradient_rows(spots, spread, k, left, right) for k in range(1, spread)]

    def in_two(terms):
        middles = [x.shape[0] // 2 for x in terms]
        return [x[:m] for x, m in zip(terms, middles)], [x[m:] for x, m in zip(terms, middles)]

    def stacked(upper, lower):
        return [jnp.concatenate(pair, axis=0) for pair in zip(upper, lower)]

    def sent_a(terms):
        return [shift_a(x, k + 1) for k, x in enumerate(terms)]

    def scattered(x):
        return lax.psum_scatter(x, "shard", scatter_dimension=0, tiled=True)

    def whole_rows(left, right):
        return gradient_rows(spots, spread, None, left, right)

    def scattered_all(x):
        return lax.psum_scatter(x, OWNERS, scatter_dimension=0, tiled=True)

    def summed(left, right, arrived):
        return scattered(gradient_rows(spots, spread, 0, left, right, arrived))

    def spread_a(x):
        return by_spread([x] + over_spread(x))

    def spread_b(x):
        return jnp.concatenate([x, swap_b(x)], axis=1)

    def spread_c(pair):
        return pair, swap_c(pair)

    def features_in_order(pairs, first, size):
        full = pairs[0].shape[1] // 2
        cut = [x[:, i * full + first : i * full + first + size] for x in pairs for i in range(2)]
        pair = [ordered(b, cut[n], cut[n + 1], 1) for n in (0, 2)]
        return natural(ordered(c, pair[0], pair[1], 1)).astype(F32)


    w_query, w_key, w_value, w_gate, w_out, w_one, w_two, w_down = weights
    g_qk = over_shards(own_units(w_query), own_units(w_key))
    g_vg = over_shards(own_units(w_value), own_units(w_gate))
    g_o = over_shards(own_features(w_out))
    g_1 = over_shards(own_units(w_one))
    g_2 = over_shards(own_units(w_two))
    w_d = [over_owners(own_units(w_down))]

    heads = HEADS // GROUP
    rates = lax.dynamic_slice_in_dim(decay_rates, quarter * heads, heads, 0)
    cuts = gather_rows_b(lengths.reshape(1, -1))
    cuts = ordered(c, cuts, swap_c(cuts), 0).reshape(GROUP, micro, -1)
    if streams == 1:
        batch = place // GROUP
        member = place % GROUP
        chosen = lax.dynamic_slice_in_dim(cuts, 2 * (member % 2) + member // 2, 1, 0)
    else:
        batch = place // 2
        chosen = lax.dynamic_index_in_dim(cuts.reshape(2, 2, micro, -1), place % 2, 0, False)
    chosen = lax.dynamic_index_in_dim(chosen, batch, 1, False)
    seq_ends = [chosen[:, 0]]
    for i in range(1, chosen.shape[1]):
        seq_ends.append(seq_ends[-1] + chosen[:, i])
    ends = jnp.stack(seq_ends, axis=1)

    x_run = bring(tokens)
    x_run, g_qk = tie(x_run, g_qk)

    x_pair = gather_rows_b(x_run)
    s_qk = over_spread(g_qk)
    x_pair, s_qk, g_vg = tie(x_pair, s_qk, g_vg)

    s_vg = over_spread(g_vg)
    w_qk = [g_qk, *s_qk]
    hidden_one, z_qk, x_scale, x_own = enter(spots, blocks, x_pair, swap_c(x_pair), w_qk)
    z_qk, hidden_one, s_vg, g_o = tie(z_qk, hidden_one, s_vg, g_o)

    s_o = over_spread(g_o)
    w_vg = [g_vg, *s_vg]
    z_vg = project(spots, hidden_one, w_vg)
    attended = attend(rates, ends, z_qk, z_vg)
    gate = z_vg[:, own:]
    o_scale = lax.rsqrt(total(jnp.sum(attended * attended, axis=-1)) / width + EPSILON)[:, None]
    lifted = (attended * gate).astype(LOW)
    lifted, s_o, g_1, cotangent = tie(lifted, s_o, g_1, cotangent)

    s_1 = over_spread(g_1)
    lifted = gather_b(lifted)
    lifted, s_1, g_2, o_scale, cotangent = tie(lifted, s_1, g_2, o_scale, cotangent)

    s_2 = over_spread(g_2)
    dy_run = bring(cotangent)
    lifted = gather_c(lifted)
    w_o = in_row_order(by_spread([g_o, *s_o]))
    branch = o_scale * matmul(lifted, w_o)
    middle = x_own.astype(F32) + branch
    low_middle = gather_b(middle.astype(LOW))
    low_middle, s_2, dy_run = tie(low_middle, s_2, dy_run)

    other_middle = swap_c(low_middle)
    dy_other = swap_b(dy_run)
    w_1, w_2 = [g_1, *s_1], [g_2, *s_2]
    hidden_two, z_one, z_two, product, m_scale = gated_unit(spots, low_middle, other_middle, w_1, w_2)
    z_one, z_two, product, dy_other, w_d[0] = tie(z_one, z_two, product, dy_other, w_d[0])

    dy_pair = ordered(b, dy_run, dy_other, 0)
    dy_all, dy_own = enter(spots, blocks, dy_pair, swap_c(dy_pair))


    d_one, d_two, lean_m = gated_unit_back(spots, dy_all, z_one, z_two, w_d)
    sent = fold_half(spots, [d_one, d_two], [w_1, w_2])
    sent, product, lean_m, dy_all = tie(sent, product, lean_m, dy_all)

    arrived = swap_c(sent)
    f_down = whole_rows(dy_all, product)
    arrived, f_down = tie(arrived, f_down)

    f_down = scattered_all(f_down)
    lean_m = lean_m[:, 0]
    lean_c = swap_c(lean_m)
    sent, mine = fold_half(spots, [d_one, d_two], [w_1, w_2], arrived)
    sent, d_one, d_two, product, lean_c = tie(sent, d_one, d_two, product, lean_c)

    crossed = swap_b(sent)
    t_two = away(hidden_two, d_two)
    lean_m = lean_m + lean_c
    lean_b = swap_b(lean_m)
    upper, lower = in_two(t_two)
    upper = sent_a(upper)
    f_one = whole_rows(hidden_two, d_one)
    result = fold_half(spots, [product], [w_d])
    crossed, result, f_one, upper, lean_b = tie(crossed, result, f_one, upper, lean_b)

    f_one = scattered_all(f_one)
    d_hidden = mine + crossed.astype(F32)
    m_normed = middle * m_scale
    lean = (lean_m + lean_b)[:, None] * (2.0 / width)
    d_middle = dy_own.astype(F32) + m_scale * (d_hidden - m_normed * lean)
    d_branch = d_middle.astype(LOW)
    lean_o = jnp.sum(d_middle * branch, axis=-1)
    sent = times_transposed(d_branch, row_half(w_o, 1 - c)).astype(LOW)
    sent, result, d_middle, lean_o = tie(sent, result, d_middle, lean_o)

    arrived = swap_c(sent)
    r_result = swap_c(result)
    lean_o = lean_o + swap_c(lean_o)
    p_out = cross_tokens(lifted, (o_scale * d_middle).astype(LOW)).astype(LOW)
    p_out = jnp.transpose(p_out.reshape(shards, spread, part, -1), (1, 0, 2, 3))
    p_out = p_out.reshape(spread, width // spread, -1)
    t_out = [lax.dynamic_index_in_dim(p_out, (a + k) % spread, 0, False) for k in range(spread)]
    d_gated = times_transposed(d_branch, row_half(w_o, c)) + arrived.astype(F32)
    sent = columns(d_gated, (1 - b) * own, own).astype(LOW)
    mine = columns(d_gated, b * own, own)
    sent, mine, r_result, t_out, lean_o = tie(sent, mine, r_result, t_out, lean_o)

    crossed = swap_b(sent)
    lean_b = swap_b(lean_o)
    r_out = sent_a(t_out[1:])
    result, result_mine = fold_half(spots, [product], [w_d], r_result)
    crossed, result, r_out, lower, lean_b, f_down = tie(crossed, result, r_out, lower, lean_b, f_down)

    lower = sent_a(lower)
    y_down = over_spread(f_down)
    result = swap_b(result)
    f_out = scattered(sum([x.astype(F32) for x in r_out], t_out[0].astype(F32)).astype(LOW))
    o_normed = attended * o_scale
    d_gated = mine + crossed.astype(F32)
    d_gate = (d_gated * o_normed).astype(LOW)
    lean = (lean_o + lean_b)[:, None] / width
    d_attended = (o_scale * (d_gated * gate - o_normed * lean)).astype(LOW)
    d_query, d_key, d_value = attend_back(rates, ends, z_qk, z_vg, d_attended)
    d_qk = joined(d_query, d_key)
    d_vg = joined(d_value, d_gate)
    t_qk = away(hidden_one, d_qk)
    d_qk, d_vg, t_qk, lower, result, y_down = tie(d_qk, d_vg, t_qk, lower, result, y_down)

    upper_qk, lower_qk = in_two(t_qk)
    upper_qk = sent_a(upper_qk)
    f_two = gradient_rows(spots, spread, 0, hidden_two, d_two, stacked(upper, lower))
    output = to_runs((middle + (result_mine + result.astype(F32))).astype(LOW))
    t_vg = away(hidden_one, d_vg)
    sent = fold_half(spots, [d_qk, d_vg], [w_qk, w_vg])
    sent, t_vg, d_qk, d_vg, f_two, output, upper_qk, lower_qk = tie(
        sent, t_vg, d_qk, d_vg, f_two, output, upper_qk, lower_qk
    )

    f_two = scattered(f_two)
    lower_qk = sent_a(lower_qk)
    y_down = by_spread([f_down, *y_down])
    x_down = swap_b(y_down)
    y_one = over_spread(f_one)
    arrived = swap_c(sent)
    lean_x = jnp.sum(z_qk * d_qk.astype(F32), axis=-1) + jnp.sum(z_vg * d_vg.astype(F32), axis=-1)
    sent, mine = fold_half(spots, [d_qk, d_vg], [w_qk, w_vg], arrived)
    lean_x = lean_x + swap_c(lean_x)
    sent, mine, lower_qk, t_vg, lean_x, x_down, y_one = tie(
        sent, mine, lower_qk, t_vg, lean_x, x_down, y_one
    )

    crossed = swap_b(sent)
    lean_b = swap_b(lean_x)
    r_vg = sent_a(t_vg)
    f_qk = scattered(gradient_rows(spots, spread, 0, hidden_one, d_qk, stacked(upper_qk, lower_qk)))
    four_down = spread_c(joined(y_down, x_down))
    crossed, d_vg, r_vg, lean_b, four_down = tie(crossed, d_vg, r_vg, lean_b, four_down)

    f_vg = gradient_rows(spots, spread, 0, hidden_one, d_vg, r_vg)
    f_vg, crossed, f_two, f_out = tie(f_vg, crossed, f_two, f_out)

    f_vg = scattered(f_vg)
    d_hidden = mine + crossed.astype(F32)
    x_normed = x_own.astype(F32) * x_scale
    lean = (lean_x + lean_b)[:, None] / width
    input_grad = to_runs((d_middle + x_scale * (d_hidden - x_normed * lean)).astype(LOW))
    output = send_back(output)
    y_one = by_spread([f_one, *y_one])
    x_one = swap_b(y_one)
    f_oqk = joined(f_out, f_qk)
    x_oqk = swap_b(f_oqk)
    y_two = over_spread(f_two)
    units = f_one.shape[1]
    [g_down] = place_quarters(spots, four_down, (0, units))
    input_grad, output, x_one, y_two, x_oqk, f_vg, g_down = tie(
        input_grad, output, x_one, y_two, x_oqk, f_vg, g_down
    )

    y_vg = over_spread(f_vg)
    y_two = by_spread([f_two, *y_two])
    x_two = swap_b(y_two)
    f_oqk = joined(f_oqk, x_oqk)
    upper, lower = in_two([f_oqk])
    upper = over_spread(upper[0])
    back_one, back_two = back_slots(input_grad)
    back_one = send_slot(back_one, 0)
    output = as_batches(output)
    [g_one] = place_quarters(spots, spread_c(joined(y_one, x_one)), (0, units))
    y_vg, x_two, upper, lower, back_one, back_two, output, g_one = tie(
        y_vg, x_two, upper, lower, back_one, back_two, output, g_one
    )

    y_vg = by_spread([f_vg, *y_vg])
    x_vg = swap_b(y_vg)
    lower = over_spread(lower[0])
    back_two = send_slot(back_two, 1)
    [g_two] = place_quarters(spots, spread_c(joined(y_two, x_two)), (0, units))
    x_vg, lower, back_two, g_two = tie(x_vg, lower, back_two, g_two)

    four_vg = spread_c(joined(y_vg, x_vg))
    four_oqk = spread_c(by_spread([f_oqk, *stacked(upper, lower)]))
    g_value, g_gate = place_quarters(spots, four_vg, (0, own), (own, own))
    g_query, g_key = place_quarters(spots, four_oqk, (own, own), (2 * own, own))
    g_out = features_in_order(four_oqk, 0, own)
    input_grad = as_batches([back_one, back_two])
    return output, input_grad, g_query, g_key, g_value, g_gate, g_out, g_one, g_two, g_down


def solution(mesh):
    reps, shards = mesh.shape["rep"], mesh.shape["shard"]
    devices = mesh.devices.reshape(reps // GROUP, 2, 2, shards)
    rep = ("a", "b", "c")
    by_tokens = P(None, (*rep, "shard"), None)
    by_rows = P("shard", None)
    return jax.shard_map(
        functools.partial(body, reps, shards),
        mesh=Mesh(devices, AXES),
        in_specs=(by_tokens, by_tokens, P(None, rep, None), P(), *[by_rows] * 8),
        out_specs=(by_tokens, by_tokens, *[by_rows] * 8),
        check_vma=False,
    )
```

```python
import functools

import jax
import jax.numpy as jnp
from jax import lax
from jax.experimental import pallas as pl
from jax.experimental.pallas import tpu as pltpu
from jax.sharding import Mesh, PartitionSpec as P

HEADS = 16
HEAD_DIM = 128
STREAM = 1024
GROUP = 4
BLOCK = 256
TILE = 256
EPSILON = 1e-06
AXES = ("a", "b", "c", "shard")
OWNERS = ("a", "shard")
LOW = jnp.bfloat16
F32 = jnp.float32


def matmul(former, latter):
    return jnp.dot(former, latter, preferred_element_type=F32)


def times_transposed(former, latter):
    return lax.dot_general(former, latter, (((1,), (1,)), ((), ())), preferred_element_type=F32)


def cross_tokens(former, latter):
    return lax.dot_general(former, latter, (((0,), (0,)), ((), ())), preferred_element_type=F32)


def masked_decay(rate, ends, first, columns):
    row = first + lax.broadcasted_iota(jnp.int32, (BLOCK, 1), 0)
    column = lax.broadcasted_iota(jnp.int32, (1, columns), 1)
    begin = jnp.zeros((BLOCK, 1), jnp.int32)
    for end in ends:
        begin = jnp.where(row >= end, end, begin)
    falling = jnp.exp(-rate * (row - first).astype(F32))
    rising = jnp.exp(rate * (column - first).astype(F32))
    allowed = (column <= row) & (column >= begin)
    return jnp.where(allowed, falling * rising, 0.0)


def attend_kernel(rates, ends, zq_ref, zk_ref, zv_ref, out_ref):
    stream, head = pl.program_id(0), pl.program_id(1)
    rate = rates[head]
    bounds = [ends[stream, i] for i in range(ends.shape[1])]
    zq, zk = zq_ref[...], zk_ref[...]
    q = (zq * jax.nn.sigmoid(zq)).astype(LOW)
    k = (zk * jax.nn.sigmoid(zk)).astype(LOW)
    v = zv_ref[...].astype(LOW)
    for first in range(0, STREAM, BLOCK):
        columns = first + BLOCK
        mask = masked_decay(rate, bounds, first, columns)
        scores = times_transposed(q[first:columns], k[:columns])
        weights = (scores * mask).astype(LOW)
        out_ref[first:columns, :] = matmul(weights, v[:columns])


def attend_back_kernel(
    rates, ends, zq_ref, zk_ref, zv_ref, do_ref, dzq_ref, dzk_ref, dzv_ref, dk_ref, dv_ref
):
    stream, head = pl.program_id(0), pl.program_id(1)
    rate = rates[head]
    bounds = [ends[stream, i] for i in range(ends.shape[1])]
    zq, zk = zq_ref[...], zk_ref[...]
    sig_q, sig_k = jax.nn.sigmoid(zq), jax.nn.sigmoid(zk)
    q = (zq * sig_q).astype(LOW)
    k = (zk * sig_k).astype(LOW)
    slope_q = sig_q * (1.0 + zq * (1.0 - sig_q))
    v = zv_ref[...].astype(LOW)
    d_o = do_ref[...]
    dk_ref[...] = jnp.zeros_like(dk_ref)
    dv_ref[...] = jnp.zeros_like(dv_ref)
    for first in range(0, STREAM, BLOCK):
        columns = first + BLOCK
        rows = slice(first, columns)
        mask = masked_decay(rate, bounds, first, columns)
        weights = (times_transposed(q[rows], k[:columns]) * mask).astype(LOW)
        d_scores = (times_transposed(d_o[rows], v[:columns]) * mask).astype(LOW)
        dzq_ref[rows, :] = (matmul(d_scores, k[:columns]) * slope_q[rows]).astype(LOW)
        dk_ref[:columns, :] += cross_tokens(d_scores, q[rows])
        dv_ref[:columns, :] += cross_tokens(weights, d_o[rows])
    dzk_ref[...] = (dk_ref[...] * (sig_k * (1.0 + zk * (1.0 - sig_k)))).astype(LOW)
    dzv_ref[...] = dv_ref[...].astype(LOW)


def head_block(offset=0):
    return pl.BlockSpec((STREAM, HEAD_DIM), lambda g, h, *_: (g, h + offset))


def attend(rates, ends, z_qk, z_vg):
    heads, streams = rates.shape[0], ends.shape[0]
    work = streams * heads * STREAM * STREAM
    return pl.pallas_call(
        attend_kernel,
        out_shape=jax.ShapeDtypeStruct((streams * STREAM, heads * HEAD_DIM), F32),
        grid_spec=pltpu.PrefetchScalarGridSpec(
            num_scalar_prefetch=2,
            grid=(streams, heads),
            in_specs=[head_block(), head_block(heads), head_block()],
            out_specs=head_block(),
        ),
        compiler_params=pltpu.CompilerParams(vmem_limit_bytes=40 << 20),
        cost_estimate=pl.CostEstimate(
            flops=4 * work * HEAD_DIM, transcendentals=work // 64,
            bytes_accessed=streams * heads * STREAM * HEAD_DIM * 16,
        ),
        name="attend",
    )(rates, ends, z_qk, z_qk, z_vg)


def attend_back(rates, ends, z_qk, z_vg, d_o):
    heads, streams = rates.shape[0], ends.shape[0]
    work = streams * heads * STREAM * STREAM
    return pl.pallas_call(
        attend_back_kernel,
        out_shape=[jax.ShapeDtypeStruct((streams * STREAM, heads * HEAD_DIM), LOW)] * 3,
        grid_spec=pltpu.PrefetchScalarGridSpec(
            num_scalar_prefetch=2,
            grid=(streams, heads),
            in_specs=[head_block(), head_block(heads), head_block(), head_block()],
            out_specs=[head_block()] * 3,
            scratch_shapes=[pltpu.VMEM((STREAM, HEAD_DIM), F32)] * 2,
        ),
        compiler_params=pltpu.CompilerParams(vmem_limit_bytes=40 << 20),
        cost_estimate=pl.CostEstimate(
            flops=10 * work * HEAD_DIM, transcendentals=work // 64,
            bytes_accessed=streams * heads * STREAM * HEAD_DIM * 20,
        ),
        name="attend_back",
    )(rates, ends, z_qk, z_qk, z_vg, d_o)


def chunk_copies(chunks, buffer, sems, turn, half=None):
    count, size = len(chunks), chunks[0].shape[0]
    if count == 1:
        rows = buffer.shape[0]
        first = 0 if half is None else pl.multiple_of(half * rows, rows)
        return [(None, pltpu.make_async_copy(chunks[0].at[pl.ds(first, rows)], buffer, sems.at[0]))]
    copies = []
    for k, chunk in enumerate(chunks):
        index = lax.rem(turn - k + count, count)
        wanted = None
        if half is not None:
            wanted = lax.div(index, count // 2) == half
            index = lax.rem(index, count // 2)
        target = buffer.at[pl.ds(pl.multiple_of(index * size, size), size)]
        copies.append((wanted, pltpu.make_async_copy(chunk, target, sems.at[k])))
    return copies


def each(copies, act):
    for wanted, copy in copies:
        if wanted is None:
            act(copy)
        else:
            pl.when(wanted)(functools.partial(act, copy))


def start(copies):
    each(copies, lambda copy: copy.start())


def finish(copies):
    each(copies, lambda copy: copy.wait())


def estimate(flops, *arrays):
    moved = sum(x.size * x.dtype.itemsize for x in arrays)
    return pl.CostEstimate(flops=flops, transcendentals=0, bytes_accessed=moved)


def limit(mebibytes):
    return pltpu.CompilerParams(vmem_limit_bytes=mebibytes << 20)


ANYWHERE = pl.BlockSpec(memory_space=pl.ANY)


def weight_buffer(chunks, share=1):
    size = len(chunks) * chunks[0].shape[0] // share
    return [pltpu.VMEM((size, chunks[0].shape[1]), LOW), pltpu.SemaphoreType.DMA((len(chunks),))]


def tile_rows(width, column=0):
    return pl.BlockSpec((TILE, width), lambda i, *_: (i, column))


def joined_rows(width, tiles):
    spec = pl.BlockSpec((TILE, width), lambda i, s: (i // (2 * tiles) * tiles + i % tiles, 0))
    return [spec, spec]


def enter_kernel(tiles, blocks, project, spots, own_ref, other_ref, *refs):
    i = pl.program_id(0)
    mine = lax.rem(lax.div(i, tiles), 2) == spots[0]
    rows = jnp.where(mine, own_ref[...], other_ref[...])
    part = rows.shape[1] // len(blocks)
    permuted = jnp.concatenate([rows[:, n * part : (n + 1) * part] for n in blocks], axis=1)
    if not project:
        all_ref, quarter_ref = refs
        all_ref[...] = permuted
        held = all_ref
    else:
        chunks, (h_ref, z_ref, scale_ref, quarter_ref, held, buffer, sems) = refs[:-7], refs[-7:]
        held[...] = permuted
        copies = chunk_copies(chunks, buffer, sems, spots[2])

        @pl.when(i == 0)
        def _():
            start(copies)

        x = rows.astype(F32)
        scale = lax.rsqrt(jnp.mean(x * x, axis=-1, keepdims=True) + EPSILON)
        scale_ref[...] = scale
        hidden = (permuted.astype(F32) * scale).astype(LOW)
        h_ref[...] = hidden

        @pl.when(i == 0)
        def _():
            finish(copies)

        z_ref[...] = matmul(hidden, buffer[...])
    size = quarter_ref.shape[1]
    quarter_ref[...] = held[:, pl.ds(pl.multiple_of(spots[1] * size, size), size)]


def enter(spots, blocks, own, other, chunks=()):
    width = own.shape[1]
    count, tiles = 2 * own.shape[0], own.shape[0] // TILE // 2
    shape = jax.ShapeDtypeStruct
    quarter = shape((count, width // GROUP), LOW)
    if chunks:
        columns = chunks[0].shape[1]
        outs = [shape((count, width), LOW), shape((count, columns), F32), shape((count, 1), F32), quarter]
        scratch = [pltpu.VMEM((TILE, width), LOW), *weight_buffer(chunks)]
    else:
        columns, scratch = 0, []
        outs = [shape((count, width), LOW), quarter]
    return pl.pallas_call(
        functools.partial(enter_kernel, tiles, blocks, bool(chunks)),
        out_shape=outs,
        grid_spec=pltpu.PrefetchScalarGridSpec(
            num_scalar_prefetch=1,
            grid=(count // TILE,),
            in_specs=joined_rows(width, tiles) + [ANYWHERE] * len(chunks),
            out_specs=[tile_rows(o.shape[1]) for o in outs],
            scratch_shapes=scratch,
        ),
        compiler_params=limit(40),
        cost_estimate=estimate(2 * count * width * columns, own, other, *chunks, *outs),
        name="enter",
    )(spots, own, other, *chunks)


def project_kernel(spots, h_ref, *refs):
    chunks, (z_ref, buffer, sems) = refs[:-3], refs[-3:]
    copies = chunk_copies(chunks, buffer, sems, spots[2])

    @pl.when(pl.program_id(0) == 0)
    def _():
        start(copies)
        finish(copies)

    z_ref[...] = matmul(h_ref[...], buffer[...])


def project(spots, hidden, chunks):
    count, width = hidden.shape
    out = jax.ShapeDtypeStruct((count, chunks[0].shape[1]), F32)
    return pl.pallas_call(
        project_kernel,
        out_shape=out,
        grid_spec=pltpu.PrefetchScalarGridSpec(
            num_scalar_prefetch=1,
            grid=(count // TILE,),
            in_specs=[tile_rows(width)] + [ANYWHERE] * len(chunks),
            out_specs=tile_rows(out.shape[1]),
            scratch_shapes=weight_buffer(chunks),
        ),
        compiler_params=limit(40),
        cost_estimate=estimate(2 * count * width * out.shape[1], hidden, *chunks, out),
        name="project",
    )(spots, hidden, *chunks)


def unit_kernel(spots, own_ref, other_ref, *refs):
    chunks, rest = refs[:-9], refs[-9:]
    h_ref, one_ref, two_ref, product_ref, scale_ref, first, second, sem_one, sem_two = rest
    split = len(chunks) // 2
    copies = [
        chunk_copies(chunks[:split], first, sem_one, spots[2]),
        chunk_copies(chunks[split:], second, sem_two, spots[2]),
    ]
    begins = pl.program_id(0) == 0

    @pl.when(begins)
    def _():
        start(copies[0])
        start(copies[1])

    mine, other = own_ref[...], other_ref[...]
    swapped = spots[0] == 1
    middle = jnp.concatenate(
        [jnp.where(swapped, other, mine), jnp.where(swapped, mine, other)], axis=1
    ).astype(F32)
    scale = lax.rsqrt(jnp.mean(middle * middle, axis=-1, keepdims=True) + EPSILON)
    scale_ref[...] = scale
    hidden = (middle * scale).astype(LOW)
    h_ref[...] = hidden

    @pl.when(begins)
    def _():
        finish(copies[0])

    z_one = matmul(hidden, first[...])

    @pl.when(begins)
    def _():
        finish(copies[1])

    z_two = matmul(hidden, second[...])
    one_ref[...] = z_one.astype(LOW)
    two_ref[...] = z_two.astype(LOW)
    product_ref[...] = (z_one * z_two).astype(LOW)


def gated_unit(spots, own, other, first, second):
    count, width, units = own.shape[0], 2 * own.shape[1], first[0].shape[1]
    shape = jax.ShapeDtypeStruct
    outs = [shape((count, width), LOW)] + [shape((count, units), LOW)] * 3 + [shape((count, 1), F32)]
    (buffer, sems) = weight_buffer(first)
    return pl.pallas_call(
        unit_kernel,
        out_shape=outs,
        grid_spec=pltpu.PrefetchScalarGridSpec(
            num_scalar_prefetch=1,
            grid=(count // TILE,),
            in_specs=[tile_rows(width // 2)] * 2 + [ANYWHERE] * (2 * len(first)),
            out_specs=[tile_rows(o.shape[1]) for o in outs],
            scratch_shapes=[buffer, buffer, sems, sems],
        ),
        compiler_params=limit(48),
        cost_estimate=estimate(4 * count * width * units, own, other, *first, *second, *outs),
        name="gated_unit",
    )(spots, own, other, *first, *second)


def unit_back_kernel(spots, dy_ref, one_ref, two_ref, *refs):
    chunks, (d_one_ref, d_two_ref, sum_ref, buffer, sems) = refs[:-5], refs[-5:]
    copies = chunk_copies(chunks, buffer, sems, spots[2])

    @pl.when(pl.program_id(0) == 0)
    def _():
        start(copies)
        finish(copies)

    d_product = matmul(dy_ref[...], buffer[...])
    z_one, z_two = one_ref[...].astype(F32), two_ref[...].astype(F32)
    d_one = d_product * z_two
    d_one_ref[...] = d_one.astype(LOW)
    d_two_ref[...] = (d_product * z_one).astype(LOW)
    sum_ref[...] = jnp.sum(d_one * z_one, axis=-1, keepdims=True)


def gated_unit_back(spots, dy, z_one, z_two, chunks):
    count, width, units = dy.shape[0], dy.shape[1], z_one.shape[1]
    shape = jax.ShapeDtypeStruct
    outs = [shape((count, units), LOW)] * 2 + [shape((count, 1), F32)]
    return pl.pallas_call(
        unit_back_kernel,
        out_shape=outs,
        grid_spec=pltpu.PrefetchScalarGridSpec(
            num_scalar_prefetch=1,
            grid=(count // TILE,),
            in_specs=[tile_rows(width), tile_rows(units), tile_rows(units)] + [ANYWHERE] * len(chunks),
            out_specs=[tile_rows(o.shape[1]) for o in outs],
            scratch_shapes=weight_buffer(chunks),
        ),
        compiler_params=limit(40),
        cost_estimate=estimate(2 * count * width * units, dy, z_one, z_two, *chunks, *outs),
        name="gated_unit_back",
    )(spots, dy, z_one, z_two, *chunks)


def fold_kernel(members, keeps, spots, *refs):
    values, refs = refs[:members], refs[members:]
    arrived, refs = (refs[0], refs[1:]) if keeps else (None, refs)
    outs = 2 if keeps else 1
    chunks, refs = refs[: -outs - 2 * members], refs[-outs - 2 * members :]
    outs, buffers, sems = refs[:outs], refs[outs : outs + members], refs[outs + members :]
    each_count = len(chunks) // members
    half = spots[0] if keeps else 1 - spots[0]
    begins = pl.program_id(0) == 0
    copies = [
        chunk_copies(chunks[m * each_count : (m + 1) * each_count], buffers[m], sems[m], spots[2], half)
        for m in range(members)
    ]

    @pl.when(begins)
    def _():
        for m in range(members):
            start(copies[m])

    whole = None
    for m in range(members):
        pl.when(begins)(functools.partial(finish, copies[m]))
        term = times_transposed(values[m][...], buffers[m][...])
        whole = term if whole is None else whole + term
    if not keeps:
        outs[0][...] = whole.astype(LOW)
    else:
        whole = whole + arrived[...].astype(F32)
        size = whole.shape[1] // 2
        upper = spots[3] == 1
        outs[0][...] = jnp.where(upper, whole[:, :size], whole[:, size:]).astype(LOW)
        outs[1][...] = jnp.where(upper, whole[:, size:], whole[:, :size])


def fold_half(spots, values, weights, arrived=None):
    count = values[0].shape[0]
    half = len(weights[0]) * weights[0][0].shape[0] // 2
    shape = jax.ShapeDtypeStruct
    if arrived is None:
        outs, extra = [shape((count, half), LOW)], []
    else:
        outs, extra = [shape((count, half // 2), LOW), shape((count, half // 2), F32)], [arrived]
    buffers, sems = zip(*[weight_buffer(w, 2) for w in weights])
    chunks = [x for w in weights for x in w]
    flops = sum(2 * count * half * v.shape[1] for v in values)
    found = pl.pallas_call(
        functools.partial(fold_kernel, len(values), arrived is not None),
        out_shape=outs,
        grid_spec=pltpu.PrefetchScalarGridSpec(
            num_scalar_prefetch=1,
            grid=(count // TILE,),
            in_specs=[tile_rows(v.shape[1]) for v in values]
            + [tile_rows(half)] * len(extra)
            + [ANYWHERE] * len(chunks),
            out_specs=[tile_rows(o.shape[1]) for o in outs],
            scratch_shapes=[*buffers, *sems],
        ),
        compiler_params=limit(40),
        cost_estimate=estimate(flops, *values, *extra, *chunks[: len(chunks) // 2], *outs),
        name="fold_half",
    )(spots, *values, *extra, *chunks)
    return found[0] if arrived is None else found


def gradient_kernel(spots, left_ref, right_ref, *refs):
    found = cross_tokens(left_ref[...], right_ref[...])
    for arrived_ref in refs[:-1]:
        found = found + arrived_ref[...].astype(F32)
    refs[-1][...] = found.astype(LOW)


def gradient_rows(spots, spread, k, left, right, arrived=()):
    count, columns = right.shape
    rows = left.shape[1] // (1 if k is None else spread)
    tiles = rows // TILE

    def block(i, s):
        return (0, i if k is None else lax.rem(s[2] + k, spread) * tiles + i)

    out = jax.ShapeDtypeStruct((rows, columns), LOW)
    return pl.pallas_call(
        gradient_kernel,
        out_shape=out,
        grid_spec=pltpu.PrefetchScalarGridSpec(
            num_scalar_prefetch=1,
            grid=(tiles,),
            in_specs=[
                pl.BlockSpec((count, TILE), block),
                pl.BlockSpec((count, columns), lambda i, s: (0, 0), pipeline_mode=pl.Buffered(1)),
            ]
            + [tile_rows(columns)] * len(arrived),
            out_specs=tile_rows(columns),
        ),
        compiler_params=limit(40),
        cost_estimate=estimate(2 * count * rows * columns, right, out, out, *arrived),
        name="gradient_rows",
    )(spots, left, right, *arrived)


def place_kernel(cuts, spots, *refs):
    quarter = pl.program_id(0)
    cross = lax.rem(lax.div(quarter, 2) + spots[0], 2) * 2 + lax.rem(lax.rem(quarter, 2) + spots[3], 2)
    for n in range(4):

        @pl.when(cross == n)
        def _():
            for (first, size), out_ref in zip(cuts, refs[4:]):
                out_ref[...] = refs[n][:, first : first + size].astype(F32)


def place_quarters(spots, pairs, *cuts):
    rows, columns = pairs[0].shape[0], pairs[0].shape[1] // 2
    outs = [jax.ShapeDtypeStruct((rows, GROUP * size), F32) for _, size in cuts]

    def block(index):
        return pl.BlockSpec((rows, columns), lambda q, s: (0, index), pipeline_mode=pl.Buffered(1))

    return pl.pallas_call(
        functools.partial(place_kernel, cuts),
        out_shape=outs,
        grid_spec=pltpu.PrefetchScalarGridSpec(
            num_scalar_prefetch=1,
            grid=(GROUP,),
            in_specs=[block(0), block(1), block(0), block(1)],
            out_specs=[pl.BlockSpec((rows, size), lambda q, s: (0, q)) for _, size in cuts],
        ),
        compiler_params=limit(40),
        cost_estimate=estimate(0, *pairs, *outs),
        name="place_quarters",
    )(spots, pairs[0], pairs[0], pairs[1], pairs[1])


def tie(*values):
    return lax.optimization_barrier(values)


def body(reps, shards, tokens, cotangent, lengths, decay_rates, *weights):
    spread = reps // GROUP
    place = lax.axis_index("shard")
    a, b, c = lax.axis_index("a"), lax.axis_index("b"), lax.axis_index("c")
    quarter = 2 * c + b
    micro, run, width = tokens.shape
    half, own = width // 2, width // GROUP
    streams = micro * GROUP // shards
    per_block = STREAM // run // GROUP * streams
    rows = width // shards
    part = rows // spread
    columns = functools.partial(lax.dynamic_slice_in_dim, axis=1)
    spots = jnp.stack([c, quarter, a, b]).astype(jnp.int32)
    blocks = [z * spread + k for k in range(spread) for z in range(shards)]

    def move(x, target):
        pairs = [(r * shards + s, target(r) * shards + s) for r in range(reps) for s in range(shards)]
        return lax.ppermute(x, AXES, pairs)

    def swap_c(x):
        return move(x, lambda r: r ^ 1)

    def swap_b(x):
        return move(x, lambda r: r ^ 2)

    def joined(*parts):
        return jnp.concatenate(parts, axis=1)

    def shift_a(x, k):
        return move(x, lambda r: (r + GROUP * k) % reps)

    def ordered(index, mine, other, axis):
        return jnp.where(
            index == 0,
            jnp.concatenate([mine, other], axis),
            jnp.concatenate([other, mine], axis),
        )


    def batch_of(s):
        return s // (shards // micro)

    def origin(r, s, p):
        run_id = (r % GROUP) * per_block + p
        stream, piece = run_id // shards, run_id % shards
        member = s % GROUP if streams == 1 else 2 * stream + s % 2
        return (r // GROUP) * GROUP + member, piece

    def routes(p):
        found = []
        for r in range(reps):
            for s in range(shards):
                from_r, from_s = origin(r, s, p ^ batch_of(s))
                found.append((from_r * shards + from_s, r * shards + s))
        return found

    def natural(x):
        return jnp.concatenate(
            [
                x[:, (k * shards + z) * part : (k * shards + z + 1) * part]
                for z in range(shards)
                for k in range(spread)
            ],
            axis=1,
        )

    def bring(x):
        arrived = [
            lax.ppermute(lax.dynamic_index_in_dim(x, (place + p) % 2, 0, False), AXES, routes(p))
            for p in range(2)
        ]
        return ordered(batch_of(place), *arrived, 0)

    def send_back(x):
        slots = natural(x).reshape(2, run, width)
        return [
            lax.ppermute(
                lax.dynamic_index_in_dim(slots, (batch_of(place) + p) % 2, 0, False),
                AXES,
                [(to, origin) for origin, to in routes(p)],
            )
            for p in range(2)
        ]

    def as_batches(arrived):
        return ordered(place % 2, arrived[0][None], arrived[1][None], 0)


    def gather_b(x):
        return ordered(b, x, swap_b(x), 1)

    def gather_c(x):
        return ordered(c, x, swap_c(x), 1)

    def gather_rows_b(x):
        return ordered(b, x, swap_b(x), 0)

    def total(x):
        x = x + swap_c(x)
        return x + swap_b(x)

    def fold_c(product):
        sent = swap_c(product(1 - c).astype(LOW))
        return product(c) + sent.astype(F32)

    def fold_b(x):
        sent = swap_b(columns(x, (1 - b) * own, own).astype(LOW))
        return columns(x, b * own, own) + sent.astype(F32)


    pick = functools.partial(lax.dynamic_index_in_dim, keepdims=False)

    def away_b(x):
        cut = x.reshape(2, 2, -1, own)
        return pick(cut, b, 0), swap_b(pick(cut, 1 - b, 0))

    def away_c(mine, arrived):
        both = ordered(b, mine, arrived, 2)
        return pick(both, c, 0), swap_c(pick(both, 1 - c, 0))

    def to_runs(x):
        return ordered(c, *away_c(*away_b(x)), 1)


    def own_features(w):
        count = shards * spread // GROUP
        cut = []
        for i in range(count):
            block = quarter * count + i
            cut.append(columns(w, (block % shards) * rows + (block // shards) * part, part))
        return jnp.concatenate(cut, axis=1)

    def own_units(w):
        return columns(w, quarter * (w.shape[1] // GROUP), w.shape[1] // GROUP)

    def over_shards(*members):
        cut = jnp.concatenate(members, axis=1) if len(members) > 1 else members[0]
        piece = lax.dynamic_slice_in_dim(cut, a * part, part, 0)
        return lax.all_gather(piece, "shard", axis=0, tiled=True)

    def over_owners(w):
        piece = lax.dynamic_slice_in_dim(w, a * part, part, 0)
        return lax.all_gather(piece, OWNERS, axis=0, tiled=True)

    def over_spread(x):
        return [shift_a(x, k) for k in range(1, spread)]

    def by_spread(relative):
        if spread == 2:
            return ordered(a, relative[0], relative[1], 0)
        stacked = jnp.stack(relative, 0)
        pick = functools.partial(lax.dynamic_index_in_dim, axis=0, keepdims=False)
        return jnp.concatenate([pick(stacked, (a - j) % spread) for j in range(spread)], axis=0)

    def in_row_order(x):
        cut = x.reshape(spread, shards, part, -1)
        return jnp.transpose(cut, (1, 0, 2, 3)).reshape(width, -1)

    def row_half(w, h):
        return lax.dynamic_slice_in_dim(w, h * half, half, 0)


    def away(left, right):
        return [gradient_rows(spots, spread, k, left, right) for k in range(1, spread)]

    def in_two(terms):
        middles = [x.shape[0] // 2 for x in terms]
        return [x[:m] for x, m in zip(terms, middles)], [x[m:] for x, m in zip(terms, middles)]

    def stacked(upper, lower):
        return [jnp.concatenate(pair, axis=0) for pair in zip(upper, lower)]

    def sent_a(terms):
        return [shift_a(x, k + 1) for k, x in enumerate(terms)]

    def scattered(x):
        return lax.psum_scatter(x, "shard", scatter_dimension=0, tiled=True)

    def whole_rows(left, right):
        return gradient_rows(spots, spread, None, left, right)

    def scattered_all(x):
        return lax.psum_scatter(x, OWNERS, scatter_dimension=0, tiled=True)

    def summed(left, right, arrived):
        return scattered(gradient_rows(spots, spread, 0, left, right, arrived))

    def spread_a(x):
        return by_spread([x] + over_spread(x))

    def spread_b(x):
        return jnp.concatenate([x, swap_b(x)], axis=1)

    def spread_c(pair):
        return pair, swap_c(pair)

    def features_in_order(pairs, first, size):
        full = pairs[0].shape[1] // 2
        cut = [x[:, i * full + first : i * full + first + size] for x in pairs for i in range(2)]
        pair = [ordered(b, cut[n], cut[n + 1], 1) for n in (0, 2)]
        return natural(ordered(c, pair[0], pair[1], 1)).astype(F32)


    w_query, w_key, w_value, w_gate, w_out, w_one, w_two, w_down = weights
    g_qk = over_shards(own_units(w_query), own_units(w_key))
    g_vg = over_shards(own_units(w_value), own_units(w_gate))
    g_o = over_shards(own_features(w_out))
    g_1 = over_shards(own_units(w_one))
    g_2 = over_shards(own_units(w_two))
    w_d = [over_owners(own_units(w_down))]

    heads = HEADS // GROUP
    rates = lax.dynamic_slice_in_dim(decay_rates, quarter * heads, heads, 0)
    cuts = gather_rows_b(lengths.reshape(1, -1))
    cuts = ordered(c, cuts, swap_c(cuts), 0).reshape(GROUP, micro, -1)
    if streams == 1:
        batch = place // GROUP
        member = place % GROUP
        chosen = lax.dynamic_slice_in_dim(cuts, 2 * (member % 2) + member // 2, 1, 0)
    else:
        batch = place // 2
        chosen = lax.dynamic_index_in_dim(cuts.reshape(2, 2, micro, -1), place % 2, 0, False)
    chosen = lax.dynamic_index_in_dim(chosen, batch, 1, False)
    seq_ends = [chosen[:, 0]]
    for i in range(1, chosen.shape[1]):
        seq_ends.append(seq_ends[-1] + chosen[:, i])
    ends = jnp.stack(seq_ends, axis=1)

    x_run = bring(tokens)
    x_run, g_qk = tie(x_run, g_qk)

    x_pair = gather_rows_b(x_run)
    s_qk = over_spread(g_qk)
    x_pair, s_qk, g_vg = tie(x_pair, s_qk, g_vg)

    s_vg = over_spread(g_vg)
    w_qk = [g_qk, *s_qk]
    hidden_one, z_qk, x_scale, x_own = enter(spots, blocks, x_pair, swap_c(x_pair), w_qk)
    z_qk, hidden_one, s_vg, g_o = tie(z_qk, hidden_one, s_vg, g_o)

    s_o = over_spread(g_o)
    w_vg = [g_vg, *s_vg]
    z_vg = project(spots, hidden_one, w_vg)
    attended = attend(rates, ends, z_qk, z_vg)
    gate = z_vg[:, own:]
    o_scale = lax.rsqrt(total(jnp.sum(attended * attended, axis=-1)) / width + EPSILON)[:, None]
    lifted = (attended * gate).astype(LOW)
    lifted, s_o, g_1, cotangent = tie(lifted, s_o, g_1, cotangent)

    s_1 = over_spread(g_1)
    lifted = gather_b(lifted)
    lifted, s_1, g_2, o_scale, cotangent = tie(lifted, s_1, g_2, o_scale, cotangent)

    s_2 = over_spread(g_2)
    dy_run = bring(cotangent)
    lifted = gather_c(lifted)
    w_o = in_row_order(by_spread([g_o, *s_o]))
    branch = o_scale * matmul(lifted, w_o)
    middle = x_own.astype(F32) + branch
    low_middle = gather_b(middle.astype(LOW))
    low_middle, s_2, dy_run = tie(low_middle, s_2, dy_run)

    other_middle = swap_c(low_middle)
    dy_other = swap_b(dy_run)
    w_1, w_2 = [g_1, *s_1], [g_2, *s_2]
    hidden_two, z_one, z_two, product, m_scale = gated_unit(spots, low_middle, other_middle, w_1, w_2)
    z_one, z_two, product, dy_other = tie(z_one, z_two, product, dy_other)

    dy_pair = ordered(b, dy_run, dy_other, 0)
    dy_all, dy_own = enter(spots, blocks, dy_pair, swap_c(dy_pair))
    f_down = whole_rows(dy_all, product)
    z_one, z_two, product, f_down, w_d[0] = tie(z_one, z_two, product, f_down, w_d[0])


    f_down = scattered_all(f_down)
    d_one, d_two, lean_m = gated_unit_back(spots, dy_all, z_one, z_two, w_d)
    sent = fold_half(spots, [d_one, d_two], [w_1, w_2])
    sent, d_two, lean_m = tie(sent, d_two, lean_m)

    arrived = swap_c(sent)
    t_two = away(hidden_two, d_two)
    lean_m = lean_m[:, 0]
    lean_c = swap_c(lean_m)
    sent, mine = fold_half(spots, [d_one, d_two], [w_1, w_2], arrived)
    sent, d_one, t_two, product, lean_c = tie(sent, d_one, t_two, product, lean_c)

    crossed = swap_b(sent)
    lean_m = lean_m + lean_c
    lean_b = swap_b(lean_m)
    upper, lower = in_two(t_two)
    upper = sent_a(upper)
    f_one = whole_rows(hidden_two, d_one)
    result = fold_half(spots, [product], [w_d])
    crossed, result, f_one, upper, f_down, lean_b = tie(crossed, result, f_one, upper, f_down, lean_b)

    f_one = scattered_all(f_one)
    d_hidden = mine + crossed.astype(F32)
    m_normed = middle * m_scale
    lean = (lean_m + lean_b)[:, None] * (2.0 / width)
    d_middle = dy_own.astype(F32) + m_scale * (d_hidden - m_normed * lean)
    d_branch = d_middle.astype(LOW)
    lean_o = jnp.sum(d_middle * branch, axis=-1)
    sent = times_transposed(d_branch, row_half(w_o, 1 - c)).astype(LOW)
    sent, result, d_middle, lean_o = tie(sent, result, d_middle, lean_o)

    arrived = swap_c(sent)
    r_result = swap_c(result)
    y_down = spread_a(f_down)
    lean_o = lean_o + swap_c(lean_o)
    p_out = cross_tokens(lifted, (o_scale * d_middle).astype(LOW)).astype(LOW)
    p_out = jnp.transpose(p_out.reshape(shards, spread, part, -1), (1, 0, 2, 3))
    p_out = p_out.reshape(spread, width // spread, -1)
    t_out = [lax.dynamic_index_in_dim(p_out, (a + k) % spread, 0, False) for k in range(spread)]
    d_gated = times_transposed(d_branch, row_half(w_o, c)) + arrived.astype(F32)
    sent = columns(d_gated, (1 - b) * own, own).astype(LOW)
    mine = columns(d_gated, b * own, own)
    sent, mine, r_result, t_out, lean_o, y_down = tie(sent, mine, r_result, t_out, lean_o, y_down)

    crossed = swap_b(sent)
    lean_b = swap_b(lean_o)
    r_out = sent_a(t_out[1:])
    result, result_mine = fold_half(spots, [product], [w_d], r_result)
    crossed, result, r_out, lower, lean_b = tie(crossed, result, r_out, lower, lean_b)

    lower = sent_a(lower)
    result = swap_b(result)
    f_out = scattered(sum([x.astype(F32) for x in r_out], t_out[0].astype(F32)).astype(LOW))
    o_normed = attended * o_scale
    d_gated = mine + crossed.astype(F32)
    d_gate = (d_gated * o_normed).astype(LOW)
    lean = (lean_o + lean_b)[:, None] / width
    d_attended = (o_scale * (d_gated * gate - o_normed * lean)).astype(LOW)
    d_query, d_key, d_value = attend_back(rates, ends, z_qk, z_vg, d_attended)
    d_qk = joined(d_query, d_key)
    d_vg = joined(d_value, d_gate)
    t_qk = away(hidden_one, d_qk)
    d_qk, d_vg, t_qk, lower, result = tie(d_qk, d_vg, t_qk, lower, result)

    qk_a, qk_b = in_two(t_qk)
    qk_a = sent_a(qk_a)
    f_two = gradient_rows(spots, spread, 0, hidden_two, d_two, stacked(upper, lower))
    output, out_b = away_b((middle + (result_mine + result.astype(F32))).astype(LOW))
    f_two, qk_a, qk_b, out_b, d_qk, d_vg = tie(f_two, qk_a, qk_b, out_b, d_qk, d_vg)

    f_two = scattered(f_two)
    qk_b = sent_a(qk_b)
    output, out_c = away_c(output, out_b)
    t_vg = away(hidden_one, d_vg)
    sent = fold_half(spots, [d_qk, d_vg], [w_qk, w_vg])
    sent, t_vg, d_qk, d_vg, out_c, qk_b = tie(sent, t_vg, d_qk, d_vg, out_c, qk_b)

    arrived = swap_c(sent)
    vg_a, vg_b = in_two(t_vg)
    vg_a = sent_a(vg_a)
    f_qk = gradient_rows(spots, spread, 0, hidden_one, d_qk, stacked(qk_a, qk_b))
    lean_x = jnp.sum(z_qk * d_qk.astype(F32), axis=-1) + jnp.sum(z_vg * d_vg.astype(F32), axis=-1)
    arrived, vg_a, vg_b, f_qk, lean_x = tie(arrived, vg_a, vg_b, f_qk, lean_x)

    f_qk = scattered(f_qk)
    vg_b = sent_a(vg_b)
    x_down = swap_b(y_down)
    lean_x = lean_x + swap_c(lean_x)
    sent, mine = fold_half(spots, [d_qk, d_vg], [w_qk, w_vg], arrived)
    sent, mine, vg_b, lean_x, x_down, d_vg, f_one = tie(sent, mine, vg_b, lean_x, x_down, d_vg, f_one)

    crossed = swap_b(sent)
    lean_b = swap_b(lean_x)
    f_vg = scattered(gradient_rows(spots, spread, 0, hidden_one, d_vg, stacked(vg_a, vg_b)))
    y_one = over_spread(f_one)
    four_down = spread_c(joined(y_down, x_down))
    crossed, lean_b, y_one, four_down, f_two, f_out = tie(crossed, lean_b, y_one, four_down, f_two, f_out)

    d_hidden = mine + crossed.astype(F32)
    x_normed = x_own.astype(F32) * x_scale
    lean = (lean_x + lean_b)[:, None] / width
    input_grad = to_runs((d_middle + x_scale * (d_hidden - x_normed * lean)).astype(LOW))
    output = send_back(ordered(c, output, out_c, 1))
    y_one = by_spread([f_one, *y_one])
    x_one = swap_b(y_one)
    f_oqk = joined(f_out, f_qk)
    x_oqk = swap_b(f_oqk)
    y_two = over_spread(f_two)
    y_vg = over_spread(f_vg)
    units = f_one.shape[1]
    [g_down] = place_quarters(spots, four_down, (0, units))
    input_grad, output, x_one, y_two, x_oqk, y_vg, g_down = tie(
        input_grad, output, x_one, y_two, x_oqk, y_vg, g_down
    )

    y_vg = by_spread([f_vg, *y_vg])
    x_vg = swap_b(y_vg)
    y_two = by_spread([f_two, *y_two])
    x_two = swap_b(y_two)
    f_oqk = joined(f_oqk, x_oqk)
    y_oqk = over_spread(f_oqk)
    input_grad = send_back(input_grad)
    output = as_batches(output)
    [g_one] = place_quarters(spots, spread_c(joined(y_one, x_one)), (0, units))
    x_vg, x_two, y_oqk, input_grad, output, g_one = tie(x_vg, x_two, y_oqk, input_grad, output, g_one)

    four_vg = spread_c(joined(y_vg, x_vg))
    four_two = spread_c(joined(y_two, x_two))
    four_oqk = spread_c(by_spread([f_oqk, *y_oqk]))
    g_query, g_key = place_quarters(spots, four_oqk, (own, own), (2 * own, own))
    g_value, g_gate = place_quarters(spots, four_vg, (0, own), (own, own))
    [g_two] = place_quarters(spots, four_two, (0, units))
    g_out = features_in_order(four_oqk, 0, own)
    return output, as_batches(input_grad), g_query, g_key, g_value, g_gate, g_out, g_one, g_two, g_down


def solution(mesh):
    reps, shards = mesh.shape["rep"], mesh.shape["shard"]
    devices = mesh.devices.reshape(reps // GROUP, 2, 2, shards)
    rep = ("a", "b", "c")
    by_tokens = P(None, (*rep, "shard"), None)
    by_rows = P("shard", None)
    return jax.shard_map(
        functools.partial(body, reps, shards),
        mesh=Mesh(devices, AXES),
        in_specs=(by_tokens, by_tokens, P(None, rep, None), P(), *[by_rows] * 8),
        out_specs=(by_tokens, by_tokens, *[by_rows] * 8),
        check_vma=False,
    )
```

```python
import functools

import jax
import jax.numpy as jnp
from jax import lax
from jax.experimental import pallas as pl
from jax.experimental.pallas import tpu as pltpu
from jax.sharding import Mesh, PartitionSpec as P

HEADS = 16
HEAD_DIM = 128
STREAM = 1024
GROUP = 4
BLOCK = 256
TILE = 256
EPSILON = 1e-06
AXES = ("a", "b", "c", "shard")
OWNERS = ("a", "shard")
LOW = jnp.bfloat16
F32 = jnp.float32


def matmul(former, latter):
    return jnp.dot(former, latter, preferred_element_type=F32)


def times_transposed(former, latter):
    return lax.dot_general(former, latter, (((1,), (1,)), ((), ())), preferred_element_type=F32)


def cross_tokens(former, latter):
    return lax.dot_general(former, latter, (((0,), (0,)), ((), ())), preferred_element_type=F32)


def masked_decay(rate, ends, first, columns):
    row = first + lax.broadcasted_iota(jnp.int32, (BLOCK, 1), 0)
    column = lax.broadcasted_iota(jnp.int32, (1, columns), 1)
    begin = jnp.zeros((BLOCK, 1), jnp.int32)
    for end in ends:
        begin = jnp.where(row >= end, end, begin)
    falling = jnp.exp(-rate * (row - first).astype(F32))
    rising = jnp.exp(rate * (column - first).astype(F32))
    allowed = (column <= row) & (column >= begin)
    return jnp.where(allowed, falling * rising, 0.0)


def attend_kernel(rates, ends, zq_ref, zk_ref, zv_ref, out_ref):
    stream, head = pl.program_id(0), pl.program_id(1)
    rate = rates[head]
    bounds = [ends[stream, i] for i in range(ends.shape[1])]
    zq, zk = zq_ref[...], zk_ref[...]
    q = (zq * jax.nn.sigmoid(zq)).astype(LOW)
    k = (zk * jax.nn.sigmoid(zk)).astype(LOW)
    v = zv_ref[...].astype(LOW)
    for first in range(0, STREAM, BLOCK):
        columns = first + BLOCK
        mask = masked_decay(rate, bounds, first, columns)
        scores = times_transposed(q[first:columns], k[:columns])
        weights = (scores * mask).astype(LOW)
        out_ref[first:columns, :] = matmul(weights, v[:columns])


def attend_back_kernel(
    rates, ends, zq_ref, zk_ref, zv_ref, do_ref, dzq_ref, dzk_ref, dzv_ref, dk_ref, dv_ref
):
    stream, head = pl.program_id(0), pl.program_id(1)
    rate = rates[head]
    bounds = [ends[stream, i] for i in range(ends.shape[1])]
    zq, zk = zq_ref[...], zk_ref[...]
    sig_q, sig_k = jax.nn.sigmoid(zq), jax.nn.sigmoid(zk)
    q = (zq * sig_q).astype(LOW)
    k = (zk * sig_k).astype(LOW)
    slope_q = sig_q * (1.0 + zq * (1.0 - sig_q))
    v = zv_ref[...].astype(LOW)
    d_o = do_ref[...]
    dk_ref[...] = jnp.zeros_like(dk_ref)
    dv_ref[...] = jnp.zeros_like(dv_ref)
    for first in range(0, STREAM, BLOCK):
        columns = first + BLOCK
        rows = slice(first, columns)
        mask = masked_decay(rate, bounds, first, columns)
        weights = (times_transposed(q[rows], k[:columns]) * mask).astype(LOW)
        d_scores = (times_transposed(d_o[rows], v[:columns]) * mask).astype(LOW)
        dzq_ref[rows, :] = (matmul(d_scores, k[:columns]) * slope_q[rows]).astype(LOW)
        dk_ref[:columns, :] += cross_tokens(d_scores, q[rows])
        dv_ref[:columns, :] += cross_tokens(weights, d_o[rows])
    dzk_ref[...] = (dk_ref[...] * (sig_k * (1.0 + zk * (1.0 - sig_k)))).astype(LOW)
    dzv_ref[...] = dv_ref[...].astype(LOW)


def head_block(offset=0):
    return pl.BlockSpec((STREAM, HEAD_DIM), lambda g, h, *_: (g, h + offset))


def attend(rates, ends, z_qk, z_vg):
    heads, streams = rates.shape[0], ends.shape[0]
    work = streams * heads * STREAM * STREAM
    return pl.pallas_call(
        attend_kernel,
        out_shape=jax.ShapeDtypeStruct((streams * STREAM, heads * HEAD_DIM), F32),
        grid_spec=pltpu.PrefetchScalarGridSpec(
            num_scalar_prefetch=2,
            grid=(streams, heads),
            in_specs=[head_block(), head_block(heads), head_block()],
            out_specs=head_block(),
        ),
        compiler_params=pltpu.CompilerParams(vmem_limit_bytes=40 << 20),
        cost_estimate=pl.CostEstimate(
            flops=4 * work * HEAD_DIM, transcendentals=work // 64,
            bytes_accessed=streams * heads * STREAM * HEAD_DIM * 16,
        ),
        name="attend",
    )(rates, ends, z_qk, z_qk, z_vg)


def attend_back(rates, ends, z_qk, z_vg, d_o):
    heads, streams = rates.shape[0], ends.shape[0]
    work = streams * heads * STREAM * STREAM
    return pl.pallas_call(
        attend_back_kernel,
        out_shape=[jax.ShapeDtypeStruct((streams * STREAM, heads * HEAD_DIM), LOW)] * 3,
        grid_spec=pltpu.PrefetchScalarGridSpec(
            num_scalar_prefetch=2,
            grid=(streams, heads),
            in_specs=[head_block(), head_block(heads), head_block(), head_block()],
            out_specs=[head_block()] * 3,
            scratch_shapes=[pltpu.VMEM((STREAM, HEAD_DIM), F32)] * 2,
        ),
        compiler_params=pltpu.CompilerParams(vmem_limit_bytes=40 << 20),
        cost_estimate=pl.CostEstimate(
            flops=10 * work * HEAD_DIM, transcendentals=work // 64,
            bytes_accessed=streams * heads * STREAM * HEAD_DIM * 20,
        ),
        name="attend_back",
    )(rates, ends, z_qk, z_qk, z_vg, d_o)


def chunk_copies(chunks, buffer, sems, turn, half=None):
    count, size = len(chunks), chunks[0].shape[0]
    if count == 1:
        rows = buffer.shape[0]
        first = 0 if half is None else pl.multiple_of(half * rows, rows)
        return [(None, pltpu.make_async_copy(chunks[0].at[pl.ds(first, rows)], buffer, sems.at[0]))]
    copies = []
    for k, chunk in enumerate(chunks):
        index = lax.rem(turn - k + count, count)
        wanted = None
        if half is not None:
            wanted = lax.div(index, count // 2) == half
            index = lax.rem(index, count // 2)
        target = buffer.at[pl.ds(pl.multiple_of(index * size, size), size)]
        copies.append((wanted, pltpu.make_async_copy(chunk, target, sems.at[k])))
    return copies


def each(copies, act):
    for wanted, copy in copies:
        if wanted is None:
            act(copy)
        else:
            pl.when(wanted)(functools.partial(act, copy))


def start(copies):
    each(copies, lambda copy: copy.start())


def finish(copies):
    each(copies, lambda copy: copy.wait())


def estimate(flops, *arrays):
    moved = sum(x.size * x.dtype.itemsize for x in arrays)
    return pl.CostEstimate(flops=flops, transcendentals=0, bytes_accessed=moved)


def limit(mebibytes):
    return pltpu.CompilerParams(vmem_limit_bytes=mebibytes << 20)


ANYWHERE = pl.BlockSpec(memory_space=pl.ANY)


def weight_buffer(chunks, share=1):
    size = len(chunks) * chunks[0].shape[0] // share
    return [pltpu.VMEM((size, chunks[0].shape[1]), LOW), pltpu.SemaphoreType.DMA((len(chunks),))]


def tile_rows(width, column=0):
    return pl.BlockSpec((TILE, width), lambda i, *_: (i, column))


def joined_rows(width, tiles):
    spec = pl.BlockSpec((TILE, width), lambda i, s: (i // (2 * tiles) * tiles + i % tiles, 0))
    return [spec, spec]


def enter_kernel(tiles, blocks, project, spots, own_ref, other_ref, *refs):
    i = pl.program_id(0)
    mine = lax.rem(lax.div(i, tiles), 2) == spots[0]
    rows = jnp.where(mine, own_ref[...], other_ref[...])
    part = rows.shape[1] // len(blocks)
    permuted = jnp.concatenate([rows[:, n * part : (n + 1) * part] for n in blocks], axis=1)
    if not project:
        all_ref, quarter_ref = refs
        all_ref[...] = permuted
        held = all_ref
    else:
        chunks, (h_ref, z_ref, scale_ref, quarter_ref, held, buffer, sems) = refs[:-7], refs[-7:]
        held[...] = permuted
        copies = chunk_copies(chunks, buffer, sems, spots[2])

        @pl.when(i == 0)
        def _():
            start(copies)

        x = rows.astype(F32)
        scale = lax.rsqrt(jnp.mean(x * x, axis=-1, keepdims=True) + EPSILON)
        scale_ref[...] = scale
        hidden = (permuted.astype(F32) * scale).astype(LOW)
        h_ref[...] = hidden

        @pl.when(i == 0)
        def _():
            finish(copies)

        z_ref[...] = matmul(hidden, buffer[...])
    size = quarter_ref.shape[1]
    quarter_ref[...] = held[:, pl.ds(pl.multiple_of(spots[1] * size, size), size)]


def enter(spots, blocks, own, other, chunks=()):
    width = own.shape[1]
    count, tiles = 2 * own.shape[0], own.shape[0] // TILE // 2
    shape = jax.ShapeDtypeStruct
    quarter = shape((count, width // GROUP), LOW)
    if chunks:
        columns = chunks[0].shape[1]
        outs = [shape((count, width), LOW), shape((count, columns), F32), shape((count, 1), F32), quarter]
        scratch = [pltpu.VMEM((TILE, width), LOW), *weight_buffer(chunks)]
    else:
        columns, scratch = 0, []
        outs = [shape((count, width), LOW), quarter]
    return pl.pallas_call(
        functools.partial(enter_kernel, tiles, blocks, bool(chunks)),
        out_shape=outs,
        grid_spec=pltpu.PrefetchScalarGridSpec(
            num_scalar_prefetch=1,
            grid=(count // TILE,),
            in_specs=joined_rows(width, tiles) + [ANYWHERE] * len(chunks),
            out_specs=[tile_rows(o.shape[1]) for o in outs],
            scratch_shapes=scratch,
        ),
        compiler_params=limit(40),
        cost_estimate=estimate(2 * count * width * columns, own, other, *chunks, *outs),
        name="enter",
    )(spots, own, other, *chunks)


def project_kernel(spots, h_ref, *refs):
    chunks, (z_ref, buffer, sems) = refs[:-3], refs[-3:]
    copies = chunk_copies(chunks, buffer, sems, spots[2])

    @pl.when(pl.program_id(0) == 0)
    def _():
        start(copies)
        finish(copies)

    z_ref[...] = matmul(h_ref[...], buffer[...])


def project(spots, hidden, chunks):
    count, width = hidden.shape
    out = jax.ShapeDtypeStruct((count, chunks[0].shape[1]), F32)
    return pl.pallas_call(
        project_kernel,
        out_shape=out,
        grid_spec=pltpu.PrefetchScalarGridSpec(
            num_scalar_prefetch=1,
            grid=(count // TILE,),
            in_specs=[tile_rows(width)] + [ANYWHERE] * len(chunks),
            out_specs=tile_rows(out.shape[1]),
            scratch_shapes=weight_buffer(chunks),
        ),
        compiler_params=limit(40),
        cost_estimate=estimate(2 * count * width * out.shape[1], hidden, *chunks, out),
        name="project",
    )(spots, hidden, *chunks)


def unit_kernel(spots, own_ref, other_ref, *refs):
    chunks, rest = refs[:-9], refs[-9:]
    h_ref, one_ref, two_ref, product_ref, scale_ref, first, second, sem_one, sem_two = rest
    split = len(chunks) // 2
    copies = [
        chunk_copies(chunks[:split], first, sem_one, spots[2]),
        chunk_copies(chunks[split:], second, sem_two, spots[2]),
    ]
    begins = pl.program_id(0) == 0

    @pl.when(begins)
    def _():
        start(copies[0])
        start(copies[1])

    mine, other = own_ref[...], other_ref[...]
    swapped = spots[0] == 1
    middle = jnp.concatenate(
        [jnp.where(swapped, other, mine), jnp.where(swapped, mine, other)], axis=1
    ).astype(F32)
    scale = lax.rsqrt(jnp.mean(middle * middle, axis=-1, keepdims=True) + EPSILON)
    scale_ref[...] = scale
    hidden = (middle * scale).astype(LOW)
    h_ref[...] = hidden

    @pl.when(begins)
    def _():
        finish(copies[0])

    z_one = matmul(hidden, first[...])

    @pl.when(begins)
    def _():
        finish(copies[1])

    z_two = matmul(hidden, second[...])
    one_ref[...] = z_one.astype(LOW)
    two_ref[...] = z_two.astype(LOW)
    product_ref[...] = (z_one * z_two).astype(LOW)


def gated_unit(spots, own, other, first, second):
    count, width, units = own.shape[0], 2 * own.shape[1], first[0].shape[1]
    shape = jax.ShapeDtypeStruct
    outs = [shape((count, width), LOW)] + [shape((count, units), LOW)] * 3 + [shape((count, 1), F32)]
    (buffer, sems) = weight_buffer(first)
    return pl.pallas_call(
        unit_kernel,
        out_shape=outs,
        grid_spec=pltpu.PrefetchScalarGridSpec(
            num_scalar_prefetch=1,
            grid=(count // TILE,),
            in_specs=[tile_rows(width // 2)] * 2 + [ANYWHERE] * (2 * len(first)),
            out_specs=[tile_rows(o.shape[1]) for o in outs],
            scratch_shapes=[buffer, buffer, sems, sems],
        ),
        compiler_params=limit(48),
        cost_estimate=estimate(4 * count * width * units, own, other, *first, *second, *outs),
        name="gated_unit",
    )(spots, own, other, *first, *second)


def unit_back_kernel(spots, dy_ref, one_ref, two_ref, *refs):
    chunks, (d_one_ref, d_two_ref, sum_ref, buffer, sems) = refs[:-5], refs[-5:]
    copies = chunk_copies(chunks, buffer, sems, spots[2])

    @pl.when(pl.program_id(0) == 0)
    def _():
        start(copies)
        finish(copies)

    d_product = matmul(dy_ref[...], buffer[...])
    z_one, z_two = one_ref[...].astype(F32), two_ref[...].astype(F32)
    d_one = d_product * z_two
    d_one_ref[...] = d_one.astype(LOW)
    d_two_ref[...] = (d_product * z_one).astype(LOW)
    sum_ref[...] = jnp.sum(d_one * z_one, axis=-1, keepdims=True)


def gated_unit_back(spots, dy, z_one, z_two, chunks):
    count, width, units = dy.shape[0], dy.shape[1], z_one.shape[1]
    shape = jax.ShapeDtypeStruct
    outs = [shape((count, units), LOW)] * 2 + [shape((count, 1), F32)]
    return pl.pallas_call(
        unit_back_kernel,
        out_shape=outs,
        grid_spec=pltpu.PrefetchScalarGridSpec(
            num_scalar_prefetch=1,
            grid=(count // TILE,),
            in_specs=[tile_rows(width), tile_rows(units), tile_rows(units)] + [ANYWHERE] * len(chunks),
            out_specs=[tile_rows(o.shape[1]) for o in outs],
            scratch_shapes=weight_buffer(chunks),
        ),
        compiler_params=limit(40),
        cost_estimate=estimate(2 * count * width * units, dy, z_one, z_two, *chunks, *outs),
        name="gated_unit_back",
    )(spots, dy, z_one, z_two, *chunks)


def fold_kernel(members, keeps, spots, *refs):
    values, refs = refs[:members], refs[members:]
    arrived, refs = (refs[0], refs[1:]) if keeps else (None, refs)
    outs = 2 if keeps else 1
    chunks, refs = refs[: -outs - 2 * members], refs[-outs - 2 * members :]
    outs, buffers, sems = refs[:outs], refs[outs : outs + members], refs[outs + members :]
    each_count = len(chunks) // members
    half = spots[0] if keeps else 1 - spots[0]
    begins = pl.program_id(0) == 0
    copies = [
        chunk_copies(chunks[m * each_count : (m + 1) * each_count], buffers[m], sems[m], spots[2], half)
        for m in range(members)
    ]

    @pl.when(begins)
    def _():
        for m in range(members):
            start(copies[m])

    whole = None
    for m in range(members):
        pl.when(begins)(functools.partial(finish, copies[m]))
        term = times_transposed(values[m][...], buffers[m][...])
        whole = term if whole is None else whole + term
    if not keeps:
        outs[0][...] = whole.astype(LOW)
    else:
        whole = whole + arrived[...].astype(F32)
        size = whole.shape[1] // 2
        upper = spots[3] == 1
        outs[0][...] = jnp.where(upper, whole[:, :size], whole[:, size:]).astype(LOW)
        outs[1][...] = jnp.where(upper, whole[:, size:], whole[:, :size])


def fold_half(spots, values, weights, arrived=None):
    count = values[0].shape[0]
    half = len(weights[0]) * weights[0][0].shape[0] // 2
    shape = jax.ShapeDtypeStruct
    if arrived is None:
        outs, extra = [shape((count, half), LOW)], []
    else:
        outs, extra = [shape((count, half // 2), LOW), shape((count, half // 2), F32)], [arrived]
    buffers, sems = zip(*[weight_buffer(w, 2) for w in weights])
    chunks = [x for w in weights for x in w]
    flops = sum(2 * count * half * v.shape[1] for v in values)
    found = pl.pallas_call(
        functools.partial(fold_kernel, len(values), arrived is not None),
        out_shape=outs,
        grid_spec=pltpu.PrefetchScalarGridSpec(
            num_scalar_prefetch=1,
            grid=(count // TILE,),
            in_specs=[tile_rows(v.shape[1]) for v in values]
            + [tile_rows(half)] * len(extra)
            + [ANYWHERE] * len(chunks),
            out_specs=[tile_rows(o.shape[1]) for o in outs],
            scratch_shapes=[*buffers, *sems],
        ),
        compiler_params=limit(40),
        cost_estimate=estimate(flops, *values, *extra, *chunks[: len(chunks) // 2], *outs),
        name="fold_half",
    )(spots, *values, *extra, *chunks)
    return found[0] if arrived is None else found


def gradient_kernel(spots, left_ref, right_ref, *refs):
    found = cross_tokens(left_ref[...], right_ref[...])
    for arrived_ref in refs[:-1]:
        found = found + arrived_ref[...].astype(F32)
    refs[-1][...] = found.astype(LOW)


def gradient_rows(spots, spread, k, left, right, arrived=()):
    count, columns = right.shape
    rows = left.shape[1] // (1 if k is None else spread)
    tiles = rows // TILE

    def block(i, s):
        return (0, i if k is None else lax.rem(s[2] + k, spread) * tiles + i)

    out = jax.ShapeDtypeStruct((rows, columns), LOW)
    return pl.pallas_call(
        gradient_kernel,
        out_shape=out,
        grid_spec=pltpu.PrefetchScalarGridSpec(
            num_scalar_prefetch=1,
            grid=(tiles,),
            in_specs=[
                pl.BlockSpec((count, TILE), block),
                pl.BlockSpec((count, columns), lambda i, s: (0, 0), pipeline_mode=pl.Buffered(1)),
            ]
            + [tile_rows(columns)] * len(arrived),
            out_specs=tile_rows(columns),
        ),
        compiler_params=limit(40),
        cost_estimate=estimate(2 * count * rows * columns, right, out, out, *arrived),
        name="gradient_rows",
    )(spots, left, right, *arrived)


def place_kernel(cuts, spots, *refs):
    quarter = pl.program_id(0)
    cross = lax.rem(lax.div(quarter, 2) + spots[0], 2) * 2 + lax.rem(lax.rem(quarter, 2) + spots[3], 2)
    for n in range(4):

        @pl.when(cross == n)
        def _():
            for (first, size), out_ref in zip(cuts, refs[4:]):
                out_ref[...] = refs[n][:, first : first + size].astype(F32)


def place_quarters(spots, pairs, *cuts):
    rows, columns = pairs[0].shape[0], pairs[0].shape[1] // 2
    outs = [jax.ShapeDtypeStruct((rows, GROUP * size), F32) for _, size in cuts]

    def block(index):
        return pl.BlockSpec((rows, columns), lambda q, s: (0, index), pipeline_mode=pl.Buffered(1))

    return pl.pallas_call(
        functools.partial(place_kernel, cuts),
        out_shape=outs,
        grid_spec=pltpu.PrefetchScalarGridSpec(
            num_scalar_prefetch=1,
            grid=(GROUP,),
            in_specs=[block(0), block(1), block(0), block(1)],
            out_specs=[pl.BlockSpec((rows, size), lambda q, s: (0, q)) for _, size in cuts],
        ),
        compiler_params=limit(40),
        cost_estimate=estimate(0, *pairs, *outs),
        name="place_quarters",
    )(spots, pairs[0], pairs[0], pairs[1], pairs[1])


def tie(*values):
    return lax.optimization_barrier(values)


def body(reps, shards, tokens, cotangent, lengths, decay_rates, *weights):
    spread = reps // GROUP
    place = lax.axis_index("shard")
    a, b, c = lax.axis_index("a"), lax.axis_index("b"), lax.axis_index("c")
    quarter = 2 * c + b
    micro, run, width = tokens.shape
    half, own = width // 2, width // GROUP
    streams = micro * GROUP // shards
    per_block = STREAM // run // GROUP * streams
    rows = width // shards
    part = rows // spread
    columns = functools.partial(lax.dynamic_slice_in_dim, axis=1)
    spots = jnp.stack([c, quarter, a, b]).astype(jnp.int32)
    blocks = [z * spread + k for k in range(spread) for z in range(shards)]

    def move(x, target):
        pairs = [(r * shards + s, target(r) * shards + s) for r in range(reps) for s in range(shards)]
        return lax.ppermute(x, AXES, pairs)

    def swap_c(x):
        return move(x, lambda r: r ^ 1)

    def swap_b(x):
        return move(x, lambda r: r ^ 2)

    def joined(*parts):
        return jnp.concatenate(parts, axis=1)

    def shift_a(x, k):
        return move(x, lambda r: (r + GROUP * k) % reps)

    def ordered(index, mine, other, axis):
        return jnp.where(
            index == 0,
            jnp.concatenate([mine, other], axis),
            jnp.concatenate([other, mine], axis),
        )


    def batch_of(s):
        return s // (shards // micro)

    def origin(r, s, p):
        run_id = (r % GROUP) * per_block + p
        stream, piece = run_id // shards, run_id % shards
        member = s % GROUP if streams == 1 else 2 * stream + s % 2
        return (r // GROUP) * GROUP + member, piece

    def routes(p):
        found = []
        for r in range(reps):
            for s in range(shards):
                from_r, from_s = origin(r, s, p ^ batch_of(s))
                found.append((from_r * shards + from_s, r * shards + s))
        return found

    def natural(x):
        return jnp.concatenate(
            [
                x[:, (k * shards + z) * part : (k * shards + z + 1) * part]
                for z in range(shards)
                for k in range(spread)
            ],
            axis=1,
        )

    def bring(x):
        arrived = [
            lax.ppermute(lax.dynamic_index_in_dim(x, (place + p) % 2, 0, False), AXES, routes(p))
            for p in range(2)
        ]
        return ordered(batch_of(place), *arrived, 0)

    def send_back(x):
        slots = natural(x).reshape(2, run, width)
        return [
            lax.ppermute(
                lax.dynamic_index_in_dim(slots, (batch_of(place) + p) % 2, 0, False),
                AXES,
                [(to, origin) for origin, to in routes(p)],
            )
            for p in range(2)
        ]

    def as_batches(arrived):
        return ordered(place % 2, arrived[0][None], arrived[1][None], 0)


    def gather_b(x):
        return ordered(b, x, swap_b(x), 1)

    def gather_c(x):
        return ordered(c, x, swap_c(x), 1)

    def gather_rows_b(x):
        return ordered(b, x, swap_b(x), 0)

    def total(x):
        x = x + swap_c(x)
        return x + swap_b(x)

    def fold_c(product):
        sent = swap_c(product(1 - c).astype(LOW))
        return product(c) + sent.astype(F32)

    def fold_b(x):
        sent = swap_b(columns(x, (1 - b) * own, own).astype(LOW))
        return columns(x, b * own, own) + sent.astype(F32)


    pick = functools.partial(lax.dynamic_index_in_dim, keepdims=False)

    def away_b(x):
        cut = x.reshape(2, 2, -1, own)
        return pick(cut, b, 0), swap_b(pick(cut, 1 - b, 0))

    def away_c(mine, arrived):
        both = ordered(b, mine, arrived, 2)
        return pick(both, c, 0), swap_c(pick(both, 1 - c, 0))

    def to_runs(x):
        return ordered(c, *away_c(*away_b(x)), 1)


    def own_features(w):
        count = shards * spread // GROUP
        cut = []
        for i in range(count):
            block = quarter * count + i
            cut.append(columns(w, (block % shards) * rows + (block // shards) * part, part))
        return jnp.concatenate(cut, axis=1)

    def own_units(w):
        return columns(w, quarter * (w.shape[1] // GROUP), w.shape[1] // GROUP)

    def over_shards(*members):
        cut = jnp.concatenate(members, axis=1) if len(members) > 1 else members[0]
        piece = lax.dynamic_slice_in_dim(cut, a * part, part, 0)
        return lax.all_gather(piece, "shard", axis=0, tiled=True)

    def over_owners(w):
        piece = lax.dynamic_slice_in_dim(w, a * part, part, 0)
        return lax.all_gather(piece, OWNERS, axis=0, tiled=True)

    def over_spread(x):
        return [shift_a(x, k) for k in range(1, spread)]

    def by_spread(relative):
        if spread == 2:
            return ordered(a, relative[0], relative[1], 0)
        stacked = jnp.stack(relative, 0)
        pick = functools.partial(lax.dynamic_index_in_dim, axis=0, keepdims=False)
        return jnp.concatenate([pick(stacked, (a - j) % spread) for j in range(spread)], axis=0)

    def in_row_order(x):
        cut = x.reshape(spread, shards, part, -1)
        return jnp.transpose(cut, (1, 0, 2, 3)).reshape(width, -1)

    def row_half(w, h):
        return lax.dynamic_slice_in_dim(w, h * half, half, 0)


    def away(left, right):
        return [gradient_rows(spots, spread, k, left, right) for k in range(1, spread)]

    def in_two(terms):
        middles = [x.shape[0] // 2 for x in terms]
        return [x[:m] for x, m in zip(terms, middles)], [x[m:] for x, m in zip(terms, middles)]

    def stacked(upper, lower):
        return [jnp.concatenate(pair, axis=0) for pair in zip(upper, lower)]

    def sent_a(terms):
        return [shift_a(x, k + 1) for k, x in enumerate(terms)]

    def scattered(x):
        return lax.psum_scatter(x, "shard", scatter_dimension=0, tiled=True)

    def whole_rows(left, right):
        return gradient_rows(spots, spread, None, left, right)

    def scattered_all(x):
        return lax.psum_scatter(x, OWNERS, scatter_dimension=0, tiled=True)

    def summed(left, right, arrived):
        return scattered(gradient_rows(spots, spread, 0, left, right, arrived))

    def spread_a(x):
        return by_spread([x] + over_spread(x))

    def spread_b(x):
        return jnp.concatenate([x, swap_b(x)], axis=1)

    def spread_c(pair):
        return pair, swap_c(pair)

    def features_in_order(pairs, first, size):
        full = pairs[0].shape[1] // 2
        cut = [x[:, i * full + first : i * full + first + size] for x in pairs for i in range(2)]
        pair = [ordered(b, cut[n], cut[n + 1], 1) for n in (0, 2)]
        return natural(ordered(c, pair[0], pair[1], 1)).astype(F32)


    w_query, w_key, w_value, w_gate, w_out, w_one, w_two, w_down = weights
    g_qk = over_shards(own_units(w_query), own_units(w_key))
    g_vg = over_shards(own_units(w_value), own_units(w_gate))
    g_o = over_shards(own_features(w_out))
    g_1 = over_shards(own_units(w_one))
    g_2 = over_shards(own_units(w_two))
    w_d = [over_owners(own_units(w_down))]

    heads = HEADS // GROUP
    rates = lax.dynamic_slice_in_dim(decay_rates, quarter * heads, heads, 0)
    cuts = gather_rows_b(lengths.reshape(1, -1))
    cuts = ordered(c, cuts, swap_c(cuts), 0).reshape(GROUP, micro, -1)
    if streams == 1:
        batch = place // GROUP
        member = place % GROUP
        chosen = lax.dynamic_slice_in_dim(cuts, 2 * (member % 2) + member // 2, 1, 0)
    else:
        batch = place // 2
        chosen = lax.dynamic_index_in_dim(cuts.reshape(2, 2, micro, -1), place % 2, 0, False)
    chosen = lax.dynamic_index_in_dim(chosen, batch, 1, False)
    seq_ends = [chosen[:, 0]]
    for i in range(1, chosen.shape[1]):
        seq_ends.append(seq_ends[-1] + chosen[:, i])
    ends = jnp.stack(seq_ends, axis=1)

    x_run = bring(tokens)
    x_run, g_qk = tie(x_run, g_qk)

    x_pair = gather_rows_b(x_run)
    s_qk = over_spread(g_qk)
    x_pair, s_qk, g_vg = tie(x_pair, s_qk, g_vg)

    s_vg = over_spread(g_vg)
    w_qk = [g_qk, *s_qk]
    hidden_one, z_qk, x_scale, x_own = enter(spots, blocks, x_pair, swap_c(x_pair), w_qk)
    z_qk, hidden_one, s_vg, g_o = tie(z_qk, hidden_one, s_vg, g_o)

    s_o = over_spread(g_o)
    w_vg = [g_vg, *s_vg]
    z_vg = project(spots, hidden_one, w_vg)
    attended = attend(rates, ends, z_qk, z_vg)
    gate = z_vg[:, own:]
    o_scale = lax.rsqrt(total(jnp.sum(attended * attended, axis=-1)) / width + EPSILON)[:, None]
    lifted = (attended * gate).astype(LOW)
    lifted, s_o, g_1, cotangent = tie(lifted, s_o, g_1, cotangent)

    s_1 = over_spread(g_1)
    lifted = gather_b(lifted)
    lifted, s_1, g_2, o_scale, cotangent = tie(lifted, s_1, g_2, o_scale, cotangent)

    s_2 = over_spread(g_2)
    dy_run = bring(cotangent)
    lifted = gather_c(lifted)
    w_o = in_row_order(by_spread([g_o, *s_o]))
    branch = o_scale * matmul(lifted, w_o)
    middle = x_own.astype(F32) + branch
    low_middle = gather_b(middle.astype(LOW))
    low_middle, s_2, dy_run = tie(low_middle, s_2, dy_run)

    other_middle = swap_c(low_middle)
    dy_other = swap_b(dy_run)
    w_1, w_2 = [g_1, *s_1], [g_2, *s_2]
    hidden_two, z_one, z_two, product, m_scale = gated_unit(spots, low_middle, other_middle, w_1, w_2)
    z_one, z_two, product, dy_other = tie(z_one, z_two, product, dy_other)

    dy_pair = ordered(b, dy_run, dy_other, 0)
    dy_all, dy_own = enter(spots, blocks, dy_pair, swap_c(dy_pair))
    f_down = whole_rows(dy_all, product)
    z_one, z_two, product, f_down, w_d[0] = tie(z_one, z_two, product, f_down, w_d[0])


    f_down = scattered_all(f_down)
    d_one, d_two, lean_m = gated_unit_back(spots, dy_all, z_one, z_two, w_d)
    sent = fold_half(spots, [d_one, d_two], [w_1, w_2])
    sent, d_two, lean_m = tie(sent, d_two, lean_m)

    arrived = swap_c(sent)
    t_two = away(hidden_two, d_two)
    lean_m = lean_m[:, 0]
    lean_c = swap_c(lean_m)
    sent, mine = fold_half(spots, [d_one, d_two], [w_1, w_2], arrived)
    sent, d_one, t_two, product, lean_c = tie(sent, d_one, t_two, product, lean_c)

    crossed = swap_b(sent)
    lean_m = lean_m + lean_c
    lean_b = swap_b(lean_m)
    upper, lower = in_two(t_two)
    upper = sent_a(upper)
    f_one = whole_rows(hidden_two, d_one)
    result = fold_half(spots, [product], [w_d])
    crossed, result, f_one, upper, f_down, lean_b = tie(crossed, result, f_one, upper, f_down, lean_b)

    f_one = scattered_all(f_one)
    d_hidden = mine + crossed.astype(F32)
    m_normed = middle * m_scale
    lean = (lean_m + lean_b)[:, None] * (2.0 / width)
    d_middle = dy_own.astype(F32) + m_scale * (d_hidden - m_normed * lean)
    d_branch = d_middle.astype(LOW)
    lean_o = jnp.sum(d_middle * branch, axis=-1)
    sent = times_transposed(d_branch, row_half(w_o, 1 - c)).astype(LOW)
    sent, result, d_middle, lean_o = tie(sent, result, d_middle, lean_o)

    arrived = swap_c(sent)
    r_result = swap_c(result)
    y_down = spread_a(f_down)
    lean_o = lean_o + swap_c(lean_o)
    p_out = cross_tokens(lifted, (o_scale * d_middle).astype(LOW)).astype(LOW)
    p_out = jnp.transpose(p_out.reshape(shards, spread, part, -1), (1, 0, 2, 3))
    p_out = p_out.reshape(spread, width // spread, -1)
    t_out = [lax.dynamic_index_in_dim(p_out, (a + k) % spread, 0, False) for k in range(spread)]
    d_gated = times_transposed(d_branch, row_half(w_o, c)) + arrived.astype(F32)
    sent = columns(d_gated, (1 - b) * own, own).astype(LOW)
    mine = columns(d_gated, b * own, own)
    sent, mine, r_result, t_out, lean_o, y_down = tie(sent, mine, r_result, t_out, lean_o, y_down)

    crossed = swap_b(sent)
    lean_b = swap_b(lean_o)
    r_out = sent_a(t_out[1:])
    result, result_mine = fold_half(spots, [product], [w_d], r_result)
    crossed, result, r_out, lower, lean_b = tie(crossed, result, r_out, lower, lean_b)

    lower = sent_a(lower)
    result = swap_b(result)
    f_out = scattered(sum([x.astype(F32) for x in r_out], t_out[0].astype(F32)).astype(LOW))
    o_normed = attended * o_scale
    d_gated = mine + crossed.astype(F32)
    d_gate = (d_gated * o_normed).astype(LOW)
    lean = (lean_o + lean_b)[:, None] / width
    d_attended = (o_scale * (d_gated * gate - o_normed * lean)).astype(LOW)
    d_query, d_key, d_value = attend_back(rates, ends, z_qk, z_vg, d_attended)
    d_qk = joined(d_query, d_key)
    d_vg = joined(d_value, d_gate)
    t_qk = away(hidden_one, d_qk)
    d_qk, d_vg, t_qk, lower, result = tie(d_qk, d_vg, t_qk, lower, result)

    qk_a, qk_b = in_two(t_qk)
    qk_a = sent_a(qk_a)
    f_two = gradient_rows(spots, spread, 0, hidden_two, d_two, stacked(upper, lower))
    output, out_b = away_b((middle + (result_mine + result.astype(F32))).astype(LOW))
    f_two, qk_a, qk_b, out_b, d_qk, d_vg, f_one = tie(f_two, qk_a, qk_b, out_b, d_qk, d_vg, f_one)

    f_two = scattered(f_two)
    qk_b = sent_a(qk_b)
    output, out_c = away_c(output, out_b)
    x_down = swap_b(y_down)
    y_one = over_spread(f_one)
    t_vg = away(hidden_one, d_vg)
    sent = fold_half(spots, [d_qk, d_vg], [w_qk, w_vg])
    sent, t_vg, d_qk, d_vg, out_c, qk_b, x_down, y_one = tie(
        sent, t_vg, d_qk, d_vg, out_c, qk_b, x_down, y_one
    )

    arrived = swap_c(sent)
    vg_a, vg_b = in_two(t_vg)
    vg_a = sent_a(vg_a)
    f_qk = gradient_rows(spots, spread, 0, hidden_one, d_qk, stacked(qk_a, qk_b))
    lean_x = jnp.sum(z_qk * d_qk.astype(F32), axis=-1) + jnp.sum(z_vg * d_vg.astype(F32), axis=-1)
    arrived, vg_a, vg_b, f_qk, lean_x = tie(arrived, vg_a, vg_b, f_qk, lean_x)

    f_qk = scattered(f_qk)
    vg_b = sent_a(vg_b)
    y_one = by_spread([f_one, *y_one])
    x_one = swap_b(y_one)
    lean_x = lean_x + swap_c(lean_x)
    sent, mine = fold_half(spots, [d_qk, d_vg], [w_qk, w_vg], arrived)
    sent, mine, vg_b, lean_x, x_one, d_vg = tie(sent, mine, vg_b, lean_x, x_one, d_vg)

    crossed = swap_b(sent)
    lean_b = swap_b(lean_x)
    f_vg = scattered(gradient_rows(spots, spread, 0, hidden_one, d_vg, stacked(vg_a, vg_b)))
    four_down = spread_c(joined(y_down, x_down))
    four_one = spread_c(joined(y_one, x_one))
    crossed, lean_b, four_one, four_down, f_two, f_out = tie(
        crossed, lean_b, four_one, four_down, f_two, f_out
    )

    d_hidden = mine + crossed.astype(F32)
    x_normed = x_own.astype(F32) * x_scale
    lean = (lean_x + lean_b)[:, None] / width
    input_grad = to_runs((d_middle + x_scale * (d_hidden - x_normed * lean)).astype(LOW))
    output = send_back(ordered(c, output, out_c, 1))
    f_oqk = joined(f_out, f_qk)
    x_oqk = swap_b(f_oqk)
    y_two = over_spread(f_two)
    y_vg = over_spread(f_vg)
    units = f_one.shape[1]
    [g_down] = place_quarters(spots, four_down, (0, units))
    [g_one] = place_quarters(spots, four_one, (0, units))
    input_grad, output, y_two, x_oqk, y_vg, g_down, g_one = tie(
        input_grad, output, y_two, x_oqk, y_vg, g_down, g_one
    )

    y_vg = by_spread([f_vg, *y_vg])
    x_vg = swap_b(y_vg)
    y_two = by_spread([f_two, *y_two])
    x_two = swap_b(y_two)
    f_oqk = joined(f_oqk, x_oqk)
    y_oqk = over_spread(f_oqk)
    input_grad = send_back(input_grad)
    output = as_batches(output)
    x_vg, x_two, y_oqk, input_grad, output = tie(x_vg, x_two, y_oqk, input_grad, output)

    four_vg = spread_c(joined(y_vg, x_vg))
    four_two = spread_c(joined(y_two, x_two))
    four_oqk = spread_c(by_spread([f_oqk, *y_oqk]))
    g_query, g_key = place_quarters(spots, four_oqk, (own, own), (2 * own, own))
    g_value, g_gate = place_quarters(spots, four_vg, (0, own), (own, own))
    [g_two] = place_quarters(spots, four_two, (0, units))
    g_out = features_in_order(four_oqk, 0, own)
    return output, as_batches(input_grad), g_query, g_key, g_value, g_gate, g_out, g_one, g_two, g_down


def solution(mesh):
    reps, shards = mesh.shape["rep"], mesh.shape["shard"]
    devices = mesh.devices.reshape(reps // GROUP, 2, 2, shards)
    rep = ("a", "b", "c")
    by_tokens = P(None, (*rep, "shard"), None)
    by_rows = P("shard", None)
    return jax.shard_map(
        functools.partial(body, reps, shards),
        mesh=Mesh(devices, AXES),
        in_specs=(by_tokens, by_tokens, P(None, rep, None), P(), *[by_rows] * 8),
        out_specs=(by_tokens, by_tokens, *[by_rows] * 8),
        check_vma=False,
    )
```

```python
import functools

import jax
import jax.numpy as jnp
from jax import lax
from jax.experimental import pallas as pl
from jax.experimental.pallas import tpu as pltpu
from jax.sharding import Mesh, PartitionSpec as P

HEADS = 16
HEAD_DIM = 128
STREAM = 1024
GROUP = 4
BLOCK = 256
TILE = 256
EPSILON = 1e-06
AXES = ("a", "b", "c", "shard")
OWNERS = ("a", "shard")
LOW = jnp.bfloat16
F32 = jnp.float32


def matmul(former, latter):
    return jnp.dot(former, latter, preferred_element_type=F32)


def times_transposed(former, latter):
    return lax.dot_general(former, latter, (((1,), (1,)), ((), ())), preferred_element_type=F32)


def cross_tokens(former, latter):
    return lax.dot_general(former, latter, (((0,), (0,)), ((), ())), preferred_element_type=F32)


def masked_decay(rate, ends, first, columns):
    row = first + lax.broadcasted_iota(jnp.int32, (BLOCK, 1), 0)
    column = lax.broadcasted_iota(jnp.int32, (1, columns), 1)
    begin = jnp.zeros((BLOCK, 1), jnp.int32)
    for end in ends:
        begin = jnp.where(row >= end, end, begin)
    falling = jnp.exp(-rate * (row - first).astype(F32))
    rising = jnp.exp(rate * (column - first).astype(F32))
    allowed = (column <= row) & (column >= begin)
    return jnp.where(allowed, falling * rising, 0.0)


def attend_kernel(rates, ends, zq_ref, zk_ref, zv_ref, out_ref):
    stream, head = pl.program_id(0), pl.program_id(1)
    rate = rates[head]
    bounds = [ends[stream, i] for i in range(ends.shape[1])]
    zq, zk = zq_ref[...], zk_ref[...]
    q = (zq * jax.nn.sigmoid(zq)).astype(LOW)
    k = (zk * jax.nn.sigmoid(zk)).astype(LOW)
    v = zv_ref[...].astype(LOW)
    for first in range(0, STREAM, BLOCK):
        columns = first + BLOCK
        mask = masked_decay(rate, bounds, first, columns)
        scores = times_transposed(q[first:columns], k[:columns])
        weights = (scores * mask).astype(LOW)
        out_ref[first:columns, :] = matmul(weights, v[:columns])


def attend_back_kernel(
    rates, ends, zq_ref, zk_ref, zv_ref, do_ref, dzq_ref, dzk_ref, dzv_ref, dk_ref, dv_ref
):
    stream, head = pl.program_id(0), pl.program_id(1)
    rate = rates[head]
    bounds = [ends[stream, i] for i in range(ends.shape[1])]
    zq, zk = zq_ref[...], zk_ref[...]
    sig_q, sig_k = jax.nn.sigmoid(zq), jax.nn.sigmoid(zk)
    q = (zq * sig_q).astype(LOW)
    k = (zk * sig_k).astype(LOW)
    slope_q = sig_q * (1.0 + zq * (1.0 - sig_q))
    v = zv_ref[...].astype(LOW)
    d_o = do_ref[...]
    dk_ref[...] = jnp.zeros_like(dk_ref)
    dv_ref[...] = jnp.zeros_like(dv_ref)
    for first in range(0, STREAM, BLOCK):
        columns = first + BLOCK
        rows = slice(first, columns)
        mask = masked_decay(rate, bounds, first, columns)
        weights = (times_transposed(q[rows], k[:columns]) * mask).astype(LOW)
        d_scores = (times_transposed(d_o[rows], v[:columns]) * mask).astype(LOW)
        dzq_ref[rows, :] = (matmul(d_scores, k[:columns]) * slope_q[rows]).astype(LOW)
        dk_ref[:columns, :] += cross_tokens(d_scores, q[rows])
        dv_ref[:columns, :] += cross_tokens(weights, d_o[rows])
    dzk_ref[...] = (dk_ref[...] * (sig_k * (1.0 + zk * (1.0 - sig_k)))).astype(LOW)
    dzv_ref[...] = dv_ref[...].astype(LOW)


def head_block(offset=0):
    return pl.BlockSpec((STREAM, HEAD_DIM), lambda g, h, *_: (g, h + offset))


def attend(rates, ends, z_qk, z_vg):
    heads, streams = rates.shape[0], ends.shape[0]
    work = streams * heads * STREAM * STREAM
    return pl.pallas_call(
        attend_kernel,
        out_shape=jax.ShapeDtypeStruct((streams * STREAM, heads * HEAD_DIM), F32),
        grid_spec=pltpu.PrefetchScalarGridSpec(
            num_scalar_prefetch=2,
            grid=(streams, heads),
            in_specs=[head_block(), head_block(heads), head_block()],
            out_specs=head_block(),
        ),
        compiler_params=pltpu.CompilerParams(vmem_limit_bytes=40 << 20),
        cost_estimate=pl.CostEstimate(
            flops=4 * work * HEAD_DIM, transcendentals=work // 64,
            bytes_accessed=streams * heads * STREAM * HEAD_DIM * 16,
        ),
        name="attend",
    )(rates, ends, z_qk, z_qk, z_vg)


def attend_back(rates, ends, z_qk, z_vg, d_o):
    heads, streams = rates.shape[0], ends.shape[0]
    work = streams * heads * STREAM * STREAM
    return pl.pallas_call(
        attend_back_kernel,
        out_shape=[jax.ShapeDtypeStruct((streams * STREAM, heads * HEAD_DIM), LOW)] * 3,
        grid_spec=pltpu.PrefetchScalarGridSpec(
            num_scalar_prefetch=2,
            grid=(streams, heads),
            in_specs=[head_block(), head_block(heads), head_block(), head_block()],
            out_specs=[head_block()] * 3,
            scratch_shapes=[pltpu.VMEM((STREAM, HEAD_DIM), F32)] * 2,
        ),
        compiler_params=pltpu.CompilerParams(vmem_limit_bytes=40 << 20),
        cost_estimate=pl.CostEstimate(
            flops=10 * work * HEAD_DIM, transcendentals=work // 64,
            bytes_accessed=streams * heads * STREAM * HEAD_DIM * 20,
        ),
        name="attend_back",
    )(rates, ends, z_qk, z_qk, z_vg, d_o)


def chunk_copies(chunks, buffer, sems, turn, half=None):
    count, size = len(chunks), chunks[0].shape[0]
    if count == 1:
        rows = buffer.shape[0]
        first = 0 if half is None else pl.multiple_of(half * rows, rows)
        return [(None, pltpu.make_async_copy(chunks[0].at[pl.ds(first, rows)], buffer, sems.at[0]))]
    copies = []
    for k, chunk in enumerate(chunks):
        index = lax.rem(turn - k + count, count)
        wanted = None
        if half is not None:
            wanted = lax.div(index, count // 2) == half
            index = lax.rem(index, count // 2)
        target = buffer.at[pl.ds(pl.multiple_of(index * size, size), size)]
        copies.append((wanted, pltpu.make_async_copy(chunk, target, sems.at[k])))
    return copies


def each(copies, act):
    for wanted, copy in copies:
        if wanted is None:
            act(copy)
        else:
            pl.when(wanted)(functools.partial(act, copy))


def start(copies):
    each(copies, lambda copy: copy.start())


def finish(copies):
    each(copies, lambda copy: copy.wait())


def estimate(flops, *arrays):
    moved = sum(x.size * x.dtype.itemsize for x in arrays)
    return pl.CostEstimate(flops=flops, transcendentals=0, bytes_accessed=moved)


def limit(mebibytes):
    return pltpu.CompilerParams(vmem_limit_bytes=mebibytes << 20)


ANYWHERE = pl.BlockSpec(memory_space=pl.ANY)


def weight_buffer(chunks, share=1):
    size = len(chunks) * chunks[0].shape[0] // share
    return [pltpu.VMEM((size, chunks[0].shape[1]), LOW), pltpu.SemaphoreType.DMA((len(chunks),))]


def tile_rows(width, column=0):
    return pl.BlockSpec((TILE, width), lambda i, *_: (i, column))


def joined_rows(width, tiles):
    spec = pl.BlockSpec((TILE, width), lambda i, s: (i // (2 * tiles) * tiles + i % tiles, 0))
    return [spec, spec]


def enter_kernel(tiles, blocks, project, spots, own_ref, other_ref, *refs):
    i = pl.program_id(0)
    mine = lax.rem(lax.div(i, tiles), 2) == spots[0]
    rows = jnp.where(mine, own_ref[...], other_ref[...])
    part = rows.shape[1] // len(blocks)
    permuted = jnp.concatenate([rows[:, n * part : (n + 1) * part] for n in blocks], axis=1)
    if not project:
        all_ref, quarter_ref = refs
        all_ref[...] = permuted
        held = all_ref
    else:
        chunks, (h_ref, z_ref, scale_ref, quarter_ref, held, buffer, sems) = refs[:-7], refs[-7:]
        held[...] = permuted
        copies = chunk_copies(chunks, buffer, sems, spots[2])

        @pl.when(i == 0)
        def _():
            start(copies)

        x = rows.astype(F32)
        scale = lax.rsqrt(jnp.mean(x * x, axis=-1, keepdims=True) + EPSILON)
        scale_ref[...] = scale
        hidden = (permuted.astype(F32) * scale).astype(LOW)
        h_ref[...] = hidden

        @pl.when(i == 0)
        def _():
            finish(copies)

        z_ref[...] = matmul(hidden, buffer[...])
    size = quarter_ref.shape[1]
    quarter_ref[...] = held[:, pl.ds(pl.multiple_of(spots[1] * size, size), size)]


def enter(spots, blocks, own, other, chunks=()):
    width = own.shape[1]
    count, tiles = 2 * own.shape[0], own.shape[0] // TILE // 2
    shape = jax.ShapeDtypeStruct
    quarter = shape((count, width // GROUP), LOW)
    if chunks:
        columns = chunks[0].shape[1]
        outs = [shape((count, width), LOW), shape((count, columns), F32), shape((count, 1), F32), quarter]
        scratch = [pltpu.VMEM((TILE, width), LOW), *weight_buffer(chunks)]
    else:
        columns, scratch = 0, []
        outs = [shape((count, width), LOW), quarter]
    return pl.pallas_call(
        functools.partial(enter_kernel, tiles, blocks, bool(chunks)),
        out_shape=outs,
        grid_spec=pltpu.PrefetchScalarGridSpec(
            num_scalar_prefetch=1,
            grid=(count // TILE,),
            in_specs=joined_rows(width, tiles) + [ANYWHERE] * len(chunks),
            out_specs=[tile_rows(o.shape[1]) for o in outs],
            scratch_shapes=scratch,
        ),
        compiler_params=limit(40),
        cost_estimate=estimate(2 * count * width * columns, own, other, *chunks, *outs),
        name="enter",
    )(spots, own, other, *chunks)


def project_kernel(spots, h_ref, *refs):
    chunks, (z_ref, buffer, sems) = refs[:-3], refs[-3:]
    copies = chunk_copies(chunks, buffer, sems, spots[2])

    @pl.when(pl.program_id(0) == 0)
    def _():
        start(copies)
        finish(copies)

    z_ref[...] = matmul(h_ref[...], buffer[...])


def project(spots, hidden, chunks):
    count, width = hidden.shape
    out = jax.ShapeDtypeStruct((count, chunks[0].shape[1]), F32)
    return pl.pallas_call(
        project_kernel,
        out_shape=out,
        grid_spec=pltpu.PrefetchScalarGridSpec(
            num_scalar_prefetch=1,
            grid=(count // TILE,),
            in_specs=[tile_rows(width)] + [ANYWHERE] * len(chunks),
            out_specs=tile_rows(out.shape[1]),
            scratch_shapes=weight_buffer(chunks),
        ),
        compiler_params=limit(40),
        cost_estimate=estimate(2 * count * width * out.shape[1], hidden, *chunks, out),
        name="project",
    )(spots, hidden, *chunks)


def unit_kernel(spots, own_ref, other_ref, *refs):
    chunks, rest = refs[:-9], refs[-9:]
    h_ref, one_ref, two_ref, product_ref, scale_ref, first, second, sem_one, sem_two = rest
    split = len(chunks) // 2
    copies = [
        chunk_copies(chunks[:split], first, sem_one, spots[2]),
        chunk_copies(chunks[split:], second, sem_two, spots[2]),
    ]
    begins = pl.program_id(0) == 0

    @pl.when(begins)
    def _():
        start(copies[0])
        start(copies[1])

    mine, other = own_ref[...], other_ref[...]
    swapped = spots[0] == 1
    middle = jnp.concatenate(
        [jnp.where(swapped, other, mine), jnp.where(swapped, mine, other)], axis=1
    ).astype(F32)
    scale = lax.rsqrt(jnp.mean(middle * middle, axis=-1, keepdims=True) + EPSILON)
    scale_ref[...] = scale
    hidden = (middle * scale).astype(LOW)
    h_ref[...] = hidden

    @pl.when(begins)
    def _():
        finish(copies[0])

    z_one = matmul(hidden, first[...])

    @pl.when(begins)
    def _():
        finish(copies[1])

    z_two = matmul(hidden, second[...])
    one_ref[...] = z_one.astype(LOW)
    two_ref[...] = z_two.astype(LOW)
    product_ref[...] = (z_one * z_two).astype(LOW)


def gated_unit(spots, own, other, first, second):
    count, width, units = own.shape[0], 2 * own.shape[1], first[0].shape[1]
    shape = jax.ShapeDtypeStruct
    outs = [shape((count, width), LOW)] + [shape((count, units), LOW)] * 3 + [shape((count, 1), F32)]
    (buffer, sems) = weight_buffer(first)
    return pl.pallas_call(
        unit_kernel,
        out_shape=outs,
        grid_spec=pltpu.PrefetchScalarGridSpec(
            num_scalar_prefetch=1,
            grid=(count // TILE,),
            in_specs=[tile_rows(width // 2)] * 2 + [ANYWHERE] * (2 * len(first)),
            out_specs=[tile_rows(o.shape[1]) for o in outs],
            scratch_shapes=[buffer, buffer, sems, sems],
        ),
        compiler_params=limit(48),
        cost_estimate=estimate(4 * count * width * units, own, other, *first, *second, *outs),
        name="gated_unit",
    )(spots, own, other, *first, *second)


def unit_back_kernel(spots, dy_ref, one_ref, two_ref, *refs):
    chunks, (d_one_ref, d_two_ref, sum_ref, buffer, sems) = refs[:-5], refs[-5:]
    copies = chunk_copies(chunks, buffer, sems, spots[2])

    @pl.when(pl.program_id(0) == 0)
    def _():
        start(copies)
        finish(copies)

    d_product = matmul(dy_ref[...], buffer[...])
    z_one, z_two = one_ref[...].astype(F32), two_ref[...].astype(F32)
    d_one = d_product * z_two
    d_one_ref[...] = d_one.astype(LOW)
    d_two_ref[...] = (d_product * z_one).astype(LOW)
    sum_ref[...] = jnp.sum(d_one * z_one, axis=-1, keepdims=True)


def gated_unit_back(spots, dy, z_one, z_two, chunks):
    count, width, units = dy.shape[0], dy.shape[1], z_one.shape[1]
    shape = jax.ShapeDtypeStruct
    outs = [shape((count, units), LOW)] * 2 + [shape((count, 1), F32)]
    return pl.pallas_call(
        unit_back_kernel,
        out_shape=outs,
        grid_spec=pltpu.PrefetchScalarGridSpec(
            num_scalar_prefetch=1,
            grid=(count // TILE,),
            in_specs=[tile_rows(width), tile_rows(units), tile_rows(units)] + [ANYWHERE] * len(chunks),
            out_specs=[tile_rows(o.shape[1]) for o in outs],
            scratch_shapes=weight_buffer(chunks),
        ),
        compiler_params=limit(40),
        cost_estimate=estimate(2 * count * width * units, dy, z_one, z_two, *chunks, *outs),
        name="gated_unit_back",
    )(spots, dy, z_one, z_two, *chunks)


def fold_kernel(members, keeps, spots, *refs):
    values, refs = refs[:members], refs[members:]
    arrived, refs = (refs[0], refs[1:]) if keeps else (None, refs)
    outs = 2 if keeps else 1
    chunks, refs = refs[: -outs - 2 * members], refs[-outs - 2 * members :]
    outs, buffers, sems = refs[:outs], refs[outs : outs + members], refs[outs + members :]
    each_count = len(chunks) // members
    half = spots[0] if keeps else 1 - spots[0]
    begins = pl.program_id(0) == 0
    copies = [
        chunk_copies(chunks[m * each_count : (m + 1) * each_count], buffers[m], sems[m], spots[2], half)
        for m in range(members)
    ]

    @pl.when(begins)
    def _():
        for m in range(members):
            start(copies[m])

    whole = None
    for m in range(members):
        pl.when(begins)(functools.partial(finish, copies[m]))
        term = times_transposed(values[m][...], buffers[m][...])
        whole = term if whole is None else whole + term
    if not keeps:
        outs[0][...] = whole.astype(LOW)
    else:
        whole = whole + arrived[...].astype(F32)
        size = whole.shape[1] // 2
        upper = spots[3] == 1
        outs[0][...] = jnp.where(upper, whole[:, :size], whole[:, size:]).astype(LOW)
        outs[1][...] = jnp.where(upper, whole[:, size:], whole[:, :size])


def fold_half(spots, values, weights, arrived=None):
    count = values[0].shape[0]
    half = len(weights[0]) * weights[0][0].shape[0] // 2
    shape = jax.ShapeDtypeStruct
    if arrived is None:
        outs, extra = [shape((count, half), LOW)], []
    else:
        outs, extra = [shape((count, half // 2), LOW), shape((count, half // 2), F32)], [arrived]
    buffers, sems = zip(*[weight_buffer(w, 2) for w in weights])
    chunks = [x for w in weights for x in w]
    flops = sum(2 * count * half * v.shape[1] for v in values)
    found = pl.pallas_call(
        functools.partial(fold_kernel, len(values), arrived is not None),
        out_shape=outs,
        grid_spec=pltpu.PrefetchScalarGridSpec(
            num_scalar_prefetch=1,
            grid=(count // TILE,),
            in_specs=[tile_rows(v.shape[1]) for v in values]
            + [tile_rows(half)] * len(extra)
            + [ANYWHERE] * len(chunks),
            out_specs=[tile_rows(o.shape[1]) for o in outs],
            scratch_shapes=[*buffers, *sems],
        ),
        compiler_params=limit(40),
        cost_estimate=estimate(flops, *values, *extra, *chunks[: len(chunks) // 2], *outs),
        name="fold_half",
    )(spots, *values, *extra, *chunks)
    return found[0] if arrived is None else found


def gradient_kernel(spots, left_ref, right_ref, *refs):
    found = cross_tokens(left_ref[...], right_ref[...])
    for arrived_ref in refs[:-1]:
        found = found + arrived_ref[...].astype(F32)
    refs[-1][...] = found.astype(LOW)


def gradient_rows(spots, spread, k, left, right, arrived=()):
    count, columns = right.shape
    rows = left.shape[1] // (1 if k is None else spread)
    tiles = rows // TILE

    def block(i, s):
        return (0, i if k is None else lax.rem(s[2] + k, spread) * tiles + i)

    out = jax.ShapeDtypeStruct((rows, columns), LOW)
    return pl.pallas_call(
        gradient_kernel,
        out_shape=out,
        grid_spec=pltpu.PrefetchScalarGridSpec(
            num_scalar_prefetch=1,
            grid=(tiles,),
            in_specs=[
                pl.BlockSpec((count, TILE), block),
                pl.BlockSpec((count, columns), lambda i, s: (0, 0), pipeline_mode=pl.Buffered(1)),
            ]
            + [tile_rows(columns)] * len(arrived),
            out_specs=tile_rows(columns),
        ),
        compiler_params=limit(40),
        cost_estimate=estimate(2 * count * rows * columns, right, out, out, *arrived),
        name="gradient_rows",
    )(spots, left, right, *arrived)


def place_kernel(cuts, spots, *refs):
    quarter = pl.program_id(0)
    cross = lax.rem(lax.div(quarter, 2) + spots[0], 2) * 2 + lax.rem(lax.rem(quarter, 2) + spots[3], 2)
    for n in range(4):

        @pl.when(cross == n)
        def _():
            for (first, size), out_ref in zip(cuts, refs[4:]):
                out_ref[...] = refs[n][:, first : first + size].astype(F32)


def place_quarters(spots, pairs, *cuts):
    rows, columns = pairs[0].shape[0], pairs[0].shape[1] // 2
    outs = [jax.ShapeDtypeStruct((rows, GROUP * size), F32) for _, size in cuts]

    def block(index):
        return pl.BlockSpec((rows, columns), lambda q, s: (0, index), pipeline_mode=pl.Buffered(1))

    return pl.pallas_call(
        functools.partial(place_kernel, cuts),
        out_shape=outs,
        grid_spec=pltpu.PrefetchScalarGridSpec(
            num_scalar_prefetch=1,
            grid=(GROUP,),
            in_specs=[block(0), block(1), block(0), block(1)],
            out_specs=[pl.BlockSpec((rows, size), lambda q, s: (0, q)) for _, size in cuts],
        ),
        compiler_params=limit(40),
        cost_estimate=estimate(0, *pairs, *outs),
        name="place_quarters",
    )(spots, pairs[0], pairs[0], pairs[1], pairs[1])


def tie(*values):
    return lax.optimization_barrier(values)


def body(reps, shards, tokens, cotangent, lengths, decay_rates, *weights):
    spread = reps // GROUP
    place = lax.axis_index("shard")
    a, b, c = lax.axis_index("a"), lax.axis_index("b"), lax.axis_index("c")
    quarter = 2 * c + b
    micro, run, width = tokens.shape
    half, own = width // 2, width // GROUP
    streams = micro * GROUP // shards
    per_block = STREAM // run // GROUP * streams
    rows = width // shards
    part = rows // spread
    columns = functools.partial(lax.dynamic_slice_in_dim, axis=1)
    spots = jnp.stack([c, quarter, a, b]).astype(jnp.int32)
    blocks = [z * spread + k for k in range(spread) for z in range(shards)]

    def move(x, target):
        pairs = [(r * shards + s, target(r) * shards + s) for r in range(reps) for s in range(shards)]
        return lax.ppermute(x, AXES, pairs)

    def swap_c(x):
        return move(x, lambda r: r ^ 1)

    def swap_b(x):
        return move(x, lambda r: r ^ 2)

    def joined(*parts):
        return jnp.concatenate(parts, axis=1)

    def shift_a(x, k):
        return move(x, lambda r: (r + GROUP * k) % reps)

    def ordered(index, mine, other, axis):
        return jnp.where(
            index == 0,
            jnp.concatenate([mine, other], axis),
            jnp.concatenate([other, mine], axis),
        )


    def batch_of(s):
        return s // (shards // micro)

    def origin(r, s, p):
        run_id = (r % GROUP) * per_block + p
        stream, piece = run_id // shards, run_id % shards
        member = s % GROUP if streams == 1 else 2 * stream + s % 2
        return (r // GROUP) * GROUP + member, piece

    def routes(p):
        found = []
        for r in range(reps):
            for s in range(shards):
                from_r, from_s = origin(r, s, p ^ batch_of(s))
                found.append((from_r * shards + from_s, r * shards + s))
        return found

    def natural(x):
        return jnp.concatenate(
            [
                x[:, (k * shards + z) * part : (k * shards + z + 1) * part]
                for z in range(shards)
                for k in range(spread)
            ],
            axis=1,
        )

    def bring(x):
        arrived = [
            lax.ppermute(lax.dynamic_index_in_dim(x, (place + p) % 2, 0, False), AXES, routes(p))
            for p in range(2)
        ]
        return ordered(batch_of(place), *arrived, 0)

    def back_slots(x):
        slots = natural(x).reshape(2, run, width)
        return [
            lax.dynamic_index_in_dim(slots, (batch_of(place) + p) % 2, 0, False) for p in range(2)
        ]

    def send_slot(x, p):
        return lax.ppermute(x, AXES, [(to, origin) for origin, to in routes(p)])

    def send_back(x):
        return [send_slot(slot, p) for p, slot in enumerate(back_slots(x))]

    def as_batches(arrived):
        return ordered(place % 2, arrived[0][None], arrived[1][None], 0)


    def gather_b(x):
        return ordered(b, x, swap_b(x), 1)

    def gather_c(x):
        return ordered(c, x, swap_c(x), 1)

    def gather_rows_b(x):
        return ordered(b, x, swap_b(x), 0)

    def total(x):
        x = x + swap_c(x)
        return x + swap_b(x)

    def fold_c(product):
        sent = swap_c(product(1 - c).astype(LOW))
        return product(c) + sent.astype(F32)

    def fold_b(x):
        sent = swap_b(columns(x, (1 - b) * own, own).astype(LOW))
        return columns(x, b * own, own) + sent.astype(F32)


    pick = functools.partial(lax.dynamic_index_in_dim, keepdims=False)

    def away_b(x):
        cut = x.reshape(2, 2, -1, own)
        return pick(cut, b, 0), swap_b(pick(cut, 1 - b, 0))

    def away_c(mine, arrived):
        both = ordered(b, mine, arrived, 2)
        return pick(both, c, 0), swap_c(pick(both, 1 - c, 0))

    def to_runs(x):
        return ordered(c, *away_c(*away_b(x)), 1)


    def own_features(w):
        count = shards * spread // GROUP
        cut = []
        for i in range(count):
            block = quarter * count + i
            cut.append(columns(w, (block % shards) * rows + (block // shards) * part, part))
        return jnp.concatenate(cut, axis=1)

    def own_units(w):
        return columns(w, quarter * (w.shape[1] // GROUP), w.shape[1] // GROUP)

    def over_shards(*members):
        cut = jnp.concatenate(members, axis=1) if len(members) > 1 else members[0]
        piece = lax.dynamic_slice_in_dim(cut, a * part, part, 0)
        return lax.all_gather(piece, "shard", axis=0, tiled=True)

    def over_owners(w):
        piece = lax.dynamic_slice_in_dim(w, a * part, part, 0)
        return lax.all_gather(piece, OWNERS, axis=0, tiled=True)

    def over_spread(x):
        return [shift_a(x, k) for k in range(1, spread)]

    def by_spread(relative):
        if spread == 2:
            return ordered(a, relative[0], relative[1], 0)
        stacked = jnp.stack(relative, 0)
        pick = functools.partial(lax.dynamic_index_in_dim, axis=0, keepdims=False)
        return jnp.concatenate([pick(stacked, (a - j) % spread) for j in range(spread)], axis=0)

    def in_row_order(x):
        cut = x.reshape(spread, shards, part, -1)
        return jnp.transpose(cut, (1, 0, 2, 3)).reshape(width, -1)

    def row_half(w, h):
        return lax.dynamic_slice_in_dim(w, h * half, half, 0)


    def away(left, right):
        return [gradient_rows(spots, spread, k, left, right) for k in range(1, spread)]

    def in_two(terms):
        middles = [x.shape[0] // 2 for x in terms]
        return [x[:m] for x, m in zip(terms, middles)], [x[m:] for x, m in zip(terms, middles)]

    def stacked(upper, lower):
        return [jnp.concatenate(pair, axis=0) for pair in zip(upper, lower)]

    def sent_a(terms):
        return [shift_a(x, k + 1) for k, x in enumerate(terms)]

    def scattered(x):
        return lax.psum_scatter(x, "shard", scatter_dimension=0, tiled=True)

    def whole_rows(left, right):
        return gradient_rows(spots, spread, None, left, right)

    def scattered_all(x):
        return lax.psum_scatter(x, OWNERS, scatter_dimension=0, tiled=True)

    def summed(left, right, arrived):
        return scattered(gradient_rows(spots, spread, 0, left, right, arrived))

    def spread_a(x):
        return by_spread([x] + over_spread(x))

    def spread_b(x):
        return jnp.concatenate([x, swap_b(x)], axis=1)

    def spread_c(pair):
        return pair, swap_c(pair)

    def features_in_order(pairs, first, size):
        full = pairs[0].shape[1] // 2
        cut = [x[:, i * full + first : i * full + first + size] for x in pairs for i in range(2)]
        pair = [ordered(b, cut[n], cut[n + 1], 1) for n in (0, 2)]
        return natural(ordered(c, pair[0], pair[1], 1)).astype(F32)


    w_query, w_key, w_value, w_gate, w_out, w_one, w_two, w_down = weights
    g_qk = over_shards(own_units(w_query), own_units(w_key))
    g_vg = over_shards(own_units(w_value), own_units(w_gate))
    g_o = over_shards(own_features(w_out))
    g_1 = over_shards(own_units(w_one))
    g_2 = over_shards(own_units(w_two))
    w_d = [over_owners(own_units(w_down))]

    heads = HEADS // GROUP
    rates = lax.dynamic_slice_in_dim(decay_rates, quarter * heads, heads, 0)
    cuts = gather_rows_b(lengths.reshape(1, -1))
    cuts = ordered(c, cuts, swap_c(cuts), 0).reshape(GROUP, micro, -1)
    if streams == 1:
        batch = place // GROUP
        member = place % GROUP
        chosen = lax.dynamic_slice_in_dim(cuts, 2 * (member % 2) + member // 2, 1, 0)
    else:
        batch = place // 2
        chosen = lax.dynamic_index_in_dim(cuts.reshape(2, 2, micro, -1), place % 2, 0, False)
    chosen = lax.dynamic_index_in_dim(chosen, batch, 1, False)
    seq_ends = [chosen[:, 0]]
    for i in range(1, chosen.shape[1]):
        seq_ends.append(seq_ends[-1] + chosen[:, i])
    ends = jnp.stack(seq_ends, axis=1)

    x_run = bring(tokens)
    x_run, g_qk = tie(x_run, g_qk)

    x_pair = gather_rows_b(x_run)
    s_qk = over_spread(g_qk)
    x_pair, s_qk, g_vg = tie(x_pair, s_qk, g_vg)

    s_vg = over_spread(g_vg)
    w_qk = [g_qk, *s_qk]
    hidden_one, z_qk, x_scale, x_own = enter(spots, blocks, x_pair, swap_c(x_pair), w_qk)
    z_qk, hidden_one, s_vg, g_o = tie(z_qk, hidden_one, s_vg, g_o)

    s_o = over_spread(g_o)
    w_vg = [g_vg, *s_vg]
    z_vg = project(spots, hidden_one, w_vg)
    attended = attend(rates, ends, z_qk, z_vg)
    gate = z_vg[:, own:]
    o_scale = lax.rsqrt(total(jnp.sum(attended * attended, axis=-1)) / width + EPSILON)[:, None]
    lifted = (attended * gate).astype(LOW)
    lifted, s_o, g_1, cotangent = tie(lifted, s_o, g_1, cotangent)

    s_1 = over_spread(g_1)
    lifted = gather_b(lifted)
    lifted, s_1, g_2, o_scale, cotangent = tie(lifted, s_1, g_2, o_scale, cotangent)

    s_2 = over_spread(g_2)
    dy_run = bring(cotangent)
    lifted = gather_c(lifted)
    w_o = in_row_order(by_spread([g_o, *s_o]))
    branch = o_scale * matmul(lifted, w_o)
    middle = x_own.astype(F32) + branch
    low_middle = gather_b(middle.astype(LOW))
    low_middle, s_2, dy_run = tie(low_middle, s_2, dy_run)

    other_middle = swap_c(low_middle)
    dy_other = swap_b(dy_run)
    w_1, w_2 = [g_1, *s_1], [g_2, *s_2]
    hidden_two, z_one, z_two, product, m_scale = gated_unit(spots, low_middle, other_middle, w_1, w_2)
    z_one, z_two, product, dy_other = tie(z_one, z_two, product, dy_other)

    dy_pair = ordered(b, dy_run, dy_other, 0)
    dy_all, dy_own = enter(spots, blocks, dy_pair, swap_c(dy_pair))
    f_down = whole_rows(dy_all, product)
    z_one, z_two, product, f_down, w_d[0] = tie(z_one, z_two, product, f_down, w_d[0])


    f_down = scattered_all(f_down)
    d_one, d_two, lean_m = gated_unit_back(spots, dy_all, z_one, z_two, w_d)
    sent = fold_half(spots, [d_one, d_two], [w_1, w_2])
    sent, d_two, lean_m = tie(sent, d_two, lean_m)

    arrived = swap_c(sent)
    t_two = away(hidden_two, d_two)
    lean_m = lean_m[:, 0]
    lean_c = swap_c(lean_m)
    sent, mine = fold_half(spots, [d_one, d_two], [w_1, w_2], arrived)
    sent, d_one, t_two, product, lean_c = tie(sent, d_one, t_two, product, lean_c)

    crossed = swap_b(sent)
    lean_m = lean_m + lean_c
    lean_b = swap_b(lean_m)
    upper, lower = in_two(t_two)
    upper = sent_a(upper)
    f_one = whole_rows(hidden_two, d_one)
    result = fold_half(spots, [product], [w_d])
    crossed, result, f_one, upper, f_down, lean_b = tie(crossed, result, f_one, upper, f_down, lean_b)

    f_one = scattered_all(f_one)
    d_hidden = mine + crossed.astype(F32)
    m_normed = middle * m_scale
    lean = (lean_m + lean_b)[:, None] * (2.0 / width)
    d_middle = dy_own.astype(F32) + m_scale * (d_hidden - m_normed * lean)
    d_branch = d_middle.astype(LOW)
    lean_o = jnp.sum(d_middle * branch, axis=-1)
    sent = times_transposed(d_branch, row_half(w_o, 1 - c)).astype(LOW)
    sent, result, d_middle, lean_o = tie(sent, result, d_middle, lean_o)

    arrived = swap_c(sent)
    r_result = swap_c(result)
    y_down = spread_a(f_down)
    lean_o = lean_o + swap_c(lean_o)
    p_out = cross_tokens(lifted, (o_scale * d_middle).astype(LOW)).astype(LOW)
    p_out = jnp.transpose(p_out.reshape(shards, spread, part, -1), (1, 0, 2, 3))
    p_out = p_out.reshape(spread, width // spread, -1)
    t_out = [lax.dynamic_index_in_dim(p_out, (a + k) % spread, 0, False) for k in range(spread)]
    d_gated = times_transposed(d_branch, row_half(w_o, c)) + arrived.astype(F32)
    sent = columns(d_gated, (1 - b) * own, own).astype(LOW)
    mine = columns(d_gated, b * own, own)
    sent, mine, r_result, t_out, lean_o, y_down = tie(sent, mine, r_result, t_out, lean_o, y_down)

    crossed = swap_b(sent)
    lean_b = swap_b(lean_o)
    r_out = sent_a(t_out[1:])
    result, result_mine = fold_half(spots, [product], [w_d], r_result)
    crossed, result, r_out, lower, lean_b = tie(crossed, result, r_out, lower, lean_b)

    lower = sent_a(lower)
    result = swap_b(result)
    f_out = scattered(sum([x.astype(F32) for x in r_out], t_out[0].astype(F32)).astype(LOW))
    o_normed = attended * o_scale
    d_gated = mine + crossed.astype(F32)
    d_gate = (d_gated * o_normed).astype(LOW)
    lean = (lean_o + lean_b)[:, None] / width
    d_attended = (o_scale * (d_gated * gate - o_normed * lean)).astype(LOW)
    d_query, d_key, d_value = attend_back(rates, ends, z_qk, z_vg, d_attended)
    d_qk = joined(d_query, d_key)
    d_vg = joined(d_value, d_gate)
    t_qk = away(hidden_one, d_qk)
    d_qk, d_vg, t_qk, lower, result = tie(d_qk, d_vg, t_qk, lower, result)

    qk_a, qk_b = in_two(t_qk)
    qk_a = sent_a(qk_a)
    f_two = gradient_rows(spots, spread, 0, hidden_two, d_two, stacked(upper, lower))
    output, out_b = away_b((middle + (result_mine + result.astype(F32))).astype(LOW))
    f_two, qk_a, qk_b, out_b, d_qk, d_vg, f_one = tie(f_two, qk_a, qk_b, out_b, d_qk, d_vg, f_one)

    f_two = scattered(f_two)
    qk_b = sent_a(qk_b)
    output, out_c = away_c(output, out_b)
    x_down = swap_b(y_down)
    y_one = over_spread(f_one)
    t_vg = away(hidden_one, d_vg)
    sent = fold_half(spots, [d_qk, d_vg], [w_qk, w_vg])
    sent, t_vg, d_qk, d_vg, out_c, qk_b, x_down, y_one = tie(
        sent, t_vg, d_qk, d_vg, out_c, qk_b, x_down, y_one
    )

    arrived = swap_c(sent)
    vg_a, vg_b = in_two(t_vg)
    vg_a = sent_a(vg_a)
    f_qk = gradient_rows(spots, spread, 0, hidden_one, d_qk, stacked(qk_a, qk_b))
    lean_x = jnp.sum(z_qk * d_qk.astype(F32), axis=-1) + jnp.sum(z_vg * d_vg.astype(F32), axis=-1)
    arrived, vg_a, vg_b, f_qk, lean_x = tie(arrived, vg_a, vg_b, f_qk, lean_x)

    f_qk = scattered(f_qk)
    vg_b = sent_a(vg_b)
    y_one = by_spread([f_one, *y_one])
    x_one = swap_b(y_one)
    lean_x = lean_x + swap_c(lean_x)
    sent, mine = fold_half(spots, [d_qk, d_vg], [w_qk, w_vg], arrived)
    sent, mine, vg_b, lean_x, x_one, d_vg = tie(sent, mine, vg_b, lean_x, x_one, d_vg)

    crossed = swap_b(sent)
    lean_b = swap_b(lean_x)
    f_vg = scattered(gradient_rows(spots, spread, 0, hidden_one, d_vg, stacked(vg_a, vg_b)))
    four_down = spread_c(joined(y_down, x_down))
    four_one = spread_c(joined(y_one, x_one))
    y_two = over_spread(f_two)
    out_one, out_two = back_slots(ordered(c, output, out_c, 1))
    crossed, lean_b, four_one, four_down, y_two, f_out, out_one, out_two = tie(
        crossed, lean_b, four_one, four_down, y_two, f_out, out_one, out_two
    )

    d_hidden = mine + crossed.astype(F32)
    x_normed = x_own.astype(F32) * x_scale
    lean = (lean_x + lean_b)[:, None] / width
    input_grad = (d_middle + x_scale * (d_hidden - x_normed * lean)).astype(LOW)
    input_grad, grad_b = away_b(input_grad)
    out_one = send_slot(out_one, 0)
    input_grad, grad_b, out_one, out_two = tie(input_grad, grad_b, out_one, out_two)

    input_grad, grad_c = away_c(input_grad, grad_b)
    out_two = send_slot(out_two, 1)
    f_oqk = joined(f_out, f_qk)
    x_oqk = swap_b(f_oqk)
    y_vg = over_spread(f_vg)
    units = f_one.shape[1]
    [g_down] = place_quarters(spots, four_down, (0, units))
    [g_one] = place_quarters(spots, four_one, (0, units))
    grad_c, out_two, x_oqk, y_vg, g_down, g_one = tie(grad_c, out_two, x_oqk, y_vg, g_down, g_one)

    y_vg = by_spread([f_vg, *y_vg])
    x_vg = swap_b(y_vg)
    y_two = by_spread([f_two, *y_two])
    x_two = swap_b(y_two)
    f_oqk = joined(f_oqk, x_oqk)
    y_oqk = over_spread(f_oqk)
    input_grad = send_back(ordered(c, input_grad, grad_c, 1))
    output = as_batches([out_one, out_two])
    x_vg, x_two, y_oqk, input_grad, output = tie(x_vg, x_two, y_oqk, input_grad, output)

    four_vg = spread_c(joined(y_vg, x_vg))
    four_two = spread_c(joined(y_two, x_two))
    four_oqk = spread_c(by_spread([f_oqk, *y_oqk]))
    g_query, g_key = place_quarters(spots, four_oqk, (own, own), (2 * own, own))
    g_value, g_gate = place_quarters(spots, four_vg, (0, own), (own, own))
    [g_two] = place_quarters(spots, four_two, (0, units))
    g_out = features_in_order(four_oqk, 0, own)
    return output, as_batches(input_grad), g_query, g_key, g_value, g_gate, g_out, g_one, g_two, g_down


def solution(mesh):
    reps, shards = mesh.shape["rep"], mesh.shape["shard"]
    devices = mesh.devices.reshape(reps // GROUP, 2, 2, shards)
    rep = ("a", "b", "c")
    by_tokens = P(None, (*rep, "shard"), None)
    by_rows = P("shard", None)
    return jax.shard_map(
        functools.partial(body, reps, shards),
        mesh=Mesh(devices, AXES),
        in_specs=(by_tokens, by_tokens, P(None, rep, None), P(), *[by_rows] * 8),
        out_specs=(by_tokens, by_tokens, *[by_rows] * 8),
        check_vma=False,
    )
```

```python
import functools

import jax
import jax.numpy as jnp
from jax import lax
from jax.experimental import pallas as pl
from jax.experimental.pallas import tpu as pltpu
from jax.sharding import Mesh, PartitionSpec as P

HEADS = 16
HEAD_DIM = 128
STREAM = 1024
GROUP = 4
BLOCK = 256
TILE = 256
EPSILON = 1e-06
AXES = ("a", "b", "c", "shard")
OWNERS = ("a", "shard")
LOW = jnp.bfloat16
F32 = jnp.float32


def matmul(former, latter):
    return jnp.dot(former, latter, preferred_element_type=F32)


def times_transposed(former, latter):
    return lax.dot_general(former, latter, (((1,), (1,)), ((), ())), preferred_element_type=F32)


def cross_tokens(former, latter):
    return lax.dot_general(former, latter, (((0,), (0,)), ((), ())), preferred_element_type=F32)


def masked_decay(rate, ends, first, columns):
    row = first + lax.broadcasted_iota(jnp.int32, (BLOCK, 1), 0)
    column = lax.broadcasted_iota(jnp.int32, (1, columns), 1)
    begin = jnp.zeros((BLOCK, 1), jnp.int32)
    for end in ends:
        begin = jnp.where(row >= end, end, begin)
    falling = jnp.exp(-rate * (row - first).astype(F32))
    rising = jnp.exp(rate * (column - first).astype(F32))
    allowed = (column <= row) & (column >= begin)
    return jnp.where(allowed, falling * rising, 0.0)


def attend_kernel(rates, ends, zq_ref, zk_ref, zv_ref, out_ref):
    stream, head = pl.program_id(0), pl.program_id(1)
    rate = rates[head]
    bounds = [ends[stream, i] for i in range(ends.shape[1])]
    zq, zk = zq_ref[...], zk_ref[...]
    q = (zq * jax.nn.sigmoid(zq)).astype(LOW)
    k = (zk * jax.nn.sigmoid(zk)).astype(LOW)
    v = zv_ref[...].astype(LOW)
    for first in range(0, STREAM, BLOCK):
        columns = first + BLOCK
        mask = masked_decay(rate, bounds, first, columns)
        scores = times_transposed(q[first:columns], k[:columns])
        weights = (scores * mask).astype(LOW)
        out_ref[first:columns, :] = matmul(weights, v[:columns])


def attend_back_kernel(
    rates, ends, zq_ref, zk_ref, zv_ref, do_ref, dzq_ref, dzk_ref, dzv_ref, dk_ref, dv_ref
):
    stream, head = pl.program_id(0), pl.program_id(1)
    rate = rates[head]
    bounds = [ends[stream, i] for i in range(ends.shape[1])]
    zq, zk = zq_ref[...], zk_ref[...]
    sig_q, sig_k = jax.nn.sigmoid(zq), jax.nn.sigmoid(zk)
    q = (zq * sig_q).astype(LOW)
    k = (zk * sig_k).astype(LOW)
    slope_q = sig_q * (1.0 + zq * (1.0 - sig_q))
    v = zv_ref[...].astype(LOW)
    d_o = do_ref[...]
    dk_ref[...] = jnp.zeros_like(dk_ref)
    dv_ref[...] = jnp.zeros_like(dv_ref)
    for first in range(0, STREAM, BLOCK):
        columns = first + BLOCK
        rows = slice(first, columns)
        mask = masked_decay(rate, bounds, first, columns)
        weights = (times_transposed(q[rows], k[:columns]) * mask).astype(LOW)
        d_scores = (times_transposed(d_o[rows], v[:columns]) * mask).astype(LOW)
        dzq_ref[rows, :] = (matmul(d_scores, k[:columns]) * slope_q[rows]).astype(LOW)
        dk_ref[:columns, :] += cross_tokens(d_scores, q[rows])
        dv_ref[:columns, :] += cross_tokens(weights, d_o[rows])
    dzk_ref[...] = (dk_ref[...] * (sig_k * (1.0 + zk * (1.0 - sig_k)))).astype(LOW)
    dzv_ref[...] = dv_ref[...].astype(LOW)


def head_block(offset=0):
    return pl.BlockSpec((STREAM, HEAD_DIM), lambda g, h, *_: (g, h + offset))


def attend(rates, ends, z_qk, z_vg):
    heads, streams = rates.shape[0], ends.shape[0]
    work = streams * heads * STREAM * STREAM
    return pl.pallas_call(
        attend_kernel,
        out_shape=jax.ShapeDtypeStruct((streams * STREAM, heads * HEAD_DIM), F32),
        grid_spec=pltpu.PrefetchScalarGridSpec(
            num_scalar_prefetch=2,
            grid=(streams, heads),
            in_specs=[head_block(), head_block(heads), head_block()],
            out_specs=head_block(),
        ),
        compiler_params=pltpu.CompilerParams(vmem_limit_bytes=40 << 20),
        cost_estimate=pl.CostEstimate(
            flops=4 * work * HEAD_DIM, transcendentals=work // 64,
            bytes_accessed=streams * heads * STREAM * HEAD_DIM * 16,
        ),
        name="attend",
    )(rates, ends, z_qk, z_qk, z_vg)


def attend_back(rates, ends, z_qk, z_vg, d_o):
    heads, streams = rates.shape[0], ends.shape[0]
    work = streams * heads * STREAM * STREAM
    return pl.pallas_call(
        attend_back_kernel,
        out_shape=[jax.ShapeDtypeStruct((streams * STREAM, heads * HEAD_DIM), LOW)] * 3,
        grid_spec=pltpu.PrefetchScalarGridSpec(
            num_scalar_prefetch=2,
            grid=(streams, heads),
            in_specs=[head_block(), head_block(heads), head_block(), head_block()],
            out_specs=[head_block()] * 3,
            scratch_shapes=[pltpu.VMEM((STREAM, HEAD_DIM), F32)] * 2,
        ),
        compiler_params=pltpu.CompilerParams(vmem_limit_bytes=40 << 20),
        cost_estimate=pl.CostEstimate(
            flops=10 * work * HEAD_DIM, transcendentals=work // 64,
            bytes_accessed=streams * heads * STREAM * HEAD_DIM * 20,
        ),
        name="attend_back",
    )(rates, ends, z_qk, z_qk, z_vg, d_o)


def chunk_copies(chunks, buffer, sems, turn, half=None):
    count, size = len(chunks), chunks[0].shape[0]
    if count == 1:
        rows = buffer.shape[0]
        first = 0 if half is None else pl.multiple_of(half * rows, rows)
        return [(None, pltpu.make_async_copy(chunks[0].at[pl.ds(first, rows)], buffer, sems.at[0]))]
    copies = []
    for k, chunk in enumerate(chunks):
        index = lax.rem(turn - k + count, count)
        wanted = None
        if half is not None:
            wanted = lax.div(index, count // 2) == half
            index = lax.rem(index, count // 2)
        target = buffer.at[pl.ds(pl.multiple_of(index * size, size), size)]
        copies.append((wanted, pltpu.make_async_copy(chunk, target, sems.at[k])))
    return copies


def each(copies, act):
    for wanted, copy in copies:
        if wanted is None:
            act(copy)
        else:
            pl.when(wanted)(functools.partial(act, copy))


def start(copies):
    each(copies, lambda copy: copy.start())


def finish(copies):
    each(copies, lambda copy: copy.wait())


def estimate(flops, *arrays):
    moved = sum(x.size * x.dtype.itemsize for x in arrays)
    return pl.CostEstimate(flops=flops, transcendentals=0, bytes_accessed=moved)


def limit(mebibytes):
    return pltpu.CompilerParams(vmem_limit_bytes=mebibytes << 20)


ANYWHERE = pl.BlockSpec(memory_space=pl.ANY)


def weight_buffer(chunks, share=1):
    size = len(chunks) * chunks[0].shape[0] // share
    return [pltpu.VMEM((size, chunks[0].shape[1]), LOW), pltpu.SemaphoreType.DMA((len(chunks),))]


def tile_rows(width, column=0):
    return pl.BlockSpec((TILE, width), lambda i, *_: (i, column))


def joined_rows(width, tiles):
    spec = pl.BlockSpec((TILE, width), lambda i, s: (i // (2 * tiles) * tiles + i % tiles, 0))
    return [spec, spec]


def enter_kernel(tiles, blocks, project, spots, own_ref, other_ref, *refs):
    i = pl.program_id(0)
    mine = lax.rem(lax.div(i, tiles), 2) == spots[0]
    rows = jnp.where(mine, own_ref[...], other_ref[...])
    part = rows.shape[1] // len(blocks)
    permuted = jnp.concatenate([rows[:, n * part : (n + 1) * part] for n in blocks], axis=1)
    if not project:
        all_ref, quarter_ref = refs
        all_ref[...] = permuted
        held = all_ref
    else:
        chunks, (h_ref, z_ref, scale_ref, quarter_ref, held, buffer, sems) = refs[:-7], refs[-7:]
        held[...] = permuted
        copies = chunk_copies(chunks, buffer, sems, spots[2])

        @pl.when(i == 0)
        def _():
            start(copies)

        x = rows.astype(F32)
        scale = lax.rsqrt(jnp.mean(x * x, axis=-1, keepdims=True) + EPSILON)
        scale_ref[...] = scale
        hidden = (permuted.astype(F32) * scale).astype(LOW)
        h_ref[...] = hidden

        @pl.when(i == 0)
        def _():
            finish(copies)

        z_ref[...] = matmul(hidden, buffer[...])
    size = quarter_ref.shape[1]
    quarter_ref[...] = held[:, pl.ds(pl.multiple_of(spots[1] * size, size), size)]


def enter(spots, blocks, own, other, chunks=()):
    width = own.shape[1]
    count, tiles = 2 * own.shape[0], own.shape[0] // TILE // 2
    shape = jax.ShapeDtypeStruct
    quarter = shape((count, width // GROUP), LOW)
    if chunks:
        columns = chunks[0].shape[1]
        outs = [shape((count, width), LOW), shape((count, columns), F32), shape((count, 1), F32), quarter]
        scratch = [pltpu.VMEM((TILE, width), LOW), *weight_buffer(chunks)]
    else:
        columns, scratch = 0, []
        outs = [shape((count, width), LOW), quarter]
    return pl.pallas_call(
        functools.partial(enter_kernel, tiles, blocks, bool(chunks)),
        out_shape=outs,
        grid_spec=pltpu.PrefetchScalarGridSpec(
            num_scalar_prefetch=1,
            grid=(count // TILE,),
            in_specs=joined_rows(width, tiles) + [ANYWHERE] * len(chunks),
            out_specs=[tile_rows(o.shape[1]) for o in outs],
            scratch_shapes=scratch,
        ),
        compiler_params=limit(40),
        cost_estimate=estimate(2 * count * width * columns, own, other, *chunks, *outs),
        name="enter",
    )(spots, own, other, *chunks)


def project_kernel(spots, h_ref, *refs):
    chunks, (z_ref, buffer, sems) = refs[:-3], refs[-3:]
    copies = chunk_copies(chunks, buffer, sems, spots[2])

    @pl.when(pl.program_id(0) == 0)
    def _():
        start(copies)
        finish(copies)

    z_ref[...] = matmul(h_ref[...], buffer[...])


def project(spots, hidden, chunks):
    count, width = hidden.shape
    out = jax.ShapeDtypeStruct((count, chunks[0].shape[1]), F32)
    return pl.pallas_call(
        project_kernel,
        out_shape=out,
        grid_spec=pltpu.PrefetchScalarGridSpec(
            num_scalar_prefetch=1,
            grid=(count // TILE,),
            in_specs=[tile_rows(width)] + [ANYWHERE] * len(chunks),
            out_specs=tile_rows(out.shape[1]),
            scratch_shapes=weight_buffer(chunks),
        ),
        compiler_params=limit(40),
        cost_estimate=estimate(2 * count * width * out.shape[1], hidden, *chunks, out),
        name="project",
    )(spots, hidden, *chunks)


def unit_kernel(spots, own_ref, other_ref, *refs):
    chunks, rest = refs[:-9], refs[-9:]
    h_ref, one_ref, two_ref, product_ref, scale_ref, first, second, sem_one, sem_two = rest
    split = len(chunks) // 2
    copies = [
        chunk_copies(chunks[:split], first, sem_one, spots[2]),
        chunk_copies(chunks[split:], second, sem_two, spots[2]),
    ]
    begins = pl.program_id(0) == 0

    @pl.when(begins)
    def _():
        start(copies[0])
        start(copies[1])

    mine, other = own_ref[...], other_ref[...]
    swapped = spots[0] == 1
    middle = jnp.concatenate(
        [jnp.where(swapped, other, mine), jnp.where(swapped, mine, other)], axis=1
    ).astype(F32)
    scale = lax.rsqrt(jnp.mean(middle * middle, axis=-1, keepdims=True) + EPSILON)
    scale_ref[...] = scale
    hidden = (middle * scale).astype(LOW)
    h_ref[...] = hidden

    @pl.when(begins)
    def _():
        finish(copies[0])

    z_one = matmul(hidden, first[...])

    @pl.when(begins)
    def _():
        finish(copies[1])

    z_two = matmul(hidden, second[...])
    one_ref[...] = z_one.astype(LOW)
    two_ref[...] = z_two.astype(LOW)
    product_ref[...] = (z_one * z_two).astype(LOW)


def gated_unit(spots, own, other, first, second):
    count, width, units = own.shape[0], 2 * own.shape[1], first[0].shape[1]
    shape = jax.ShapeDtypeStruct
    outs = [shape((count, width), LOW)] + [shape((count, units), LOW)] * 3 + [shape((count, 1), F32)]
    (buffer, sems) = weight_buffer(first)
    return pl.pallas_call(
        unit_kernel,
        out_shape=outs,
        grid_spec=pltpu.PrefetchScalarGridSpec(
            num_scalar_prefetch=1,
            grid=(count // TILE,),
            in_specs=[tile_rows(width // 2)] * 2 + [ANYWHERE] * (2 * len(first)),
            out_specs=[tile_rows(o.shape[1]) for o in outs],
            scratch_shapes=[buffer, buffer, sems, sems],
        ),
        compiler_params=limit(48),
        cost_estimate=estimate(4 * count * width * units, own, other, *first, *second, *outs),
        name="gated_unit",
    )(spots, own, other, *first, *second)


def unit_back_kernel(spots, dy_ref, one_ref, two_ref, *refs):
    chunks, (d_one_ref, d_two_ref, sum_ref, buffer, sems) = refs[:-5], refs[-5:]
    copies = chunk_copies(chunks, buffer, sems, spots[2])

    @pl.when(pl.program_id(0) == 0)
    def _():
        start(copies)
        finish(copies)

    d_product = matmul(dy_ref[...], buffer[...])
    z_one, z_two = one_ref[...].astype(F32), two_ref[...].astype(F32)
    d_one = d_product * z_two
    d_one_ref[...] = d_one.astype(LOW)
    d_two_ref[...] = (d_product * z_one).astype(LOW)
    sum_ref[...] = jnp.sum(d_one * z_one, axis=-1, keepdims=True)


def gated_unit_back(spots, dy, z_one, z_two, chunks):
    count, width, units = dy.shape[0], dy.shape[1], z_one.shape[1]
    shape = jax.ShapeDtypeStruct
    outs = [shape((count, units), LOW)] * 2 + [shape((count, 1), F32)]
    return pl.pallas_call(
        unit_back_kernel,
        out_shape=outs,
        grid_spec=pltpu.PrefetchScalarGridSpec(
            num_scalar_prefetch=1,
            grid=(count // TILE,),
            in_specs=[tile_rows(width), tile_rows(units), tile_rows(units)] + [ANYWHERE] * len(chunks),
            out_specs=[tile_rows(o.shape[1]) for o in outs],
            scratch_shapes=weight_buffer(chunks),
        ),
        compiler_params=limit(40),
        cost_estimate=estimate(2 * count * width * units, dy, z_one, z_two, *chunks, *outs),
        name="gated_unit_back",
    )(spots, dy, z_one, z_two, *chunks)


def fold_kernel(members, keeps, spots, *refs):
    values, refs = refs[:members], refs[members:]
    arrived, refs = (refs[0], refs[1:]) if keeps else (None, refs)
    outs = 2 if keeps else 1
    chunks, refs = refs[: -outs - 2 * members], refs[-outs - 2 * members :]
    outs, buffers, sems = refs[:outs], refs[outs : outs + members], refs[outs + members :]
    each_count = len(chunks) // members
    half = spots[0] if keeps else 1 - spots[0]
    begins = pl.program_id(0) == 0
    copies = [
        chunk_copies(chunks[m * each_count : (m + 1) * each_count], buffers[m], sems[m], spots[2], half)
        for m in range(members)
    ]

    @pl.when(begins)
    def _():
        for m in range(members):
            start(copies[m])

    whole = None
    for m in range(members):
        pl.when(begins)(functools.partial(finish, copies[m]))
        term = times_transposed(values[m][...], buffers[m][...])
        whole = term if whole is None else whole + term
    if not keeps:
        outs[0][...] = whole.astype(LOW)
    else:
        whole = whole + arrived[...].astype(F32)
        size = whole.shape[1] // 2
        upper = spots[3] == 1
        outs[0][...] = jnp.where(upper, whole[:, :size], whole[:, size:]).astype(LOW)
        outs[1][...] = jnp.where(upper, whole[:, size:], whole[:, :size])


def fold_half(spots, values, weights, arrived=None):
    count = values[0].shape[0]
    half = len(weights[0]) * weights[0][0].shape[0] // 2
    shape = jax.ShapeDtypeStruct
    if arrived is None:
        outs, extra = [shape((count, half), LOW)], []
    else:
        outs, extra = [shape((count, half // 2), LOW), shape((count, half // 2), F32)], [arrived]
    buffers, sems = zip(*[weight_buffer(w, 2) for w in weights])
    chunks = [x for w in weights for x in w]
    flops = sum(2 * count * half * v.shape[1] for v in values)
    found = pl.pallas_call(
        functools.partial(fold_kernel, len(values), arrived is not None),
        out_shape=outs,
        grid_spec=pltpu.PrefetchScalarGridSpec(
            num_scalar_prefetch=1,
            grid=(count // TILE,),
            in_specs=[tile_rows(v.shape[1]) for v in values]
            + [tile_rows(half)] * len(extra)
            + [ANYWHERE] * len(chunks),
            out_specs=[tile_rows(o.shape[1]) for o in outs],
            scratch_shapes=[*buffers, *sems],
        ),
        compiler_params=limit(40),
        cost_estimate=estimate(flops, *values, *extra, *chunks[: len(chunks) // 2], *outs),
        name="fold_half",
    )(spots, *values, *extra, *chunks)
    return found[0] if arrived is None else found


def gradient_kernel(spots, left_ref, right_ref, *refs):
    found = cross_tokens(left_ref[...], right_ref[...])
    for arrived_ref in refs[:-1]:
        found = found + arrived_ref[...].astype(F32)
    refs[-1][...] = found.astype(LOW)


def gradient_rows(spots, spread, k, left, right, arrived=()):
    count, columns = right.shape
    rows = left.shape[1] // (1 if k is None else spread)
    tiles = rows // TILE

    def block(i, s):
        return (0, i if k is None else lax.rem(s[2] + k, spread) * tiles + i)

    out = jax.ShapeDtypeStruct((rows, columns), LOW)
    return pl.pallas_call(
        gradient_kernel,
        out_shape=out,
        grid_spec=pltpu.PrefetchScalarGridSpec(
            num_scalar_prefetch=1,
            grid=(tiles,),
            in_specs=[
                pl.BlockSpec((count, TILE), block),
                pl.BlockSpec((count, columns), lambda i, s: (0, 0), pipeline_mode=pl.Buffered(1)),
            ]
            + [tile_rows(columns)] * len(arrived),
            out_specs=tile_rows(columns),
        ),
        compiler_params=limit(40),
        cost_estimate=estimate(2 * count * rows * columns, right, out, out, *arrived),
        name="gradient_rows",
    )(spots, left, right, *arrived)


def place_kernel(cuts, spots, *refs):
    quarter = pl.program_id(0)
    cross = lax.rem(lax.div(quarter, 2) + spots[0], 2) * 2 + lax.rem(lax.rem(quarter, 2) + spots[3], 2)
    for n in range(4):

        @pl.when(cross == n)
        def _():
            for (first, size), out_ref in zip(cuts, refs[4:]):
                out_ref[...] = refs[n][:, first : first + size].astype(F32)


def place_quarters(spots, pairs, *cuts):
    rows, columns = pairs[0].shape[0], pairs[0].shape[1] // 2
    outs = [jax.ShapeDtypeStruct((rows, GROUP * size), F32) for _, size in cuts]

    def block(index):
        return pl.BlockSpec((rows, columns), lambda q, s: (0, index), pipeline_mode=pl.Buffered(1))

    return pl.pallas_call(
        functools.partial(place_kernel, cuts),
        out_shape=outs,
        grid_spec=pltpu.PrefetchScalarGridSpec(
            num_scalar_prefetch=1,
            grid=(GROUP,),
            in_specs=[block(0), block(1), block(0), block(1)],
            out_specs=[pl.BlockSpec((rows, size), lambda q, s: (0, q)) for _, size in cuts],
        ),
        compiler_params=limit(40),
        cost_estimate=estimate(0, *pairs, *outs),
        name="place_quarters",
    )(spots, pairs[0], pairs[0], pairs[1], pairs[1])


def tie(*values):
    return lax.optimization_barrier(values)


def body(reps, shards, tokens, cotangent, lengths, decay_rates, *weights):
    spread = reps // GROUP
    place = lax.axis_index("shard")
    a, b, c = lax.axis_index("a"), lax.axis_index("b"), lax.axis_index("c")
    quarter = 2 * c + b
    micro, run, width = tokens.shape
    half, own = width // 2, width // GROUP
    streams = micro * GROUP // shards
    per_block = STREAM // run // GROUP * streams
    rows = width // shards
    part = rows // spread
    columns = functools.partial(lax.dynamic_slice_in_dim, axis=1)
    spots = jnp.stack([c, quarter, a, b]).astype(jnp.int32)
    blocks = [z * spread + k for k in range(spread) for z in range(shards)]

    def move(x, target):
        pairs = [(r * shards + s, target(r) * shards + s) for r in range(reps) for s in range(shards)]
        return lax.ppermute(x, AXES, pairs)

    def swap_c(x):
        return move(x, lambda r: r ^ 1)

    def swap_b(x):
        return move(x, lambda r: r ^ 2)

    def joined(*parts):
        return jnp.concatenate(parts, axis=1)

    def shift_a(x, k):
        return move(x, lambda r: (r + GROUP * k) % reps)

    def ordered(index, mine, other, axis):
        return jnp.where(
            index == 0,
            jnp.concatenate([mine, other], axis),
            jnp.concatenate([other, mine], axis),
        )


    def batch_of(s):
        return s // (shards // micro)

    def origin(r, s, p):
        run_id = (r % GROUP) * per_block + p
        stream, piece = run_id // shards, run_id % shards
        member = s % GROUP if streams == 1 else 2 * stream + s % 2
        return (r // GROUP) * GROUP + member, piece

    def routes(p):
        found = []
        for r in range(reps):
            for s in range(shards):
                from_r, from_s = origin(r, s, p ^ batch_of(s))
                found.append((from_r * shards + from_s, r * shards + s))
        return found

    def natural(x):
        return jnp.concatenate(
            [
                x[:, (k * shards + z) * part : (k * shards + z + 1) * part]
                for z in range(shards)
                for k in range(spread)
            ],
            axis=1,
        )

    def bring(x):
        arrived = [
            lax.ppermute(lax.dynamic_index_in_dim(x, (place + p) % 2, 0, False), AXES, routes(p))
            for p in range(2)
        ]
        return ordered(batch_of(place), *arrived, 0)

    def back_slots(x):
        slots = natural(x).reshape(2, run, width)
        return [
            lax.dynamic_index_in_dim(slots, (batch_of(place) + p) % 2, 0, False) for p in range(2)
        ]

    def send_slot(x, p):
        return lax.ppermute(x, AXES, [(to, origin) for origin, to in routes(p)])

    def send_back(x):
        return [send_slot(slot, p) for p, slot in enumerate(back_slots(x))]

    def as_batches(arrived):
        return ordered(place % 2, arrived[0][None], arrived[1][None], 0)


    def gather_b(x):
        return ordered(b, x, swap_b(x), 1)

    def gather_c(x):
        return ordered(c, x, swap_c(x), 1)

    def gather_rows_b(x):
        return ordered(b, x, swap_b(x), 0)

    def total(x):
        x = x + swap_c(x)
        return x + swap_b(x)

    def fold_c(product):
        sent = swap_c(product(1 - c).astype(LOW))
        return product(c) + sent.astype(F32)

    def fold_b(x):
        sent = swap_b(columns(x, (1 - b) * own, own).astype(LOW))
        return columns(x, b * own, own) + sent.astype(F32)


    pick = functools.partial(lax.dynamic_index_in_dim, keepdims=False)

    def away_b(x):
        cut = x.reshape(2, 2, -1, own)
        return pick(cut, b, 0), swap_b(pick(cut, 1 - b, 0))

    def away_c(mine, arrived):
        both = ordered(b, mine, arrived, 2)
        return pick(both, c, 0), swap_c(pick(both, 1 - c, 0))

    def to_runs(x):
        return ordered(c, *away_c(*away_b(x)), 1)


    def own_features(w):
        count = shards * spread // GROUP
        cut = []
        for i in range(count):
            block = quarter * count + i
            cut.append(columns(w, (block % shards) * rows + (block // shards) * part, part))
        return jnp.concatenate(cut, axis=1)

    def own_units(w):
        return columns(w, quarter * (w.shape[1] // GROUP), w.shape[1] // GROUP)

    def over_shards(*members):
        cut = jnp.concatenate(members, axis=1) if len(members) > 1 else members[0]
        piece = lax.dynamic_slice_in_dim(cut, a * part, part, 0)
        return lax.all_gather(piece, "shard", axis=0, tiled=True)

    def over_owners(w):
        piece = lax.dynamic_slice_in_dim(w, a * part, part, 0)
        return lax.all_gather(piece, OWNERS, axis=0, tiled=True)

    def over_spread(x):
        return [shift_a(x, k) for k in range(1, spread)]

    def by_spread(relative):
        if spread == 2:
            return ordered(a, relative[0], relative[1], 0)
        stacked = jnp.stack(relative, 0)
        pick = functools.partial(lax.dynamic_index_in_dim, axis=0, keepdims=False)
        return jnp.concatenate([pick(stacked, (a - j) % spread) for j in range(spread)], axis=0)

    def in_row_order(x):
        cut = x.reshape(spread, shards, part, -1)
        return jnp.transpose(cut, (1, 0, 2, 3)).reshape(width, -1)

    def row_half(w, h):
        return lax.dynamic_slice_in_dim(w, h * half, half, 0)


    def away(left, right):
        return [gradient_rows(spots, spread, k, left, right) for k in range(1, spread)]

    def in_two(terms):
        middles = [x.shape[0] // 2 for x in terms]
        return [x[:m] for x, m in zip(terms, middles)], [x[m:] for x, m in zip(terms, middles)]

    def stacked(upper, lower):
        return [jnp.concatenate(pair, axis=0) for pair in zip(upper, lower)]

    def sent_a(terms):
        return [shift_a(x, k + 1) for k, x in enumerate(terms)]

    def scattered(x):
        return lax.psum_scatter(x, "shard", scatter_dimension=0, tiled=True)

    def whole_rows(left, right):
        return gradient_rows(spots, spread, None, left, right)

    def scattered_all(x):
        return lax.psum_scatter(x, OWNERS, scatter_dimension=0, tiled=True)

    def summed(left, right, arrived):
        return scattered(gradient_rows(spots, spread, 0, left, right, arrived))

    def spread_a(x):
        return by_spread([x] + over_spread(x))

    def spread_b(x):
        return jnp.concatenate([x, swap_b(x)], axis=1)

    def spread_c(pair):
        return pair, swap_c(pair)

    def features_in_order(pairs, first, size):
        full = pairs[0].shape[1] // 2
        cut = [x[:, i * full + first : i * full + first + size] for x in pairs for i in range(2)]
        pair = [ordered(b, cut[n], cut[n + 1], 1) for n in (0, 2)]
        return natural(ordered(c, pair[0], pair[1], 1)).astype(F32)


    w_query, w_key, w_value, w_gate, w_out, w_one, w_two, w_down = weights
    g_qk = over_shards(own_units(w_query), own_units(w_key))
    g_vg = over_shards(own_units(w_value), own_units(w_gate))
    g_o = over_shards(own_features(w_out))
    g_1 = over_shards(own_units(w_one))
    g_2 = over_shards(own_units(w_two))
    w_d = [over_owners(own_units(w_down))]

    heads = HEADS // GROUP
    rates = lax.dynamic_slice_in_dim(decay_rates, quarter * heads, heads, 0)
    cuts = gather_rows_b(lengths.reshape(1, -1))
    cuts = ordered(c, cuts, swap_c(cuts), 0).reshape(GROUP, micro, -1)
    if streams == 1:
        batch = place // GROUP
        member = place % GROUP
        chosen = lax.dynamic_slice_in_dim(cuts, 2 * (member % 2) + member // 2, 1, 0)
    else:
        batch = place // 2
        chosen = lax.dynamic_index_in_dim(cuts.reshape(2, 2, micro, -1), place % 2, 0, False)
    chosen = lax.dynamic_index_in_dim(chosen, batch, 1, False)
    seq_ends = [chosen[:, 0]]
    for i in range(1, chosen.shape[1]):
        seq_ends.append(seq_ends[-1] + chosen[:, i])
    ends = jnp.stack(seq_ends, axis=1)

    x_run = bring(tokens)
    x_run, g_qk = tie(x_run, g_qk)

    x_pair = gather_rows_b(x_run)
    s_qk = over_spread(g_qk)
    x_pair, s_qk, g_vg = tie(x_pair, s_qk, g_vg)

    s_vg = over_spread(g_vg)
    w_qk = [g_qk, *s_qk]
    hidden_one, z_qk, x_scale, x_own = enter(spots, blocks, x_pair, swap_c(x_pair), w_qk)
    z_qk, hidden_one, s_vg, g_o = tie(z_qk, hidden_one, s_vg, g_o)

    s_o = over_spread(g_o)
    w_vg = [g_vg, *s_vg]
    z_vg = project(spots, hidden_one, w_vg)
    attended = attend(rates, ends, z_qk, z_vg)
    gate = z_vg[:, own:]
    o_scale = lax.rsqrt(total(jnp.sum(attended * attended, axis=-1)) / width + EPSILON)[:, None]
    lifted = (attended * gate).astype(LOW)
    lifted, s_o, g_1, cotangent = tie(lifted, s_o, g_1, cotangent)

    s_1 = over_spread(g_1)
    lifted = gather_b(lifted)
    lifted, s_1, g_2, o_scale, cotangent = tie(lifted, s_1, g_2, o_scale, cotangent)

    s_2 = over_spread(g_2)
    dy_run = bring(cotangent)
    lifted = gather_c(lifted)
    w_o = in_row_order(by_spread([g_o, *s_o]))
    branch = o_scale * matmul(lifted, w_o)
    middle = x_own.astype(F32) + branch
    low_middle = gather_b(middle.astype(LOW))
    low_middle, s_2, dy_run = tie(low_middle, s_2, dy_run)

    other_middle = swap_c(low_middle)
    dy_other = swap_b(dy_run)
    w_1, w_2 = [g_1, *s_1], [g_2, *s_2]
    hidden_two, z_one, z_two, product, m_scale = gated_unit(spots, low_middle, other_middle, w_1, w_2)
    z_one, z_two, product, dy_other = tie(z_one, z_two, product, dy_other)

    dy_pair = ordered(b, dy_run, dy_other, 0)
    dy_all, dy_own = enter(spots, blocks, dy_pair, swap_c(dy_pair))
    f_down = whole_rows(dy_all, product)
    z_one, z_two, product, f_down, w_d[0] = tie(z_one, z_two, product, f_down, w_d[0])


    f_down = scattered_all(f_down)
    d_one, d_two, lean_m = gated_unit_back(spots, dy_all, z_one, z_two, w_d)
    sent = fold_half(spots, [d_one, d_two], [w_1, w_2])
    sent, d_two, lean_m = tie(sent, d_two, lean_m)

    arrived = swap_c(sent)
    t_two = away(hidden_two, d_two)
    lean_m = lean_m[:, 0]
    lean_c = swap_c(lean_m)
    sent, mine = fold_half(spots, [d_one, d_two], [w_1, w_2], arrived)
    sent, d_one, t_two, product, lean_c = tie(sent, d_one, t_two, product, lean_c)

    crossed = swap_b(sent)
    lean_m = lean_m + lean_c
    lean_b = swap_b(lean_m)
    upper, lower = in_two(t_two)
    upper = sent_a(upper)
    f_one = whole_rows(hidden_two, d_one)
    result = fold_half(spots, [product], [w_d])
    crossed, result, f_one, upper, f_down, lean_b = tie(crossed, result, f_one, upper, f_down, lean_b)

    f_one = scattered_all(f_one)
    d_hidden = mine + crossed.astype(F32)
    m_normed = middle * m_scale
    lean = (lean_m + lean_b)[:, None] * (2.0 / width)
    d_middle = dy_own.astype(F32) + m_scale * (d_hidden - m_normed * lean)
    d_branch = d_middle.astype(LOW)
    lean_o = jnp.sum(d_middle * branch, axis=-1)
    sent = times_transposed(d_branch, row_half(w_o, 1 - c)).astype(LOW)
    sent, result, d_middle, lean_o = tie(sent, result, d_middle, lean_o)

    arrived = swap_c(sent)
    r_result = swap_c(result)
    y_down = spread_a(f_down)
    lean_o = lean_o + swap_c(lean_o)
    p_out = cross_tokens(lifted, (o_scale * d_middle).astype(LOW)).astype(LOW)
    p_out = jnp.transpose(p_out.reshape(shards, spread, part, -1), (1, 0, 2, 3))
    p_out = p_out.reshape(spread, width // spread, -1)
    t_out = [lax.dynamic_index_in_dim(p_out, (a + k) % spread, 0, False) for k in range(spread)]
    d_gated = times_transposed(d_branch, row_half(w_o, c)) + arrived.astype(F32)
    sent = columns(d_gated, (1 - b) * own, own).astype(LOW)
    mine = columns(d_gated, b * own, own)
    sent, mine, r_result, t_out, lean_o, y_down = tie(sent, mine, r_result, t_out, lean_o, y_down)

    crossed = swap_b(sent)
    lean_b = swap_b(lean_o)
    r_out = sent_a(t_out[1:])
    result, result_mine = fold_half(spots, [product], [w_d], r_result)
    crossed, result, r_out, lower, lean_b = tie(crossed, result, r_out, lower, lean_b)

    lower = sent_a(lower)
    result = swap_b(result)
    f_out = scattered(sum([x.astype(F32) for x in r_out], t_out[0].astype(F32)).astype(LOW))
    o_normed = attended * o_scale
    d_gated = mine + crossed.astype(F32)
    d_gate = (d_gated * o_normed).astype(LOW)
    lean = (lean_o + lean_b)[:, None] / width
    d_attended = (o_scale * (d_gated * gate - o_normed * lean)).astype(LOW)
    d_query, d_key, d_value = attend_back(rates, ends, z_qk, z_vg, d_attended)
    d_qk = joined(d_query, d_key)
    d_vg = joined(d_value, d_gate)
    t_qk = away(hidden_one, d_qk)
    d_qk, d_vg, t_qk, lower, result = tie(d_qk, d_vg, t_qk, lower, result)

    qk_a, qk_b = in_two(t_qk)
    qk_a = sent_a(qk_a)
    f_two = gradient_rows(spots, spread, 0, hidden_two, d_two, stacked(upper, lower))
    output, out_b = away_b((middle + (result_mine + result.astype(F32))).astype(LOW))
    f_two, qk_a, qk_b, out_b, d_qk, d_vg, f_one = tie(f_two, qk_a, qk_b, out_b, d_qk, d_vg, f_one)

    f_two = scattered(f_two)
    qk_b = sent_a(qk_b)
    output, out_c = away_c(output, out_b)
    x_down = swap_b(y_down)
    y_one = over_spread(f_one)
    t_vg = away(hidden_one, d_vg)
    sent = fold_half(spots, [d_qk, d_vg], [w_qk, w_vg])
    sent, t_vg, d_qk, d_vg, out_c, qk_b, x_down, y_one = tie(
        sent, t_vg, d_qk, d_vg, out_c, qk_b, x_down, y_one
    )

    arrived = swap_c(sent)
    vg_a, vg_b = in_two(t_vg)
    vg_a = sent_a(vg_a)
    f_qk = gradient_rows(spots, spread, 0, hidden_one, d_qk, stacked(qk_a, qk_b))
    lean_x = jnp.sum(z_qk * d_qk.astype(F32), axis=-1) + jnp.sum(z_vg * d_vg.astype(F32), axis=-1)
    arrived, vg_a, vg_b, f_qk, lean_x = tie(arrived, vg_a, vg_b, f_qk, lean_x)

    f_qk = scattered(f_qk)
    vg_b = sent_a(vg_b)
    y_one = by_spread([f_one, *y_one])
    x_one = swap_b(y_one)
    lean_x = lean_x + swap_c(lean_x)
    sent, mine = fold_half(spots, [d_qk, d_vg], [w_qk, w_vg], arrived)
    sent, mine, vg_b, lean_x, x_one, d_vg = tie(sent, mine, vg_b, lean_x, x_one, d_vg)

    crossed = swap_b(sent)
    lean_b = swap_b(lean_x)
    f_vg = scattered(gradient_rows(spots, spread, 0, hidden_one, d_vg, stacked(vg_a, vg_b)))
    four_down = spread_c(joined(y_down, x_down))
    four_one = spread_c(joined(y_one, x_one))
    y_two = over_spread(f_two)
    out_one, out_two = back_slots(ordered(c, output, out_c, 1))
    crossed, lean_b, four_one, four_down, y_two, f_out, out_one, out_two = tie(
        crossed, lean_b, four_one, four_down, y_two, f_out, out_one, out_two
    )

    d_hidden = mine + crossed.astype(F32)
    x_normed = x_own.astype(F32) * x_scale
    lean = (lean_x + lean_b)[:, None] / width
    input_grad = (d_middle + x_scale * (d_hidden - x_normed * lean)).astype(LOW)
    input_grad, grad_b = away_b(input_grad)
    out_one = send_slot(out_one, 0)
    input_grad, grad_b, out_one, out_two = tie(input_grad, grad_b, out_one, out_two)

    input_grad, grad_c = away_c(input_grad, grad_b)
    out_two = send_slot(out_two, 1)
    f_oqk = joined(f_out, f_qk)
    x_oqk = swap_b(f_oqk)
    y_vg = over_spread(f_vg)
    units = f_one.shape[1]
    [g_down] = place_quarters(spots, four_down, (0, units))
    grad_c, out_two, x_oqk, y_vg, g_down, *four_one = tie(grad_c, out_two, x_oqk, y_vg, g_down, *four_one)

    y_vg = by_spread([f_vg, *y_vg])
    x_vg = swap_b(y_vg)
    y_two = by_spread([f_two, *y_two])
    x_two = swap_b(y_two)
    f_oqk = joined(f_oqk, x_oqk)
    y_oqk = over_spread(f_oqk)
    input_grad = send_back(ordered(c, input_grad, grad_c, 1))
    output = as_batches([out_one, out_two])
    [g_one] = place_quarters(spots, four_one, (0, units))
    x_vg, x_two, y_oqk, input_grad, output, g_one = tie(x_vg, x_two, y_oqk, input_grad, output, g_one)

    four_vg = spread_c(joined(y_vg, x_vg))
    four_two = spread_c(joined(y_two, x_two))
    four_oqk = spread_c(by_spread([f_oqk, *y_oqk]))
    g_query, g_key = place_quarters(spots, four_oqk, (own, own), (2 * own, own))
    g_value, g_gate = place_quarters(spots, four_vg, (0, own), (own, own))
    [g_two] = place_quarters(spots, four_two, (0, units))
    g_out = features_in_order(four_oqk, 0, own)
    return output, as_batches(input_grad), g_query, g_key, g_value, g_gate, g_out, g_one, g_two, g_down


def solution(mesh):
    reps, shards = mesh.shape["rep"], mesh.shape["shard"]
    devices = mesh.devices.reshape(reps // GROUP, 2, 2, shards)
    rep = ("a", "b", "c")
    by_tokens = P(None, (*rep, "shard"), None)
    by_rows = P("shard", None)
    return jax.shard_map(
        functools.partial(body, reps, shards),
        mesh=Mesh(devices, AXES),
        in_specs=(by_tokens, by_tokens, P(None, rep, None), P(), *[by_rows] * 8),
        out_specs=(by_tokens, by_tokens, *[by_rows] * 8),
        check_vma=False,
    )
```
